32 devices in a mesh: expert: 4 (over x, core), fsdp: 8 (over z, y).
Axes of the slice: x: 2, y: 2, z: 4, core: 2. Of those that a mesh axis runs over, the one named last changes fastest.
Arguments:
- inputs: bfloat16 [12288, 1024], P(('expert', 'fsdp')), may hold values from -6 to 6
- w_qkv: bfloat16 [1024, 3072], P(('expert', 'fsdp')), may hold values from -0.1875 to 0.1875
- w_out: bfloat16 [1024, 1024], P(('expert', 'fsdp')), may hold values from -3 to 3
- attn_gain: bfloat16 [1024], P(('expert', 'fsdp')), may hold values from 0.5 to 1.5
- moe_gain: bfloat16 [1024], P(('expert', 'fsdp')), may hold values from 0.5 to 1.5
- w_router: bfloat16 [1024, 4], P(('expert', 'fsdp')), may hold values from -0.125 to 0.125
- bias_table: bfloat16 [512], P(('expert', 'fsdp')), may hold values from -4 to 4
- w_gate: bfloat16 [4, 1024, 2816], P('expert', None, 'fsdp'), may hold values from -0.1875 to 0.1875
- w_up: bfloat16 [4, 1024, 2816], P('expert', None, 'fsdp'), may hold values from -0.1875 to 0.1875
- w_down: bfloat16 [4, 2816, 1024], P('expert', 'fsdp'), may hold values from -0.15625 to 0.15625
- routes: int32 [12288, 2], P(('expert', 'fsdp')), may hold values from 0 to 3, as said below
- slot_order: int32 [12288, 2], P(('expert', 'fsdp')), may hold values from 0 to 240, as said below
- group_map: int32 [32], P(('expert', 'fsdp')), may hold values from 0 to 1, as said below
- buckets: int32 [1152], replicated, may hold values from 0 to 31, as said below
- grad_output: bfloat16 [12288, 1024], P(('expert', 'fsdp')), may hold values from -6 to 6
Outputs:
- output: bfloat16 [12288, 1024], P(('expert', 'fsdp'))
- router_losses: float32 [32, 2], P(('expert', 'fsdp'))
- grad_inputs: float32 [12288, 1024], P(('expert', 'fsdp'))
- grad_w_qkv: float32 [1024, 3072], P(('expert', 'fsdp'))
- grad_w_out: float32 [1024, 1024], P(('expert', 'fsdp'))
- grad_attn_gain: float32 [1024], P(('expert', 'fsdp'))
- grad_moe_gain: float32 [1024], P(('expert', 'fsdp'))
- grad_w_router: float32 [1024, 4], P(('expert', 'fsdp'))
- grad_bias_table: float32 [512], P(('expert', 'fsdp'))
- grad_w_gate: float32 [4, 1024, 2816], P('expert', None, 'fsdp')
- grad_w_up: float32 [4, 1024, 2816], P('expert', None, 'fsdp')
- grad_w_down: float32 [4, 2816, 1024], P('expert', 'fsdp')
The draws below stay inside these ranges and needn't reach their ends.
Inputs may be any that keep to these rules, and one draw needn't show every extreme that they name: `routes`: the two experts of a token differ. `slot_order`: within one routing group the choices that name one expert hold the distinct slots 0, 1, 2 and so on up to 239, and every further choice holds 240 and is dropped; in every draw one expert is named by more than 240 choices in every routing group. `group_map`: within a line each of its 2 prompts is named by exactly 4 continuations. `buckets`: non-decreasing in the distance, 0 at distance 0, every bucket used.
All inputs are finite; a program needn't handle non-finite values.
Results may differ from the reference program's by a relative error of at most 0.015.
Values may be sent and summed in bfloat16 or wider, within the bound.
A program may use at most 320 MiB of HBM per device.

```python
from functools import partial
import jax
import jax.numpy as jnp
from jax import lax

D = 1024
HEADS = 16
HDIM = 64
FF = 2816
BUCKETS = 32
TOPK = 2
PLEN = 1024
CLEN = 128
G_LINE = 2
CONT_DEV = 1
TOK_DEV = 384
TOKENS = 12288
ROUTE_GROUPS = 32
EXPERTS = 4
CAP = 240
SPAN = 1152
LINE_CONTS = 8
NCONT = 4
CONTS = 32
N_EXPERT = 4
N_FSDP = 8


def route_table(key):
    base = jax.random.fold_in(key, 7)
    keys = jax.random.split(base, 4)
    blocks = TOKENS // TOK_DEV
    ranking = jax.random.randint(keys[0], (blocks, TOK_DEV, EXPERTS), 0, 4096)
    favour = jax.random.randint(keys[1], (EXPERTS,), 0, 3) * 1024
    scores = (ranking + favour[None, None, :]) * EXPERTS + jnp.arange(EXPERTS, dtype=jnp.int32)[None, None, :]
    chosen = lax.top_k(scores, 2)[1].astype(jnp.int32)
    hottest = jax.random.randint(keys[2], (), 0, EXPERTS)
    orders = jax.vmap(lambda order_key: jax.random.permutation(order_key, TOK_DEV))(jax.random.split(keys[3], blocks))
    places = jnp.argsort(orders, axis=-1)
    heated = places < CAP + 1
    leading = jnp.where(heated, hottest, chosen[..., 0])
    trailing = jnp.where(heated, jnp.where(chosen[..., 0] == hottest, chosen[..., 1], chosen[..., 0]), chosen[..., 1])
    return jnp.stack([leading, trailing], -1).astype(jnp.int32)


def draw_routes(key, part):
    return route_table(key).reshape(TOKENS, 2)


def draw_slot_order(key, part):
    table = route_table(key)
    blocks = TOKENS // TOK_DEV
    flat = table.reshape(blocks, 2 * TOK_DEV)
    order_keys = jax.random.split(jax.random.fold_in(key, 9), blocks)
    priority = jax.vmap(lambda order_key: jax.random.permutation(order_key, 2 * TOK_DEV))(order_keys)
    same_expert = flat[:, :, None] == flat[:, None, :]
    earlier = priority[:, None, :] < priority[:, :, None]
    slots = jnp.sum((same_expert & earlier).astype(jnp.int32), axis=-1)
    slots = jnp.minimum(slots, CAP)
    return slots.reshape(TOKENS, 2).astype(jnp.int32)


def draw_group_map(key, part):
    lines = CONTS // LINE_CONTS
    line_keys = jax.random.split(jax.random.fold_in(key, 5), lines)
    orders = jax.vmap(lambda line_key: jax.random.permutation(line_key, LINE_CONTS))(line_keys)
    return (orders // NCONT).reshape(CONTS).astype(jnp.int32)


def draw_buckets(key, part):
    cuts = jax.random.permutation(jax.random.fold_in(key, 3), SPAN - 1)[:BUCKETS - 1] + 1
    distance = jnp.arange(SPAN, dtype=jnp.int32)
    return jnp.sum((distance[:, None] >= cuts[None, :]).astype(jnp.int32), axis=-1).astype(jnp.int32)


def block_levels(stream_key, extent, cuts, least, high):
    def one(dim, blocks):
        heights = jax.random.uniform(jax.random.fold_in(jax.random.fold_in(stream_key, 6), dim), (blocks,), jnp.float32, least / len(cuts), high / len(cuts))
        return jnp.repeat(jnp.exp(heights), extent[dim] // blocks).reshape((-1,) + (1,) * (len(extent) - dim - 1))

    loudness = one(*cuts[0])
    for cut in cuts[1:]:
        loudness = loudness * one(*cut)
    return loudness


def centred(key, shape, width, reach, cuts=(), kind=jnp.bfloat16):
    loudness = block_levels(key, shape, cuts, -0.22, 0.18) if cuts else 1.0
    drawn = jax.random.normal(key, shape, jnp.float32) * width * loudness
    return jnp.minimum(jnp.maximum(drawn, -reach), reach).astype(kind)


def setup_inputs(seed: int = 0) -> dict:
    key_of = jax.random.split(jax.random.key(seed), 16)
    return {
        "inputs": centred(key_of[0], (TOKENS, D), 1.0, 6.0, ((0, 32),)),
        "w_qkv": centred(key_of[1], (D, 3 * D), D ** -0.5, 0.1875, ((0, 32),)),
        "w_out": centred(key_of[2], (D, D), 4 ** -0.5, 3.0, ((0, 32),)),
        "attn_gain": jnp.clip(1.0 + 0.1 * jax.random.normal(key_of[3], (D,), jnp.float32), 0.5, 1.5).astype(jnp.bfloat16),
        "moe_gain": jnp.clip(1.0 + 0.1 * jax.random.normal(key_of[4], (D,), jnp.float32), 0.5, 1.5).astype(jnp.bfloat16),
        "w_router": centred(key_of[5], (D, EXPERTS), (2 * D) ** -0.5, 0.125, ((0, 32),)),
        "bias_table": centred(key_of[6], (HEADS * BUCKETS,), 1.0, 4.0, ((0, 32),)),
        "w_gate": centred(key_of[7], (EXPERTS, D, FF), D ** -0.5, 0.1875, ((0, 4), (2, 8))),
        "w_up": centred(key_of[8], (EXPERTS, D, FF), D ** -0.5, 0.1875, ((0, 4), (2, 8))),
        "w_down": centred(key_of[9], (EXPERTS, FF, D), (FF // 2) ** -0.5, 0.15625, ((0, 4), (1, 8))),
        "routes": draw_routes(jax.random.fold_in(key_of[15], 71), 0),
        "slot_order": draw_slot_order(jax.random.fold_in(key_of[15], 71), 0),
        "group_map": draw_group_map(jax.random.fold_in(key_of[15], 71), 0),
        "buckets": draw_buckets(jax.random.fold_in(key_of[15], 71), 0),
        "grad_output": centred(key_of[14], (TOKENS, D), 1.0, 6.0, ((0, 32),)),
    }


EPSILON = 1e-06
ZLOSS_FACTOR = 0.001
BALANCE_FACTOR = 0.01
MASK_VALUE = -1e+30
HIGHEST = lax.Precision.HIGHEST

@jax.custom_vjp
def low(v):
    return lax.optimization_barrier(v.astype(jnp.bfloat16)).astype(jnp.float32)

@jax.custom_vjp
def low_back(v):
    return v

def low_keep(v):
    return (low(v), None)

def low_pass(kept, grad):
    return (grad,)

def back_keep(v):
    return (v, None)

def back_low(kept, grad):
    return (low(grad),)
low.defvjp(low_keep, low_pass)
low_back.defvjp(back_keep, back_low)

def rms_scale(values, scale_row):
    inverse = lax.rsqrt(lax.optimization_barrier(jnp.mean(values * values, axis=-1, keepdims=True)) + EPSILON)
    return values * inverse * scale_row

def attend(queries, key_heads, value_heads, bias_grid, allowed):
    scores = jnp.einsum('qbhd,kbhd->bhqk', queries, key_heads, precision=HIGHEST) * HDIM ** (-0.5) + bias_grid
    scores = jnp.where(allowed, low_back(scores), MASK_VALUE)
    weights = low(jax.nn.softmax(scores, axis=-1))
    return jnp.einsum('bhqk,kbhd->qbhd', weights, value_heads, precision=HIGHEST)

def split_heads(block_rows):
    length, batch_count = (block_rows.shape[0], block_rows.shape[1])
    shaped = block_rows.reshape(length, batch_count, 3, HEADS, HDIM)
    return (shaped[:, :, 0], shaped[:, :, 1], shaped[:, :, 2])

def line_attention(packed, bias_dist):
    line_qkv, line_groups = packed
    prompt_part = PLEN // N_FSDP
    prompt_rows = prompt_part * G_LINE
    blocks = line_qkv.reshape(N_FSDP, TOK_DEV, 3 * D)
    prompt_block = blocks[:, :prompt_rows].reshape(PLEN, G_LINE, 3 * D)
    cont_block = blocks[:, prompt_rows:].reshape(LINE_CONTS, CLEN, 3 * D).transpose(1, 0, 2)
    prompt_q, prompt_k, prompt_v = split_heads(prompt_block)
    prompt_pos = jnp.arange(PLEN, dtype=jnp.int32)
    prompt_dist = prompt_pos[:, None] - prompt_pos[None, :]
    prompt_bias = jnp.take(bias_dist, jnp.clip(prompt_dist, 0, SPAN - 1), axis=1)
    prompt_att = attend(prompt_q, prompt_k, prompt_v, prompt_bias, prompt_dist >= 0)
    cont_q, cont_k, cont_v = split_heads(cont_block)
    all_keys = jnp.concatenate([jnp.take(prompt_k, line_groups, axis=1), cont_k], 0)
    all_values = jnp.concatenate([jnp.take(prompt_v, line_groups, axis=1), cont_v], 0)
    cont_pos = PLEN + jnp.arange(CLEN, dtype=jnp.int32)
    key_pos = jnp.concatenate([prompt_pos, cont_pos])
    cont_dist = cont_pos[:, None] - key_pos[None, :]
    cont_bias = jnp.take(bias_dist, jnp.clip(cont_dist, 0, SPAN - 1), axis=1)
    cont_att = attend(cont_q, all_keys, all_values, cont_bias, cont_dist >= 0)
    prompt_flat = prompt_att.reshape(N_FSDP, prompt_rows, D)
    cont_flat = cont_att.transpose(1, 0, 2, 3).reshape(N_FSDP, CONT_DEV * CLEN, D)
    return jnp.concatenate([prompt_flat, cont_flat], 1).reshape(N_FSDP * TOK_DEV, D)

def expert_block(packed):
    expert_rows, gate_weight, up_weight, down_weight = packed
    gate_pre = low_back(jnp.dot(expert_rows, gate_weight, precision=HIGHEST))
    up_pre = low_back(jnp.dot(expert_rows, up_weight, precision=HIGHEST))
    hidden = low(jax.nn.gelu(gate_pre, approximate=True) * up_pre)
    return low_back(low(jnp.dot(hidden, down_weight, precision=HIGHEST)))

def forward(inputs, w_qkv, w_out, attn_gain, moe_gain, w_router, bias_table, w_gate, w_up, w_down, routes, slot_order, group_map, buckets):
    normed = low(rms_scale(inputs, attn_gain))
    qkv_rows = low_back(low(jnp.dot(normed, w_qkv, precision=HIGHEST)))
    bias_dist = jnp.take(bias_table.reshape(HEADS, BUCKETS), buckets, axis=1)
    line_qkv = qkv_rows.reshape(N_EXPERT, N_FSDP * TOK_DEV, 3 * D)
    line_groups = group_map.reshape(N_EXPERT, LINE_CONTS)
    attended = lax.map(jax.checkpoint(partial(line_attention, bias_dist=bias_dist)), (line_qkv, line_groups))
    attended = low_back(low(attended.reshape(TOKENS, D)))
    middle = inputs + low_back(jnp.dot(attended, w_out, precision=HIGHEST))
    second = rms_scale(middle, moe_gain)
    logits = jnp.dot(second, w_router, precision=HIGHEST)
    log_total = jax.nn.logsumexp(logits, axis=-1)
    chances = jnp.exp(logits - log_total[:, None])
    expert_ids = jnp.arange(EXPERTS, dtype=jnp.int32)
    first_hot = (routes[:, 0:1] == expert_ids[None, :]).astype(jnp.float32)
    second_hot = (routes[:, 1:2] == expert_ids[None, :]).astype(jnp.float32)
    first_chance = lax.optimization_barrier(jnp.sum(chances * first_hot, axis=-1))
    second_chance = lax.optimization_barrier(jnp.sum(chances * second_hot, axis=-1))
    both_chances = first_chance + second_chance
    kept_mask = (slot_order < CAP).astype(jnp.float32)
    gate_kept = jnp.stack([first_chance / both_chances, second_chance / both_chances], -1) * kept_mask
    group_ids = jnp.broadcast_to((jnp.arange(TOKENS, dtype=jnp.int32) // TOK_DEV)[:, None], (TOKENS, TOPK))
    sent_rows = jnp.broadcast_to(low(second)[:, None, :], (TOKENS, TOPK, D))
    buffers = jnp.zeros((ROUTE_GROUPS, EXPERTS, CAP, D), jnp.float32).at[group_ids, routes, slot_order].add(sent_rows, mode='drop')
    buffers = low_back(buffers)
    per_expert = buffers.transpose(1, 0, 2, 3).reshape(EXPERTS, ROUTE_GROUPS * CAP, D)
    results = lax.map(jax.checkpoint(expert_block), (per_expert, w_gate, w_up, w_down))
    results = results.reshape(EXPERTS, ROUTE_GROUPS, CAP, D)
    picked = results[routes, group_ids, jnp.clip(slot_order, 0, CAP - 1)]
    block_out = middle + lax.optimization_barrier(jnp.sum(gate_kept[:, :, None] * picked, axis=1))
    z_loss = lax.optimization_barrier(jnp.mean((log_total * log_total).reshape(ROUTE_GROUPS, TOK_DEV), axis=-1))
    counts = lax.optimization_barrier(jnp.sum((first_hot + second_hot).reshape(ROUTE_GROUPS, TOK_DEV, EXPERTS), axis=1)) / (TOPK * TOK_DEV)
    mean_chance = lax.optimization_barrier(jnp.mean(chances.reshape(ROUTE_GROUPS, TOK_DEV, EXPERTS), axis=1))
    balance = EXPERTS * lax.optimization_barrier(jnp.sum(counts * mean_chance, axis=-1))
    return (block_out, jnp.stack([z_loss, balance], -1))

def reference(inputs, w_qkv, w_out, attn_gain, moe_gain, w_router, bias_table, w_gate, w_up, w_down, routes, slot_order, group_map, buckets, grad_output):
    floats = (inputs.astype(jnp.float32), w_qkv.astype(jnp.float32), w_out.astype(jnp.float32), attn_gain.astype(jnp.float32), moe_gain.astype(jnp.float32), w_router.astype(jnp.float32), bias_table.astype(jnp.float32), w_gate.astype(jnp.float32), w_up.astype(jnp.float32), w_down.astype(jnp.float32))

    def objective(input_float, qkv_float, out_float, attn_float, moe_float, router_float, table_float, gate_float, up_float, down_float):
        return forward(input_float, qkv_float, out_float, attn_float, moe_float, router_float, table_float, gate_float, up_float, down_float, routes, slot_order, group_map, buckets)
    primal, pullback = jax.vjp(objective, *floats)
    block_out, losses = primal
    loss_weights = jnp.broadcast_to(jnp.array([ZLOSS_FACTOR, BALANCE_FACTOR], jnp.float32) / ROUTE_GROUPS, (ROUTE_GROUPS, 2))
    grads = pullback((grad_output.astype(jnp.float32), loss_weights))
    return (block_out.astype(jnp.bfloat16), losses, grads[0], grads[1], grads[2], grads[3], grads[4], grads[5], grads[6], grads[7], grads[8], grads[9])
```

```python
import functools

import jax
import jax.numpy as jnp
from jax import lax
from jax.experimental import pallas as pl
from jax.experimental.pallas import tpu as pltpu
from jax.sharding import PartitionSpec as P

D = 1024
HEADS = 16
HDIM = 64
BUCKETS = 32
TOPK = 2
PLEN = 1024
CLEN = 128
G_LINE = 2

EPSILON = 1e-06
ZLOSS_FACTOR = 0.001
BALANCE_FACTOR = 0.01
MASK_VALUE = -1e30
LOG2E = 1.4426950408889634
HIGHEST = lax.Precision.HIGHEST
TILE = 256
HALF = 128
SPAN_BLOCKS = (PLEN + CLEN) // HALF
BF = jnp.bfloat16
F32 = jnp.float32
NT = (((1,), (1,)), ((), ()))
TN = (((0,), (0,)), ((), ()))


def rms_scale(values, scale_row):
    inverse = lax.rsqrt(jnp.mean(values * values, axis=-1, keepdims=True) + EPSILON)
    return values * inverse * scale_row


def gated_unit(gate_pre, up_pre):
    return jax.nn.gelu(gate_pre, approximate=True) * up_pre


def activation_grads(gate_pre, up_pre, grad_hidden):
    activated, act_pull = jax.vjp(gated_unit, gate_pre, up_pre)
    grad_gate_pre, grad_up_pre = act_pull(grad_hidden)
    return (grad_gate_pre.astype(BF), grad_up_pre.astype(BF))


def route_local(normed, router, routes):
    logits = jnp.dot(normed, router, precision=HIGHEST)
    log_total = jax.nn.logsumexp(logits, axis=-1)
    chances = jnp.exp(logits - log_total[:, None])
    expert_ids = jnp.arange(router.shape[1], dtype=jnp.int32)
    first_hot = (routes[:, 0:1] == expert_ids[None, :]).astype(F32)
    second_hot = (routes[:, 1:2] == expert_ids[None, :]).astype(F32)
    first_chance = jnp.sum(chances * first_hot, axis=-1)
    second_chance = jnp.sum(chances * second_hot, axis=-1)
    both_chances = first_chance + second_chance
    gate_pair = jnp.stack([first_chance / both_chances, second_chance / both_chances], -1)
    z_loss = jnp.mean(log_total * log_total)
    expert_share = jnp.sum(first_hot + second_hot, axis=0) / (TOPK * routes.shape[0])
    balance = router.shape[1] * jnp.sum(expert_share * jnp.mean(chances, axis=0))
    return (gate_pair, jnp.stack([z_loss, balance]))


class Shape:
    def __init__(self, fsdp_count):
        self.srcs = fsdp_count
        self.hp = HEADS // fsdp_count
        self.width = self.hp * HDIM
        self.part = PLEN // fsdp_count
        self.rows = G_LINE * self.part + CLEN
        self.spt = TILE // self.part
        self.tiles = PLEN // TILE
        self.pairs = fsdp_count // 2
        self.prompt_pairs = self.pairs // G_LINE
        self.units = G_LINE * self.tiles + self.pairs


def order_conts(sh, group_ref, perm_ref):
    counts = [jnp.int32(0), jnp.int32(sh.srcs // G_LINE)]
    for c in range(sh.srcs):
        first = group_ref[c] == 0
        perm_ref[jnp.where(first, counts[0], counts[1])] = jnp.int32(c)
        step = first.astype(jnp.int32)
        counts = [counts[0] + step, counts[1] + 1 - step]


def build_bias(sh, table_ref, bucket_ref, bias_ref):
    bucket = bucket_ref[...]
    for h in range(sh.hp):
        dist = jnp.zeros(bucket.shape, F32)
        for b in range(BUCKETS):
            dist = jnp.where(bucket == b, table_ref[h, b] * LOG2E, dist)
        bias_ref[h, 0] = jnp.full((HALF, HALF), MASK_VALUE, F32)
        before = jnp.full((1, HALF), MASK_VALUE, F32)
        for n in range(SPAN_BLOCKS):
            now = dist[n : n + 1, :]
            both = jnp.broadcast_to(jnp.concatenate([before, now], axis=1), (HALF, 2 * HALF))
            turned = pltpu.roll(both, HALF, 1, stride=1, stride_axis=0)
            bias_ref[h, 1 + n] = turned[:, :HALF]
            before = now


def head_mask(sh, h, rows):
    if sh.hp == 1:
        return None
    lane = lax.broadcasted_iota(jnp.int32, (1, sh.width), 1)
    return (lane >= h * HDIM) & (lane < (h + 1) * HDIM)


def only_head(sh, h, x):
    mask = head_mask(sh, h, x.shape[0])
    return x if mask is None else jnp.where(mask, x, jnp.zeros_like(x))


def prompt_rows_of(sh, ref, g, t, part):
    lanes = slice(part * sh.width, (part + 1) * sh.width)
    start = pl.multiple_of(g * sh.part, sh.part)
    return jnp.concatenate(
        [ref[t * sh.spt + s, pl.ds(start, sh.part), lanes] for s in range(sh.spt)], axis=0
    )


def cont_rows_of(sh, ref, c, part):
    lanes = slice(part * sh.width, (part + 1) * sh.width)
    return ref[c, G_LINE * sh.part :, lanes]


def put_prompt_rows(sh, ref, g, t, part, value):
    lanes = slice(part * sh.width, (part + 1) * sh.width)
    start = pl.multiple_of(g * sh.part, sh.part)
    for s in range(sh.spt):
        ref[t * sh.spt + s, pl.ds(start, sh.part), lanes] = value[
            s * sh.part : (s + 1) * sh.part
        ].astype(ref.dtype)


def transpose_low(x):
    return x.astype(F32).T.astype(BF)


def add_bias(scores, bias_ref, h, base, step_q):
    rows = []
    for a in range(2):
        cols = []
        for b in range(2):
            part = scores[a * HALF : (a + 1) * HALF, b * HALF : (b + 1) * HALF]
            cols.append(part * LOG2E + bias_ref[h, base + b * step_q - a])
        rows.append(jnp.concatenate(cols, axis=1))
    return jnp.concatenate(rows, axis=0)


def fold_max(x):
    return jnp.max(x.reshape(-1, 8, x.shape[-1]), axis=0)


def fold_sum(x):
    return jnp.sum(x.reshape(-1, 8, x.shape[-1]), axis=0)


def attn_forward_kernel(
    sh, group_ref, table_ref, bucket_ref, x_ref, o_ref, ot_ref, lse_ref, bias, vt, vtc, sc, perm
):
    order_conts(sh, group_ref, perm)
    build_bias(sh, table_ref, bucket_ref, bias)

    def make_vt(i, _):
        g, t = i // sh.tiles, lax.rem(i, sh.tiles)
        vt[i] = transpose_low(prompt_rows_of(sh, x_ref, g, t, 2))
        return 0

    lax.fori_loop(0, G_LINE * sh.tiles, make_vt, 0)

    def make_vtc(c, _):
        vtc[c] = transpose_low(cont_rows_of(sh, x_ref, c, 2))
        return 0

    lax.fori_loop(0, sh.srcs, make_vtc, 0)

    def scores_tile(keys, qh, base, step_q, kt, peaks):
        out = []
        for h in range(sh.hp):
            s = lax.dot_general(keys, qh[h], NT, preferred_element_type=F32)
            s = add_bias(s, bias, h, base, step_q)
            sc[h, pl.ds(pl.multiple_of(kt * TILE, TILE), TILE), :] = s
            out.append(jnp.maximum(peaks[h], fold_max(s)))
        return tuple(out)

    def value_tile(g, kt, peaks, carry):
        out = []
        for h in range(sh.hp):
            total, acc = carry[h]
            p = jnp.exp2(sc[h, pl.ds(pl.multiple_of(kt * TILE, TILE), TILE), :] - peaks[h])
            total = total + fold_sum(p)
            values = vt[g * sh.tiles + kt, h * HDIM : (h + 1) * HDIM, :]
            acc = acc + jnp.dot(values, p.astype(BF), preferred_element_type=F32)
            out.append((total, acc))
        return tuple(out)

    first_peaks = tuple(jnp.full((8, TILE), MASK_VALUE, F32) for _ in range(sh.hp))
    first_carry = tuple(
        (jnp.zeros((8, TILE), F32), jnp.zeros((HDIM, TILE), F32)) for _ in range(sh.hp)
    )

    def finish(unit, peaks, carry):
        outs = []
        for h in range(sh.hp):
            total = jnp.sum(carry[h][0], axis=0, keepdims=True)
            outs.append(carry[h][1] / total)
            lse_ref[unit, h : h + 1, :] = peaks[h] + jnp.log2(total)
        whole = jnp.concatenate(outs, axis=0) if sh.hp > 1 else outs[0]
        ot_ref[unit] = whole
        return whole.T

    def prompt_unit(i, _):
        g, qt = i // sh.tiles, lax.rem(i, sh.tiles)
        q = prompt_rows_of(sh, x_ref, g, qt, 0) * BF(HDIM**-0.5)
        qh = [only_head(sh, h, q) for h in range(sh.hp)]

        def first(kt, peaks):
            keys = prompt_rows_of(sh, x_ref, g, kt, 1)
            return scores_tile(keys, qh, 2 * (qt - kt) + 1, 1, kt, peaks)

        peaks = lax.fori_loop(0, qt + 1, first, first_peaks)
        peaks = [jnp.max(p, axis=0, keepdims=True) for p in peaks]
        carry = lax.fori_loop(0, qt + 1, lambda kt, c: value_tile(g, kt, peaks, c), first_carry)
        put_prompt_rows(sh, o_ref, g, qt, 0, finish(i, peaks, carry))
        return 0

    lax.fori_loop(0, G_LINE * sh.tiles, prompt_unit, 0)

    def cont_unit(i, _):
        conts = [perm[2 * i], perm[2 * i + 1]]
        g = i // sh.prompt_pairs
        q = jnp.concatenate([cont_rows_of(sh, x_ref, c, 0) for c in conts], axis=0)
        q = q * BF(HDIM**-0.5)
        qh = [only_head(sh, h, q) for h in range(sh.hp)]

        def first(kt, peaks):
            keys = prompt_rows_of(sh, x_ref, g, kt, 1)
            return scores_tile(keys, qh, SPAN_BLOCKS - 2 * kt, 0, kt, peaks)

        peaks = lax.fori_loop(0, sh.tiles, first, first_peaks)
        own = []
        next_peaks = []
        for h in range(sh.hp):
            parts = []
            for b in range(2):
                keys = cont_rows_of(sh, x_ref, conts[b], 1)
                s = lax.dot_general(
                    keys, qh[h][b * HALF : (b + 1) * HALF], NT, preferred_element_type=F32
                )
                parts.append(s * LOG2E + bias[h, 1])
            own.append(jnp.concatenate(parts, axis=1))
            next_peaks.append(jnp.maximum(peaks[h], fold_max(own[h])))
        peaks = [jnp.max(p, axis=0, keepdims=True) for p in next_peaks]
        start = []
        for h in range(sh.hp):
            p = jnp.exp2(own[h] - peaks[h])
            low = p.astype(BF)
            acc = jnp.concatenate(
                [
                    jnp.dot(
                        vtc[conts[b], h * HDIM : (h + 1) * HDIM, :],
                        low[:, b * HALF : (b + 1) * HALF],
                        preferred_element_type=F32,
                    )
                    for b in range(2)
                ],
                axis=1,
            )
            start.append((fold_sum(p), acc))
        carry = lax.fori_loop(
            0, sh.tiles, lambda kt, c: value_tile(g, kt, peaks, c), tuple(start)
        )
        done = finish(G_LINE * sh.tiles + i, peaks, carry)
        for b in range(2):
            o_ref[conts[b], G_LINE * sh.part :, :] = done[b * HALF : (b + 1) * HALF].astype(BF)
        return 0

    lax.fori_loop(0, sh.pairs, cont_unit, 0)


def attn_backward_kernel(
    sh,
    group_ref,
    table_ref,
    bucket_ref,
    x_ref,
    do_ref,
    ot_ref,
    lse_ref,
    dx_ref,
    dtable_ref,
    bias,
    dbias,
    ktr,
    ktc,
    dk,
    dv,
    perm,
):
    order_conts(sh, group_ref, perm)
    build_bias(sh, table_ref, bucket_ref, bias)
    dbias[...] = jnp.zeros_like(dbias)
    dk[...] = jnp.zeros_like(dk)
    dv[...] = jnp.zeros_like(dv)

    def make_kt(i, _):
        g, t = i // sh.tiles, lax.rem(i, sh.tiles)
        ktr[i] = transpose_low(prompt_rows_of(sh, x_ref, g, t, 1))
        return 0

    lax.fori_loop(0, G_LINE * sh.tiles, make_kt, 0)

    def make_ktc(c, _):
        ktc[c] = transpose_low(cont_rows_of(sh, x_ref, c, 1))
        return 0

    lax.fori_loop(0, sh.srcs, make_ktc, 0)

    def inner_terms(unit, do):
        outs = []
        turned = do.astype(F32).T
        for h in range(sh.hp):
            rows = slice(h * HDIM, (h + 1) * HDIM)
            prod = ot_ref[unit, rows, :] * turned[rows, :]
            outs.append(jnp.sum(prod, axis=0, keepdims=True))
        return outs

    def grads_tile(g, kt, qh, doh, lse, inner, base, step_q, dqs):
        keys = prompt_rows_of(sh, x_ref, g, kt, 1)
        values = prompt_rows_of(sh, x_ref, g, kt, 2)
        slot = g * sh.tiles + kt
        out = []
        dkey = dvalue = None
        for h in range(sh.hp):
            s = lax.dot_general(keys, qh[h], NT, preferred_element_type=F32)
            dp = lax.dot_general(values, doh[h], NT, preferred_element_type=F32)
            p = jnp.exp2(add_bias(s, bias, h, base, step_q) - lse[h])
            ds = p * (dp - inner[h])
            for a in range(2):
                for b in range(2):
                    dbias[h, base + b * step_q - a] += ds[
                        a * HALF : (a + 1) * HALF, b * HALF : (b + 1) * HALF
                    ]
            low = ds.astype(BF)
            more_k = jnp.dot(low, qh[h], preferred_element_type=F32)
            more_v = jnp.dot(p.astype(BF), doh[h], preferred_element_type=F32)
            dkey = more_k if dkey is None else dkey + more_k
            dvalue = more_v if dvalue is None else dvalue + more_v
            turned = ktr[slot, h * HDIM : (h + 1) * HDIM, :]
            out.append(dqs[h] + jnp.dot(turned, low, preferred_element_type=F32))
        dk[slot] += dkey
        dv[slot] += dvalue
        return tuple(out)

    def finish(dqs):
        whole = jnp.concatenate(dqs, axis=0) if sh.hp > 1 else dqs[0]
        return whole.T * (HDIM**-0.5)

    first_dq = tuple(jnp.zeros((HDIM, TILE), F32) for _ in range(sh.hp))

    def prompt_unit(i, _):
        g, qt = i // sh.tiles, lax.rem(i, sh.tiles)
        q = prompt_rows_of(sh, x_ref, g, qt, 0) * BF(HDIM**-0.5)
        do = prompt_rows_of(sh, do_ref, g, qt, 0)
        qh = [only_head(sh, h, q) for h in range(sh.hp)]
        doh = [only_head(sh, h, do) for h in range(sh.hp)]
        inner = inner_terms(i, do)
        lse = [lse_ref[i, h : h + 1, :] for h in range(sh.hp)]

        def body(kt, dqs):
            return grads_tile(g, kt, qh, doh, lse, inner, 2 * (qt - kt) + 1, 1, dqs)

        dqs = lax.fori_loop(0, qt + 1, body, first_dq)
        put_prompt_rows(sh, dx_ref, g, qt, 0, finish(dqs))
        return 0

    lax.fori_loop(0, G_LINE * sh.tiles, prompt_unit, 0)

    def cont_unit(i, _):
        conts = [perm[2 * i], perm[2 * i + 1]]
        unit = G_LINE * sh.tiles + i
        g = i // sh.prompt_pairs
        q = jnp.concatenate([cont_rows_of(sh, x_ref, c, 0) for c in conts], axis=0)
        q = q * BF(HDIM**-0.5)
        do = jnp.concatenate([cont_rows_of(sh, do_ref, c, 0) for c in conts], axis=0)
        qh = [only_head(sh, h, q) for h in range(sh.hp)]
        doh = [only_head(sh, h, do) for h in range(sh.hp)]
        inner = inner_terms(unit, do)
        lse = [lse_ref[unit, h : h + 1, :] for h in range(sh.hp)]

        def body(kt, dqs):
            return grads_tile(g, kt, qh, doh, lse, inner, SPAN_BLOCKS - 2 * kt, 0, dqs)

        dqs = lax.fori_loop(0, sh.tiles, body, first_dq)
        more = [[None] * 2 for _ in range(sh.hp)]
        for b in range(2):
            cols = slice(b * HALF, (b + 1) * HALF)
            keys = cont_rows_of(sh, x_ref, conts[b], 1)
            values = cont_rows_of(sh, x_ref, conts[b], 2)
            dkey = dvalue = None
            for h in range(sh.hp):
                s = lax.dot_general(keys, qh[h][cols], NT, preferred_element_type=F32)
                dp = lax.dot_general(values, doh[h][cols], NT, preferred_element_type=F32)
                p = jnp.exp2(s * LOG2E + bias[h, 1] - lse[h][:, cols])
                ds = p * (dp - inner[h][:, cols])
                dbias[h, 1] += ds
                low = ds.astype(BF)
                more_k = jnp.dot(low, qh[h][cols], preferred_element_type=F32)
                more_v = jnp.dot(p.astype(BF), doh[h][cols], preferred_element_type=F32)
                dkey = more_k if dkey is None else dkey + more_k
                dvalue = more_v if dvalue is None else dvalue + more_v
                turned = ktc[conts[b], h * HDIM : (h + 1) * HDIM, :]
                more[h][b] = jnp.dot(turned, low, preferred_element_type=F32)
            w = sh.width
            dx_ref[conts[b], G_LINE * sh.part :, w : 2 * w] = dkey.astype(BF)
            dx_ref[conts[b], G_LINE * sh.part :, 2 * w :] = dvalue.astype(BF)
        dqs = [dqs[h] + jnp.concatenate(more[h], axis=1) for h in range(sh.hp)]
        done = finish(dqs)
        for b in range(2):
            dx_ref[conts[b], G_LINE * sh.part :, : sh.width] = done[
                b * HALF : (b + 1) * HALF
            ].astype(BF)
        return 0

    lax.fori_loop(0, sh.pairs, cont_unit, 0)

    def put_keys(i, _):
        g, t = i // sh.tiles, lax.rem(i, sh.tiles)
        put_prompt_rows(sh, dx_ref, g, t, 1, dk[i])
        put_prompt_rows(sh, dx_ref, g, t, 2, dv[i])
        return 0

    lax.fori_loop(0, G_LINE * sh.tiles, put_keys, 0)

    bucket = bucket_ref[...]
    key_row = lax.broadcasted_iota(jnp.int32, (HALF, 2 * HALF), 0)
    for h in range(sh.hp):
        spread = []
        for n in range(SPAN_BLOCKS):
            wide = jnp.concatenate(
                [jnp.zeros((HALF, HALF), F32), dbias[h, 1 + n]], axis=1
            )
            for bit in range(7):
                moved = pltpu.roll(wide, 2 * HALF - (1 << bit), 1)
                wide = jnp.where((key_row & (1 << bit)) != 0, moved, wide)
            spread.append(jnp.sum(wide, axis=0, keepdims=True))
        rows = []
        for n in range(SPAN_BLOCKS):
            row = spread[n][:, HALF:]
            if n + 1 < SPAN_BLOCKS:
                row = row + spread[n + 1][:, :HALF]
            rows.append(row)
        by_dist = jnp.concatenate(rows, axis=0)
        sums = [
            jnp.sum(jnp.where(bucket == b, by_dist, 0.0), axis=0, keepdims=True)
            for b in range(BUCKETS)
        ]
        lanes = jnp.concatenate(sums, axis=0)
        dtable_ref[h * BUCKETS : (h + 1) * BUCKETS, :] = jnp.broadcast_to(
            jnp.sum(lanes, axis=1, keepdims=True), (BUCKETS, HALF)
        )


SMEM_SPEC = pl.BlockSpec(memory_space=pltpu.SMEM)
VMEM_SPEC = pl.BlockSpec(memory_space=pltpu.VMEM)
GRANT = 48 * 1024 * 1024


def attend_forward(sh, group, table, bucket, x):
    return pl.pallas_call(
        functools.partial(attn_forward_kernel, sh),
        out_shape=(
            jax.ShapeDtypeStruct((sh.srcs, sh.rows, sh.width), BF),
            jax.ShapeDtypeStruct((sh.units, sh.width, TILE), F32),
            jax.ShapeDtypeStruct((sh.units, 8, TILE), F32),
        ),
        in_specs=[SMEM_SPEC, SMEM_SPEC, VMEM_SPEC, VMEM_SPEC],
        out_specs=(VMEM_SPEC, VMEM_SPEC, VMEM_SPEC),
        scratch_shapes=[
            pltpu.VMEM((sh.hp, SPAN_BLOCKS + 1, HALF, HALF), F32),
            pltpu.VMEM((G_LINE * sh.tiles, sh.width, TILE), BF),
            pltpu.VMEM((sh.srcs, sh.width, HALF), BF),
            pltpu.VMEM((sh.hp, PLEN, TILE), F32),
            pltpu.SMEM((sh.srcs,), jnp.int32),
        ],
        compiler_params=pltpu.CompilerParams(vmem_limit_bytes=GRANT),
        cost_estimate=pl.CostEstimate(
            flops=10**10, bytes_accessed=8 * 10**6, transcendentals=5 * 10**6
        ),
        name="attend_forward",
    )(group, table, bucket, x)


def attend_backward(sh, group, table, bucket, x, do, ot, lse):
    return pl.pallas_call(
        functools.partial(attn_backward_kernel, sh),
        out_shape=(
            jax.ShapeDtypeStruct((sh.srcs, sh.rows, 3 * sh.width), BF),
            jax.ShapeDtypeStruct((sh.hp * BUCKETS, HALF), F32),
        ),
        in_specs=[SMEM_SPEC, SMEM_SPEC, VMEM_SPEC, VMEM_SPEC, VMEM_SPEC, VMEM_SPEC, VMEM_SPEC],
        out_specs=(VMEM_SPEC, VMEM_SPEC),
        scratch_shapes=[
            pltpu.VMEM((sh.hp, SPAN_BLOCKS + 1, HALF, HALF), F32),
            pltpu.VMEM((sh.hp, SPAN_BLOCKS + 1, HALF, HALF), F32),
            pltpu.VMEM((G_LINE * sh.tiles, sh.width, TILE), BF),
            pltpu.VMEM((sh.srcs, sh.width, HALF), BF),
            pltpu.VMEM((G_LINE * sh.tiles, TILE, sh.width), F32),
            pltpu.VMEM((G_LINE * sh.tiles, TILE, sh.width), F32),
            pltpu.SMEM((sh.srcs,), jnp.int32),
        ],
        compiler_params=pltpu.CompilerParams(vmem_limit_bytes=GRANT),
        cost_estimate=pl.CostEstimate(
            flops=2 * 10**10, bytes_accessed=12 * 10**6, transcendentals=5 * 10**6
        ),
        name="attend_backward",
    )(group, table, bucket, x, do, ot, lse)


def ring_order(count):
    deep, wide = 4, count // 4
    order = [a * wide for a in range(deep)]
    for turn, a in enumerate(reversed(range(deep))):
        row = [a * wide + b for b in range(1, wide)]
        order += row if turn % 2 == 0 else row[::-1]
    return order


def ring_hop(x, count, step):
    ring = ring_order(count)
    return lax.ppermute(x, "fsdp", [(ring[i], ring[(i + step) % count]) for i in range(count)])


def ring_gather(x, count):
    chunks = [None] * count
    chunks[0] = x
    right = left = x
    for s in range(1, count // 2 + 1):
        right = ring_hop(right, count, 1)
        chunks[count - s] = right
        if s < count // 2:
            left = ring_hop(left, count, -1)
            chunks[s] = left
    return chunks


def ring_scatter(part, count):
    right = part(count - 1, 0).astype(BF)
    left = part(1, 1).astype(BF)
    for s in range(1, count):
        right = ring_hop(right, count, 1)
        left = ring_hop(left, count, -1)
        right = right.astype(F32) + part(count - 1 - s, 0).astype(F32)
        left = left.astype(F32) + part((1 + s) % count, 1).astype(F32)
        if s < count - 1:
            right, left = right.astype(BF), left.astype(BF)
    return right, left


def local(
    inputs,
    w_qkv,
    w_out,
    attn_gain,
    moe_gain,
    w_router,
    bias_table,
    w_gate,
    w_up,
    w_down,
    routes,
    slot_order,
    group_map,
    buckets,
    grad_output,
):
    tok_count = inputs.shape[0]
    expert_count = w_router.shape[1]
    capacity = (5 * TOPK * tok_count + 4 * expert_count - 1) // (4 * expert_count)
    fsdp_count = lax.axis_size("fsdp")
    fsdp_place = lax.axis_index("fsdp")
    expert_place = lax.axis_index("expert")
    group_count = lax.axis_size("expert") * fsdp_count
    sh = Shape(fsdp_count)
    prompt_rows = sh.part * G_LINE
    slot_total = expert_count * capacity
    shard = w_qkv.shape[0]
    ff_shard = w_down.shape[1]

    def by_prompt(x):
        head = x[:prompt_rows].reshape(sh.part, G_LINE, -1).transpose(1, 0, 2)
        return jnp.concatenate([head.reshape(prompt_rows, -1), x[prompt_rows:]], 0)

    def by_token(x):
        head = x[:prompt_rows].reshape(G_LINE, sh.part, -1).transpose(1, 0, 2)
        return jnp.concatenate([head.reshape(prompt_rows, -1), x[prompt_rows:]], 0)

    small = jnp.concatenate(
        [attn_gain, moe_gain, w_router.reshape(-1), bias_table, group_map.astype(BF)]
    )
    small_rows = -(-small.shape[0] // D)
    small_rows = -(-small_rows // 16) * 16
    small = jnp.pad(small, (0, small_rows * D - small.shape[0])).reshape(small_rows, D)
    pack = jnp.concatenate([w_qkv[:, i * D : (i + 1) * D] for i in range(3)] + [w_out, small], 0)
    gathered = lax.all_gather(pack, ("expert", "fsdp"), axis=0, tiled=False)
    qkv_full = jnp.concatenate(
        [gathered[:, i * shard : (i + 1) * shard].reshape(D, D) for i in range(3)], 1
    )
    out_full = gathered[:, 3 * shard : 4 * shard].reshape(D, D)
    tail = gathered[:, 4 * shard]
    marks = [0, shard, 2 * shard, 2 * shard + shard * expert_count]
    marks += [marks[-1] + bias_table.shape[0]]
    attn_scale = tail[:, marks[0] : marks[1]].reshape(D).astype(F32)
    moe_scale = tail[:, marks[1] : marks[2]].reshape(D).astype(F32)
    router = tail[:, marks[2] : marks[3]].reshape(D, expert_count).astype(F32)
    table = tail[:, marks[3] : marks[4]].reshape(fsdp_count, sh.hp, BUCKETS)
    my_table = lax.dynamic_index_in_dim(table, fsdp_place, 0, keepdims=False).astype(F32)
    groups = tail[:, marks[4]].reshape(-1, fsdp_count)
    my_groups = lax.dynamic_index_in_dim(groups, expert_place, 0, keepdims=False)
    my_groups = my_groups.astype(jnp.int32)
    bucket = buckets.reshape(SPAN_BLOCKS, HALF)

    gate_chunks = ring_gather(w_gate[0].T, fsdp_count)
    up_chunks = ring_gather(w_up[0].T, fsdp_count)
    down_chunks = ring_gather(w_down[0], fsdp_count)

    token_input = by_prompt(inputs)
    grad_rows_low = by_prompt(grad_output)
    routes = by_prompt(routes)
    slot_order = by_prompt(slot_order)

    input_float = token_input.astype(F32)
    normed, first_pull = jax.vjp(rms_scale, input_float, attn_scale)
    normed_low = normed.astype(BF)
    qkv_rows = jnp.dot(normed_low, qkv_full, preferred_element_type=F32).astype(BF)
    by_heads = (
        qkv_rows.reshape(tok_count, 3, fsdp_count, sh.width)
        .transpose(2, 0, 1, 3)
        .reshape(fsdp_count, tok_count, 3 * sh.width)
    )
    head_qkv = lax.all_to_all(by_heads, "fsdp", split_axis=0, concat_axis=0, tiled=True)
    head_att, att_turned, att_lse = attend_forward(sh, my_groups, my_table, bucket, head_qkv)
    att_back = lax.all_to_all(head_att, "fsdp", split_axis=0, concat_axis=0, tiled=True)
    attn_low = att_back.transpose(1, 0, 2).reshape(tok_count, D)

    middle = input_float + jnp.dot(attn_low, out_full, preferred_element_type=F32)
    second_normed, second_pull = jax.vjp(rms_scale, middle, moe_scale)
    (gate_pair, losses), router_pull = jax.vjp(
        lambda normed_rows, router_rows: route_local(normed_rows, router_rows, routes),
        second_normed,
        router,
    )
    kept_mask = (slot_order < capacity).astype(F32)
    gate_kept = gate_pair * kept_mask
    slot_ids = jnp.arange(slot_total, dtype=jnp.int32)
    slot_place = jnp.where(slot_order < capacity, routes * capacity + slot_order, -1)
    hot = [slot_place[:, k : k + 1] == slot_ids[None, :] for k in range(TOPK)]
    any_low = (hot[0] | hot[1]).astype(BF)
    outgoing = lax.dot_general(
        any_low, second_normed.astype(BF), TN, preferred_element_type=F32
    ).astype(BF)

    def swap_experts(rows):
        rows = rows.reshape(expert_count, capacity, D)
        rows = lax.all_to_all(rows, "expert", split_axis=0, concat_axis=0, tiled=True)
        return rows.reshape(slot_total, D)

    expert_rows = swap_experts(outgoing)
    slot_gate = jnp.sum(
        jnp.where(hot[0], gate_kept[:, 0:1], 0.0) + jnp.where(hot[1], gate_kept[:, 1:2], 0.0),
        axis=0,
    )
    slot_grad = lax.dot_general(any_low, grad_rows_low, TN, preferred_element_type=F32)
    grad_result = swap_experts((slot_gate[:, None] * slot_grad).astype(BF))

    gate_whole = jnp.concatenate(gate_chunks, 0)
    up_whole = jnp.concatenate(up_chunks, 0)
    down_whole = jnp.concatenate(down_chunks, 0)
    gate_pre = lax.dot_general(expert_rows, gate_whole, NT, preferred_element_type=F32)
    up_pre = lax.dot_general(expert_rows, up_whole, NT, preferred_element_type=F32)
    hidden = gated_unit(gate_pre, up_pre).astype(BF)
    result_rows = jnp.dot(hidden, down_whole, preferred_element_type=F32).astype(BF)
    returned = swap_experts(result_rows)

    grad_hidden = lax.dot_general(grad_result, down_whole, NT, preferred_element_type=F32)
    grad_gate_pre, grad_up_pre = activation_grads(gate_pre, up_pre, grad_hidden)
    grad_rows = jnp.dot(grad_gate_pre, gate_whole, preferred_element_type=F32) + jnp.dot(
        grad_up_pre, up_whole, preferred_element_type=F32
    )
    grad_sent = swap_experts(grad_rows.astype(BF))
    down_total = lax.dot_general(hidden, grad_result, TN, preferred_element_type=F32).astype(BF)
    gate_total = lax.dot_general(
        grad_gate_pre, expert_rows, TN, preferred_element_type=F32
    ).astype(BF)
    up_total = lax.dot_general(grad_up_pre, expert_rows, TN, preferred_element_type=F32).astype(BF)

    half_shard = ff_shard // 2

    def shares(total):
        def part(k, half):
            start = k * ff_shard + half * half_shard
            return total[start : start + half_shard]

        return jnp.concatenate(ring_scatter(part, fsdp_count), 0)

    grad_down = shares(down_total)
    grad_gate = shares(gate_total).T
    grad_up = shares(up_total).T

    picked = [
        jnp.dot(h.astype(BF), returned, preferred_element_type=F32) for h in hot
    ]
    block_out = middle + gate_kept[:, 0:1] * picked[0] + gate_kept[:, 1:2] * picked[1]
    output = by_token(block_out.astype(BF))
    grad_final = grad_rows_low.astype(F32)
    grad_pair = (
        jnp.stack([jnp.sum(grad_final * p, axis=-1) for p in picked], -1) * kept_mask
    )
    grad_second = jnp.dot(any_low, grad_sent, preferred_element_type=F32)
    loss_weights = jnp.array([ZLOSS_FACTOR, BALANCE_FACTOR], F32) / group_count
    router_normed, grad_router = router_pull((grad_pair, loss_weights))
    grad_middle_part, grad_moe_gain = second_pull(grad_second + router_normed)
    grad_middle = grad_final + grad_middle_part
    grad_branch = grad_middle.astype(BF)
    grad_attn = lax.dot_general(grad_branch, out_full, NT, preferred_element_type=F32).astype(BF)
    head_grad = (
        grad_attn.reshape(tok_count, fsdp_count, sh.width).transpose(1, 0, 2)
    )
    head_grad = lax.all_to_all(head_grad, "fsdp", split_axis=0, concat_axis=0, tiled=True)
    head_dqkv, head_table = attend_backward(
        sh, my_groups, my_table, bucket, head_qkv, head_grad, att_turned, att_lse
    )
    back_dqkv = lax.all_to_all(head_dqkv, "fsdp", split_axis=0, concat_axis=0, tiled=True)
    grad_qkv = (
        back_dqkv.reshape(fsdp_count, tok_count, 3, sh.width)
        .transpose(1, 2, 0, 3)
        .reshape(tok_count, 3 * D)
    )
    grad_out_w = lax.dot_general(attn_low, grad_branch, TN, preferred_element_type=F32)
    grad_qkv_w = lax.dot_general(normed_low, grad_qkv, TN, preferred_element_type=F32)
    grad_normed = lax.dot_general(grad_qkv, qkv_full, NT, preferred_element_type=F32)
    grad_input_part, grad_attn_gain = first_pull(grad_normed)
    grad_inputs = by_token(grad_middle + grad_input_part)

    def rows_of(x):
        return x.astype(BF).reshape(group_count, shard, -1)

    def small_block(parts):
        flat = jnp.concatenate([p.astype(BF).reshape(group_count, -1) for p in parts], 1)
        flat = jnp.pad(flat, ((0, 0), (0, 16 * D - flat.shape[1])))
        return flat.reshape(group_count, 16, D)

    def sum_shards(parts):
        whole = jnp.concatenate(parts, 1)
        count = whole.shape[1]
        flat = whole.reshape(group_count * count, D)
        return lax.psum_scatter(
            flat, ("expert", "fsdp"), scatter_dimension=0, tiled=True
        ).astype(F32)

    early = sum_shards([rows_of(grad_out_w), small_block([grad_moe_gain, grad_router])])
    sum_out = early[:shard]
    sum_moe = early[shard, :shard]
    sum_router = early[shard, shard : shard + shard * expert_count].reshape(shard, expert_count)
    place_table = (jnp.arange(fsdp_count) == fsdp_place).astype(F32)
    whole_table = place_table[:, None] * head_table[:, 0][None, :]
    late = sum_shards(
        [rows_of(grad_qkv_w[:, i * D : (i + 1) * D]) for i in range(3)]
        + [small_block([grad_attn_gain, whole_table.reshape(-1)])]
    )
    sum_qkv = jnp.concatenate([late[i * shard : (i + 1) * shard] for i in range(3)], 1)
    sum_attn = late[3 * shard, :shard]
    sum_table = late[3 * shard, shard : shard + bias_table.shape[0]]
    return (
        output,
        losses[None, :],
        grad_inputs,
        sum_qkv,
        sum_out,
        sum_attn,
        sum_moe,
        sum_router,
        sum_table,
        grad_gate[None],
        grad_up[None],
        grad_down[None],
    )


def solution(mesh):
    rows = P(("expert", "fsdp"), None)
    flat = P(("expert", "fsdp"))
    cols = P("expert", None, "fsdp")
    deep = P("expert", "fsdp", None)
    in_specs = (
        rows, rows, rows, flat, flat, rows, flat, cols, cols, deep, rows, rows, flat, P(), rows,
    )
    out_specs = (rows, rows, rows, rows, rows, flat, flat, rows, flat, cols, cols, deep)
    return jax.shard_map(local, mesh=mesh, in_specs=in_specs, out_specs=out_specs, check_vma=False)
```

```python
import functools

import jax
import jax.numpy as jnp
from jax import lax
from jax.experimental import pallas as pl
from jax.experimental.pallas import tpu as pltpu
from jax.sharding import PartitionSpec as P

D = 1024
HEADS = 16
HDIM = 64
BUCKETS = 32
TOPK = 2
PLEN = 1024
CLEN = 128
G_LINE = 2

EPSILON = 1e-06
ZLOSS_FACTOR = 0.001
BALANCE_FACTOR = 0.01
MASK_VALUE = -1e30
LOG2E = 1.4426950408889634
HIGHEST = lax.Precision.HIGHEST
TILE = 256
HALF = 128
SPAN_BLOCKS = (PLEN + CLEN) // HALF
BF = jnp.bfloat16
F32 = jnp.float32
NT = (((1,), (1,)), ((), ()))
TN = (((0,), (0,)), ((), ()))


def rms_scale(values, scale_row):
    inverse = lax.rsqrt(jnp.mean(values * values, axis=-1, keepdims=True) + EPSILON)
    return values * inverse * scale_row


def gated_unit(gate_pre, up_pre):
    return jax.nn.gelu(gate_pre, approximate=True) * up_pre


def activation_grads(gate_pre, up_pre, grad_hidden):
    activated, act_pull = jax.vjp(gated_unit, gate_pre, up_pre)
    grad_gate_pre, grad_up_pre = act_pull(grad_hidden)
    return (grad_gate_pre.astype(BF), grad_up_pre.astype(BF))


def route_local(normed, router, routes):
    logits = jnp.dot(normed, router, precision=HIGHEST)
    log_total = jax.nn.logsumexp(logits, axis=-1)
    chances = jnp.exp(logits - log_total[:, None])
    expert_ids = jnp.arange(router.shape[1], dtype=jnp.int32)
    first_hot = (routes[:, 0:1] == expert_ids[None, :]).astype(F32)
    second_hot = (routes[:, 1:2] == expert_ids[None, :]).astype(F32)
    first_chance = jnp.sum(chances * first_hot, axis=-1)
    second_chance = jnp.sum(chances * second_hot, axis=-1)
    both_chances = first_chance + second_chance
    gate_pair = jnp.stack([first_chance / both_chances, second_chance / both_chances], -1)
    z_loss = jnp.mean(log_total * log_total)
    expert_share = jnp.sum(first_hot + second_hot, axis=0) / (TOPK * routes.shape[0])
    balance = router.shape[1] * jnp.sum(expert_share * jnp.mean(chances, axis=0))
    return (gate_pair, jnp.stack([z_loss, balance]))


class Shape:
    def __init__(self, fsdp_count):
        self.srcs = fsdp_count
        self.hp = HEADS // fsdp_count
        self.width = self.hp * HDIM
        self.part = PLEN // fsdp_count
        self.rows = G_LINE * self.part + CLEN
        self.spt = TILE // self.part
        self.tiles = PLEN // TILE
        self.pairs = fsdp_count // 2
        self.prompt_pairs = self.pairs // G_LINE
        self.units = G_LINE * self.tiles + self.pairs


def order_conts(sh, group_ref, perm_ref):
    counts = [jnp.int32(0), jnp.int32(sh.srcs // G_LINE)]
    for c in range(sh.srcs):
        first = group_ref[c] == 0
        perm_ref[jnp.where(first, counts[0], counts[1])] = jnp.int32(c)
        step = first.astype(jnp.int32)
        counts = [counts[0] + step, counts[1] + 1 - step]


def build_bias(sh, table_ref, bucket_ref, bias_ref):
    bucket = bucket_ref[...]
    for h in range(sh.hp):
        dist = jnp.zeros(bucket.shape, F32)
        for b in range(BUCKETS):
            dist = jnp.where(bucket == b, table_ref[h, b] * LOG2E, dist)
        bias_ref[h, 0] = jnp.full((HALF, HALF), MASK_VALUE, F32)
        before = jnp.full((1, HALF), MASK_VALUE, F32)
        for n in range(SPAN_BLOCKS):
            now = dist[n : n + 1, :]
            both = jnp.broadcast_to(jnp.concatenate([before, now], axis=1), (HALF, 2 * HALF))
            turned = pltpu.roll(both, HALF, 1, stride=1, stride_axis=0)
            bias_ref[h, 1 + n] = turned[:, :HALF]
            before = now


def head_mask(sh, h, rows):
    if sh.hp == 1:
        return None
    lane = lax.broadcasted_iota(jnp.int32, (1, sh.width), 1)
    return (lane >= h * HDIM) & (lane < (h + 1) * HDIM)


def only_head(sh, h, x):
    mask = head_mask(sh, h, x.shape[0])
    return x if mask is None else jnp.where(mask, x, jnp.zeros_like(x))


def prompt_rows_of(sh, ref, g, t, part):
    lanes = slice(part * sh.width, (part + 1) * sh.width)
    start = pl.multiple_of(g * sh.part, sh.part)
    return jnp.concatenate(
        [ref[t * sh.spt + s, pl.ds(start, sh.part), lanes] for s in range(sh.spt)], axis=0
    )


def cont_rows_of(sh, ref, c, part):
    lanes = slice(part * sh.width, (part + 1) * sh.width)
    return ref[c, G_LINE * sh.part :, lanes]


def put_prompt_rows(sh, ref, g, t, part, value):
    lanes = slice(part * sh.width, (part + 1) * sh.width)
    start = pl.multiple_of(g * sh.part, sh.part)
    for s in range(sh.spt):
        ref[t * sh.spt + s, pl.ds(start, sh.part), lanes] = value[
            s * sh.part : (s + 1) * sh.part
        ].astype(ref.dtype)


def transpose_low(x):
    return x.astype(F32).T.astype(BF)


def add_bias(scores, bias_ref, h, base, step_q):
    rows = []
    for a in range(2):
        cols = []
        for b in range(2):
            part = scores[a * HALF : (a + 1) * HALF, b * HALF : (b + 1) * HALF]
            cols.append(part * LOG2E + bias_ref[h, base + b * step_q - a])
        rows.append(jnp.concatenate(cols, axis=1))
    return jnp.concatenate(rows, axis=0)


def fold_max(x):
    return jnp.max(x.reshape(-1, 8, x.shape[-1]), axis=0)


def fold_sum(x):
    return jnp.sum(x.reshape(-1, 8, x.shape[-1]), axis=0)


def attn_forward_kernel(
    sh, group_ref, table_ref, bucket_ref, x_ref, o_ref, ot_ref, lse_ref, bias, vt, vtc, sc, perm
):
    order_conts(sh, group_ref, perm)
    build_bias(sh, table_ref, bucket_ref, bias)

    def make_vt(i, _):
        g, t = i // sh.tiles, lax.rem(i, sh.tiles)
        vt[i] = transpose_low(prompt_rows_of(sh, x_ref, g, t, 2))
        return 0

    lax.fori_loop(0, G_LINE * sh.tiles, make_vt, 0)

    def make_vtc(c, _):
        vtc[c] = transpose_low(cont_rows_of(sh, x_ref, c, 2))
        return 0

    lax.fori_loop(0, sh.srcs, make_vtc, 0)

    def scores_tile(keys, qh, base, step_q, kt, peaks):
        out = []
        for h in range(sh.hp):
            s = lax.dot_general(keys, qh[h], NT, preferred_element_type=F32)
            s = add_bias(s, bias, h, base, step_q)
            sc[h, pl.ds(pl.multiple_of(kt * TILE, TILE), TILE), :] = s
            out.append(jnp.maximum(peaks[h], fold_max(s)))
        return tuple(out)

    def value_tile(g, kt, peaks, carry):
        out = []
        for h in range(sh.hp):
            total, acc = carry[h]
            p = jnp.exp2(sc[h, pl.ds(pl.multiple_of(kt * TILE, TILE), TILE), :] - peaks[h])
            total = total + fold_sum(p)
            values = vt[g * sh.tiles + kt, h * HDIM : (h + 1) * HDIM, :]
            acc = acc + jnp.dot(values, p.astype(BF), preferred_element_type=F32)
            out.append((total, acc))
        return tuple(out)

    first_peaks = tuple(jnp.full((8, TILE), MASK_VALUE, F32) for _ in range(sh.hp))
    first_carry = tuple(
        (jnp.zeros((8, TILE), F32), jnp.zeros((HDIM, TILE), F32)) for _ in range(sh.hp)
    )

    def finish(unit, peaks, carry):
        outs = []
        for h in range(sh.hp):
            total = jnp.sum(carry[h][0], axis=0, keepdims=True)
            outs.append(carry[h][1] / total)
            lse_ref[unit, h : h + 1, :] = peaks[h] + jnp.log2(total)
        whole = jnp.concatenate(outs, axis=0) if sh.hp > 1 else outs[0]
        ot_ref[unit] = whole
        return whole.T

    def prompt_unit(i, _):
        g, qt = i // sh.tiles, lax.rem(i, sh.tiles)
        q = prompt_rows_of(sh, x_ref, g, qt, 0) * BF(HDIM**-0.5)
        qh = [only_head(sh, h, q) for h in range(sh.hp)]

        def first(kt, peaks):
            keys = prompt_rows_of(sh, x_ref, g, kt, 1)
            return scores_tile(keys, qh, 2 * (qt - kt) + 1, 1, kt, peaks)

        peaks = lax.fori_loop(0, qt + 1, first, first_peaks)
        peaks = [jnp.max(p, axis=0, keepdims=True) for p in peaks]
        carry = lax.fori_loop(0, qt + 1, lambda kt, c: value_tile(g, kt, peaks, c), first_carry)
        put_prompt_rows(sh, o_ref, g, qt, 0, finish(i, peaks, carry))
        return 0

    lax.fori_loop(0, G_LINE * sh.tiles, prompt_unit, 0)

    def cont_unit(i, _):
        conts = [perm[2 * i], perm[2 * i + 1]]
        g = i // sh.prompt_pairs
        q = jnp.concatenate([cont_rows_of(sh, x_ref, c, 0) for c in conts], axis=0)
        q = q * BF(HDIM**-0.5)
        qh = [only_head(sh, h, q) for h in range(sh.hp)]

        def first(kt, peaks):
            keys = prompt_rows_of(sh, x_ref, g, kt, 1)
            return scores_tile(keys, qh, SPAN_BLOCKS - 2 * kt, 0, kt, peaks)

        peaks = lax.fori_loop(0, sh.tiles, first, first_peaks)
        own = []
        next_peaks = []
        for h in range(sh.hp):
            parts = []
            for b in range(2):
                keys = cont_rows_of(sh, x_ref, conts[b], 1)
                s = lax.dot_general(
                    keys, qh[h][b * HALF : (b + 1) * HALF], NT, preferred_element_type=F32
                )
                parts.append(s * LOG2E + bias[h, 1])
            own.append(jnp.concatenate(parts, axis=1))
            next_peaks.append(jnp.maximum(peaks[h], fold_max(own[h])))
        peaks = [jnp.max(p, axis=0, keepdims=True) for p in next_peaks]
        start = []
        for h in range(sh.hp):
            p = jnp.exp2(own[h] - peaks[h])
            low = p.astype(BF)
            acc = jnp.concatenate(
                [
                    jnp.dot(
                        vtc[conts[b], h * HDIM : (h + 1) * HDIM, :],
                        low[:, b * HALF : (b + 1) * HALF],
                        preferred_element_type=F32,
                    )
                    for b in range(2)
                ],
                axis=1,
            )
            start.append((fold_sum(p), acc))
        carry = lax.fori_loop(
            0, sh.tiles, lambda kt, c: value_tile(g, kt, peaks, c), tuple(start)
        )
        done = finish(G_LINE * sh.tiles + i, peaks, carry)
        for b in range(2):
            o_ref[conts[b], G_LINE * sh.part :, :] = done[b * HALF : (b + 1) * HALF].astype(BF)
        return 0

    lax.fori_loop(0, sh.pairs, cont_unit, 0)


def attn_backward_kernel(
    sh,
    group_ref,
    table_ref,
    bucket_ref,
    x_ref,
    do_ref,
    ot_ref,
    lse_ref,
    dx_ref,
    dtable_ref,
    bias,
    dbias,
    ktr,
    ktc,
    dk,
    dv,
    perm,
):
    order_conts(sh, group_ref, perm)
    build_bias(sh, table_ref, bucket_ref, bias)
    dbias[...] = jnp.zeros_like(dbias)
    dk[...] = jnp.zeros_like(dk)
    dv[...] = jnp.zeros_like(dv)

    def make_kt(i, _):
        g, t = i // sh.tiles, lax.rem(i, sh.tiles)
        ktr[i] = transpose_low(prompt_rows_of(sh, x_ref, g, t, 1))
        return 0

    lax.fori_loop(0, G_LINE * sh.tiles, make_kt, 0)

    def make_ktc(c, _):
        ktc[c] = transpose_low(cont_rows_of(sh, x_ref, c, 1))
        return 0

    lax.fori_loop(0, sh.srcs, make_ktc, 0)

    def inner_terms(unit, do):
        outs = []
        turned = do.astype(F32).T
        for h in range(sh.hp):
            rows = slice(h * HDIM, (h + 1) * HDIM)
            prod = ot_ref[unit, rows, :] * turned[rows, :]
            outs.append(jnp.sum(prod, axis=0, keepdims=True))
        return outs

    def grads_tile(g, kt, qh, doh, lse, inner, base, step_q, dqs):
        keys = prompt_rows_of(sh, x_ref, g, kt, 1)
        values = prompt_rows_of(sh, x_ref, g, kt, 2)
        slot = g * sh.tiles + kt
        out = []
        dkey = dvalue = None
        for h in range(sh.hp):
            s = lax.dot_general(keys, qh[h], NT, preferred_element_type=F32)
            dp = lax.dot_general(values, doh[h], NT, preferred_element_type=F32)
            p = jnp.exp2(add_bias(s, bias, h, base, step_q) - lse[h])
            ds = p * (dp - inner[h])
            for a in range(2):
                for b in range(2):
                    dbias[h, base + b * step_q - a] += ds[
                        a * HALF : (a + 1) * HALF, b * HALF : (b + 1) * HALF
                    ]
            low = ds.astype(BF)
            more_k = jnp.dot(low, qh[h], preferred_element_type=F32)
            more_v = jnp.dot(p.astype(BF), doh[h], preferred_element_type=F32)
            dkey = more_k if dkey is None else dkey + more_k
            dvalue = more_v if dvalue is None else dvalue + more_v
            turned = ktr[slot, h * HDIM : (h + 1) * HDIM, :]
            out.append(dqs[h] + jnp.dot(turned, low, preferred_element_type=F32))
        dk[slot] += dkey
        dv[slot] += dvalue
        return tuple(out)

    def finish(dqs):
        whole = jnp.concatenate(dqs, axis=0) if sh.hp > 1 else dqs[0]
        return whole.T * (HDIM**-0.5)

    first_dq = tuple(jnp.zeros((HDIM, TILE), F32) for _ in range(sh.hp))

    def prompt_unit(i, _):
        g, qt = i // sh.tiles, lax.rem(i, sh.tiles)
        q = prompt_rows_of(sh, x_ref, g, qt, 0) * BF(HDIM**-0.5)
        do = prompt_rows_of(sh, do_ref, g, qt, 0)
        qh = [only_head(sh, h, q) for h in range(sh.hp)]
        doh = [only_head(sh, h, do) for h in range(sh.hp)]
        inner = inner_terms(i, do)
        lse = [lse_ref[i, h : h + 1, :] for h in range(sh.hp)]

        def body(kt, dqs):
            return grads_tile(g, kt, qh, doh, lse, inner, 2 * (qt - kt) + 1, 1, dqs)

        dqs = lax.fori_loop(0, qt + 1, body, first_dq)
        put_prompt_rows(sh, dx_ref, g, qt, 0, finish(dqs))
        return 0

    lax.fori_loop(0, G_LINE * sh.tiles, prompt_unit, 0)

    def cont_unit(i, _):
        conts = [perm[2 * i], perm[2 * i + 1]]
        unit = G_LINE * sh.tiles + i
        g = i // sh.prompt_pairs
        q = jnp.concatenate([cont_rows_of(sh, x_ref, c, 0) for c in conts], axis=0)
        q = q * BF(HDIM**-0.5)
        do = jnp.concatenate([cont_rows_of(sh, do_ref, c, 0) for c in conts], axis=0)
        qh = [only_head(sh, h, q) for h in range(sh.hp)]
        doh = [only_head(sh, h, do) for h in range(sh.hp)]
        inner = inner_terms(unit, do)
        lse = [lse_ref[unit, h : h + 1, :] for h in range(sh.hp)]

        def body(kt, dqs):
            return grads_tile(g, kt, qh, doh, lse, inner, SPAN_BLOCKS - 2 * kt, 0, dqs)

        dqs = lax.fori_loop(0, sh.tiles, body, first_dq)
        more = [[None] * 2 for _ in range(sh.hp)]
        for b in range(2):
            cols = slice(b * HALF, (b + 1) * HALF)
            keys = cont_rows_of(sh, x_ref, conts[b], 1)
            values = cont_rows_of(sh, x_ref, conts[b], 2)
            dkey = dvalue = None
            for h in range(sh.hp):
                s = lax.dot_general(keys, qh[h][cols], NT, preferred_element_type=F32)
                dp = lax.dot_general(values, doh[h][cols], NT, preferred_element_type=F32)
                p = jnp.exp2(s * LOG2E + bias[h, 1] - lse[h][:, cols])
                ds = p * (dp - inner[h][:, cols])
                dbias[h, 1] += ds
                low = ds.astype(BF)
                more_k = jnp.dot(low, qh[h][cols], preferred_element_type=F32)
                more_v = jnp.dot(p.astype(BF), doh[h][cols], preferred_element_type=F32)
                dkey = more_k if dkey is None else dkey + more_k
                dvalue = more_v if dvalue is None else dvalue + more_v
                turned = ktc[conts[b], h * HDIM : (h + 1) * HDIM, :]
                more[h][b] = jnp.dot(turned, low, preferred_element_type=F32)
            w = sh.width
            dx_ref[conts[b], G_LINE * sh.part :, w : 2 * w] = dkey.astype(BF)
            dx_ref[conts[b], G_LINE * sh.part :, 2 * w :] = dvalue.astype(BF)
        dqs = [dqs[h] + jnp.concatenate(more[h], axis=1) for h in range(sh.hp)]
        done = finish(dqs)
        for b in range(2):
            dx_ref[conts[b], G_LINE * sh.part :, : sh.width] = done[
                b * HALF : (b + 1) * HALF
            ].astype(BF)
        return 0

    lax.fori_loop(0, sh.pairs, cont_unit, 0)

    def put_keys(i, _):
        g, t = i // sh.tiles, lax.rem(i, sh.tiles)
        put_prompt_rows(sh, dx_ref, g, t, 1, dk[i])
        put_prompt_rows(sh, dx_ref, g, t, 2, dv[i])
        return 0

    lax.fori_loop(0, G_LINE * sh.tiles, put_keys, 0)

    bucket = bucket_ref[...]
    key_row = lax.broadcasted_iota(jnp.int32, (HALF, 2 * HALF), 0)
    for h in range(sh.hp):
        spread = []
        for n in range(SPAN_BLOCKS):
            wide = jnp.concatenate(
                [jnp.zeros((HALF, HALF), F32), dbias[h, 1 + n]], axis=1
            )
            for bit in range(7):
                moved = pltpu.roll(wide, 2 * HALF - (1 << bit), 1)
                wide = jnp.where((key_row & (1 << bit)) != 0, moved, wide)
            spread.append(jnp.sum(wide, axis=0, keepdims=True))
        rows = []
        for n in range(SPAN_BLOCKS):
            row = spread[n][:, HALF:]
            if n + 1 < SPAN_BLOCKS:
                row = row + spread[n + 1][:, :HALF]
            rows.append(row)
        by_dist = jnp.concatenate(rows, axis=0)
        sums = [
            jnp.sum(jnp.where(bucket == b, by_dist, 0.0), axis=0, keepdims=True)
            for b in range(BUCKETS)
        ]
        lanes = jnp.concatenate(sums, axis=0)
        dtable_ref[h * BUCKETS : (h + 1) * BUCKETS, :] = jnp.broadcast_to(
            jnp.sum(lanes, axis=1, keepdims=True), (BUCKETS, HALF)
        )


SMEM_SPEC = pl.BlockSpec(memory_space=pltpu.SMEM)
VMEM_SPEC = pl.BlockSpec(memory_space=pltpu.VMEM)
GRANT = 48 * 1024 * 1024


def attend_forward(sh, group, table, bucket, x):
    return pl.pallas_call(
        functools.partial(attn_forward_kernel, sh),
        out_shape=(
            jax.ShapeDtypeStruct((sh.srcs, sh.rows, sh.width), BF),
            jax.ShapeDtypeStruct((sh.units, sh.width, TILE), F32),
            jax.ShapeDtypeStruct((sh.units, 8, TILE), F32),
        ),
        in_specs=[SMEM_SPEC, SMEM_SPEC, VMEM_SPEC, VMEM_SPEC],
        out_specs=(VMEM_SPEC, VMEM_SPEC, VMEM_SPEC),
        scratch_shapes=[
            pltpu.VMEM((sh.hp, SPAN_BLOCKS + 1, HALF, HALF), F32),
            pltpu.VMEM((G_LINE * sh.tiles, sh.width, TILE), BF),
            pltpu.VMEM((sh.srcs, sh.width, HALF), BF),
            pltpu.VMEM((sh.hp, PLEN, TILE), F32),
            pltpu.SMEM((sh.srcs,), jnp.int32),
        ],
        compiler_params=pltpu.CompilerParams(vmem_limit_bytes=GRANT),
        cost_estimate=pl.CostEstimate(
            flops=10**10, bytes_accessed=8 * 10**6, transcendentals=5 * 10**6
        ),
        name="attend_forward",
    )(group, table, bucket, x)


def attend_backward(sh, group, table, bucket, x, do, ot, lse):
    return pl.pallas_call(
        functools.partial(attn_backward_kernel, sh),
        out_shape=(
            jax.ShapeDtypeStruct((sh.srcs, sh.rows, 3 * sh.width), BF),
            jax.ShapeDtypeStruct((sh.hp * BUCKETS, HALF), F32),
        ),
        in_specs=[SMEM_SPEC, SMEM_SPEC, VMEM_SPEC, VMEM_SPEC, VMEM_SPEC, VMEM_SPEC, VMEM_SPEC],
        out_specs=(VMEM_SPEC, VMEM_SPEC),
        scratch_shapes=[
            pltpu.VMEM((sh.hp, SPAN_BLOCKS + 1, HALF, HALF), F32),
            pltpu.VMEM((sh.hp, SPAN_BLOCKS + 1, HALF, HALF), F32),
            pltpu.VMEM((G_LINE * sh.tiles, sh.width, TILE), BF),
            pltpu.VMEM((sh.srcs, sh.width, HALF), BF),
            pltpu.VMEM((G_LINE * sh.tiles, TILE, sh.width), F32),
            pltpu.VMEM((G_LINE * sh.tiles, TILE, sh.width), F32),
            pltpu.SMEM((sh.srcs,), jnp.int32),
        ],
        compiler_params=pltpu.CompilerParams(vmem_limit_bytes=GRANT),
        cost_estimate=pl.CostEstimate(
            flops=2 * 10**10, bytes_accessed=12 * 10**6, transcendentals=5 * 10**6
        ),
        name="attend_backward",
    )(group, table, bucket, x, do, ot, lse)


def ring_order(count):
    deep, wide = 4, count // 4
    order = [a * wide for a in range(deep)]
    for turn, a in enumerate(reversed(range(deep))):
        row = [a * wide + b for b in range(1, wide)]
        order += row if turn % 2 == 0 else row[::-1]
    return order


def ring_hop(x, count, step):
    ring = ring_order(count)
    return lax.ppermute(x, "fsdp", [(ring[i], ring[(i + step) % count]) for i in range(count)])


def tied(*values):
    return lax.optimization_barrier(values)


class RingGather:
    def __init__(self, own, count):
        self.count = count
        self.chunks = [None] * count
        self.chunks[0] = own
        self.right = self.left = own
        self.done = 0
        self.steps = count // 2

    def step(self):
        self.done += 1
        s = self.done
        if s < self.steps:
            self.right = ring_hop(self.right, self.count, 1)
            self.left = ring_hop(self.left, self.count, -1)
        else:
            half = self.right.shape[0] // 2
            self.right = ring_hop(self.right[:half], self.count, 1)
            self.left = ring_hop(self.left[half:], self.count, -1)
        self.keep()

    def keep(self):
        s = self.done
        if s < self.steps:
            self.chunks[self.count - s] = self.right
            self.chunks[s] = self.left
        else:
            self.chunks[s] = jnp.concatenate([self.right, self.left], 0)

    def tie(self, value):
        value, self.right, self.left = tied(value, self.right, self.left)
        self.keep()
        return value


class RingScatter:
    def __init__(self, part, count):
        self.part, self.count = part, count
        self.right = self.left = None
        self.done = 0
        self.steps = count // 2

    def step(self):
        count, s = self.count, self.done
        away = self.steps - s
        if s == 0:
            far = self.part(away)
            half = far.shape[0] // 2
            send_left, send_right = far[:half], far[half:]
        else:
            near_left = self.part(count - away).astype(F32)
            near_right = self.part(away).astype(F32)
            if s == 1:
                half = near_left.shape[0] // 2
                send_left = jnp.concatenate(
                    [near_left[:half] + self.left.astype(F32), near_left[half:]], 0
                )
                send_right = jnp.concatenate(
                    [near_right[:half], near_right[half:] + self.right.astype(F32)], 0
                )
            else:
                send_left = near_left + self.left.astype(F32)
                send_right = near_right + self.right.astype(F32)
        self.left = ring_hop(send_left.astype(BF), count, -1)
        self.right = ring_hop(send_right.astype(BF), count, 1)
        self.done += 1

    def tie(self, value):
        value, self.right, self.left = tied(value, self.right, self.left)
        return value

    def finish(self):
        return self.part(0).astype(F32) + self.right.astype(F32) + self.left.astype(F32)


MESH_ID = pl.DeviceIdType.MESH
DEEP = 4


class Spot:
    def __init__(self):
        e, f = lax.axis_index("expert"), lax.axis_index("fsdp")
        self.x, self.c = e // 2, lax.rem(e, 2)
        self.z, self.y = f // 2, lax.rem(f, 2)
        self.ox, self.oy, self.oc = 1 - self.x, 1 - self.y, 1 - self.c

    def place(self, x=None, y=None, z=None, c=None):
        x = self.x if x is None else x
        y = self.y if y is None else y
        z = self.z if z is None else z
        c = self.c if c is None else c
        return {"expert": x * 2 + c, "fsdp": z * 2 + y}

    def block(self, x, y, z, c):
        return (x * 2 + c) * 8 + z * 2 + y

    def greet(self):
        barrier = pltpu.get_barrier_semaphore()
        for target in (self.place(x=self.ox), self.place(y=self.oy), self.place(c=self.oc)):
            pl.semaphore_signal(barrier, inc=1, device_id=target, device_id_type=MESH_ID)
        for step in (-1, 1):

            @pl.when(self.inside(self.z + step))
            def _(step=step):
                pl.semaphore_signal(
                    barrier, inc=1, device_id=self.along(step), device_id_type=MESH_ID
                )

        pl.semaphore_wait(barrier, 4 + self.z * (DEEP - 1 - self.z) // 2)

    def wrap(self, step):
        return lax.rem(self.z + step + DEEP, DEEP)

    def along(self, step):
        return self.place(z=self.wrap(step))

    def inside(self, z):
        return (z >= 0) & (z < DEEP)


def dense_gather_kernel(cut, x_ref, out_ref, send_sems, recv_sems, own_sem):
    me = Spot()
    rows = x_ref.shape[0]
    spans = [(0, cut), (cut, rows - cut)]
    pending = []

    def view(ref, h):
        return ref.at[pl.ds(*spans[h])]

    def send(src, blk, h, target, cond):
        copy = pltpu.make_async_remote_copy(
            src_ref=src,
            dst_ref=view(out_ref.at[blk], h),
            send_sem=send_sems.at[len(pending)],
            recv_sem=recv_sems.at[blk, h],
            device_id=target,
            device_id_type=MESH_ID,
        )
        pending.append((copy, cond))
        if cond is None:
            copy.start()
        else:
            pl.when(cond)(copy.start)

    def arrive(blk, h, cond):
        copy = pltpu.make_async_remote_copy(
            src_ref=view(out_ref.at[blk], h),
            dst_ref=view(out_ref.at[blk], h),
            send_sem=send_sems.at[0],
            recv_sem=recv_sems.at[blk, h],
            device_id=me.place(c=me.oc),
            device_id_type=MESH_ID,
        )
        if cond is None:
            copy.wait_recv()
        else:
            pl.when(cond)(copy.wait_recv)

    def both(a, b):
        return b if a is None else (a if b is None else a & b)

    by_y, by_x = me.place(y=me.oy), me.place(x=me.ox)
    core = me.place(c=me.oc)
    me.greet()
    mine = me.block(me.x, me.y, me.z, me.c)
    own = pltpu.make_async_copy(x_ref, out_ref.at[mine], own_sem)
    own.start()
    for h in range(2):
        for step in (-1, 1):
            send(view(x_ref, h), mine, h, me.along(step), me.inside(me.z + step))
    for h in range(2):
        for target in (by_y, by_x, core):
            send(view(x_ref, h), mine, h, target, None)

    def line(dist):
        if dist == 0:
            return [(me.z, None, 0)]
        return [(me.wrap(s * dist), me.inside(me.z + s * dist), s) for s in (-1, 1)]

    def from_line(dist):
        for zb, cond, sign in line(dist):
            blk = me.block(me.x, me.y, zb, me.c)
            for h in range(2):
                arrive(blk, h, cond)
                src = view(out_ref.at[blk], h)
                send(src, blk, h, me.along(-sign), both(cond, me.inside(me.z - sign)))
                for target in (by_y, by_x, core):
                    send(src, blk, h, target, cond)

    def from_side(dist):
        for zb, cond, _ in line(dist):
            for h in range(2):
                one = me.block(me.x, me.oy, zb, me.c)
                two = me.block(me.ox, me.y, zb, me.c)
                onward, last = ((one, by_x), two) if h == 0 else ((two, by_y), one)
                arrive(onward[0], h, cond)
                src = view(out_ref.at[onward[0]], h)
                send(src, onward[0], h, onward[1], cond)
                send(src, onward[0], h, core, cond)
                arrive(last, h, cond)
                send(view(out_ref.at[last], h), last, h, core, cond)

    def from_corner(dist):
        for zb, cond, _ in line(dist):
            blk = me.block(me.ox, me.oy, zb, me.c)
            for h in range(2):
                arrive(blk, h, cond)
                send(view(out_ref.at[blk], h), blk, h, core, cond)

    for dist in range(DEEP):
        if dist > 0:
            from_line(dist)
        from_side(dist)
        if dist > 0:
            from_corner(dist - 1)
    from_corner(DEEP - 1)
    for x in range(2):
        for y in range(2):
            for z in range(DEEP):
                for h in range(2):
                    arrive(me.block(x, y, z, me.oc), h, None)
    own.wait()
    for copy, cond in pending:
        if cond is None:
            copy.wait_send()
        else:
            pl.when(cond)(copy.wait_send)


def dense_gather(x, count):
    rows = x.shape[0]
    if count != 32 or lax.axis_size("fsdp") != 2 * DEEP:
        return lax.all_gather(x, ("expert", "fsdp"), axis=0, tiled=False)
    cut = rows // 32 * 16 + 16 * (rows // 16 % 2)
    return pl.pallas_call(
        functools.partial(dense_gather_kernel, cut),
        out_shape=jax.ShapeDtypeStruct((count,) + x.shape, x.dtype),
        in_specs=[pl.BlockSpec(memory_space=pltpu.VMEM)],
        out_specs=pl.BlockSpec(memory_space=pl.ANY),
        scratch_shapes=[
            pltpu.SemaphoreType.DMA((128,)),
            pltpu.SemaphoreType.DMA((count, 2)),
            pltpu.SemaphoreType.DMA,
        ],
        compiler_params=pltpu.CompilerParams(collective_id=0, has_side_effects=True),
        cost_estimate=pl.CostEstimate(
            flops=0, bytes_accessed=100 * 10**6, transcendentals=0
        ),
        name="dense_gather",
    )(x)


def add_into(dst, src):
    def body(i, _):
        at = pl.ds(pl.multiple_of(i * 16, 16), 16)
        dst[at, :] = (dst[at, :].astype(F32) + src[at, :].astype(F32)).astype(BF)
        return 0

    lax.fori_loop(0, dst.shape[0] // 16, body, 0)


def dense_sum_kernel(
    cut, g_ref, out_ref, acc, cbuf, xbuf, ybuf, zbuf, send_sems, recv_sems, load_sems
):
    me = Spot()
    rows = out_ref.shape[0]
    top, low = pl.ds(0, cut), pl.ds(cut, rows - cut)
    pending = []

    def send(src, dst, at, target, cond=None):
        copy = pltpu.make_async_remote_copy(
            src_ref=src,
            dst_ref=dst,
            send_sem=send_sems.at[len(pending)],
            recv_sem=recv_sems.at[at],
            device_id=target,
            device_id_type=MESH_ID,
        )
        pending.append((copy, cond))
        if cond is None:
            copy.start()
        else:
            pl.when(cond)(copy.start)

    def arrive(dst, at):
        pltpu.make_async_remote_copy(
            src_ref=dst,
            dst_ref=dst,
            send_sem=send_sems.at[0],
            recv_sem=recv_sems.at[at],
            device_id=me.place(c=me.oc),
            device_id_type=MESH_ID,
        ).wait_recv()

    by_y, by_x, core = me.place(y=me.oy), me.place(x=me.ox), me.place(c=me.oc)
    me.greet()
    offsets = (2, 3, 1, 0)
    zs = [me.wrap(k) for k in offsets]
    loads = []
    for k in range(DEEP):
        for x in range(2):
            at = x * DEEP + k
            theirs = (x * 2 + me.oc) * 8 + zs[k] * 2
            send(g_ref.at[pl.ds(theirs, 2)], cbuf.at[at], at, core)
            ours = (x * 2 + me.c) * 8 + zs[k] * 2
            load = pltpu.make_async_copy(g_ref.at[pl.ds(ours, 2)], acc.at[at], load_sems.at[at])
            load.start()
            loads.append(load)

    def first(k):
        for x in range(2):
            at = x * DEEP + k
            loads[k * 2 + x].wait()
            arrive(cbuf.at[at], at)
            for y in range(2):
                add_into(acc.at[at, y], cbuf.at[at, y])
        base = 8 + k * 6
        for y in range(2):
            send(acc.at[me.ox * DEEP + k, y, top], xbuf.at[k, y, top], base + y, by_x)
        for x in range(2):
            send(acc.at[x * DEEP + k, me.oy, low], ybuf.at[k, x, low], base + 2 + x, by_y)

    def second(k):
        base = 8 + k * 6
        for y in range(2):
            arrive(xbuf.at[k, y, top], base + y)
            add_into(acc.at[me.x * DEEP + k, y, top], xbuf.at[k, y, top])
        for x in range(2):
            arrive(ybuf.at[k, x, low], base + 2 + x)
            add_into(acc.at[x * DEEP + k, me.y, low], ybuf.at[k, x, low])
        send(acc.at[me.x * DEEP + k, me.oy, top], ybuf.at[k, 0, top], base + 4, by_y)
        send(acc.at[me.ox * DEEP + k, me.y, low], xbuf.at[k, 0, low], base + 5, by_x)

    def third(k):
        base = 8 + k * 6
        block = acc.at[me.x * DEEP + k, me.y]
        arrive(ybuf.at[k, 0, top], base + 4)
        add_into(block.at[top], ybuf.at[k, 0, top])
        arrive(xbuf.at[k, 0, low], base + 5)
        add_into(block.at[low], xbuf.at[k, 0, low])

    for step in range(DEEP + 2):
        if step < DEEP:
            first(step)
        if 0 <= step - 1 < DEEP:
            second(step - 1)
        if 0 <= step - 2 < DEEP:
            third(step - 2)

    for dist in (3, 2, 1):
        for sign in (-1, 1):
            side = (sign + 1) // 2
            term = acc.at[me.x * DEEP + offsets.index(sign * dist % DEEP), me.y]
            if dist < 3:

                @pl.when(me.inside(me.z + sign * dist) & me.inside(me.z - sign))
                def _(term=term, dist=dist, side=side):
                    buf = zbuf.at[dist * 2 + side]
                    arrive(buf, 34 + dist * 2 + side)
                    add_into(term, buf)

            send(
                term,
                zbuf.at[(dist - 1) * 2 + side],
                32 + dist * 2 + side,
                me.along(sign),
                me.inside(me.z + sign * dist),
            )
    block = acc.at[me.x * DEEP + DEEP - 1, me.y]
    for sign in (-1, 1):

        @pl.when(me.inside(me.z - sign))
        def _(sign=sign):
            buf = zbuf.at[(sign + 1) // 2]
            arrive(buf, 32 + 2 + (sign + 1) // 2)
            add_into(block, buf)

    def put(i, _):
        at = pl.ds(pl.multiple_of(i * 16, 16), 16)
        out_ref[at, :] = block[at, :].astype(F32)
        return 0

    lax.fori_loop(0, rows // 16, put, 0)
    for copy, cond in pending:
        if cond is None:
            copy.wait_send()
        else:
            pl.when(cond)(copy.wait_send)


def dense_sum(x):
    count, rows, width = x.shape
    if count != 32 or lax.axis_size("fsdp") != 2 * DEEP:
        flat = x.reshape(count * rows, width)
        return lax.psum_scatter(
            flat, ("expert", "fsdp"), scatter_dimension=0, tiled=True
        ).astype(F32)
    cut = rows // 32 * 16 + 16 * (rows // 16 % 2)
    pair = (2 * DEEP, 2, rows, width)
    return pl.pallas_call(
        functools.partial(dense_sum_kernel, cut),
        out_shape=jax.ShapeDtypeStruct((rows, width), F32),
        in_specs=[pl.BlockSpec(memory_space=pl.ANY)],
        out_specs=pl.BlockSpec(memory_space=pltpu.VMEM),
        scratch_shapes=[
            pltpu.VMEM(pair, BF),
            pltpu.VMEM(pair, BF),
            pltpu.VMEM((DEEP, 2, rows, width), BF),
            pltpu.VMEM((DEEP, 2, rows, width), BF),
            pltpu.VMEM((6, rows, width), BF),
            pltpu.SemaphoreType.DMA((48,)),
            pltpu.SemaphoreType.DMA((48,)),
            pltpu.SemaphoreType.DMA((8,)),
        ],
        compiler_params=pltpu.CompilerParams(
            collective_id=1, has_side_effects=True, vmem_limit_bytes=40 * 1024 * 1024
        ),
        cost_estimate=pl.CostEstimate(
            flops=0, bytes_accessed=100 * 10**6, transcendentals=0
        ),
        name="dense_sum",
    )(x)


def local(
    inputs,
    w_qkv,
    w_out,
    attn_gain,
    moe_gain,
    w_router,
    bias_table,
    w_gate,
    w_up,
    w_down,
    routes,
    slot_order,
    group_map,
    buckets,
    grad_output,
):
    tok_count = inputs.shape[0]
    expert_count = w_router.shape[1]
    capacity = (5 * TOPK * tok_count + 4 * expert_count - 1) // (4 * expert_count)
    fsdp_count = lax.axis_size("fsdp")
    fsdp_place = lax.axis_index("fsdp")
    expert_place = lax.axis_index("expert")
    group_count = lax.axis_size("expert") * fsdp_count
    sh = Shape(fsdp_count)
    prompt_rows = sh.part * G_LINE
    slot_total = expert_count * capacity
    shard = w_qkv.shape[0]
    ff_shard = w_down.shape[1]

    def by_prompt(x):
        head = x[:prompt_rows].reshape(sh.part, G_LINE, -1).transpose(1, 0, 2)
        return jnp.concatenate([head.reshape(prompt_rows, -1), x[prompt_rows:]], 0)

    def by_token(x):
        head = x[:prompt_rows].reshape(G_LINE, sh.part, -1).transpose(1, 0, 2)
        return jnp.concatenate([head.reshape(prompt_rows, -1), x[prompt_rows:]], 0)

    weights = RingGather(jnp.concatenate([w_gate[0].T, w_up[0].T, w_down[0]], 0), fsdp_count)
    spread = [fsdp_count // 8] * 4
    spread[0] += fsdp_count // 2 - sum(spread)

    def run(ring, count):
        for _ in range(count):
            ring.step()

    small = jnp.concatenate(
        [attn_gain, moe_gain, w_router.reshape(-1), bias_table, group_map.astype(BF)]
    )
    small_rows = -(-small.shape[0] // D)
    small_rows = -(-small_rows // 16) * 16
    small = jnp.pad(small, (0, small_rows * D - small.shape[0])).reshape(small_rows, D)
    pack = jnp.concatenate([w_qkv[:, i * D : (i + 1) * D] for i in range(3)] + [w_out, small], 0)
    gathered = dense_gather(pack, group_count)
    run(weights, spread[0])
    qkv_full = jnp.concatenate(
        [gathered[:, i * shard : (i + 1) * shard].reshape(D, D) for i in range(3)], 1
    )
    qkv_full = weights.tie(qkv_full)
    out_full = gathered[:, 3 * shard : 4 * shard].reshape(D, D)
    tail = gathered[:, 4 * shard]
    marks = [0, shard, 2 * shard, 2 * shard + shard * expert_count]
    marks += [marks[-1] + bias_table.shape[0]]
    attn_scale = tail[:, marks[0] : marks[1]].reshape(D).astype(F32)
    moe_scale = tail[:, marks[1] : marks[2]].reshape(D).astype(F32)
    router = tail[:, marks[2] : marks[3]].reshape(D, expert_count).astype(F32)
    table = tail[:, marks[3] : marks[4]].reshape(fsdp_count, sh.hp, BUCKETS)
    my_table = lax.dynamic_index_in_dim(table, fsdp_place, 0, keepdims=False).astype(F32)
    groups = tail[:, marks[4]].reshape(-1, fsdp_count)
    my_groups = lax.dynamic_index_in_dim(groups, expert_place, 0, keepdims=False)
    my_groups = my_groups.astype(jnp.int32)
    bucket = buckets.reshape(SPAN_BLOCKS, HALF)

    token_input = by_prompt(inputs)
    grad_rows_low = by_prompt(grad_output)
    routes = by_prompt(routes)
    slot_order = by_prompt(slot_order)

    input_float = token_input.astype(F32)
    normed, first_pull = jax.vjp(rms_scale, input_float, attn_scale)
    normed_low = normed.astype(BF)
    qkv_rows = jnp.dot(normed_low, qkv_full, preferred_element_type=F32).astype(BF)
    by_heads = (
        qkv_rows.reshape(tok_count, 3, fsdp_count, sh.width)
        .transpose(2, 0, 1, 3)
        .reshape(fsdp_count, tok_count, 3 * sh.width)
    )
    head_qkv = lax.all_to_all(by_heads, "fsdp", split_axis=0, concat_axis=0, tiled=True)
    run(weights, spread[1])
    head_qkv = weights.tie(head_qkv)
    head_att, att_turned, att_lse = attend_forward(sh, my_groups, my_table, bucket, head_qkv)
    att_back = lax.all_to_all(head_att, "fsdp", split_axis=0, concat_axis=0, tiled=True)
    run(weights, spread[2])
    att_back = weights.tie(att_back)
    attn_low = att_back.transpose(1, 0, 2).reshape(tok_count, D)

    middle = input_float + jnp.dot(attn_low, out_full, preferred_element_type=F32)
    second_normed, second_pull = jax.vjp(rms_scale, middle, moe_scale)
    (gate_pair, losses), router_pull = jax.vjp(
        lambda normed_rows, router_rows: route_local(normed_rows, router_rows, routes),
        second_normed,
        router,
    )
    kept_mask = (slot_order < capacity).astype(F32)
    gate_kept = gate_pair * kept_mask
    slot_ids = jnp.arange(slot_total, dtype=jnp.int32)
    slot_place = jnp.where(slot_order < capacity, routes * capacity + slot_order, -1)
    hot = [slot_place[:, k : k + 1] == slot_ids[None, :] for k in range(TOPK)]
    any_low = (hot[0] | hot[1]).astype(BF)
    outgoing = lax.dot_general(
        any_low, second_normed.astype(BF), TN, preferred_element_type=F32
    ).astype(BF)

    def swap_experts(rows):
        rows = rows.reshape(expert_count, capacity, D)
        rows = lax.all_to_all(rows, "expert", split_axis=0, concat_axis=0, tiled=True)
        return rows.reshape(slot_total, D)

    expert_rows = swap_experts(outgoing)
    run(weights, spread[3])
    expert_rows = weights.tie(expert_rows)
    slot_gate = jnp.sum(
        jnp.where(hot[0], gate_kept[:, 0:1], 0.0) + jnp.where(hot[1], gate_kept[:, 1:2], 0.0),
        axis=0,
    )
    slot_grad = lax.dot_general(any_low, grad_rows_low, TN, preferred_element_type=F32)
    grad_result = swap_experts((slot_gate[:, None] * slot_grad).astype(BF))

    gate_whole, up_whole, down_whole = (
        jnp.concatenate([c[i * ff_shard : (i + 1) * ff_shard] for c in weights.chunks], 0)
        for i in range(3)
    )
    gate_pre = lax.dot_general(expert_rows, gate_whole, NT, preferred_element_type=F32)
    up_pre = lax.dot_general(expert_rows, up_whole, NT, preferred_element_type=F32)
    hidden = gated_unit(gate_pre, up_pre).astype(BF)
    result_rows = jnp.dot(hidden, down_whole, preferred_element_type=F32).astype(BF)
    returned = swap_experts(result_rows)

    grad_hidden = lax.dot_general(grad_result, down_whole, NT, preferred_element_type=F32)
    grad_gate_pre, grad_up_pre = activation_grads(gate_pre, up_pre, grad_hidden)
    grad_rows = jnp.dot(grad_gate_pre, gate_whole, preferred_element_type=F32) + jnp.dot(
        grad_up_pre, up_whole, preferred_element_type=F32
    )
    grad_sent = swap_experts(grad_rows.astype(BF))
    down_total = lax.dot_general(hidden, grad_result, TN, preferred_element_type=F32).astype(BF)
    gate_total = lax.dot_general(
        grad_gate_pre, expert_rows, TN, preferred_element_type=F32
    ).astype(BF)
    up_total = lax.dot_general(grad_up_pre, expert_rows, TN, preferred_element_type=F32).astype(BF)

    def part(k):
        rows = slice(k * ff_shard, (k + 1) * ff_shard)
        return jnp.concatenate([gate_total[rows], up_total[rows], down_total[rows]], 0)

    sums = RingScatter(part, fsdp_count)
    run(sums, spread[0])
    grad_sent = sums.tie(grad_sent)

    picked = [
        jnp.dot(h.astype(BF), returned, preferred_element_type=F32) for h in hot
    ]
    block_out = middle + gate_kept[:, 0:1] * picked[0] + gate_kept[:, 1:2] * picked[1]
    output = by_token(block_out.astype(BF))
    grad_final = grad_rows_low.astype(F32)
    grad_pair = (
        jnp.stack([jnp.sum(grad_final * p, axis=-1) for p in picked], -1) * kept_mask
    )
    grad_second = jnp.dot(any_low, grad_sent, preferred_element_type=F32)
    loss_weights = jnp.array([ZLOSS_FACTOR, BALANCE_FACTOR], F32) / group_count
    router_normed, grad_router = router_pull((grad_pair, loss_weights))
    grad_middle_part, grad_moe_gain = second_pull(grad_second + router_normed)
    grad_middle = grad_final + grad_middle_part
    grad_branch = grad_middle.astype(BF)
    grad_attn = lax.dot_general(grad_branch, out_full, NT, preferred_element_type=F32).astype(BF)
    head_grad = (
        grad_attn.reshape(tok_count, fsdp_count, sh.width).transpose(1, 0, 2)
    )
    head_grad = lax.all_to_all(head_grad, "fsdp", split_axis=0, concat_axis=0, tiled=True)
    run(sums, spread[1])
    head_grad = sums.tie(head_grad)
    head_dqkv, head_table = attend_backward(
        sh, my_groups, my_table, bucket, head_qkv, head_grad, att_turned, att_lse
    )
    run(sums, spread[2])
    head_dqkv = sums.tie(head_dqkv)
    back_dqkv = lax.all_to_all(head_dqkv, "fsdp", split_axis=0, concat_axis=0, tiled=True)
    run(sums, spread[3])
    back_dqkv = sums.tie(back_dqkv)
    expert_sums = sums.finish()
    grad_gate = expert_sums[:ff_shard].T
    grad_up = expert_sums[ff_shard : 2 * ff_shard].T
    grad_down = expert_sums[2 * ff_shard :]
    grad_qkv = (
        back_dqkv.reshape(fsdp_count, tok_count, 3, sh.width)
        .transpose(1, 2, 0, 3)
        .reshape(tok_count, 3 * D)
    )
    grad_out_w = lax.dot_general(attn_low, grad_branch, TN, preferred_element_type=F32)
    grad_qkv_w = lax.dot_general(normed_low, grad_qkv, TN, preferred_element_type=F32)
    grad_normed = lax.dot_general(grad_qkv, qkv_full, NT, preferred_element_type=F32)
    grad_input_part, grad_attn_gain = first_pull(grad_normed)
    grad_inputs = by_token(grad_middle + grad_input_part)

    def rows_of(x):
        return x.astype(BF).reshape(group_count, shard, -1)

    def small_block(parts):
        flat = jnp.concatenate([p.astype(BF).reshape(group_count, -1) for p in parts], 1)
        flat = jnp.pad(flat, ((0, 0), (0, 16 * D - flat.shape[1])))
        return flat.reshape(group_count, 16, D)

    place_table = (jnp.arange(fsdp_count) == fsdp_place).astype(F32)
    whole_table = place_table[:, None] * head_table[:, 0][None, :]
    parts = [rows_of(grad_qkv_w[:, i * D : (i + 1) * D]) for i in range(3)]
    parts.append(rows_of(grad_out_w))
    parts.append(
        small_block([grad_attn_gain, grad_moe_gain, grad_router, whole_table.reshape(-1)])
    )
    sums_dense = dense_sum(jnp.concatenate(parts, 1))
    sum_qkv = jnp.concatenate([sums_dense[i * shard : (i + 1) * shard] for i in range(3)], 1)
    sum_out = sums_dense[3 * shard : 4 * shard]
    sum_small = sums_dense[4 * shard]
    sum_attn = sum_small[marks[0] : marks[1]]
    sum_moe = sum_small[marks[1] : marks[2]]
    sum_router = sum_small[marks[2] : marks[3]].reshape(shard, expert_count)
    sum_table = sum_small[marks[3] : marks[4]]
    return (
        output,
        losses[None, :],
        grad_inputs,
        sum_qkv,
        sum_out,
        sum_attn,
        sum_moe,
        sum_router,
        sum_table,
        grad_gate[None],
        grad_up[None],
        grad_down[None],
    )


def solution(mesh):
    rows = P(("expert", "fsdp"), None)
    flat = P(("expert", "fsdp"))
    cols = P("expert", None, "fsdp")
    deep = P("expert", "fsdp", None)
    in_specs = (
        rows, rows, rows, flat, flat, rows, flat, cols, cols, deep, rows, rows, flat, P(), rows,
    )
    out_specs = (rows, rows, rows, rows, rows, flat, flat, rows, flat, cols, cols, deep)
    return jax.shard_map(local, mesh=mesh, in_specs=in_specs, out_specs=out_specs, check_vma=False)
```

```python
import functools

import jax
import jax.numpy as jnp
from jax import lax
from jax.experimental import pallas as pl
from jax.experimental.pallas import tpu as pltpu
from jax.sharding import PartitionSpec as P


D = 1024
HEADS = 16
HDIM = 64
BUCKETS = 32
TOPK = 2
PLEN = 1024
CLEN = 128
G_LINE = 2

EPSILON = 1e-06
ZLOSS_FACTOR = 0.001
BALANCE_FACTOR = 0.01
MASK_VALUE = -1e30
LOG2E = 1.4426950408889634
HIGHEST = lax.Precision.HIGHEST
TILE = 256
HALF = 128
SPAN_BLOCKS = (PLEN + CLEN) // HALF
BF = jnp.bfloat16
F32 = jnp.float32
NT = (((1,), (1,)), ((), ()))
TN = (((0,), (0,)), ((), ()))


def rms_scale(values, scale_row):
    inverse = lax.rsqrt(jnp.mean(values * values, axis=-1, keepdims=True) + EPSILON)
    return values * inverse * scale_row


def route_local(normed, router, routes):
    logits = jnp.dot(normed, router, precision=HIGHEST)
    log_total = jax.nn.logsumexp(logits, axis=-1)
    chances = jnp.exp(logits - log_total[:, None])
    expert_ids = jnp.arange(router.shape[1], dtype=jnp.int32)
    first_hot = (routes[:, 0:1] == expert_ids[None, :]).astype(F32)
    second_hot = (routes[:, 1:2] == expert_ids[None, :]).astype(F32)
    first_chance = jnp.sum(chances * first_hot, axis=-1)
    second_chance = jnp.sum(chances * second_hot, axis=-1)
    both_chances = first_chance + second_chance
    gate_pair = jnp.stack([first_chance / both_chances, second_chance / both_chances], -1)
    z_loss = jnp.mean(log_total * log_total)
    expert_share = jnp.sum(first_hot + second_hot, axis=0) / (TOPK * routes.shape[0])
    balance = router.shape[1] * jnp.sum(expert_share * jnp.mean(chances, axis=0))
    return (gate_pair, jnp.stack([z_loss, balance]))


class Shape:
    def __init__(self, fsdp_count):
        self.srcs = fsdp_count
        self.hp = HEADS // fsdp_count
        self.width = self.hp * HDIM
        self.part = PLEN // fsdp_count
        self.rows = G_LINE * self.part + CLEN
        self.spt = TILE // self.part
        self.tiles = PLEN // TILE
        self.pairs = fsdp_count // 2
        self.prompt_pairs = self.pairs // G_LINE
        self.units = G_LINE * self.tiles + self.pairs


def order_conts(sh, group_ref, perm_ref):
    counts = [jnp.int32(0), jnp.int32(sh.srcs // G_LINE)]
    for c in range(sh.srcs):
        first = group_ref[c] == 0
        perm_ref[jnp.where(first, counts[0], counts[1])] = jnp.int32(c)
        step = first.astype(jnp.int32)
        counts = [counts[0] + step, counts[1] + 1 - step]


def build_bias(sh, table_ref, bucket_ref, bias_ref):
    bucket = bucket_ref[...]
    for h in range(sh.hp):
        dist = jnp.zeros(bucket.shape, F32)
        for b in range(BUCKETS):
            dist = jnp.where(bucket == b, table_ref[h, b] * LOG2E, dist)
        bias_ref[h, 0] = jnp.full((HALF, HALF), MASK_VALUE, F32)
        before = jnp.full((1, HALF), MASK_VALUE, F32)
        for n in range(SPAN_BLOCKS):
            now = dist[n : n + 1, :]
            both = jnp.broadcast_to(jnp.concatenate([before, now], axis=1), (HALF, 2 * HALF))
            turned = pltpu.roll(both, HALF, 1, stride=1, stride_axis=0)
            bias_ref[h, 1 + n] = turned[:, :HALF]
            before = now


def head_mask(sh, h):
    if sh.hp == 1:
        return None
    lane = lax.broadcasted_iota(jnp.int32, (1, sh.width), 1)
    return (lane >= h * HDIM) & (lane < (h + 1) * HDIM)


def only_head(sh, h, x):
    mask = head_mask(sh, h)
    return x if mask is None else jnp.where(mask, x, jnp.zeros_like(x))


def prompt_rows_of(sh, ref, g, t, part):
    lanes = slice(part * sh.width, (part + 1) * sh.width)
    start = pl.multiple_of(g * sh.part, sh.part)
    return jnp.concatenate(
        [ref[t * sh.spt + s, pl.ds(start, sh.part), lanes] for s in range(sh.spt)], axis=0
    )


def cont_rows_of(sh, ref, c, part):
    lanes = slice(part * sh.width, (part + 1) * sh.width)
    return ref[c, G_LINE * sh.part :, lanes]


def put_prompt_rows(sh, ref, g, t, part, value):
    lanes = slice(part * sh.width, (part + 1) * sh.width)
    start = pl.multiple_of(g * sh.part, sh.part)
    for s in range(sh.spt):
        ref[t * sh.spt + s, pl.ds(start, sh.part), lanes] = value[
            s * sh.part : (s + 1) * sh.part
        ].astype(ref.dtype)


def transpose_low(x):
    return x.astype(F32).T.astype(BF)


def add_bias(scores, bias_ref, h, base, step_q):
    rows = []
    for a in range(2):
        cols = []
        for b in range(2):
            part = scores[a * HALF : (a + 1) * HALF, b * HALF : (b + 1) * HALF]
            cols.append(part * LOG2E + bias_ref[h, base + b * step_q - a])
        rows.append(jnp.concatenate(cols, axis=1))
    return jnp.concatenate(rows, axis=0)


def fold_max(x):
    return jnp.max(x.reshape(-1, 8, x.shape[-1]), axis=0)


def fold_sum(x):
    return jnp.sum(x.reshape(-1, 8, x.shape[-1]), axis=0)


def attn_forward_kernel(
    sh, group_ref, table_ref, bucket_ref, x_ref, o_ref, ot_ref, lse_ref, bias, vt, vtc, sc, perm
):
    order_conts(sh, group_ref, perm)
    build_bias(sh, table_ref, bucket_ref, bias)

    def make_vt(i, _):
        g, t = i // sh.tiles, lax.rem(i, sh.tiles)
        vt[i] = transpose_low(prompt_rows_of(sh, x_ref, g, t, 2))
        return 0

    lax.fori_loop(0, G_LINE * sh.tiles, make_vt, 0)

    def make_vtc(c, _):
        vtc[c] = transpose_low(cont_rows_of(sh, x_ref, c, 2))
        return 0

    lax.fori_loop(0, sh.srcs, make_vtc, 0)

    def scores_tile(keys, qh, base, step_q, kt, peaks):
        out = []
        for h in range(sh.hp):
            s = lax.dot_general(keys, qh[h], NT, preferred_element_type=F32)
            s = add_bias(s, bias, h, base, step_q)
            sc[h, pl.ds(pl.multiple_of(kt * TILE, TILE), TILE), :] = s
            out.append(jnp.maximum(peaks[h], fold_max(s)))
        return tuple(out)

    def value_tile(g, kt, peaks, carry):
        out = []
        for h in range(sh.hp):
            total, acc = carry[h]
            p = jnp.exp2(sc[h, pl.ds(pl.multiple_of(kt * TILE, TILE), TILE), :] - peaks[h])
            total = total + fold_sum(p)
            values = vt[g * sh.tiles + kt, h * HDIM : (h + 1) * HDIM, :]
            acc = acc + jnp.dot(values, p.astype(BF), preferred_element_type=F32)
            out.append((total, acc))
        return tuple(out)

    first_peaks = tuple(jnp.full((8, TILE), MASK_VALUE, F32) for _ in range(sh.hp))
    first_carry = tuple(
        (jnp.zeros((8, TILE), F32), jnp.zeros((HDIM, TILE), F32)) for _ in range(sh.hp)
    )

    def finish(unit, peaks, carry):
        outs = []
        for h in range(sh.hp):
            total = jnp.sum(carry[h][0], axis=0, keepdims=True)
            outs.append(carry[h][1] / total)
            lse_ref[unit, h : h + 1, :] = peaks[h] + jnp.log2(total)
        whole = jnp.concatenate(outs, axis=0) if sh.hp > 1 else outs[0]
        ot_ref[unit] = whole
        return whole.T

    def prompt_unit(i, _):
        g, qt = i // sh.tiles, lax.rem(i, sh.tiles)
        q = prompt_rows_of(sh, x_ref, g, qt, 0) * BF(HDIM**-0.5)
        qh = [only_head(sh, h, q) for h in range(sh.hp)]

        def first(kt, peaks):
            keys = prompt_rows_of(sh, x_ref, g, kt, 1)
            return scores_tile(keys, qh, 2 * (qt - kt) + 1, 1, kt, peaks)

        peaks = lax.fori_loop(0, qt + 1, first, first_peaks)
        peaks = [jnp.max(p, axis=0, keepdims=True) for p in peaks]
        carry = lax.fori_loop(0, qt + 1, lambda kt, c: value_tile(g, kt, peaks, c), first_carry)
        put_prompt_rows(sh, o_ref, g, qt, 0, finish(i, peaks, carry))
        return 0

    lax.fori_loop(0, G_LINE * sh.tiles, prompt_unit, 0)

    def cont_unit(i, _):
        conts = [perm[2 * i], perm[2 * i + 1]]
        g = i // sh.prompt_pairs
        q = jnp.concatenate([cont_rows_of(sh, x_ref, c, 0) for c in conts], axis=0)
        q = q * BF(HDIM**-0.5)
        qh = [only_head(sh, h, q) for h in range(sh.hp)]

        def first(kt, peaks):
            keys = prompt_rows_of(sh, x_ref, g, kt, 1)
            return scores_tile(keys, qh, SPAN_BLOCKS - 2 * kt, 0, kt, peaks)

        peaks = lax.fori_loop(0, sh.tiles, first, first_peaks)
        own = []
        next_peaks = []
        for h in range(sh.hp):
            parts = []
            for b in range(2):
                keys = cont_rows_of(sh, x_ref, conts[b], 1)
                s = lax.dot_general(
                    keys, qh[h][b * HALF : (b + 1) * HALF], NT, preferred_element_type=F32
                )
                parts.append(s * LOG2E + bias[h, 1])
            own.append(jnp.concatenate(parts, axis=1))
            next_peaks.append(jnp.maximum(peaks[h], fold_max(own[h])))
        peaks = [jnp.max(p, axis=0, keepdims=True) for p in next_peaks]
        start = []
        for h in range(sh.hp):
            p = jnp.exp2(own[h] - peaks[h])
            low = p.astype(BF)
            acc = jnp.concatenate(
                [
                    jnp.dot(
                        vtc[conts[b], h * HDIM : (h + 1) * HDIM, :],
                        low[:, b * HALF : (b + 1) * HALF],
                        preferred_element_type=F32,
                    )
                    for b in range(2)
                ],
                axis=1,
            )
            start.append((fold_sum(p), acc))
        carry = lax.fori_loop(
            0, sh.tiles, lambda kt, c: value_tile(g, kt, peaks, c), tuple(start)
        )
        done = finish(G_LINE * sh.tiles + i, peaks, carry)
        for b in range(2):
            o_ref[conts[b], G_LINE * sh.part :, :] = done[b * HALF : (b + 1) * HALF].astype(BF)
        return 0

    lax.fori_loop(0, sh.pairs, cont_unit, 0)


def attn_backward_kernel(
    sh,
    group_ref,
    table_ref,
    bucket_ref,
    x_ref,
    do_ref,
    ot_ref,
    lse_ref,
    dx_ref,
    dtable_ref,
    bias,
    dbias,
    ktr,
    ktc,
    dk,
    dv,
    perm,
):
    order_conts(sh, group_ref, perm)
    build_bias(sh, table_ref, bucket_ref, bias)
    dbias[...] = jnp.zeros_like(dbias)
    dk[...] = jnp.zeros_like(dk)
    dv[...] = jnp.zeros_like(dv)

    def make_kt(i, _):
        g, t = i // sh.tiles, lax.rem(i, sh.tiles)
        ktr[i] = transpose_low(prompt_rows_of(sh, x_ref, g, t, 1))
        return 0

    lax.fori_loop(0, G_LINE * sh.tiles, make_kt, 0)

    def make_ktc(c, _):
        ktc[c] = transpose_low(cont_rows_of(sh, x_ref, c, 1))
        return 0

    lax.fori_loop(0, sh.srcs, make_ktc, 0)

    def inner_terms(unit, do):
        outs = []
        turned = do.astype(F32).T
        for h in range(sh.hp):
            rows = slice(h * HDIM, (h + 1) * HDIM)
            prod = ot_ref[unit, rows, :] * turned[rows, :]
            outs.append(jnp.sum(prod, axis=0, keepdims=True))
        return outs

    def grads_tile(g, kt, qh, doh, lse, inner, base, step_q, dqs):
        keys = prompt_rows_of(sh, x_ref, g, kt, 1)
        values = prompt_rows_of(sh, x_ref, g, kt, 2)
        slot = g * sh.tiles + kt
        out = []
        dkey = dvalue = None
        for h in range(sh.hp):
            s = lax.dot_general(keys, qh[h], NT, preferred_element_type=F32)
            dp = lax.dot_general(values, doh[h], NT, preferred_element_type=F32)
            p = jnp.exp2(add_bias(s, bias, h, base, step_q) - lse[h])
            ds = p * (dp - inner[h])
            for a in range(2):
                for b in range(2):
                    dbias[h, base + b * step_q - a] += ds[
                        a * HALF : (a + 1) * HALF, b * HALF : (b + 1) * HALF
                    ]
            low = ds.astype(BF)
            more_k = jnp.dot(low, qh[h], preferred_element_type=F32)
            more_v = jnp.dot(p.astype(BF), doh[h], preferred_element_type=F32)
            dkey = more_k if dkey is None else dkey + more_k
            dvalue = more_v if dvalue is None else dvalue + more_v
            turned = ktr[slot, h * HDIM : (h + 1) * HDIM, :]
            out.append(dqs[h] + jnp.dot(turned, low, preferred_element_type=F32))
        dk[slot] += dkey
        dv[slot] += dvalue
        return tuple(out)

    def finish(dqs):
        whole = jnp.concatenate(dqs, axis=0) if sh.hp > 1 else dqs[0]
        return whole.T * (HDIM**-0.5)

    first_dq = tuple(jnp.zeros((HDIM, TILE), F32) for _ in range(sh.hp))

    def prompt_unit(i, _):
        g, qt = i // sh.tiles, lax.rem(i, sh.tiles)
        q = prompt_rows_of(sh, x_ref, g, qt, 0) * BF(HDIM**-0.5)
        do = prompt_rows_of(sh, do_ref, g, qt, 0)
        qh = [only_head(sh, h, q) for h in range(sh.hp)]
        doh = [only_head(sh, h, do) for h in range(sh.hp)]
        inner = inner_terms(i, do)
        lse = [lse_ref[i, h : h + 1, :] for h in range(sh.hp)]

        def body(kt, dqs):
            return grads_tile(g, kt, qh, doh, lse, inner, 2 * (qt - kt) + 1, 1, dqs)

        dqs = lax.fori_loop(0, qt + 1, body, first_dq)
        put_prompt_rows(sh, dx_ref, g, qt, 0, finish(dqs))
        return 0

    lax.fori_loop(0, G_LINE * sh.tiles, prompt_unit, 0)

    def cont_unit(i, _):
        conts = [perm[2 * i], perm[2 * i + 1]]
        unit = G_LINE * sh.tiles + i
        g = i // sh.prompt_pairs
        q = jnp.concatenate([cont_rows_of(sh, x_ref, c, 0) for c in conts], axis=0)
        q = q * BF(HDIM**-0.5)
        do = jnp.concatenate([cont_rows_of(sh, do_ref, c, 0) for c in conts], axis=0)
        qh = [only_head(sh, h, q) for h in range(sh.hp)]
        doh = [only_head(sh, h, do) for h in range(sh.hp)]
        inner = inner_terms(unit, do)
        lse = [lse_ref[unit, h : h + 1, :] for h in range(sh.hp)]

        def body(kt, dqs):
            return grads_tile(g, kt, qh, doh, lse, inner, SPAN_BLOCKS - 2 * kt, 0, dqs)

        dqs = lax.fori_loop(0, sh.tiles, body, first_dq)
        more = [[None] * 2 for _ in range(sh.hp)]
        for b in range(2):
            cols = slice(b * HALF, (b + 1) * HALF)
            keys = cont_rows_of(sh, x_ref, conts[b], 1)
            values = cont_rows_of(sh, x_ref, conts[b], 2)
            dkey = dvalue = None
            for h in range(sh.hp):
                s = lax.dot_general(keys, qh[h][cols], NT, preferred_element_type=F32)
                dp = lax.dot_general(values, doh[h][cols], NT, preferred_element_type=F32)
                p = jnp.exp2(s * LOG2E + bias[h, 1] - lse[h][:, cols])
                ds = p * (dp - inner[h][:, cols])
                dbias[h, 1] += ds
                low = ds.astype(BF)
                more_k = jnp.dot(low, qh[h][cols], preferred_element_type=F32)
                more_v = jnp.dot(p.astype(BF), doh[h][cols], preferred_element_type=F32)
                dkey = more_k if dkey is None else dkey + more_k
                dvalue = more_v if dvalue is None else dvalue + more_v
                turned = ktc[conts[b], h * HDIM : (h + 1) * HDIM, :]
                more[h][b] = jnp.dot(turned, low, preferred_element_type=F32)
            w = sh.width
            dx_ref[conts[b], G_LINE * sh.part :, w : 2 * w] = dkey.astype(BF)
            dx_ref[conts[b], G_LINE * sh.part :, 2 * w :] = dvalue.astype(BF)
        dqs = [dqs[h] + jnp.concatenate(more[h], axis=1) for h in range(sh.hp)]
        done = finish(dqs)
        for b in range(2):
            dx_ref[conts[b], G_LINE * sh.part :, : sh.width] = done[
                b * HALF : (b + 1) * HALF
            ].astype(BF)
        return 0

    lax.fori_loop(0, sh.pairs, cont_unit, 0)

    def put_keys(i, _):
        g, t = i // sh.tiles, lax.rem(i, sh.tiles)
        put_prompt_rows(sh, dx_ref, g, t, 1, dk[i])
        put_prompt_rows(sh, dx_ref, g, t, 2, dv[i])
        return 0

    lax.fori_loop(0, G_LINE * sh.tiles, put_keys, 0)

    bucket = bucket_ref[...]
    key_row = lax.broadcasted_iota(jnp.int32, (HALF, 2 * HALF), 0)
    for h in range(sh.hp):
        spread = []
        for n in range(SPAN_BLOCKS):
            wide = jnp.concatenate(
                [jnp.zeros((HALF, HALF), F32), dbias[h, 1 + n]], axis=1
            )
            for bit in range(7):
                moved = pltpu.roll(wide, 2 * HALF - (1 << bit), 1)
                wide = jnp.where((key_row & (1 << bit)) != 0, moved, wide)
            spread.append(jnp.sum(wide, axis=0, keepdims=True))
        rows = []
        for n in range(SPAN_BLOCKS):
            row = spread[n][:, HALF:]
            if n + 1 < SPAN_BLOCKS:
                row = row + spread[n + 1][:, :HALF]
            rows.append(row)
        by_dist = jnp.concatenate(rows, axis=0)
        sums = [
            jnp.sum(jnp.where(bucket == b, by_dist, 0.0), axis=0, keepdims=True)
            for b in range(BUCKETS)
        ]
        lanes = jnp.concatenate(sums, axis=0)
        dtable_ref[h * BUCKETS : (h + 1) * BUCKETS, :] = jnp.broadcast_to(
            jnp.sum(lanes, axis=1, keepdims=True), (BUCKETS, HALF)
        )


SMEM_SPEC = pl.BlockSpec(memory_space=pltpu.SMEM)
VMEM_SPEC = pl.BlockSpec(memory_space=pltpu.VMEM)
GRANT = 48 * 1024 * 1024


def attend_forward(sh, group, table, bucket, x):
    return pl.pallas_call(
        functools.partial(attn_forward_kernel, sh),
        out_shape=(
            jax.ShapeDtypeStruct((sh.srcs, sh.rows, sh.width), BF),
            jax.ShapeDtypeStruct((sh.units, sh.width, TILE), F32),
            jax.ShapeDtypeStruct((sh.units, 8, TILE), F32),
        ),
        in_specs=[SMEM_SPEC, SMEM_SPEC, VMEM_SPEC, VMEM_SPEC],
        out_specs=(VMEM_SPEC, VMEM_SPEC, VMEM_SPEC),
        scratch_shapes=[
            pltpu.VMEM((sh.hp, SPAN_BLOCKS + 1, HALF, HALF), F32),
            pltpu.VMEM((G_LINE * sh.tiles, sh.width, TILE), BF),
            pltpu.VMEM((sh.srcs, sh.width, HALF), BF),
            pltpu.VMEM((sh.hp, PLEN, TILE), F32),
            pltpu.SMEM((sh.srcs,), jnp.int32),
        ],
        compiler_params=pltpu.CompilerParams(vmem_limit_bytes=GRANT),
        cost_estimate=pl.CostEstimate(
            flops=10**10, bytes_accessed=8 * 10**6, transcendentals=5 * 10**6
        ),
        name="attend_forward",
    )(group, table, bucket, x)


def attend_backward(sh, group, table, bucket, x, do, ot, lse):
    return pl.pallas_call(
        functools.partial(attn_backward_kernel, sh),
        out_shape=(
            jax.ShapeDtypeStruct((sh.srcs, sh.rows, 3 * sh.width), BF),
            jax.ShapeDtypeStruct((sh.hp * BUCKETS, HALF), F32),
        ),
        in_specs=[SMEM_SPEC, SMEM_SPEC, VMEM_SPEC, VMEM_SPEC, VMEM_SPEC, VMEM_SPEC, VMEM_SPEC],
        out_specs=(VMEM_SPEC, VMEM_SPEC),
        scratch_shapes=[
            pltpu.VMEM((sh.hp, SPAN_BLOCKS + 1, HALF, HALF), F32),
            pltpu.VMEM((sh.hp, SPAN_BLOCKS + 1, HALF, HALF), F32),
            pltpu.VMEM((G_LINE * sh.tiles, sh.width, TILE), BF),
            pltpu.VMEM((sh.srcs, sh.width, HALF), BF),
            pltpu.VMEM((G_LINE * sh.tiles, TILE, sh.width), F32),
            pltpu.VMEM((G_LINE * sh.tiles, TILE, sh.width), F32),
            pltpu.SMEM((sh.srcs,), jnp.int32),
        ],
        compiler_params=pltpu.CompilerParams(vmem_limit_bytes=GRANT),
        cost_estimate=pl.CostEstimate(
            flops=2 * 10**10, bytes_accessed=12 * 10**6, transcendentals=5 * 10**6
        ),
        name="attend_backward",
    )(group, table, bucket, x, do, ot, lse)


def ring_order(count):
    deep, wide = 4, count // 4
    order = [a * wide for a in range(deep)]
    for turn, a in enumerate(reversed(range(deep))):
        row = [a * wide + b for b in range(1, wide)]
        order += row if turn % 2 == 0 else row[::-1]
    return order


def ring_hop(x, count, step):
    ring = ring_order(count)
    return lax.ppermute(x, "fsdp", [(ring[i], ring[(i + step) % count]) for i in range(count)])


def tied(*values):
    return lax.optimization_barrier(values)


class RingGather:
    def __init__(self, own, count):
        self.count = count
        self.chunks = [None] * count
        self.chunks[0] = own
        self.right = self.left = own
        self.done = 0
        self.steps = count // 2

    def step(self):
        self.done += 1
        s = self.done
        if s < self.steps:
            self.right = ring_hop(self.right, self.count, 1)
            self.left = ring_hop(self.left, self.count, -1)
        else:
            half = self.right.shape[0] // 2
            self.right = ring_hop(self.right[:half], self.count, 1)
            self.left = ring_hop(self.left[half:], self.count, -1)
        self.keep()

    def keep(self):
        s = self.done
        if s < self.steps:
            self.chunks[self.count - s] = self.right
            self.chunks[s] = self.left
        else:
            self.chunks[s] = (self.right, self.left)

    def tie(self, value):
        value, self.right, self.left = tied(value, self.right, self.left)
        self.keep()
        return value


class RingScatter:
    def __init__(self, part, count):
        self.part, self.count = part, count
        self.right = self.left = None
        self.done = 0
        self.steps = count // 2

    def step(self):
        count, s = self.count, self.done
        away = self.steps - s
        if s == 0:
            send_left, send_right = self.part(away)
        else:
            near_left = self.part(count - away).astype(F32)
            near_right = self.part(away).astype(F32)
            if s == 1:
                half = near_left.shape[0] // 2
                send_left = jnp.concatenate(
                    [near_left[:half] + self.left.astype(F32), near_left[half:]], 0
                )
                send_right = jnp.concatenate(
                    [near_right[:half], near_right[half:] + self.right.astype(F32)], 0
                )
            else:
                send_left = near_left + self.left.astype(F32)
                send_right = near_right + self.right.astype(F32)
        self.left = ring_hop(send_left.astype(BF), count, -1)
        self.right = ring_hop(send_right.astype(BF), count, 1)
        self.done += 1

    def tie(self, value):
        value, self.right, self.left = tied(value, self.right, self.left)
        return value

    def finish(self):
        return self.part(0).astype(F32) + self.right.astype(F32) + self.left.astype(F32)


MESH_ID = pl.DeviceIdType.MESH
DEEP = 4


class Spot:
    def __init__(self):
        e, f = lax.axis_index("expert"), lax.axis_index("fsdp")
        self.x, self.c = e // 2, lax.rem(e, 2)
        self.z, self.y = f // 2, lax.rem(f, 2)
        self.ox, self.oy, self.oc = 1 - self.x, 1 - self.y, 1 - self.c

    def place(self, x=None, y=None, z=None, c=None):
        x = self.x if x is None else x
        y = self.y if y is None else y
        z = self.z if z is None else z
        c = self.c if c is None else c
        return {"expert": x * 2 + c, "fsdp": z * 2 + y}

    def block(self, x, y, z, c):
        return (x * 2 + c) * 8 + z * 2 + y

    def greet(self):
        barrier = pltpu.get_barrier_semaphore()
        for target in (self.place(x=self.ox), self.place(y=self.oy), self.place(c=self.oc)):
            pl.semaphore_signal(barrier, inc=1, device_id=target, device_id_type=MESH_ID)
        for step in (-1, 1):

            @pl.when(self.inside(self.z + step))
            def _(step=step):
                pl.semaphore_signal(
                    barrier, inc=1, device_id=self.along(step), device_id_type=MESH_ID
                )

        pl.semaphore_wait(barrier, 4 + self.z * (DEEP - 1 - self.z) // 2)

    def wrap(self, step):
        return lax.rem(self.z + step + DEEP, DEEP)

    def along(self, step):
        return self.place(z=self.wrap(step))

    def inside(self, z):
        return (z >= 0) & (z < DEEP)


def dense_gather_kernel(cut, x_ref, out_ref, send_sems, recv_sems, own_sem):
    me = Spot()
    rows = x_ref.shape[0]
    spans = [(0, cut), (cut, rows - cut)]
    pending = []

    def view(ref, h):
        return ref.at[pl.ds(*spans[h])]

    def send(src, blk, h, target, cond):
        copy = pltpu.make_async_remote_copy(
            src_ref=src,
            dst_ref=view(out_ref.at[blk], h),
            send_sem=send_sems.at[len(pending)],
            recv_sem=recv_sems.at[blk, h],
            device_id=target,
            device_id_type=MESH_ID,
        )
        pending.append((copy, cond))
        if cond is None:
            copy.start()
        else:
            pl.when(cond)(copy.start)

    def arrive(blk, h, cond):
        copy = pltpu.make_async_remote_copy(
            src_ref=view(out_ref.at[blk], h),
            dst_ref=view(out_ref.at[blk], h),
            send_sem=send_sems.at[0],
            recv_sem=recv_sems.at[blk, h],
            device_id=me.place(c=me.oc),
            device_id_type=MESH_ID,
        )
        if cond is None:
            copy.wait_recv()
        else:
            pl.when(cond)(copy.wait_recv)

    def both(a, b):
        return b if a is None else (a if b is None else a & b)

    by_y, by_x = me.place(y=me.oy), me.place(x=me.ox)
    core = me.place(c=me.oc)
    me.greet()
    mine = me.block(me.x, me.y, me.z, me.c)
    own = pltpu.make_async_copy(x_ref, out_ref.at[mine], own_sem)
    own.start()
    for h in range(2):
        for step in (-1, 1):
            send(view(x_ref, h), mine, h, me.along(step), me.inside(me.z + step))
    for h in range(2):
        for target in (by_y, by_x, core):
            send(view(x_ref, h), mine, h, target, None)

    def line(dist):
        if dist == 0:
            return [(me.z, None, 0)]
        return [(me.wrap(s * dist), me.inside(me.z + s * dist), s) for s in (-1, 1)]

    def from_line(dist):
        for zb, cond, sign in line(dist):
            blk = me.block(me.x, me.y, zb, me.c)
            for h in range(2):
                arrive(blk, h, cond)
                src = view(out_ref.at[blk], h)
                send(src, blk, h, me.along(-sign), both(cond, me.inside(me.z - sign)))
                for target in (by_y, by_x, core):
                    send(src, blk, h, target, cond)

    def from_side(dist):
        for zb, cond, _ in line(dist):
            for h in range(2):
                one = me.block(me.x, me.oy, zb, me.c)
                two = me.block(me.ox, me.y, zb, me.c)
                onward, last = ((one, by_x), two) if h == 0 else ((two, by_y), one)
                arrive(onward[0], h, cond)
                src = view(out_ref.at[onward[0]], h)
                send(src, onward[0], h, onward[1], cond)
                send(src, onward[0], h, core, cond)
                arrive(last, h, cond)
                send(view(out_ref.at[last], h), last, h, core, cond)

    def from_corner(dist):
        for zb, cond, _ in line(dist):
            blk = me.block(me.ox, me.oy, zb, me.c)
            for h in range(2):
                arrive(blk, h, cond)
                send(view(out_ref.at[blk], h), blk, h, core, cond)

    for dist in range(DEEP):
        if dist > 0:
            from_line(dist)
        from_side(dist)
        if dist > 0:
            from_corner(dist - 1)
    from_corner(DEEP - 1)
    for x in range(2):
        for y in range(2):
            for z in range(DEEP):
                for h in range(2):
                    arrive(me.block(x, y, z, me.oc), h, None)
    own.wait()
    for copy, cond in pending:
        if cond is None:
            copy.wait_send()
        else:
            pl.when(cond)(copy.wait_send)


def dense_gather(x, count):
    rows = x.shape[0]
    if count != 32 or lax.axis_size("fsdp") != 2 * DEEP:
        return lax.all_gather(x, ("expert", "fsdp"), axis=0, tiled=False)
    cut = rows - 16
    return pl.pallas_call(
        functools.partial(dense_gather_kernel, cut),
        out_shape=jax.ShapeDtypeStruct((count,) + x.shape, x.dtype),
        in_specs=[pl.BlockSpec(memory_space=pltpu.VMEM)],
        out_specs=pl.BlockSpec(memory_space=pl.ANY),
        scratch_shapes=[
            pltpu.SemaphoreType.DMA((128,)),
            pltpu.SemaphoreType.DMA((count, 2)),
            pltpu.SemaphoreType.DMA,
        ],
        compiler_params=pltpu.CompilerParams(collective_id=0, has_side_effects=True),
        cost_estimate=pl.CostEstimate(
            flops=0, bytes_accessed=100 * 10**6, transcendentals=0
        ),
        name="dense_gather",
    )(x)


def add_into(dst, src):
    def body(i, _):
        at = pl.ds(pl.multiple_of(i * 16, 16), 16)
        dst[at, :] = (dst[at, :].astype(F32) + src[at, :].astype(F32)).astype(BF)
        return 0

    lax.fori_loop(0, dst.shape[0] // 16, body, 0)


def dense_sum_kernel(
    cut, g_ref, out_ref, acc, cbuf, xbuf, ybuf, zbuf, send_sems, recv_sems, load_sems
):
    me = Spot()
    rows = out_ref.shape[0]
    top, low = pl.ds(0, cut), pl.ds(cut, rows - cut)
    pending = []

    def send(src, dst, at, target, cond=None):
        copy = pltpu.make_async_remote_copy(
            src_ref=src,
            dst_ref=dst,
            send_sem=send_sems.at[len(pending)],
            recv_sem=recv_sems.at[at],
            device_id=target,
            device_id_type=MESH_ID,
        )
        pending.append((copy, cond))
        if cond is None:
            copy.start()
        else:
            pl.when(cond)(copy.start)

    def arrive(dst, at):
        pltpu.make_async_remote_copy(
            src_ref=dst,
            dst_ref=dst,
            send_sem=send_sems.at[0],
            recv_sem=recv_sems.at[at],
            device_id=me.place(c=me.oc),
            device_id_type=MESH_ID,
        ).wait_recv()

    by_y, by_x, core = me.place(y=me.oy), me.place(x=me.ox), me.place(c=me.oc)
    me.greet()
    offsets = (2, 3, 1, 0)
    zs = [me.wrap(k) for k in offsets]
    loads = []
    for k in range(DEEP):
        for x in range(2):
            at = x * DEEP + k
            theirs = (x * 2 + me.oc) * 8 + zs[k] * 2
            send(g_ref.at[pl.ds(theirs, 2)], cbuf.at[at], at, core)
            ours = (x * 2 + me.c) * 8 + zs[k] * 2
            load = pltpu.make_async_copy(g_ref.at[pl.ds(ours, 2)], acc.at[at], load_sems.at[at])
            load.start()
            loads.append(load)

    def first(k):
        for x in range(2):
            at = x * DEEP + k
            loads[k * 2 + x].wait()
            arrive(cbuf.at[at], at)
            for y in range(2):
                add_into(acc.at[at, y], cbuf.at[at, y])
        base = 8 + k * 6
        for y in range(2):
            send(acc.at[me.ox * DEEP + k, y, top], xbuf.at[k, y, top], base + y, by_x)
        for x in range(2):
            send(acc.at[x * DEEP + k, me.oy, low], ybuf.at[k, x, low], base + 2 + x, by_y)

    def second(k):
        base = 8 + k * 6
        for y in range(2):
            arrive(xbuf.at[k, y, top], base + y)
            add_into(acc.at[me.x * DEEP + k, y, top], xbuf.at[k, y, top])
        for x in range(2):
            arrive(ybuf.at[k, x, low], base + 2 + x)
            add_into(acc.at[x * DEEP + k, me.y, low], ybuf.at[k, x, low])
        send(acc.at[me.x * DEEP + k, me.oy, top], ybuf.at[k, 0, top], base + 4, by_y)
        send(acc.at[me.ox * DEEP + k, me.y, low], xbuf.at[k, 0, low], base + 5, by_x)

    def third(k):
        base = 8 + k * 6
        block = acc.at[me.x * DEEP + k, me.y]
        arrive(ybuf.at[k, 0, top], base + 4)
        add_into(block.at[top], ybuf.at[k, 0, top])
        arrive(xbuf.at[k, 0, low], base + 5)
        add_into(block.at[low], xbuf.at[k, 0, low])

    for step in range(DEEP + 2):
        if step < DEEP:
            first(step)
        if 0 <= step - 1 < DEEP:
            second(step - 1)
        if 0 <= step - 2 < DEEP:
            third(step - 2)

    for dist in (3, 2, 1):
        for sign in (-1, 1):
            side = (sign + 1) // 2
            term = acc.at[me.x * DEEP + offsets.index(sign * dist % DEEP), me.y]
            if dist < 3:

                @pl.when(me.inside(me.z + sign * dist) & me.inside(me.z - sign))
                def _(term=term, dist=dist, side=side):
                    buf = zbuf.at[dist * 2 + side]
                    arrive(buf, 34 + dist * 2 + side)
                    add_into(term, buf)

            send(
                term,
                zbuf.at[(dist - 1) * 2 + side],
                32 + dist * 2 + side,
                me.along(sign),
                me.inside(me.z + sign * dist),
            )
    block = acc.at[me.x * DEEP + DEEP - 1, me.y]
    for sign in (-1, 1):

        @pl.when(me.inside(me.z - sign))
        def _(sign=sign):
            buf = zbuf.at[(sign + 1) // 2]
            arrive(buf, 32 + 2 + (sign + 1) // 2)
            add_into(block, buf)

    def put(i, _):
        at = pl.ds(pl.multiple_of(i * 16, 16), 16)
        out_ref[at, :] = block[at, :].astype(F32)
        return 0

    lax.fori_loop(0, rows // 16, put, 0)
    for copy, cond in pending:
        if cond is None:
            copy.wait_send()
        else:
            pl.when(cond)(copy.wait_send)


def dense_sum(x):
    count, rows, width = x.shape
    if count != 32 or lax.axis_size("fsdp") != 2 * DEEP:
        flat = x.reshape(count * rows, width)
        return lax.psum_scatter(
            flat, ("expert", "fsdp"), scatter_dimension=0, tiled=True
        ).astype(F32)
    cut = rows // 32 * 16 + 16 * (rows // 16 % 2)
    pair = (2 * DEEP, 2, rows, width)
    return pl.pallas_call(
        functools.partial(dense_sum_kernel, cut),
        out_shape=jax.ShapeDtypeStruct((rows, width), F32),
        in_specs=[pl.BlockSpec(memory_space=pl.ANY)],
        out_specs=pl.BlockSpec(memory_space=pltpu.VMEM),
        scratch_shapes=[
            pltpu.VMEM(pair, BF),
            pltpu.VMEM(pair, BF),
            pltpu.VMEM((DEEP, 2, rows, width), BF),
            pltpu.VMEM((DEEP, 2, rows, width), BF),
            pltpu.VMEM((6, rows, width), BF),
            pltpu.SemaphoreType.DMA((48,)),
            pltpu.SemaphoreType.DMA((48,)),
            pltpu.SemaphoreType.DMA((8,)),
        ],
        compiler_params=pltpu.CompilerParams(
            collective_id=1, has_side_effects=True, vmem_limit_bytes=40 * 1024 * 1024
        ),
        cost_estimate=pl.CostEstimate(
            flops=0, bytes_accessed=100 * 10**6, transcendentals=0
        ),
        name="dense_sum",
    )(x)


SLICE = 256


def gelu_terms(x):
    root = 0.7978845608028654
    square = x * x
    t = jnp.tanh(root * (x + 0.044715 * square * x))
    half = 0.5 * (1.0 + t)
    slope = half + 0.5 * x * (1.0 - t * t) * (root * (1.0 + 3 * 0.044715 * square))
    return x * half, slope


def chunk_pieces(index, split, ff_shard):
    if not split:
        return [(0, m * ff_shard, m, index * ff_shard, ff_shard) for m in range(3)]
    half = ff_shard // 2
    base = index * ff_shard
    return [
        (0, 0, 0, base, ff_shard),
        (0, ff_shard, 1, base, half),
        (1, 0, 1, base + half, half),
        (1, half, 2, base, ff_shard),
    ]


def chunk_copies(refs, whole, sems, ff_shard, outward):
    count = len(refs) - 1
    far = count // 2
    out = []
    for k in range(count):
        own = refs[k : k + 1] if k < far else (refs[k : k + 2] if k == far else refs[k + 1 : k + 2])
        pieces = []
        for n, (src, at, m, row, rows) in enumerate(chunk_pieces(k, k == far, ff_shard)):
            block = own[src].at[pl.ds(at, rows)]
            spot = whole.at[m, pl.ds(row, rows)]
            a, b = (spot, block) if outward else (block, spot)
            pieces.append(pltpu.make_async_copy(a, b, sems.at[k, n]))
        out.append(pieces)
    return out


def fetch_weights(refs, whole, sems, ff_shard, t):
    copies = chunk_copies(refs, whole, sems, ff_shard, False)

    @pl.when(t == 0)
    def _():
        for pieces in copies:
            for c in pieces:
                c.start()

    for k, pieces in enumerate(copies):

        @pl.when(t == k * ff_shard // SLICE)
        def _(pieces=pieces):
            for c in pieces:
                c.wait()


def ffn_forward_kernel(count, ff_shard, rows_ref, *refs):
    chunks, (out_ref, gate_ref, up_ref, whole, acc, sems) = refs[: count + 1], refs[count + 1 :]
    t = pl.program_id(0)
    fetch_weights(chunks, whole, sems, ff_shard, t)
    at = pl.ds(pl.multiple_of(t * SLICE, SLICE), SLICE)
    rows = rows_ref[...]
    gate = lax.dot_general(rows, whole[0, at], NT, preferred_element_type=F32)
    up = lax.dot_general(rows, whole[1, at], NT, preferred_element_type=F32)
    gate_ref[0] = gate
    up_ref[0] = up
    hidden = (gelu_terms(gate)[0] * up).astype(BF)
    more = jnp.dot(hidden, whole[2, at], preferred_element_type=F32)

    @pl.when(t == 0)
    def _():
        acc[...] = more

    @pl.when(t > 0)
    def _():
        acc[...] += more

    @pl.when(t == pl.num_programs(0) - 1)
    def _():
        out_ref[...] = acc[...].astype(BF)


def ffn_backward_kernel(count, ff_shard, grad_ref, gate_ref, up_ref, *refs):
    chunks, rest = refs[: count + 1], refs[count + 1 :]
    out_ref, hid_ref, dgate_ref, dup_ref, whole, acc, sems = rest
    t = pl.program_id(0)
    fetch_weights(chunks, whole, sems, ff_shard, t)
    at = pl.ds(pl.multiple_of(t * SLICE, SLICE), SLICE)
    dhid = lax.dot_general(grad_ref[...], whole[2, at], NT, preferred_element_type=F32)
    up = up_ref[0]
    act, slope = gelu_terms(gate_ref[0])
    hid_ref[0] = (act * up).astype(BF)
    dgate = (dhid * up * slope).astype(BF)
    dup = (dhid * act).astype(BF)
    dgate_ref[0] = dgate
    dup_ref[0] = dup
    more = jnp.dot(dgate, whole[0, at], preferred_element_type=F32) + jnp.dot(
        dup, whole[1, at], preferred_element_type=F32
    )

    @pl.when(t == 0)
    def _():
        acc[...] = more

    @pl.when(t > 0)
    def _():
        acc[...] += more

    @pl.when(t == pl.num_programs(0) - 1)
    def _():
        out_ref[...] = acc[...].astype(BF)


def ffn_weights_kernel(count, ff_shard, rows_ref, grad_ref, hid_ref, dgate_ref, dup_ref, *refs):
    chunks, (whole, sems) = refs[: count + 1], refs[count + 1 :]
    t = pl.program_id(0)
    at = pl.ds(pl.multiple_of(t * SLICE, SLICE), SLICE)
    for m, (left, right) in enumerate(
        ((dgate_ref, rows_ref), (dup_ref, rows_ref), (hid_ref, grad_ref))
    ):
        whole[m, at] = lax.dot_general(
            left[0], right[...], TN, preferred_element_type=F32
        ).astype(BF)
    copies = chunk_copies(chunks, whole, sems, ff_shard, True)
    for k, pieces in enumerate(copies):

        @pl.when(t == ((k + 1) * ff_shard - 1) // SLICE)
        def _(pieces=pieces):
            for c in pieces:
                c.start()

    @pl.when(t == pl.num_programs(0) - 1)
    def _():
        for pieces in copies:
            for c in pieces:
                c.wait()


def fixed(shape):
    return pl.BlockSpec(shape, lambda t: (0,) * len(shape))


def stepped(shape):
    return pl.BlockSpec(shape, lambda t: (t, 0, 0))


ANY_SPEC = pl.BlockSpec(memory_space=pl.ANY)


def ffn_cost(slots, hidden):
    work = 6 * slots * D * hidden
    return pl.CostEstimate(flops=work, bytes_accessed=40 * 10**6, transcendentals=slots * hidden)


def ffn_params():
    return pltpu.CompilerParams(
        dimension_semantics=("arbitrary",), vmem_limit_bytes=60 * 1024 * 1024
    )


def ffn_forward(rows, chunks, ff_shard):
    slots, count = rows.shape[0], len(chunks) - 1
    hidden = count * ff_shard
    steps = hidden // SLICE
    return pl.pallas_call(
        functools.partial(ffn_forward_kernel, count, ff_shard),
        grid=(steps,),
        out_shape=(
            jax.ShapeDtypeStruct((slots, D), BF),
            jax.ShapeDtypeStruct((steps, slots, SLICE), F32),
            jax.ShapeDtypeStruct((steps, slots, SLICE), F32),
        ),
        in_specs=[fixed((slots, D))] + [ANY_SPEC] * (count + 1),
        out_specs=(
            fixed((slots, D)),
            stepped((1, slots, SLICE)),
            stepped((1, slots, SLICE)),
        ),
        scratch_shapes=[
            pltpu.VMEM((3, hidden, D), BF),
            pltpu.VMEM((slots, D), F32),
            pltpu.SemaphoreType.DMA((count, 4)),
        ],
        compiler_params=ffn_params(),
        cost_estimate=ffn_cost(slots, hidden),
        name="ffn_forward",
    )(rows, *chunks)


def ffn_backward(grad, gate, up, chunks, ff_shard):
    slots, count = grad.shape[0], len(chunks) - 1
    hidden = count * ff_shard
    steps = hidden // SLICE
    tile = jax.ShapeDtypeStruct((steps, slots, SLICE), BF)
    return pl.pallas_call(
        functools.partial(ffn_backward_kernel, count, ff_shard),
        grid=(steps,),
        out_shape=(jax.ShapeDtypeStruct((slots, D), BF), tile, tile, tile),
        in_specs=[fixed((slots, D))]
        + [stepped((1, slots, SLICE))] * 2
        + [ANY_SPEC] * (count + 1),
        out_specs=(fixed((slots, D)),) + (stepped((1, slots, SLICE)),) * 3,
        scratch_shapes=[
            pltpu.VMEM((3, hidden, D), BF),
            pltpu.VMEM((slots, D), F32),
            pltpu.SemaphoreType.DMA((count, 4)),
        ],
        compiler_params=ffn_params(),
        cost_estimate=ffn_cost(slots, hidden),
        name="ffn_backward",
    )(grad, gate, up, *chunks)


def ffn_weights(rows, grad, hid, dgate, dup, count, ff_shard):
    slots = rows.shape[0]
    hidden = count * ff_shard
    steps = hidden // SLICE
    full = jax.ShapeDtypeStruct((3 * ff_shard, D), BF)
    half = jax.ShapeDtypeStruct((3 * ff_shard // 2, D), BF)
    far = count // 2
    shapes = [full] * far + [half] * 2 + [full] * (count - far - 1)
    return pl.pallas_call(
        functools.partial(ffn_weights_kernel, count, ff_shard),
        grid=(steps,),
        out_shape=tuple(shapes),
        in_specs=[fixed((slots, D))] * 2 + [stepped((1, slots, SLICE))] * 3,
        out_specs=(ANY_SPEC,) * (count + 1),
        scratch_shapes=[
            pltpu.VMEM((3, hidden, D), BF),
            pltpu.SemaphoreType.DMA((count, 4)),
        ],
        compiler_params=ffn_params(),
        cost_estimate=ffn_cost(slots, hidden),
        name="ffn_weights",
    )(rows, grad, hid, dgate, dup)


def local(
    inputs,
    w_qkv,
    w_out,
    attn_gain,
    moe_gain,
    w_router,
    bias_table,
    w_gate,
    w_up,
    w_down,
    routes,
    slot_order,
    group_map,
    buckets,
    grad_output,
):
    tok_count = inputs.shape[0]
    expert_count = w_router.shape[1]
    capacity = (5 * TOPK * tok_count + 4 * expert_count - 1) // (4 * expert_count)
    fsdp_count = lax.axis_size("fsdp")
    fsdp_place = lax.axis_index("fsdp")
    expert_place = lax.axis_index("expert")
    group_count = lax.axis_size("expert") * fsdp_count
    sh = Shape(fsdp_count)
    prompt_rows = sh.part * G_LINE
    slot_total = expert_count * capacity
    shard = w_qkv.shape[0]
    ff_shard = w_down.shape[1]

    def by_prompt(x):
        head = x[:prompt_rows].reshape(sh.part, G_LINE, -1).transpose(1, 0, 2)
        return jnp.concatenate([head.reshape(prompt_rows, -1), x[prompt_rows:]], 0)

    def by_token(x):
        head = x[:prompt_rows].reshape(G_LINE, sh.part, -1).transpose(1, 0, 2)
        return jnp.concatenate([head.reshape(prompt_rows, -1), x[prompt_rows:]], 0)

    weights = RingGather(jnp.concatenate([w_gate[0].T, w_up[0].T, w_down[0]], 0), fsdp_count)
    spread = [fsdp_count // 8] * 4
    spread[0] += fsdp_count // 2 - sum(spread)

    def run(ring, count):
        for _ in range(count):
            ring.step()

    small = jnp.concatenate(
        [attn_gain, moe_gain, w_router.reshape(-1), bias_table, group_map.astype(BF)]
    )
    small_rows = -(-small.shape[0] // D)
    small_rows = -(-small_rows // 16) * 16
    small = jnp.pad(small, (0, small_rows * D - small.shape[0])).reshape(small_rows, D)
    pack = jnp.concatenate([w_qkv[:, i * D : (i + 1) * D] for i in range(3)] + [w_out, small], 0)
    gathered = dense_gather(pack, group_count)
    run(weights, spread[0])
    qkv_full = jnp.concatenate(
        [gathered[:, i * shard : (i + 1) * shard].reshape(D, D) for i in range(3)], 1
    )
    qkv_full = weights.tie(qkv_full)
    out_full = gathered[:, 3 * shard : 4 * shard].reshape(D, D)
    tail = gathered[:, 4 * shard]
    marks = [0, shard, 2 * shard, 2 * shard + shard * expert_count]
    marks += [marks[-1] + bias_table.shape[0]]
    attn_scale = tail[:, marks[0] : marks[1]].reshape(D).astype(F32)
    moe_scale = tail[:, marks[1] : marks[2]].reshape(D).astype(F32)
    router = tail[:, marks[2] : marks[3]].reshape(D, expert_count).astype(F32)
    table = tail[:, marks[3] : marks[4]].reshape(fsdp_count, sh.hp, BUCKETS)
    my_table = lax.dynamic_index_in_dim(table, fsdp_place, 0, keepdims=False).astype(F32)
    groups = tail[:, marks[4]].reshape(-1, fsdp_count)
    my_groups = lax.dynamic_index_in_dim(groups, expert_place, 0, keepdims=False)
    my_groups = my_groups.astype(jnp.int32)
    bucket = buckets.reshape(SPAN_BLOCKS, HALF)

    token_input = by_prompt(inputs)
    grad_rows_low = by_prompt(grad_output)
    routes = by_prompt(routes)
    slot_order = by_prompt(slot_order)

    input_float = token_input.astype(F32)
    normed, first_pull = jax.vjp(rms_scale, input_float, attn_scale)
    normed_low = normed.astype(BF)
    qkv_rows = jnp.dot(normed_low, qkv_full, preferred_element_type=F32).astype(BF)
    by_heads = (
        qkv_rows.reshape(tok_count, 3, fsdp_count, sh.width)
        .transpose(2, 0, 1, 3)
        .reshape(fsdp_count, tok_count, 3 * sh.width)
    )
    head_qkv = lax.all_to_all(by_heads, "fsdp", split_axis=0, concat_axis=0, tiled=True)
    run(weights, spread[1])
    head_qkv = weights.tie(head_qkv)
    head_att, att_turned, att_lse = attend_forward(sh, my_groups, my_table, bucket, head_qkv)
    att_back = lax.all_to_all(head_att, "fsdp", split_axis=0, concat_axis=0, tiled=True)
    run(weights, spread[2])
    att_back = weights.tie(att_back)
    attn_low = att_back.transpose(1, 0, 2).reshape(tok_count, D)

    middle = input_float + jnp.dot(attn_low, out_full, preferred_element_type=F32)
    second_normed, second_pull = jax.vjp(rms_scale, middle, moe_scale)
    (gate_pair, losses), router_pull = jax.vjp(
        lambda normed_rows, router_rows: route_local(normed_rows, router_rows, routes),
        second_normed,
        router,
    )
    kept_mask = (slot_order < capacity).astype(F32)
    gate_kept = gate_pair * kept_mask
    slot_ids = jnp.arange(slot_total, dtype=jnp.int32)
    slot_place = jnp.where(slot_order < capacity, routes * capacity + slot_order, -1)
    hot = [slot_place[:, k : k + 1] == slot_ids[None, :] for k in range(TOPK)]
    any_low = (hot[0] | hot[1]).astype(BF)
    outgoing = lax.dot_general(
        any_low, second_normed.astype(BF), TN, preferred_element_type=F32
    ).astype(BF)

    def swap_experts(rows):
        rows = rows.reshape(expert_count, capacity, D)
        rows = lax.all_to_all(rows, "expert", split_axis=0, concat_axis=0, tiled=True)
        return rows.reshape(slot_total, D)

    expert_rows = swap_experts(outgoing)
    run(weights, spread[3])
    expert_rows = weights.tie(expert_rows)
    slot_gate = jnp.sum(
        jnp.where(hot[0], gate_kept[:, 0:1], 0.0) + jnp.where(hot[1], gate_kept[:, 1:2], 0.0),
        axis=0,
    )
    slot_grad = lax.dot_general(any_low, grad_rows_low, TN, preferred_element_type=F32)
    grad_result = swap_experts((slot_gate[:, None] * slot_grad).astype(BF))

    far = fsdp_count // 2
    blocks = weights.chunks[:far] + list(weights.chunks[far]) + weights.chunks[far + 1 :]
    result_rows, gate_pre, up_pre = ffn_forward(expert_rows, blocks, ff_shard)
    returned = swap_experts(result_rows)
    grad_rows, hidden, grad_gate_pre, grad_up_pre = ffn_backward(
        grad_result, gate_pre, up_pre, blocks, ff_shard
    )
    grad_sent = swap_experts(grad_rows)
    totals = ffn_weights(
        expert_rows, grad_result, hidden, grad_gate_pre, grad_up_pre, fsdp_count, ff_shard
    )

    def part(k):
        if k == far:
            return totals[far : far + 2]
        return totals[k if k < far else k + 1]

    sums = RingScatter(part, fsdp_count)
    run(sums, spread[0])
    grad_sent = sums.tie(grad_sent)

    picked = [
        jnp.dot(h.astype(BF), returned, preferred_element_type=F32) for h in hot
    ]
    block_out = middle + gate_kept[:, 0:1] * picked[0] + gate_kept[:, 1:2] * picked[1]
    output = by_token(block_out.astype(BF))
    grad_final = grad_rows_low.astype(F32)
    grad_pair = (
        jnp.stack([jnp.sum(grad_final * p, axis=-1) for p in picked], -1) * kept_mask
    )
    grad_second = jnp.dot(any_low, grad_sent, preferred_element_type=F32)
    loss_weights = jnp.array([ZLOSS_FACTOR, BALANCE_FACTOR], F32) / group_count
    router_normed, grad_router = router_pull((grad_pair, loss_weights))
    grad_middle_part, grad_moe_gain = second_pull(grad_second + router_normed)
    grad_middle = grad_final + grad_middle_part
    grad_branch = grad_middle.astype(BF)
    grad_attn = lax.dot_general(grad_branch, out_full, NT, preferred_element_type=F32).astype(BF)
    head_grad = (
        grad_attn.reshape(tok_count, fsdp_count, sh.width).transpose(1, 0, 2)
    )
    head_grad = lax.all_to_all(head_grad, "fsdp", split_axis=0, concat_axis=0, tiled=True)
    run(sums, spread[1])
    head_grad = sums.tie(head_grad)
    head_dqkv, head_table = attend_backward(
        sh, my_groups, my_table, bucket, head_qkv, head_grad, att_turned, att_lse
    )
    run(sums, spread[2])
    head_dqkv = sums.tie(head_dqkv)
    back_dqkv = lax.all_to_all(head_dqkv, "fsdp", split_axis=0, concat_axis=0, tiled=True)
    run(sums, spread[3])
    back_dqkv = sums.tie(back_dqkv)
    expert_sums = sums.finish()
    grad_gate = expert_sums[:ff_shard].T
    grad_up = expert_sums[ff_shard : 2 * ff_shard].T
    grad_down = expert_sums[2 * ff_shard :]
    grad_qkv = (
        back_dqkv.reshape(fsdp_count, tok_count, 3, sh.width)
        .transpose(1, 2, 0, 3)
        .reshape(tok_count, 3 * D)
    )
    grad_out_w = lax.dot_general(attn_low, grad_branch, TN, preferred_element_type=F32)
    grad_qkv_w = lax.dot_general(normed_low, grad_qkv, TN, preferred_element_type=F32)
    grad_normed = lax.dot_general(grad_qkv, qkv_full, NT, preferred_element_type=F32)
    grad_input_part, grad_attn_gain = first_pull(grad_normed)
    grad_inputs = by_token(grad_middle + grad_input_part)

    def rows_of(x):
        return x.astype(BF).reshape(group_count, shard, -1)

    def small_block(parts):
        flat = jnp.concatenate([p.astype(BF).reshape(group_count, -1) for p in parts], 1)
        flat = jnp.pad(flat, ((0, 0), (0, 16 * D - flat.shape[1])))
        return flat.reshape(group_count, 16, D)

    place_table = (jnp.arange(fsdp_count) == fsdp_place).astype(F32)
    whole_table = place_table[:, None] * head_table[:, 0][None, :]
    parts = [rows_of(grad_qkv_w[:, i * D : (i + 1) * D]) for i in range(3)]
    parts.append(rows_of(grad_out_w))
    parts.append(
        small_block([grad_attn_gain, grad_moe_gain, grad_router, whole_table.reshape(-1)])
    )
    sums_dense = dense_sum(jnp.concatenate(parts, 1))
    sum_qkv = jnp.concatenate([sums_dense[i * shard : (i + 1) * shard] for i in range(3)], 1)
    sum_out = sums_dense[3 * shard : 4 * shard]
    sum_small = sums_dense[4 * shard]
    sum_attn = sum_small[marks[0] : marks[1]]
    sum_moe = sum_small[marks[1] : marks[2]]
    sum_router = sum_small[marks[2] : marks[3]].reshape(shard, expert_count)
    sum_table = sum_small[marks[3] : marks[4]]
    return (
        output,
        losses[None, :],
        grad_inputs,
        sum_qkv,
        sum_out,
        sum_attn,
        sum_moe,
        sum_router,
        sum_table,
        grad_gate[None],
        grad_up[None],
        grad_down[None],
    )


def solution(mesh):
    rows = P(("expert", "fsdp"), None)
    flat = P(("expert", "fsdp"))
    cols = P("expert", None, "fsdp")
    deep = P("expert", "fsdp", None)
    in_specs = (
        rows, rows, rows, flat, flat, rows, flat, cols, cols, deep, rows, rows, flat, P(), rows,
    )
    out_specs = (rows, rows, rows, rows, rows, flat, flat, rows, flat, cols, cols, deep)

    return jax.shard_map(local, mesh=mesh, in_specs=in_specs, out_specs=out_specs, check_vma=False)
```

```python
import functools

import jax
import jax.numpy as jnp
from jax import lax
from jax.experimental import pallas as pl
from jax.experimental.pallas import tpu as pltpu
from jax.sharding import PartitionSpec as P


D = 1024
HEADS = 16
HDIM = 64
BUCKETS = 32
TOPK = 2
PLEN = 1024
CLEN = 128
G_LINE = 2

EPSILON = 1e-06
ZLOSS_FACTOR = 0.001
BALANCE_FACTOR = 0.01
MASK_VALUE = -1e30
LOG2E = 1.4426950408889634
HIGHEST = lax.Precision.HIGHEST
TILE = 256
HALF = 128
SPAN_BLOCKS = (PLEN + CLEN) // HALF
BF = jnp.bfloat16
F32 = jnp.float32
NT = (((1,), (1,)), ((), ()))
TN = (((0,), (0,)), ((), ()))


def rms_scale(values, scale_row):
    inverse = lax.rsqrt(jnp.mean(values * values, axis=-1, keepdims=True) + EPSILON)
    return values * inverse * scale_row


def route_local(normed, router, routes):
    logits = jnp.dot(normed, router, precision=HIGHEST)
    log_total = jax.nn.logsumexp(logits, axis=-1)
    chances = jnp.exp(logits - log_total[:, None])
    expert_ids = jnp.arange(router.shape[1], dtype=jnp.int32)
    first_hot = (routes[:, 0:1] == expert_ids[None, :]).astype(F32)
    second_hot = (routes[:, 1:2] == expert_ids[None, :]).astype(F32)
    first_chance = jnp.sum(chances * first_hot, axis=-1)
    second_chance = jnp.sum(chances * second_hot, axis=-1)
    both_chances = first_chance + second_chance
    gate_pair = jnp.stack([first_chance / both_chances, second_chance / both_chances], -1)
    z_loss = jnp.mean(log_total * log_total)
    expert_share = jnp.sum(first_hot + second_hot, axis=0) / (TOPK * routes.shape[0])
    balance = router.shape[1] * jnp.sum(expert_share * jnp.mean(chances, axis=0))
    return (gate_pair, jnp.stack([z_loss, balance]))


class Shape:
    def __init__(self, fsdp_count):
        self.srcs = fsdp_count
        self.hp = HEADS // fsdp_count
        self.width = self.hp * HDIM
        self.part = PLEN // fsdp_count
        self.rows = G_LINE * self.part + CLEN
        self.spt = TILE // self.part
        self.tiles = PLEN // TILE
        self.pairs = fsdp_count // 2
        self.prompt_pairs = self.pairs // G_LINE
        self.units = G_LINE * self.tiles + self.pairs


def order_conts(sh, group_ref, perm_ref):
    counts = [jnp.int32(0), jnp.int32(sh.srcs // G_LINE)]
    for c in range(sh.srcs):
        first = group_ref[c] == 0
        perm_ref[jnp.where(first, counts[0], counts[1])] = jnp.int32(c)
        step = first.astype(jnp.int32)
        counts = [counts[0] + step, counts[1] + 1 - step]


def build_bias(sh, table_ref, bucket_ref, bias_ref):
    bucket = bucket_ref[...]
    for h in range(sh.hp):
        dist = jnp.zeros(bucket.shape, F32)
        for b in range(BUCKETS):
            dist = jnp.where(bucket == b, table_ref[h, b] * LOG2E, dist)
        bias_ref[h, 0] = jnp.full((HALF, HALF), MASK_VALUE, F32)
        before = jnp.full((1, HALF), MASK_VALUE, F32)
        for n in range(SPAN_BLOCKS):
            now = dist[n : n + 1, :]
            both = jnp.broadcast_to(jnp.concatenate([before, now], axis=1), (HALF, 2 * HALF))
            turned = pltpu.roll(both, HALF, 1, stride=1, stride_axis=0)
            bias_ref[h, 1 + n] = turned[:, :HALF]
            before = now


def head_mask(sh, h):
    if sh.hp == 1:
        return None
    lane = lax.broadcasted_iota(jnp.int32, (1, sh.width), 1)
    return (lane >= h * HDIM) & (lane < (h + 1) * HDIM)


def only_head(sh, h, x):
    mask = head_mask(sh, h)
    return x if mask is None else jnp.where(mask, x, jnp.zeros_like(x))


def prompt_rows_of(sh, ref, g, t, part):
    lanes = slice(part * sh.width, (part + 1) * sh.width)
    start = pl.multiple_of(g * sh.part, sh.part)
    return jnp.concatenate(
        [ref[t * sh.spt + s, pl.ds(start, sh.part), lanes] for s in range(sh.spt)], axis=0
    )


def cont_rows_of(sh, ref, c, part):
    lanes = slice(part * sh.width, (part + 1) * sh.width)
    return ref[c, G_LINE * sh.part :, lanes]


def put_prompt_rows(sh, ref, g, t, part, value):
    lanes = slice(part * sh.width, (part + 1) * sh.width)
    start = pl.multiple_of(g * sh.part, sh.part)
    for s in range(sh.spt):
        ref[t * sh.spt + s, pl.ds(start, sh.part), lanes] = value[
            s * sh.part : (s + 1) * sh.part
        ].astype(ref.dtype)


def transpose_low(x):
    return x.astype(F32).T.astype(BF)


def add_bias(scores, bias_ref, h, base, step_q):
    rows = []
    for a in range(2):
        cols = []
        for b in range(2):
            part = scores[a * HALF : (a + 1) * HALF, b * HALF : (b + 1) * HALF]
            cols.append(part * LOG2E + bias_ref[h, base + b * step_q - a])
        rows.append(jnp.concatenate(cols, axis=1))
    return jnp.concatenate(rows, axis=0)


def fold_max(x):
    return jnp.max(x.reshape(-1, 8, x.shape[-1]), axis=0)


def fold_sum(x):
    return jnp.sum(x.reshape(-1, 8, x.shape[-1]), axis=0)


def attn_forward_kernel(
    sh, group_ref, table_ref, bucket_ref, x_ref, o_ref, ot_ref, lse_ref, bias, vt, vtc, sc, perm
):
    order_conts(sh, group_ref, perm)
    build_bias(sh, table_ref, bucket_ref, bias)

    def make_vt(i, _):
        g, t = i // sh.tiles, lax.rem(i, sh.tiles)
        vt[i] = transpose_low(prompt_rows_of(sh, x_ref, g, t, 2))
        return 0

    lax.fori_loop(0, G_LINE * sh.tiles, make_vt, 0)

    def make_vtc(c, _):
        vtc[c] = transpose_low(cont_rows_of(sh, x_ref, c, 2))
        return 0

    lax.fori_loop(0, sh.srcs, make_vtc, 0)

    def scores_tile(keys, qh, base, step_q, kt, peaks):
        out = []
        for h in range(sh.hp):
            s = lax.dot_general(keys, qh[h], NT, preferred_element_type=F32)
            s = add_bias(s, bias, h, base, step_q)
            sc[h, pl.ds(pl.multiple_of(kt * TILE, TILE), TILE), :] = s
            out.append(jnp.maximum(peaks[h], fold_max(s)))
        return tuple(out)

    def value_tile(g, kt, peaks, carry):
        out = []
        for h in range(sh.hp):
            total, acc = carry[h]
            p = jnp.exp2(sc[h, pl.ds(pl.multiple_of(kt * TILE, TILE), TILE), :] - peaks[h])
            total = total + fold_sum(p)
            values = vt[g * sh.tiles + kt, h * HDIM : (h + 1) * HDIM, :]
            acc = acc + jnp.dot(values, p.astype(BF), preferred_element_type=F32)
            out.append((total, acc))
        return tuple(out)

    first_peaks = tuple(jnp.full((8, TILE), MASK_VALUE, F32) for _ in range(sh.hp))
    first_carry = tuple(
        (jnp.zeros((8, TILE), F32), jnp.zeros((HDIM, TILE), F32)) for _ in range(sh.hp)
    )

    def finish(unit, peaks, carry):
        outs = []
        for h in range(sh.hp):
            total = jnp.sum(carry[h][0], axis=0, keepdims=True)
            outs.append(carry[h][1] / total)
            lse_ref[unit, h : h + 1, :] = peaks[h] + jnp.log2(total)
        whole = jnp.concatenate(outs, axis=0) if sh.hp > 1 else outs[0]
        ot_ref[unit] = whole
        return whole.T

    def prompt_unit(i, _):
        g, qt = i // sh.tiles, lax.rem(i, sh.tiles)
        q = prompt_rows_of(sh, x_ref, g, qt, 0) * BF(HDIM**-0.5)
        qh = [only_head(sh, h, q) for h in range(sh.hp)]

        def first(kt, peaks):
            keys = prompt_rows_of(sh, x_ref, g, kt, 1)
            return scores_tile(keys, qh, 2 * (qt - kt) + 1, 1, kt, peaks)

        peaks = lax.fori_loop(0, qt + 1, first, first_peaks)
        peaks = [jnp.max(p, axis=0, keepdims=True) for p in peaks]
        carry = lax.fori_loop(0, qt + 1, lambda kt, c: value_tile(g, kt, peaks, c), first_carry)
        put_prompt_rows(sh, o_ref, g, qt, 0, finish(i, peaks, carry))
        return 0

    lax.fori_loop(0, G_LINE * sh.tiles, prompt_unit, 0)

    def cont_unit(i, _):
        conts = [perm[2 * i], perm[2 * i + 1]]
        g = i // sh.prompt_pairs
        q = jnp.concatenate([cont_rows_of(sh, x_ref, c, 0) for c in conts], axis=0)
        q = q * BF(HDIM**-0.5)
        qh = [only_head(sh, h, q) for h in range(sh.hp)]

        def first(kt, peaks):
            keys = prompt_rows_of(sh, x_ref, g, kt, 1)
            return scores_tile(keys, qh, SPAN_BLOCKS - 2 * kt, 0, kt, peaks)

        peaks = lax.fori_loop(0, sh.tiles, first, first_peaks)
        own = []
        next_peaks = []
        for h in range(sh.hp):
            parts = []
            for b in range(2):
                keys = cont_rows_of(sh, x_ref, conts[b], 1)
                s = lax.dot_general(
                    keys, qh[h][b * HALF : (b + 1) * HALF], NT, preferred_element_type=F32
                )
                parts.append(s * LOG2E + bias[h, 1])
            own.append(jnp.concatenate(parts, axis=1))
            next_peaks.append(jnp.maximum(peaks[h], fold_max(own[h])))
        peaks = [jnp.max(p, axis=0, keepdims=True) for p in next_peaks]
        start = []
        for h in range(sh.hp):
            p = jnp.exp2(own[h] - peaks[h])
            low = p.astype(BF)
            acc = jnp.concatenate(
                [
                    jnp.dot(
                        vtc[conts[b], h * HDIM : (h + 1) * HDIM, :],
                        low[:, b * HALF : (b + 1) * HALF],
                        preferred_element_type=F32,
                    )
                    for b in range(2)
                ],
                axis=1,
            )
            start.append((fold_sum(p), acc))
        carry = lax.fori_loop(
            0, sh.tiles, lambda kt, c: value_tile(g, kt, peaks, c), tuple(start)
        )
        done = finish(G_LINE * sh.tiles + i, peaks, carry)
        for b in range(2):
            o_ref[conts[b], G_LINE * sh.part :, :] = done[b * HALF : (b + 1) * HALF].astype(BF)
        return 0

    lax.fori_loop(0, sh.pairs, cont_unit, 0)


def attn_backward_kernel(
    sh,
    group_ref,
    table_ref,
    bucket_ref,
    x_ref,
    do_ref,
    ot_ref,
    lse_ref,
    dx_ref,
    dtable_ref,
    bias,
    dbias,
    ktr,
    ktc,
    dk,
    dv,
    perm,
):
    order_conts(sh, group_ref, perm)
    build_bias(sh, table_ref, bucket_ref, bias)
    dbias[...] = jnp.zeros_like(dbias)
    dk[...] = jnp.zeros_like(dk)
    dv[...] = jnp.zeros_like(dv)

    def make_kt(i, _):
        g, t = i // sh.tiles, lax.rem(i, sh.tiles)
        ktr[i] = transpose_low(prompt_rows_of(sh, x_ref, g, t, 1))
        return 0

    lax.fori_loop(0, G_LINE * sh.tiles, make_kt, 0)

    def make_ktc(c, _):
        ktc[c] = transpose_low(cont_rows_of(sh, x_ref, c, 1))
        return 0

    lax.fori_loop(0, sh.srcs, make_ktc, 0)

    def inner_terms(unit, do):
        outs = []
        turned = do.astype(F32).T
        for h in range(sh.hp):
            rows = slice(h * HDIM, (h + 1) * HDIM)
            prod = ot_ref[unit, rows, :] * turned[rows, :]
            outs.append(jnp.sum(prod, axis=0, keepdims=True))
        return outs

    def grads_tile(g, kt, qh, doh, lse, inner, base, step_q, dqs):
        keys = prompt_rows_of(sh, x_ref, g, kt, 1)
        values = prompt_rows_of(sh, x_ref, g, kt, 2)
        slot = g * sh.tiles + kt
        out = []
        dkey = dvalue = None
        for h in range(sh.hp):
            s = lax.dot_general(keys, qh[h], NT, preferred_element_type=F32)
            dp = lax.dot_general(values, doh[h], NT, preferred_element_type=F32)
            p = jnp.exp2(add_bias(s, bias, h, base, step_q) - lse[h])
            ds = p * (dp - inner[h])
            for a in range(2):
                for b in range(2):
                    dbias[h, base + b * step_q - a] += ds[
                        a * HALF : (a + 1) * HALF, b * HALF : (b + 1) * HALF
                    ]
            low = ds.astype(BF)
            more_k = jnp.dot(low, qh[h], preferred_element_type=F32)
            more_v = jnp.dot(p.astype(BF), doh[h], preferred_element_type=F32)
            dkey = more_k if dkey is None else dkey + more_k
            dvalue = more_v if dvalue is None else dvalue + more_v
            turned = ktr[slot, h * HDIM : (h + 1) * HDIM, :]
            out.append(dqs[h] + jnp.dot(turned, low, preferred_element_type=F32))
        dk[slot] += dkey
        dv[slot] += dvalue
        return tuple(out)

    def finish(dqs):
        whole = jnp.concatenate(dqs, axis=0) if sh.hp > 1 else dqs[0]
        return whole.T * (HDIM**-0.5)

    first_dq = tuple(jnp.zeros((HDIM, TILE), F32) for _ in range(sh.hp))

    def prompt_unit(i, _):
        g, qt = i // sh.tiles, lax.rem(i, sh.tiles)
        q = prompt_rows_of(sh, x_ref, g, qt, 0) * BF(HDIM**-0.5)
        do = prompt_rows_of(sh, do_ref, g, qt, 0)
        qh = [only_head(sh, h, q) for h in range(sh.hp)]
        doh = [only_head(sh, h, do) for h in range(sh.hp)]
        inner = inner_terms(i, do)
        lse = [lse_ref[i, h : h + 1, :] for h in range(sh.hp)]

        def body(kt, dqs):
            return grads_tile(g, kt, qh, doh, lse, inner, 2 * (qt - kt) + 1, 1, dqs)

        dqs = lax.fori_loop(0, qt + 1, body, first_dq)
        put_prompt_rows(sh, dx_ref, g, qt, 0, finish(dqs))
        return 0

    lax.fori_loop(0, G_LINE * sh.tiles, prompt_unit, 0)

    def cont_unit(i, _):
        conts = [perm[2 * i], perm[2 * i + 1]]
        unit = G_LINE * sh.tiles + i
        g = i // sh.prompt_pairs
        q = jnp.concatenate([cont_rows_of(sh, x_ref, c, 0) for c in conts], axis=0)
        q = q * BF(HDIM**-0.5)
        do = jnp.concatenate([cont_rows_of(sh, do_ref, c, 0) for c in conts], axis=0)
        qh = [only_head(sh, h, q) for h in range(sh.hp)]
        doh = [only_head(sh, h, do) for h in range(sh.hp)]
        inner = inner_terms(unit, do)
        lse = [lse_ref[unit, h : h + 1, :] for h in range(sh.hp)]

        def body(kt, dqs):
            return grads_tile(g, kt, qh, doh, lse, inner, SPAN_BLOCKS - 2 * kt, 0, dqs)

        dqs = lax.fori_loop(0, sh.tiles, body, first_dq)
        more = [[None] * 2 for _ in range(sh.hp)]
        for b in range(2):
            cols = slice(b * HALF, (b + 1) * HALF)
            keys = cont_rows_of(sh, x_ref, conts[b], 1)
            values = cont_rows_of(sh, x_ref, conts[b], 2)
            dkey = dvalue = None
            for h in range(sh.hp):
                s = lax.dot_general(keys, qh[h][cols], NT, preferred_element_type=F32)
                dp = lax.dot_general(values, doh[h][cols], NT, preferred_element_type=F32)
                p = jnp.exp2(s * LOG2E + bias[h, 1] - lse[h][:, cols])
                ds = p * (dp - inner[h][:, cols])
                dbias[h, 1] += ds
                low = ds.astype(BF)
                more_k = jnp.dot(low, qh[h][cols], preferred_element_type=F32)
                more_v = jnp.dot(p.astype(BF), doh[h][cols], preferred_element_type=F32)
                dkey = more_k if dkey is None else dkey + more_k
                dvalue = more_v if dvalue is None else dvalue + more_v
                turned = ktc[conts[b], h * HDIM : (h + 1) * HDIM, :]
                more[h][b] = jnp.dot(turned, low, preferred_element_type=F32)
            w = sh.width
            dx_ref[conts[b], G_LINE * sh.part :, w : 2 * w] = dkey.astype(BF)
            dx_ref[conts[b], G_LINE * sh.part :, 2 * w :] = dvalue.astype(BF)
        dqs = [dqs[h] + jnp.concatenate(more[h], axis=1) for h in range(sh.hp)]
        done = finish(dqs)
        for b in range(2):
            dx_ref[conts[b], G_LINE * sh.part :, : sh.width] = done[
                b * HALF : (b + 1) * HALF
            ].astype(BF)
        return 0

    lax.fori_loop(0, sh.pairs, cont_unit, 0)

    def put_keys(i, _):
        g, t = i // sh.tiles, lax.rem(i, sh.tiles)
        put_prompt_rows(sh, dx_ref, g, t, 1, dk[i])
        put_prompt_rows(sh, dx_ref, g, t, 2, dv[i])
        return 0

    lax.fori_loop(0, G_LINE * sh.tiles, put_keys, 0)

    bucket = bucket_ref[...]
    key_row = lax.broadcasted_iota(jnp.int32, (HALF, 2 * HALF), 0)
    for h in range(sh.hp):
        spread = []
        for n in range(SPAN_BLOCKS):
            wide = jnp.concatenate(
                [jnp.zeros((HALF, HALF), F32), dbias[h, 1 + n]], axis=1
            )
            for bit in range(7):
                moved = pltpu.roll(wide, 2 * HALF - (1 << bit), 1)
                wide = jnp.where((key_row & (1 << bit)) != 0, moved, wide)
            spread.append(jnp.sum(wide, axis=0, keepdims=True))
        rows = []
        for n in range(SPAN_BLOCKS):
            row = spread[n][:, HALF:]
            if n + 1 < SPAN_BLOCKS:
                row = row + spread[n + 1][:, :HALF]
            rows.append(row)
        by_dist = jnp.concatenate(rows, axis=0)
        sums = [
            jnp.sum(jnp.where(bucket == b, by_dist, 0.0), axis=0, keepdims=True)
            for b in range(BUCKETS)
        ]
        lanes = jnp.concatenate(sums, axis=0)
        dtable_ref[h * BUCKETS : (h + 1) * BUCKETS, :] = jnp.broadcast_to(
            jnp.sum(lanes, axis=1, keepdims=True), (BUCKETS, HALF)
        )


SMEM_SPEC = pl.BlockSpec(memory_space=pltpu.SMEM)
VMEM_SPEC = pl.BlockSpec(memory_space=pltpu.VMEM)
GRANT = 48 * 1024 * 1024


def attend_forward(sh, group, table, bucket, x):
    return pl.pallas_call(
        functools.partial(attn_forward_kernel, sh),
        out_shape=(
            jax.ShapeDtypeStruct((sh.srcs, sh.rows, sh.width), BF),
            jax.ShapeDtypeStruct((sh.units, sh.width, TILE), F32),
            jax.ShapeDtypeStruct((sh.units, 8, TILE), F32),
        ),
        in_specs=[SMEM_SPEC, SMEM_SPEC, VMEM_SPEC, VMEM_SPEC],
        out_specs=(VMEM_SPEC, VMEM_SPEC, VMEM_SPEC),
        scratch_shapes=[
            pltpu.VMEM((sh.hp, SPAN_BLOCKS + 1, HALF, HALF), F32),
            pltpu.VMEM((G_LINE * sh.tiles, sh.width, TILE), BF),
            pltpu.VMEM((sh.srcs, sh.width, HALF), BF),
            pltpu.VMEM((sh.hp, PLEN, TILE), F32),
            pltpu.SMEM((sh.srcs,), jnp.int32),
        ],
        compiler_params=pltpu.CompilerParams(vmem_limit_bytes=GRANT),
        cost_estimate=pl.CostEstimate(
            flops=10**10, bytes_accessed=8 * 10**6, transcendentals=5 * 10**6
        ),
        name="attend_forward",
    )(group, table, bucket, x)


def attend_backward(sh, group, table, bucket, x, do, ot, lse):
    return pl.pallas_call(
        functools.partial(attn_backward_kernel, sh),
        out_shape=(
            jax.ShapeDtypeStruct((sh.srcs, sh.rows, 3 * sh.width), BF),
            jax.ShapeDtypeStruct((sh.hp * BUCKETS, HALF), F32),
        ),
        in_specs=[SMEM_SPEC, SMEM_SPEC, VMEM_SPEC, VMEM_SPEC, VMEM_SPEC, VMEM_SPEC, VMEM_SPEC],
        out_specs=(VMEM_SPEC, VMEM_SPEC),
        scratch_shapes=[
            pltpu.VMEM((sh.hp, SPAN_BLOCKS + 1, HALF, HALF), F32),
            pltpu.VMEM((sh.hp, SPAN_BLOCKS + 1, HALF, HALF), F32),
            pltpu.VMEM((G_LINE * sh.tiles, sh.width, TILE), BF),
            pltpu.VMEM((sh.srcs, sh.width, HALF), BF),
            pltpu.VMEM((G_LINE * sh.tiles, TILE, sh.width), F32),
            pltpu.VMEM((G_LINE * sh.tiles, TILE, sh.width), F32),
            pltpu.SMEM((sh.srcs,), jnp.int32),
        ],
        compiler_params=pltpu.CompilerParams(vmem_limit_bytes=GRANT),
        cost_estimate=pl.CostEstimate(
            flops=2 * 10**10, bytes_accessed=12 * 10**6, transcendentals=5 * 10**6
        ),
        name="attend_backward",
    )(group, table, bucket, x, do, ot, lse)


def ring_order(count):
    deep, wide = 4, count // 4
    order = [a * wide for a in range(deep)]
    for turn, a in enumerate(reversed(range(deep))):
        row = [a * wide + b for b in range(1, wide)]
        order += row if turn % 2 == 0 else row[::-1]
    return order


def ring_hop(x, count, step):
    ring = ring_order(count)
    return lax.ppermute(x, "fsdp", [(ring[i], ring[(i + step) % count]) for i in range(count)])


def tied(*values):
    return lax.optimization_barrier(values)


class RingGather:
    def __init__(self, own, count):
        self.count = count
        self.chunks = [None] * count
        self.chunks[0] = own
        self.right = self.left = own
        self.done = 0
        self.steps = count // 2

    def step(self):
        self.done += 1
        s = self.done
        if s < self.steps:
            self.right = ring_hop(self.right, self.count, 1)
            self.left = ring_hop(self.left, self.count, -1)
        else:
            half = self.right.shape[0] // 2
            self.right = ring_hop(self.right[:half], self.count, 1)
            self.left = ring_hop(self.left[half:], self.count, -1)
        self.keep()

    def keep(self):
        s = self.done
        if s < self.steps:
            self.chunks[self.count - s] = self.right
            self.chunks[s] = self.left
        else:
            self.chunks[s] = (self.right, self.left)

    def tie(self, value):
        value, self.right, self.left = tied(value, self.right, self.left)
        self.keep()
        return value


class RingScatter:
    def __init__(self, part, count):
        self.part, self.count = part, count
        self.right = self.left = None
        self.done = 0
        self.steps = count // 2

    def step(self, after=None):
        count, s = self.count, self.done
        away = self.steps - s
        if s == 0:
            send_left, send_right = self.part(away)
        else:
            near_left = self.part(count - away).astype(F32)
            near_right = self.part(away).astype(F32)
            if s == 1:
                half = near_left.shape[0] // 2
                send_left = jnp.concatenate(
                    [near_left[:half] + self.left.astype(F32), near_left[half:]], 0
                )
                send_right = jnp.concatenate(
                    [near_right[:half], near_right[half:] + self.right.astype(F32)], 0
                )
            else:
                send_left = near_left + self.left.astype(F32)
                send_right = near_right + self.right.astype(F32)
        send_left, send_right = send_left.astype(BF), send_right.astype(BF)
        if after is not None:
            after, send_left, send_right = tied(after, send_left, send_right)
        self.left = ring_hop(send_left, count, -1)
        self.right = ring_hop(send_right, count, 1)
        self.done += 1
        return after

    def tie(self, value):
        value, self.right, self.left = tied(value, self.right, self.left)
        return value

    def finish(self):
        return self.part(0).astype(F32) + self.right.astype(F32) + self.left.astype(F32)


MESH_ID = pl.DeviceIdType.MESH
DEEP = 4


class Spot:
    def __init__(self):
        e, f = lax.axis_index("expert"), lax.axis_index("fsdp")
        self.x, self.c = e // 2, lax.rem(e, 2)
        self.z, self.y = f // 2, lax.rem(f, 2)
        self.ox, self.oy, self.oc = 1 - self.x, 1 - self.y, 1 - self.c

    def place(self, x=None, y=None, z=None, c=None):
        x = self.x if x is None else x
        y = self.y if y is None else y
        z = self.z if z is None else z
        c = self.c if c is None else c
        return {"expert": x * 2 + c, "fsdp": z * 2 + y}

    def block(self, x, y, z, c):
        return (x * 2 + c) * 8 + z * 2 + y

    def greet(self):
        barrier = pltpu.get_barrier_semaphore()
        for target in (self.place(x=self.ox), self.place(y=self.oy), self.place(c=self.oc)):
            pl.semaphore_signal(barrier, inc=1, device_id=target, device_id_type=MESH_ID)
        for step in (-1, 1):

            @pl.when(self.inside(self.z + step))
            def _(step=step):
                pl.semaphore_signal(
                    barrier, inc=1, device_id=self.along(step), device_id_type=MESH_ID
                )

        pl.semaphore_wait(barrier, 4 + self.z * (DEEP - 1 - self.z) // 2)

    def wrap(self, step):
        return lax.rem(self.z + step + DEEP, DEEP)

    def along(self, step):
        return self.place(z=self.wrap(step))

    def inside(self, z):
        return (z >= 0) & (z < DEEP)


def dense_gather_kernel(cut, x_ref, out_ref, send_sems, recv_sems, own_sem):
    me = Spot()
    rows = x_ref.shape[0]
    spans = [(0, cut), (cut, rows - cut)]
    pending = []

    def view(ref, h):
        return ref.at[pl.ds(*spans[h])]

    def send(src, blk, h, target, cond):
        copy = pltpu.make_async_remote_copy(
            src_ref=src,
            dst_ref=view(out_ref.at[blk], h),
            send_sem=send_sems.at[len(pending)],
            recv_sem=recv_sems.at[blk, h],
            device_id=target,
            device_id_type=MESH_ID,
        )
        pending.append((copy, cond))
        if cond is None:
            copy.start()
        else:
            pl.when(cond)(copy.start)

    def arrive(blk, h, cond):
        copy = pltpu.make_async_remote_copy(
            src_ref=view(out_ref.at[blk], h),
            dst_ref=view(out_ref.at[blk], h),
            send_sem=send_sems.at[0],
            recv_sem=recv_sems.at[blk, h],
            device_id=me.place(c=me.oc),
            device_id_type=MESH_ID,
        )
        if cond is None:
            copy.wait_recv()
        else:
            pl.when(cond)(copy.wait_recv)

    def both(a, b):
        return b if a is None else (a if b is None else a & b)

    by_y, by_x = me.place(y=me.oy), me.place(x=me.ox)
    core = me.place(c=me.oc)
    me.greet()
    mine = me.block(me.x, me.y, me.z, me.c)
    own = pltpu.make_async_copy(x_ref, out_ref.at[mine], own_sem)
    own.start()
    for h in range(2):
        for step in (-1, 1):
            send(view(x_ref, h), mine, h, me.along(step), me.inside(me.z + step))
    for h in range(2):
        for target in (by_y, by_x, core):
            send(view(x_ref, h), mine, h, target, None)

    def line(dist):
        if dist == 0:
            return [(me.z, None, 0)]
        return [(me.wrap(s * dist), me.inside(me.z + s * dist), s) for s in (-1, 1)]

    def from_line(dist):
        for zb, cond, sign in line(dist):
            blk = me.block(me.x, me.y, zb, me.c)
            for h in range(2):
                arrive(blk, h, cond)
                src = view(out_ref.at[blk], h)
                send(src, blk, h, me.along(-sign), both(cond, me.inside(me.z - sign)))
                for target in (by_y, by_x, core):
                    send(src, blk, h, target, cond)

    def from_side(dist):
        for zb, cond, _ in line(dist):
            for h in range(2):
                one = me.block(me.x, me.oy, zb, me.c)
                two = me.block(me.ox, me.y, zb, me.c)
                onward, last = ((one, by_x), two) if h == 0 else ((two, by_y), one)
                arrive(onward[0], h, cond)
                src = view(out_ref.at[onward[0]], h)
                send(src, onward[0], h, onward[1], cond)
                send(src, onward[0], h, core, cond)
                arrive(last, h, cond)
                send(view(out_ref.at[last], h), last, h, core, cond)

    def from_corner(dist):
        for zb, cond, _ in line(dist):
            blk = me.block(me.ox, me.oy, zb, me.c)
            for h in range(2):
                arrive(blk, h, cond)
                send(view(out_ref.at[blk], h), blk, h, core, cond)

    for dist in range(DEEP):
        if dist > 0:
            from_line(dist)
        from_side(dist)
        if dist > 0:
            from_corner(dist - 1)
    from_corner(DEEP - 1)
    for x in range(2):
        for y in range(2):
            for z in range(DEEP):
                for h in range(2):
                    arrive(me.block(x, y, z, me.oc), h, None)
    own.wait()
    for copy, cond in pending:
        if cond is None:
            copy.wait_send()
        else:
            pl.when(cond)(copy.wait_send)


def dense_gather(x, count):
    rows = x.shape[0]
    if count != 32 or lax.axis_size("fsdp") != 2 * DEEP:
        return lax.all_gather(x, ("expert", "fsdp"), axis=0, tiled=False)
    cut = rows // 32 * 16 + 16 * (rows // 16 % 2)
    return pl.pallas_call(
        functools.partial(dense_gather_kernel, cut),
        out_shape=jax.ShapeDtypeStruct((count,) + x.shape, x.dtype),
        in_specs=[pl.BlockSpec(memory_space=pltpu.VMEM)],
        out_specs=pl.BlockSpec(memory_space=pl.ANY),
        scratch_shapes=[
            pltpu.SemaphoreType.DMA((128,)),
            pltpu.SemaphoreType.DMA((count, 2)),
            pltpu.SemaphoreType.DMA,
        ],
        compiler_params=pltpu.CompilerParams(collective_id=0, has_side_effects=True),
        cost_estimate=pl.CostEstimate(
            flops=0, bytes_accessed=100 * 10**6, transcendentals=0
        ),
        name="dense_gather",
    )(x)


def add_into(dst, src):
    def body(i, _):
        at = pl.ds(pl.multiple_of(i * 16, 16), 16)
        dst[at, :] = (dst[at, :].astype(F32) + src[at, :].astype(F32)).astype(BF)
        return 0

    lax.fori_loop(0, dst.shape[0] // 16, body, 0)


def dense_sum_kernel(
    cut, g_ref, out_ref, acc, cbuf, xbuf, ybuf, zbuf, send_sems, recv_sems, load_sems
):
    me = Spot()
    rows = out_ref.shape[0]
    top, low = pl.ds(0, cut), pl.ds(cut, rows - cut)
    pending = []

    def send(src, dst, at, target, cond=None):
        copy = pltpu.make_async_remote_copy(
            src_ref=src,
            dst_ref=dst,
            send_sem=send_sems.at[len(pending)],
            recv_sem=recv_sems.at[at],
            device_id=target,
            device_id_type=MESH_ID,
        )
        pending.append((copy, cond))
        if cond is None:
            copy.start()
        else:
            pl.when(cond)(copy.start)

    def arrive(dst, at):
        pltpu.make_async_remote_copy(
            src_ref=dst,
            dst_ref=dst,
            send_sem=send_sems.at[0],
            recv_sem=recv_sems.at[at],
            device_id=me.place(c=me.oc),
            device_id_type=MESH_ID,
        ).wait_recv()

    by_y, by_x, core = me.place(y=me.oy), me.place(x=me.ox), me.place(c=me.oc)
    me.greet()
    offsets = (2, 3, 1, 0)
    zs = [me.wrap(k) for k in offsets]
    loads = []
    for k in range(DEEP):
        for x in range(2):
            at = x * DEEP + k
            theirs = (x * 2 + me.oc) * 8 + zs[k] * 2
            send(g_ref.at[pl.ds(theirs, 2)], cbuf.at[at], at, core)
            ours = (x * 2 + me.c) * 8 + zs[k] * 2
            load = pltpu.make_async_copy(g_ref.at[pl.ds(ours, 2)], acc.at[at], load_sems.at[at])
            load.start()
            loads.append(load)

    def first(k):
        for x in range(2):
            at = x * DEEP + k
            loads[k * 2 + x].wait()
            arrive(cbuf.at[at], at)
            for y in range(2):
                add_into(acc.at[at, y], cbuf.at[at, y])
        base = 8 + k * 6
        for y in range(2):
            send(acc.at[me.ox * DEEP + k, y, top], xbuf.at[k, y, top], base + y, by_x)
        for x in range(2):
            send(acc.at[x * DEEP + k, me.oy, low], ybuf.at[k, x, low], base + 2 + x, by_y)

    def second(k):
        base = 8 + k * 6
        for y in range(2):
            arrive(xbuf.at[k, y, top], base + y)
            add_into(acc.at[me.x * DEEP + k, y, top], xbuf.at[k, y, top])
        for x in range(2):
            arrive(ybuf.at[k, x, low], base + 2 + x)
            add_into(acc.at[x * DEEP + k, me.y, low], ybuf.at[k, x, low])
        send(acc.at[me.x * DEEP + k, me.oy, top], ybuf.at[k, 0, top], base + 4, by_y)
        send(acc.at[me.ox * DEEP + k, me.y, low], xbuf.at[k, 0, low], base + 5, by_x)

    def third(k):
        base = 8 + k * 6
        block = acc.at[me.x * DEEP + k, me.y]
        arrive(ybuf.at[k, 0, top], base + 4)
        add_into(block.at[top], ybuf.at[k, 0, top])
        arrive(xbuf.at[k, 0, low], base + 5)
        add_into(block.at[low], xbuf.at[k, 0, low])

    for step in range(DEEP + 2):
        if step < DEEP:
            first(step)
        if 0 <= step - 1 < DEEP:
            second(step - 1)
        if 0 <= step - 2 < DEEP:
            third(step - 2)

    for dist in (3, 2, 1):
        for sign in (-1, 1):
            side = (sign + 1) // 2
            term = acc.at[me.x * DEEP + offsets.index(sign * dist % DEEP), me.y]
            if dist < 3:

                @pl.when(me.inside(me.z + sign * dist) & me.inside(me.z - sign))
                def _(term=term, dist=dist, side=side):
                    buf = zbuf.at[dist * 2 + side]
                    arrive(buf, 34 + dist * 2 + side)
                    add_into(term, buf)

            send(
                term,
                zbuf.at[(dist - 1) * 2 + side],
                32 + dist * 2 + side,
                me.along(sign),
                me.inside(me.z + sign * dist),
            )
    block = acc.at[me.x * DEEP + DEEP - 1, me.y]
    for sign in (-1, 1):

        @pl.when(me.inside(me.z - sign))
        def _(sign=sign):
            buf = zbuf.at[(sign + 1) // 2]
            arrive(buf, 32 + 2 + (sign + 1) // 2)
            add_into(block, buf)

    def put(i, _):
        at = pl.ds(pl.multiple_of(i * 16, 16), 16)
        out_ref[at, :] = block[at, :].astype(F32)
        return 0

    lax.fori_loop(0, rows // 16, put, 0)
    for copy, cond in pending:
        if cond is None:
            copy.wait_send()
        else:
            pl.when(cond)(copy.wait_send)


def dense_sum(x):
    count, rows, width = x.shape
    if count != 32 or lax.axis_size("fsdp") != 2 * DEEP:
        flat = x.reshape(count * rows, width)
        return lax.psum_scatter(
            flat, ("expert", "fsdp"), scatter_dimension=0, tiled=True
        ).astype(F32)
    cut = rows // 32 * 16 + 16 * (rows // 16 % 2)
    pair = (2 * DEEP, 2, rows, width)
    return pl.pallas_call(
        functools.partial(dense_sum_kernel, cut),
        out_shape=jax.ShapeDtypeStruct((rows, width), F32),
        in_specs=[pl.BlockSpec(memory_space=pl.ANY)],
        out_specs=pl.BlockSpec(memory_space=pltpu.VMEM),
        scratch_shapes=[
            pltpu.VMEM(pair, BF),
            pltpu.VMEM(pair, BF),
            pltpu.VMEM((DEEP, 2, rows, width), BF),
            pltpu.VMEM((DEEP, 2, rows, width), BF),
            pltpu.VMEM((6, rows, width), BF),
            pltpu.SemaphoreType.DMA((48,)),
            pltpu.SemaphoreType.DMA((48,)),
            pltpu.SemaphoreType.DMA((8,)),
        ],
        compiler_params=pltpu.CompilerParams(
            collective_id=1, has_side_effects=True, vmem_limit_bytes=40 * 1024 * 1024
        ),
        cost_estimate=pl.CostEstimate(
            flops=0, bytes_accessed=100 * 10**6, transcendentals=0
        ),
        name="dense_sum",
    )(x)


SLICE = 256


def gelu_terms(x):
    root = 0.7978845608028654
    square = x * x
    t = jnp.tanh(root * (x + 0.044715 * square * x))
    half = 0.5 * (1.0 + t)
    slope = half + 0.5 * x * (1.0 - t * t) * (root * (1.0 + 3 * 0.044715 * square))
    return x * half, slope


def chunk_pieces(index, split, ff_shard):
    if not split:
        return [(0, m * ff_shard, m, index * ff_shard, ff_shard) for m in range(3)]
    half = ff_shard // 2
    base = index * ff_shard
    return [
        (0, 0, 0, base, ff_shard),
        (0, ff_shard, 1, base, half),
        (1, 0, 1, base + half, half),
        (1, half, 2, base, ff_shard),
    ]


def chunk_copies(refs, whole, sems, ff_shard, outward):
    count = len(refs) - 1
    far = count // 2
    out = []
    for k in range(count):
        own = refs[k : k + 1] if k < far else (refs[k : k + 2] if k == far else refs[k + 1 : k + 2])
        pieces = []
        for n, (src, at, m, row, rows) in enumerate(chunk_pieces(k, k == far, ff_shard)):
            block = own[src].at[pl.ds(at, rows)]
            spot = whole.at[m, pl.ds(row, rows)]
            a, b = (spot, block) if outward else (block, spot)
            pieces.append(pltpu.make_async_copy(a, b, sems.at[k, n]))
        out.append(pieces)
    return out


def fetch_weights(refs, whole, sems, ff_shard, t):
    copies = chunk_copies(refs, whole, sems, ff_shard, False)

    @pl.when(t == 0)
    def _():
        for pieces in copies:
            for c in pieces:
                c.start()

    for k, pieces in enumerate(copies):

        @pl.when(t == k * ff_shard // SLICE)
        def _(pieces=pieces):
            for c in pieces:
                c.wait()


def ffn_forward_kernel(count, ff_shard, rows_ref, *refs):
    chunks, rest = refs[: count + 1], refs[count + 1 :]
    out_ref, act_ref, turn_ref, hid_ref, whole, acc, sems = rest
    t = pl.program_id(0)
    fetch_weights(chunks, whole, sems, ff_shard, t)
    at = pl.ds(pl.multiple_of(t * SLICE, SLICE), SLICE)
    rows = rows_ref[...]
    gate = lax.dot_general(rows, whole[0, at], NT, preferred_element_type=F32)
    up = lax.dot_general(rows, whole[1, at], NT, preferred_element_type=F32)
    act, slope = gelu_terms(gate)
    hidden = (act * up).astype(BF)
    act_ref[0] = act
    turn_ref[0] = up * slope
    hid_ref[0] = hidden
    more = jnp.dot(hidden, whole[2, at], preferred_element_type=F32)

    @pl.when(t == 0)
    def _():
        acc[...] = more

    @pl.when(t > 0)
    def _():
        acc[...] += more

    @pl.when(t == pl.num_programs(0) - 1)
    def _():
        out_ref[...] = acc[...].astype(BF)


def ffn_backward_kernel(count, ff_shard, grad_ref, act_ref, turn_ref, *refs):
    chunks, rest = refs[: count + 1], refs[count + 1 :]
    out_ref, dgate_ref, dup_ref, whole, acc, sems = rest
    t = pl.program_id(0)
    fetch_weights(chunks, whole, sems, ff_shard, t)
    at = pl.ds(pl.multiple_of(t * SLICE, SLICE), SLICE)
    dhid = lax.dot_general(grad_ref[...], whole[2, at], NT, preferred_element_type=F32)
    dgate = (dhid * turn_ref[0]).astype(BF)
    dup = (dhid * act_ref[0]).astype(BF)
    dgate_ref[0] = dgate
    dup_ref[0] = dup
    more = jnp.dot(dgate, whole[0, at], preferred_element_type=F32) + jnp.dot(
        dup, whole[1, at], preferred_element_type=F32
    )

    @pl.when(t == 0)
    def _():
        acc[...] = more

    @pl.when(t > 0)
    def _():
        acc[...] += more

    @pl.when(t == pl.num_programs(0) - 1)
    def _():
        out_ref[...] = acc[...].astype(BF)


def ffn_weights_kernel(count, ff_shard, rows_ref, grad_ref, hid_ref, dgate_ref, dup_ref, *refs):
    chunks, (whole, sems) = refs[: count + 1], refs[count + 1 :]
    t = pl.program_id(0)
    at = pl.ds(pl.multiple_of(t * SLICE, SLICE), SLICE)
    for m, (left, right) in enumerate(
        ((dgate_ref, rows_ref), (dup_ref, rows_ref), (hid_ref, grad_ref))
    ):
        whole[m, at] = lax.dot_general(
            left[0], right[...], TN, preferred_element_type=F32
        ).astype(BF)
    copies = chunk_copies(chunks, whole, sems, ff_shard, True)
    for k, pieces in enumerate(copies):

        @pl.when(t == ((k + 1) * ff_shard - 1) // SLICE)
        def _(pieces=pieces):
            for c in pieces:
                c.start()

    @pl.when(t == pl.num_programs(0) - 1)
    def _():
        for pieces in copies:
            for c in pieces:
                c.wait()


def fixed(shape):
    return pl.BlockSpec(shape, lambda t: (0,) * len(shape))


def stepped(shape):
    return pl.BlockSpec(shape, lambda t: (t, 0, 0))


ANY_SPEC = pl.BlockSpec(memory_space=pl.ANY)


def ffn_cost(slots, hidden):
    work = 6 * slots * D * hidden
    return pl.CostEstimate(flops=work, bytes_accessed=40 * 10**6, transcendentals=slots * hidden)


def ffn_params():
    return pltpu.CompilerParams(
        dimension_semantics=("arbitrary",), vmem_limit_bytes=60 * 1024 * 1024
    )


def ffn_forward(rows, chunks, ff_shard):
    slots, count = rows.shape[0], len(chunks) - 1
    hidden = count * ff_shard
    steps = hidden // SLICE
    return pl.pallas_call(
        functools.partial(ffn_forward_kernel, count, ff_shard),
        grid=(steps,),
        out_shape=(
            jax.ShapeDtypeStruct((slots, D), BF),
            jax.ShapeDtypeStruct((steps, slots, SLICE), F32),
            jax.ShapeDtypeStruct((steps, slots, SLICE), F32),
            jax.ShapeDtypeStruct((steps, slots, SLICE), BF),
        ),
        in_specs=[fixed((slots, D))] + [ANY_SPEC] * (count + 1),
        out_specs=(
            fixed((slots, D)),
            stepped((1, slots, SLICE)),
            stepped((1, slots, SLICE)),
            stepped((1, slots, SLICE)),
        ),
        scratch_shapes=[
            pltpu.VMEM((3, hidden, D), BF),
            pltpu.VMEM((slots, D), F32),
            pltpu.SemaphoreType.DMA((count, 4)),
        ],
        compiler_params=ffn_params(),
        cost_estimate=ffn_cost(slots, hidden),
        name="ffn_forward",
    )(rows, *chunks)


def ffn_backward(grad, act, turn, chunks, ff_shard):
    slots, count = grad.shape[0], len(chunks) - 1
    hidden = count * ff_shard
    steps = hidden // SLICE
    tile = jax.ShapeDtypeStruct((steps, slots, SLICE), BF)
    return pl.pallas_call(
        functools.partial(ffn_backward_kernel, count, ff_shard),
        grid=(steps,),
        out_shape=(jax.ShapeDtypeStruct((slots, D), BF), tile, tile),
        in_specs=[fixed((slots, D))]
        + [stepped((1, slots, SLICE))] * 2
        + [ANY_SPEC] * (count + 1),
        out_specs=(fixed((slots, D)),) + (stepped((1, slots, SLICE)),) * 2,
        scratch_shapes=[
            pltpu.VMEM((3, hidden, D), BF),
            pltpu.VMEM((slots, D), F32),
            pltpu.SemaphoreType.DMA((count, 4)),
        ],
        compiler_params=ffn_params(),
        cost_estimate=ffn_cost(slots, hidden),
        name="ffn_backward",
    )(grad, act, turn, *chunks)


def ffn_weights(rows, grad, hid, dgate, dup, count, ff_shard):
    slots = rows.shape[0]
    hidden = count * ff_shard
    steps = hidden // SLICE
    full = jax.ShapeDtypeStruct((3 * ff_shard, D), BF)
    half = jax.ShapeDtypeStruct((3 * ff_shard // 2, D), BF)
    far = count // 2
    shapes = [full] * far + [half] * 2 + [full] * (count - far - 1)
    return pl.pallas_call(
        functools.partial(ffn_weights_kernel, count, ff_shard),
        grid=(steps,),
        out_shape=tuple(shapes),
        in_specs=[fixed((slots, D))] * 2 + [stepped((1, slots, SLICE))] * 3,
        out_specs=(ANY_SPEC,) * (count + 1),
        scratch_shapes=[
            pltpu.VMEM((3, hidden, D), BF),
            pltpu.SemaphoreType.DMA((count, 4)),
        ],
        compiler_params=ffn_params(),
        cost_estimate=ffn_cost(slots, hidden),
        name="ffn_weights",
    )(rows, grad, hid, dgate, dup)


def local(
    inputs,
    w_qkv,
    w_out,
    attn_gain,
    moe_gain,
    w_router,
    bias_table,
    w_gate,
    w_up,
    w_down,
    routes,
    slot_order,
    group_map,
    buckets,
    grad_output,
):
    tok_count = inputs.shape[0]
    expert_count = w_router.shape[1]
    capacity = (5 * TOPK * tok_count + 4 * expert_count - 1) // (4 * expert_count)
    fsdp_count = lax.axis_size("fsdp")
    fsdp_place = lax.axis_index("fsdp")
    expert_place = lax.axis_index("expert")
    group_count = lax.axis_size("expert") * fsdp_count
    sh = Shape(fsdp_count)
    prompt_rows = sh.part * G_LINE
    slot_total = expert_count * capacity
    shard = w_qkv.shape[0]
    ff_shard = w_down.shape[1]

    def by_prompt(x):
        head = x[:prompt_rows].reshape(sh.part, G_LINE, -1).transpose(1, 0, 2)
        return jnp.concatenate([head.reshape(prompt_rows, -1), x[prompt_rows:]], 0)

    def by_token(x):
        head = x[:prompt_rows].reshape(G_LINE, sh.part, -1).transpose(1, 0, 2)
        return jnp.concatenate([head.reshape(prompt_rows, -1), x[prompt_rows:]], 0)

    own_weights = jnp.concatenate([w_gate[0].T, w_up[0].T, w_down[0]], 0)
    spread = [fsdp_count // 8] * 4
    spread[0] += fsdp_count // 2 - sum(spread)

    def run(ring, count):
        for _ in range(count):
            ring.step()

    small = jnp.concatenate(
        [attn_gain, moe_gain, w_router.reshape(-1), bias_table, group_map.astype(BF)]
    )
    small_rows = -(-small.shape[0] // D)
    small_rows = -(-small_rows // 16) * 16
    small = jnp.pad(small, (0, small_rows * D - small.shape[0])).reshape(small_rows, D)
    pack = jnp.concatenate([w_qkv[:, i * D : (i + 1) * D] for i in range(3)] + [w_out, small], 0)
    gathered = dense_gather(pack, group_count)
    own_weights, tail = tied(own_weights, gathered[:, 4 * shard])
    weights = RingGather(own_weights, fsdp_count)
    run(weights, spread[0])
    qkv_full = jnp.concatenate(
        [gathered[:, i * shard : (i + 1) * shard].reshape(D, D) for i in range(3)], 1
    )
    out_full = gathered[:, 3 * shard : 4 * shard].reshape(D, D)
    marks = [0, shard, 2 * shard, 2 * shard + shard * expert_count]
    marks += [marks[-1] + bias_table.shape[0]]
    attn_scale = tail[:, marks[0] : marks[1]].reshape(D).astype(F32)
    moe_scale = tail[:, marks[1] : marks[2]].reshape(D).astype(F32)
    router = tail[:, marks[2] : marks[3]].reshape(D, expert_count).astype(F32)
    table = tail[:, marks[3] : marks[4]].reshape(fsdp_count, sh.hp, BUCKETS)
    my_table = lax.dynamic_index_in_dim(table, fsdp_place, 0, keepdims=False).astype(F32)
    groups = tail[:, marks[4]].reshape(-1, fsdp_count)
    my_groups = lax.dynamic_index_in_dim(groups, expert_place, 0, keepdims=False)
    my_groups = my_groups.astype(jnp.int32)
    bucket = buckets.reshape(SPAN_BLOCKS, HALF)

    token_input = by_prompt(inputs)
    grad_rows_low = by_prompt(grad_output)
    routes = by_prompt(routes)
    slot_order = by_prompt(slot_order)

    input_float = token_input.astype(F32)
    normed, first_pull = jax.vjp(rms_scale, input_float, attn_scale)
    normed_low = normed.astype(BF)
    qkv_rows = jnp.dot(normed_low, qkv_full, preferred_element_type=F32).astype(BF)
    by_heads = (
        qkv_rows.reshape(tok_count, 3, fsdp_count, sh.width)
        .transpose(2, 0, 1, 3)
        .reshape(fsdp_count, tok_count, 3 * sh.width)
    )
    head_qkv = lax.all_to_all(by_heads, "fsdp", split_axis=0, concat_axis=0, tiled=True)
    head_qkv = weights.tie(head_qkv)
    run(weights, spread[1])
    head_att, att_turned, att_lse = attend_forward(sh, my_groups, my_table, bucket, head_qkv)
    att_back = lax.all_to_all(head_att, "fsdp", split_axis=0, concat_axis=0, tiled=True)
    att_back = weights.tie(att_back)
    run(weights, spread[2])
    run(weights, spread[3])
    attn_low = att_back.transpose(1, 0, 2).reshape(tok_count, D)

    middle = input_float + jnp.dot(attn_low, out_full, preferred_element_type=F32)
    second_normed, second_pull = jax.vjp(rms_scale, middle, moe_scale)
    (gate_pair, losses), router_pull = jax.vjp(
        lambda normed_rows, router_rows: route_local(normed_rows, router_rows, routes),
        second_normed,
        router,
    )
    kept_mask = (slot_order < capacity).astype(F32)
    gate_kept = gate_pair * kept_mask
    slot_ids = jnp.arange(slot_total, dtype=jnp.int32)
    slot_place = jnp.where(slot_order < capacity, routes * capacity + slot_order, -1)
    hot = [slot_place[:, k : k + 1] == slot_ids[None, :] for k in range(TOPK)]
    any_low = (hot[0] | hot[1]).astype(BF)
    outgoing = lax.dot_general(
        any_low, second_normed.astype(BF), TN, preferred_element_type=F32
    ).astype(BF)

    def swap_experts(rows):
        rows = rows.reshape(expert_count, capacity, D)
        rows = lax.all_to_all(rows, "expert", split_axis=0, concat_axis=0, tiled=True)
        return rows.reshape(slot_total, D)

    expert_rows = swap_experts(outgoing)
    slot_gate = jnp.sum(
        jnp.where(hot[0], gate_kept[:, 0:1], 0.0) + jnp.where(hot[1], gate_kept[:, 1:2], 0.0),
        axis=0,
    )
    slot_grad = lax.dot_general(any_low, grad_rows_low, TN, preferred_element_type=F32)
    grad_result = swap_experts((slot_gate[:, None] * slot_grad).astype(BF))

    far = fsdp_count // 2
    blocks = weights.chunks[:far] + list(weights.chunks[far]) + weights.chunks[far + 1 :]
    result_rows, act, turn, hidden = ffn_forward(expert_rows, blocks, ff_shard)
    returned = swap_experts(result_rows)
    grad_rows, grad_gate_pre, grad_up_pre = ffn_backward(
        grad_result, act, turn, blocks, ff_shard
    )
    grad_sent = swap_experts(grad_rows)
    totals = ffn_weights(
        expert_rows, grad_result, hidden, grad_gate_pre, grad_up_pre, fsdp_count, ff_shard
    )

    def part(k):
        if k == far:
            return totals[far : far + 2]
        return totals[k if k < far else k + 1]

    sums = RingScatter(part, fsdp_count)
    run(sums, spread[0])
    grad_sent = sums.tie(grad_sent)

    picked = [
        jnp.dot(h.astype(BF), returned, preferred_element_type=F32) for h in hot
    ]
    block_out = middle + gate_kept[:, 0:1] * picked[0] + gate_kept[:, 1:2] * picked[1]
    output = by_token(block_out.astype(BF))
    grad_final = grad_rows_low.astype(F32)
    grad_pair = (
        jnp.stack([jnp.sum(grad_final * p, axis=-1) for p in picked], -1) * kept_mask
    )
    grad_second = jnp.dot(any_low, grad_sent, preferred_element_type=F32)
    loss_weights = jnp.array([ZLOSS_FACTOR, BALANCE_FACTOR], F32) / group_count
    router_normed, grad_router = router_pull((grad_pair, loss_weights))
    grad_middle_part, grad_moe_gain = second_pull(grad_second + router_normed)
    grad_middle = grad_final + grad_middle_part
    grad_branch = grad_middle.astype(BF)
    grad_attn = lax.dot_general(grad_branch, out_full, NT, preferred_element_type=F32).astype(BF)
    head_grad = (
        grad_attn.reshape(tok_count, fsdp_count, sh.width).transpose(1, 0, 2)
    )
    head_grad = lax.all_to_all(head_grad, "fsdp", split_axis=0, concat_axis=0, tiled=True)
    run(sums, spread[1])
    head_grad = sums.tie(head_grad)
    head_dqkv, head_table = attend_backward(
        sh, my_groups, my_table, bucket, head_qkv, head_grad, att_turned, att_lse
    )
    run(sums, spread[2])
    head_dqkv = sums.tie(head_dqkv)
    back_dqkv = lax.all_to_all(head_dqkv, "fsdp", split_axis=0, concat_axis=0, tiled=True)
    back_dqkv = sums.step(back_dqkv)
    run(sums, spread[3] - 1)
    expert_sums = sums.finish()
    grad_gate = expert_sums[:ff_shard].T
    grad_up = expert_sums[ff_shard : 2 * ff_shard].T
    grad_down = expert_sums[2 * ff_shard :]
    grad_qkv = (
        back_dqkv.reshape(fsdp_count, tok_count, 3, sh.width)
        .transpose(1, 2, 0, 3)
        .reshape(tok_count, 3 * D)
    )
    grad_out_w = lax.dot_general(attn_low, grad_branch, TN, preferred_element_type=F32)
    grad_qkv_w = lax.dot_general(normed_low, grad_qkv, TN, preferred_element_type=F32)
    grad_normed = lax.dot_general(grad_qkv, qkv_full, NT, preferred_element_type=F32)
    grad_input_part, grad_attn_gain = first_pull(grad_normed)
    grad_inputs = by_token(grad_middle + grad_input_part)

    def rows_of(x):
        return x.astype(BF).reshape(group_count, shard, -1)

    def small_block(parts):
        flat = jnp.concatenate([p.astype(BF).reshape(group_count, -1) for p in parts], 1)
        flat = jnp.pad(flat, ((0, 0), (0, 16 * D - flat.shape[1])))
        return flat.reshape(group_count, 16, D)

    place_table = (jnp.arange(fsdp_count) == fsdp_place).astype(F32)
    whole_table = place_table[:, None] * head_table[:, 0][None, :]
    parts = [rows_of(grad_qkv_w[:, i * D : (i + 1) * D]) for i in range(3)]
    parts.append(rows_of(grad_out_w))
    parts.append(
        small_block([grad_attn_gain, grad_moe_gain, grad_router, whole_table.reshape(-1)])
    )
    sums_dense = dense_sum(jnp.concatenate(parts, 1))
    sum_qkv = jnp.concatenate([sums_dense[i * shard : (i + 1) * shard] for i in range(3)], 1)
    sum_out = sums_dense[3 * shard : 4 * shard]
    sum_small = sums_dense[4 * shard]
    sum_attn = sum_small[marks[0] : marks[1]]
    sum_moe = sum_small[marks[1] : marks[2]]
    sum_router = sum_small[marks[2] : marks[3]].reshape(shard, expert_count)
    sum_table = sum_small[marks[3] : marks[4]]
    return (
        output,
        losses[None, :],
        grad_inputs,
        sum_qkv,
        sum_out,
        sum_attn,
        sum_moe,
        sum_router,
        sum_table,
        grad_gate[None],
        grad_up[None],
        grad_down[None],
    )


def solution(mesh):
    rows = P(("expert", "fsdp"), None)
    flat = P(("expert", "fsdp"))
    cols = P("expert", None, "fsdp")
    deep = P("expert", "fsdp", None)
    in_specs = (
        rows, rows, rows, flat, flat, rows, flat, cols, cols, deep, rows, rows, flat, P(), rows,
    )
    out_specs = (rows, rows, rows, rows, rows, flat, flat, rows, flat, cols, cols, deep)

    return jax.shard_map(local, mesh=mesh, in_specs=in_specs, out_specs=out_specs, check_vma=False)
```

```python
import functools

import jax
import jax.numpy as jnp
from jax import lax
from jax.experimental import pallas as pl
from jax.experimental.pallas import tpu as pltpu
from jax.sharding import PartitionSpec as P


D = 1024
HEADS = 16
HDIM = 64
BUCKETS = 32
TOPK = 2
PLEN = 1024
CLEN = 128
G_LINE = 2

EPSILON = 1e-06
ZLOSS_FACTOR = 0.001
BALANCE_FACTOR = 0.01
MASK_VALUE = -1e30
LOG2E = 1.4426950408889634
HIGHEST = lax.Precision.HIGHEST
TILE = 256
HALF = 128
SPAN_BLOCKS = (PLEN + CLEN) // HALF
BF = jnp.bfloat16
F32 = jnp.float32
NT = (((1,), (1,)), ((), ()))
TN = (((0,), (0,)), ((), ()))


def rms_scale(values, scale_row):
    inverse = lax.rsqrt(jnp.mean(values * values, axis=-1, keepdims=True) + EPSILON)
    return values * inverse * scale_row


def route_local(normed, router, routes):
    logits = jnp.dot(normed, router, precision=HIGHEST)
    log_total = jax.nn.logsumexp(logits, axis=-1)
    chances = jnp.exp(logits - log_total[:, None])
    expert_ids = jnp.arange(router.shape[1], dtype=jnp.int32)
    first_hot = (routes[:, 0:1] == expert_ids[None, :]).astype(F32)
    second_hot = (routes[:, 1:2] == expert_ids[None, :]).astype(F32)
    first_chance = jnp.sum(chances * first_hot, axis=-1)
    second_chance = jnp.sum(chances * second_hot, axis=-1)
    both_chances = first_chance + second_chance
    gate_pair = jnp.stack([first_chance / both_chances, second_chance / both_chances], -1)
    z_loss = jnp.mean(log_total * log_total)
    expert_share = jnp.sum(first_hot + second_hot, axis=0) / (TOPK * routes.shape[0])
    balance = router.shape[1] * jnp.sum(expert_share * jnp.mean(chances, axis=0))
    return (gate_pair, jnp.stack([z_loss, balance]))


class Shape:
    def __init__(self, fsdp_count):
        self.srcs = fsdp_count
        self.hp = HEADS // fsdp_count
        self.width = self.hp * HDIM
        self.part = PLEN // fsdp_count
        self.rows = G_LINE * self.part + CLEN
        self.spt = TILE // self.part
        self.tiles = PLEN // TILE
        self.pairs = fsdp_count // 2
        self.prompt_pairs = self.pairs // G_LINE
        self.units = G_LINE * self.tiles + self.pairs


def order_conts(sh, group_ref, perm_ref):
    counts = [jnp.int32(0), jnp.int32(sh.srcs // G_LINE)]
    for c in range(sh.srcs):
        first = group_ref[c] == 0
        perm_ref[jnp.where(first, counts[0], counts[1])] = jnp.int32(c)
        step = first.astype(jnp.int32)
        counts = [counts[0] + step, counts[1] + 1 - step]


def build_bias(sh, table_ref, bucket_ref, bias_ref):
    bucket = bucket_ref[...]
    for h in range(sh.hp):
        dist = jnp.zeros(bucket.shape, F32)
        for b in range(BUCKETS):
            dist = jnp.where(bucket == b, table_ref[h, b] * LOG2E, dist)
        bias_ref[h, 0] = jnp.full((HALF, HALF), MASK_VALUE, F32)
        before = jnp.full((1, HALF), MASK_VALUE, F32)
        for n in range(SPAN_BLOCKS):
            now = dist[n : n + 1, :]
            both = jnp.broadcast_to(jnp.concatenate([before, now], axis=1), (HALF, 2 * HALF))
            turned = pltpu.roll(both, HALF, 1, stride=1, stride_axis=0)
            bias_ref[h, 1 + n] = turned[:, :HALF]
            before = now


def head_mask(sh, h):
    if sh.hp == 1:
        return None
    lane = lax.broadcasted_iota(jnp.int32, (1, sh.width), 1)
    return (lane >= h * HDIM) & (lane < (h + 1) * HDIM)


def only_head(sh, h, x):
    mask = head_mask(sh, h)
    return x if mask is None else jnp.where(mask, x, jnp.zeros_like(x))


def prompt_rows_of(sh, ref, g, t, part):
    lanes = slice(part * sh.width, (part + 1) * sh.width)
    start = pl.multiple_of(g * sh.part, sh.part)
    return jnp.concatenate(
        [ref[t * sh.spt + s, pl.ds(start, sh.part), lanes] for s in range(sh.spt)], axis=0
    )


def cont_rows_of(sh, ref, c, part):
    lanes = slice(part * sh.width, (part + 1) * sh.width)
    return ref[c, G_LINE * sh.part :, lanes]


def put_prompt_rows(sh, ref, g, t, part, value):
    lanes = slice(part * sh.width, (part + 1) * sh.width)
    start = pl.multiple_of(g * sh.part, sh.part)
    for s in range(sh.spt):
        ref[t * sh.spt + s, pl.ds(start, sh.part), lanes] = value[
            s * sh.part : (s + 1) * sh.part
        ].astype(ref.dtype)


def transpose_low(x):
    return x.astype(F32).T.astype(BF)


def add_bias(scores, bias_ref, h, base, step_q):
    rows = []
    for a in range(2):
        cols = []
        for b in range(2):
            part = scores[a * HALF : (a + 1) * HALF, b * HALF : (b + 1) * HALF]
            cols.append(part * LOG2E + bias_ref[h, base + b * step_q - a])
        rows.append(jnp.concatenate(cols, axis=1))
    return jnp.concatenate(rows, axis=0)


def fold_max(x):
    return jnp.max(x.reshape(-1, 8, x.shape[-1]), axis=0)


def fold_sum(x):
    return jnp.sum(x.reshape(-1, 8, x.shape[-1]), axis=0)


def attn_forward_kernel(
    sh, group_ref, table_ref, bucket_ref, x_ref, o_ref, ot_ref, lse_ref, bias, vt, vtc, sc, perm
):
    order_conts(sh, group_ref, perm)
    build_bias(sh, table_ref, bucket_ref, bias)

    def make_vt(i, _):
        g, t = i // sh.tiles, lax.rem(i, sh.tiles)
        vt[i] = transpose_low(prompt_rows_of(sh, x_ref, g, t, 2))
        return 0

    lax.fori_loop(0, G_LINE * sh.tiles, make_vt, 0)

    def make_vtc(c, _):
        vtc[c] = transpose_low(cont_rows_of(sh, x_ref, c, 2))
        return 0

    lax.fori_loop(0, sh.srcs, make_vtc, 0)

    def scores_tile(keys, qh, base, step_q, kt, peaks):
        out = []
        for h in range(sh.hp):
            s = lax.dot_general(keys, qh[h], NT, preferred_element_type=F32)
            s = add_bias(s, bias, h, base, step_q)
            sc[h, pl.ds(pl.multiple_of(kt * TILE, TILE), TILE), :] = s
            out.append(jnp.maximum(peaks[h], fold_max(s)))
        return tuple(out)

    def value_tile(g, kt, peaks, carry):
        out = []
        for h in range(sh.hp):
            total, acc = carry[h]
            p = jnp.exp2(sc[h, pl.ds(pl.multiple_of(kt * TILE, TILE), TILE), :] - peaks[h])
            total = total + fold_sum(p)
            values = vt[g * sh.tiles + kt, h * HDIM : (h + 1) * HDIM, :]
            acc = acc + jnp.dot(values, p.astype(BF), preferred_element_type=F32)
            out.append((total, acc))
        return tuple(out)

    first_peaks = tuple(jnp.full((8, TILE), MASK_VALUE, F32) for _ in range(sh.hp))
    first_carry = tuple(
        (jnp.zeros((8, TILE), F32), jnp.zeros((HDIM, TILE), F32)) for _ in range(sh.hp)
    )

    def finish(unit, peaks, carry):
        outs = []
        for h in range(sh.hp):
            total = jnp.sum(carry[h][0], axis=0, keepdims=True)
            outs.append(carry[h][1] / total)
            lse_ref[unit, h : h + 1, :] = peaks[h] + jnp.log2(total)
        whole = jnp.concatenate(outs, axis=0) if sh.hp > 1 else outs[0]
        ot_ref[unit] = whole
        return whole.T

    def prompt_unit(i, _):
        g, qt = i // sh.tiles, lax.rem(i, sh.tiles)
        q = prompt_rows_of(sh, x_ref, g, qt, 0) * BF(HDIM**-0.5)
        qh = [only_head(sh, h, q) for h in range(sh.hp)]

        def first(kt, peaks):
            keys = prompt_rows_of(sh, x_ref, g, kt, 1)
            return scores_tile(keys, qh, 2 * (qt - kt) + 1, 1, kt, peaks)

        peaks = lax.fori_loop(0, qt + 1, first, first_peaks)
        peaks = [jnp.max(p, axis=0, keepdims=True) for p in peaks]
        carry = lax.fori_loop(0, qt + 1, lambda kt, c: value_tile(g, kt, peaks, c), first_carry)
        put_prompt_rows(sh, o_ref, g, qt, 0, finish(i, peaks, carry))
        return 0

    lax.fori_loop(0, G_LINE * sh.tiles, prompt_unit, 0)

    def cont_unit(i, _):
        conts = [perm[2 * i], perm[2 * i + 1]]
        g = i // sh.prompt_pairs
        q = jnp.concatenate([cont_rows_of(sh, x_ref, c, 0) for c in conts], axis=0)
        q = q * BF(HDIM**-0.5)
        qh = [only_head(sh, h, q) for h in range(sh.hp)]

        def first(kt, peaks):
            keys = prompt_rows_of(sh, x_ref, g, kt, 1)
            return scores_tile(keys, qh, SPAN_BLOCKS - 2 * kt, 0, kt, peaks)

        peaks = lax.fori_loop(0, sh.tiles, first, first_peaks)
        own = []
        next_peaks = []
        for h in range(sh.hp):
            parts = []
            for b in range(2):
                keys = cont_rows_of(sh, x_ref, conts[b], 1)
                s = lax.dot_general(
                    keys, qh[h][b * HALF : (b + 1) * HALF], NT, preferred_element_type=F32
                )
                parts.append(s * LOG2E + bias[h, 1])
            own.append(jnp.concatenate(parts, axis=1))
            next_peaks.append(jnp.maximum(peaks[h], fold_max(own[h])))
        peaks = [jnp.max(p, axis=0, keepdims=True) for p in next_peaks]
        start = []
        for h in range(sh.hp):
            p = jnp.exp2(own[h] - peaks[h])
            low = p.astype(BF)
            acc = jnp.concatenate(
                [
                    jnp.dot(
                        vtc[conts[b], h * HDIM : (h + 1) * HDIM, :],
                        low[:, b * HALF : (b + 1) * HALF],
                        preferred_element_type=F32,
                    )
                    for b in range(2)
                ],
                axis=1,
            )
            start.append((fold_sum(p), acc))
        carry = lax.fori_loop(
            0, sh.tiles, lambda kt, c: value_tile(g, kt, peaks, c), tuple(start)
        )
        done = finish(G_LINE * sh.tiles + i, peaks, carry)
        for b in range(2):
            o_ref[conts[b], G_LINE * sh.part :, :] = done[b * HALF : (b + 1) * HALF].astype(BF)
        return 0

    lax.fori_loop(0, sh.pairs, cont_unit, 0)


def attn_backward_kernel(
    sh,
    group_ref,
    table_ref,
    bucket_ref,
    x_ref,
    do_ref,
    ot_ref,
    lse_ref,
    dx_ref,
    dtable_ref,
    bias,
    dbias,
    ktr,
    ktc,
    dk,
    dv,
    perm,
):
    order_conts(sh, group_ref, perm)
    build_bias(sh, table_ref, bucket_ref, bias)
    dbias[...] = jnp.zeros_like(dbias)
    dk[...] = jnp.zeros_like(dk)
    dv[...] = jnp.zeros_like(dv)

    def make_kt(i, _):
        g, t = i // sh.tiles, lax.rem(i, sh.tiles)
        ktr[i] = transpose_low(prompt_rows_of(sh, x_ref, g, t, 1))
        return 0

    lax.fori_loop(0, G_LINE * sh.tiles, make_kt, 0)

    def make_ktc(c, _):
        ktc[c] = transpose_low(cont_rows_of(sh, x_ref, c, 1))
        return 0

    lax.fori_loop(0, sh.srcs, make_ktc, 0)

    def inner_terms(unit, do):
        outs = []
        turned = do.astype(F32).T
        for h in range(sh.hp):
            rows = slice(h * HDIM, (h + 1) * HDIM)
            prod = ot_ref[unit, rows, :] * turned[rows, :]
            outs.append(jnp.sum(prod, axis=0, keepdims=True))
        return outs

    def grads_tile(g, kt, qh, doh, lse, inner, base, step_q, dqs):
        keys = prompt_rows_of(sh, x_ref, g, kt, 1)
        values = prompt_rows_of(sh, x_ref, g, kt, 2)
        slot = g * sh.tiles + kt
        out = []
        dkey = dvalue = None
        for h in range(sh.hp):
            s = lax.dot_general(keys, qh[h], NT, preferred_element_type=F32)
            dp = lax.dot_general(values, doh[h], NT, preferred_element_type=F32)
            p = jnp.exp2(add_bias(s, bias, h, base, step_q) - lse[h])
            ds = p * (dp - inner[h])
            for a in range(2):
                for b in range(2):
                    dbias[h, base + b * step_q - a] += ds[
                        a * HALF : (a + 1) * HALF, b * HALF : (b + 1) * HALF
                    ]
            low = ds.astype(BF)
            more_k = jnp.dot(low, qh[h], preferred_element_type=F32)
            more_v = jnp.dot(p.astype(BF), doh[h], preferred_element_type=F32)
            dkey = more_k if dkey is None else dkey + more_k
            dvalue = more_v if dvalue is None else dvalue + more_v
            turned = ktr[slot, h * HDIM : (h + 1) * HDIM, :]
            out.append(dqs[h] + jnp.dot(turned, low, preferred_element_type=F32))
        dk[slot] += dkey
        dv[slot] += dvalue
        return tuple(out)

    def finish(dqs):
        whole = jnp.concatenate(dqs, axis=0) if sh.hp > 1 else dqs[0]
        return whole.T * (HDIM**-0.5)

    first_dq = tuple(jnp.zeros((HDIM, TILE), F32) for _ in range(sh.hp))

    def prompt_unit(i, _):
        g, qt = i // sh.tiles, lax.rem(i, sh.tiles)
        q = prompt_rows_of(sh, x_ref, g, qt, 0) * BF(HDIM**-0.5)
        do = prompt_rows_of(sh, do_ref, g, qt, 0)
        qh = [only_head(sh, h, q) for h in range(sh.hp)]
        doh = [only_head(sh, h, do) for h in range(sh.hp)]
        inner = inner_terms(i, do)
        lse = [lse_ref[i, h : h + 1, :] for h in range(sh.hp)]

        def body(kt, dqs):
            return grads_tile(g, kt, qh, doh, lse, inner, 2 * (qt - kt) + 1, 1, dqs)

        dqs = lax.fori_loop(0, qt + 1, body, first_dq)
        put_prompt_rows(sh, dx_ref, g, qt, 0, finish(dqs))
        return 0

    lax.fori_loop(0, G_LINE * sh.tiles, prompt_unit, 0)

    def cont_unit(i, _):
        conts = [perm[2 * i], perm[2 * i + 1]]
        unit = G_LINE * sh.tiles + i
        g = i // sh.prompt_pairs
        q = jnp.concatenate([cont_rows_of(sh, x_ref, c, 0) for c in conts], axis=0)
        q = q * BF(HDIM**-0.5)
        do = jnp.concatenate([cont_rows_of(sh, do_ref, c, 0) for c in conts], axis=0)
        qh = [only_head(sh, h, q) for h in range(sh.hp)]
        doh = [only_head(sh, h, do) for h in range(sh.hp)]
        inner = inner_terms(unit, do)
        lse = [lse_ref[unit, h : h + 1, :] for h in range(sh.hp)]

        def body(kt, dqs):
            return grads_tile(g, kt, qh, doh, lse, inner, SPAN_BLOCKS - 2 * kt, 0, dqs)

        dqs = lax.fori_loop(0, sh.tiles, body, first_dq)
        more = [[None] * 2 for _ in range(sh.hp)]
        for b in range(2):
            cols = slice(b * HALF, (b + 1) * HALF)
            keys = cont_rows_of(sh, x_ref, conts[b], 1)
            values = cont_rows_of(sh, x_ref, conts[b], 2)
            dkey = dvalue = None
            for h in range(sh.hp):
                s = lax.dot_general(keys, qh[h][cols], NT, preferred_element_type=F32)
                dp = lax.dot_general(values, doh[h][cols], NT, preferred_element_type=F32)
                p = jnp.exp2(s * LOG2E + bias[h, 1] - lse[h][:, cols])
                ds = p * (dp - inner[h][:, cols])
                dbias[h, 1] += ds
                low = ds.astype(BF)
                more_k = jnp.dot(low, qh[h][cols], preferred_element_type=F32)
                more_v = jnp.dot(p.astype(BF), doh[h][cols], preferred_element_type=F32)
                dkey = more_k if dkey is None else dkey + more_k
                dvalue = more_v if dvalue is None else dvalue + more_v
                turned = ktc[conts[b], h * HDIM : (h + 1) * HDIM, :]
                more[h][b] = jnp.dot(turned, low, preferred_element_type=F32)
            w = sh.width
            dx_ref[conts[b], G_LINE * sh.part :, w : 2 * w] = dkey.astype(BF)
            dx_ref[conts[b], G_LINE * sh.part :, 2 * w :] = dvalue.astype(BF)
        dqs = [dqs[h] + jnp.concatenate(more[h], axis=1) for h in range(sh.hp)]
        done = finish(dqs)
        for b in range(2):
            dx_ref[conts[b], G_LINE * sh.part :, : sh.width] = done[
                b * HALF : (b + 1) * HALF
            ].astype(BF)
        return 0

    lax.fori_loop(0, sh.pairs, cont_unit, 0)

    def put_keys(i, _):
        g, t = i // sh.tiles, lax.rem(i, sh.tiles)
        put_prompt_rows(sh, dx_ref, g, t, 1, dk[i])
        put_prompt_rows(sh, dx_ref, g, t, 2, dv[i])
        return 0

    lax.fori_loop(0, G_LINE * sh.tiles, put_keys, 0)

    bucket = bucket_ref[...]
    key_row = lax.broadcasted_iota(jnp.int32, (HALF, 2 * HALF), 0)
    for h in range(sh.hp):
        spread = []
        for n in range(SPAN_BLOCKS):
            wide = jnp.concatenate(
                [jnp.zeros((HALF, HALF), F32), dbias[h, 1 + n]], axis=1
            )
            for bit in range(7):
                moved = pltpu.roll(wide, 2 * HALF - (1 << bit), 1)
                wide = jnp.where((key_row & (1 << bit)) != 0, moved, wide)
            spread.append(jnp.sum(wide, axis=0, keepdims=True))
        rows = []
        for n in range(SPAN_BLOCKS):
            row = spread[n][:, HALF:]
            if n + 1 < SPAN_BLOCKS:
                row = row + spread[n + 1][:, :HALF]
            rows.append(row)
        by_dist = jnp.concatenate(rows, axis=0)
        sums = [
            jnp.sum(jnp.where(bucket == b, by_dist, 0.0), axis=0, keepdims=True)
            for b in range(BUCKETS)
        ]
        lanes = jnp.concatenate(sums, axis=0)
        dtable_ref[h * BUCKETS : (h + 1) * BUCKETS, :] = jnp.broadcast_to(
            jnp.sum(lanes, axis=1, keepdims=True), (BUCKETS, HALF)
        )


SMEM_SPEC = pl.BlockSpec(memory_space=pltpu.SMEM)
VMEM_SPEC = pl.BlockSpec(memory_space=pltpu.VMEM)
GRANT = 48 * 1024 * 1024


def attend_forward(sh, group, table, bucket, x):
    return pl.pallas_call(
        functools.partial(attn_forward_kernel, sh),
        out_shape=(
            jax.ShapeDtypeStruct((sh.srcs, sh.rows, sh.width), BF),
            jax.ShapeDtypeStruct((sh.units, sh.width, TILE), F32),
            jax.ShapeDtypeStruct((sh.units, 8, TILE), F32),
        ),
        in_specs=[SMEM_SPEC, SMEM_SPEC, VMEM_SPEC, VMEM_SPEC],
        out_specs=(VMEM_SPEC, VMEM_SPEC, VMEM_SPEC),
        scratch_shapes=[
            pltpu.VMEM((sh.hp, SPAN_BLOCKS + 1, HALF, HALF), F32),
            pltpu.VMEM((G_LINE * sh.tiles, sh.width, TILE), BF),
            pltpu.VMEM((sh.srcs, sh.width, HALF), BF),
            pltpu.VMEM((sh.hp, PLEN, TILE), F32),
            pltpu.SMEM((sh.srcs,), jnp.int32),
        ],
        compiler_params=pltpu.CompilerParams(vmem_limit_bytes=GRANT),
        cost_estimate=pl.CostEstimate(
            flops=10**10, bytes_accessed=8 * 10**6, transcendentals=5 * 10**6
        ),
        name="attend_forward",
    )(group, table, bucket, x)


def attend_backward(sh, group, table, bucket, x, do, ot, lse):
    return pl.pallas_call(
        functools.partial(attn_backward_kernel, sh),
        out_shape=(
            jax.ShapeDtypeStruct((sh.srcs, sh.rows, 3 * sh.width), BF),
            jax.ShapeDtypeStruct((sh.hp * BUCKETS, HALF), F32),
        ),
        in_specs=[SMEM_SPEC, SMEM_SPEC, VMEM_SPEC, VMEM_SPEC, VMEM_SPEC, VMEM_SPEC, VMEM_SPEC],
        out_specs=(VMEM_SPEC, VMEM_SPEC),
        scratch_shapes=[
            pltpu.VMEM((sh.hp, SPAN_BLOCKS + 1, HALF, HALF), F32),
            pltpu.VMEM((sh.hp, SPAN_BLOCKS + 1, HALF, HALF), F32),
            pltpu.VMEM((G_LINE * sh.tiles, sh.width, TILE), BF),
            pltpu.VMEM((sh.srcs, sh.width, HALF), BF),
            pltpu.VMEM((G_LINE * sh.tiles, TILE, sh.width), F32),
            pltpu.VMEM((G_LINE * sh.tiles, TILE, sh.width), F32),
            pltpu.SMEM((sh.srcs,), jnp.int32),
        ],
        compiler_params=pltpu.CompilerParams(vmem_limit_bytes=GRANT),
        cost_estimate=pl.CostEstimate(
            flops=2 * 10**10, bytes_accessed=12 * 10**6, transcendentals=5 * 10**6
        ),
        name="attend_backward",
    )(group, table, bucket, x, do, ot, lse)


def ring_order(count):
    deep, wide = 4, count // 4
    order = [a * wide for a in range(deep)]
    for turn, a in enumerate(reversed(range(deep))):
        row = [a * wide + b for b in range(1, wide)]
        order += row if turn % 2 == 0 else row[::-1]
    return order


def ring_hop(x, count, step):
    ring = ring_order(count)
    return lax.ppermute(x, "fsdp", [(ring[i], ring[(i + step) % count]) for i in range(count)])


def tied(*values):
    return lax.optimization_barrier(values)


class RingGather:
    def __init__(self, own, count):
        self.count = count
        self.chunks = [None] * count
        self.chunks[0] = own
        self.right = self.left = own
        self.done = 0
        self.steps = count // 2

    def step(self):
        self.done += 1
        s = self.done
        if s < self.steps:
            self.right = ring_hop(self.right, self.count, 1)
            self.left = ring_hop(self.left, self.count, -1)
        else:
            half = self.right.shape[0] // 2
            self.right = ring_hop(self.right[:half], self.count, 1)
            self.left = ring_hop(self.left[half:], self.count, -1)
        self.keep()

    def keep(self):
        s = self.done
        if s < self.steps:
            self.chunks[self.count - s] = self.right
            self.chunks[s] = self.left
        else:
            self.chunks[s] = (self.right, self.left)

    def tie(self, value):
        value, self.right, self.left = tied(value, self.right, self.left)
        self.keep()
        return value


class RingScatter:
    def __init__(self, part, count):
        self.part, self.count = part, count
        self.right = self.left = None
        self.done = 0
        self.steps = count // 2

    def step(self, after=None):
        count, s = self.count, self.done
        away = self.steps - s
        if s == 0:
            send_left, send_right = self.part(away)
        else:
            near_left = self.part(count - away).astype(F32)
            near_right = self.part(away).astype(F32)
            if s == 1:
                half = near_left.shape[0] // 2
                send_left = jnp.concatenate(
                    [near_left[:half] + self.left.astype(F32), near_left[half:]], 0
                )
                send_right = jnp.concatenate(
                    [near_right[:half], near_right[half:] + self.right.astype(F32)], 0
                )
            else:
                send_left = near_left + self.left.astype(F32)
                send_right = near_right + self.right.astype(F32)
        send_left, send_right = send_left.astype(BF), send_right.astype(BF)
        if after is not None:
            after, send_left, send_right = tied(after, send_left, send_right)
        self.left = ring_hop(send_left, count, -1)
        self.right = ring_hop(send_right, count, 1)
        self.done += 1
        return after

    def tie(self, value):
        value, self.right, self.left = tied(value, self.right, self.left)
        return value

    def finish(self):
        return self.part(0).astype(F32) + self.right.astype(F32) + self.left.astype(F32)


MESH_ID = pl.DeviceIdType.MESH
DEEP = 4


class Spot:
    def __init__(self):
        e, f = lax.axis_index("expert"), lax.axis_index("fsdp")
        self.x, self.c = e // 2, lax.rem(e, 2)
        self.z, self.y = f // 2, lax.rem(f, 2)
        self.ox, self.oy, self.oc = 1 - self.x, 1 - self.y, 1 - self.c

    def place(self, x=None, y=None, z=None, c=None):
        x = self.x if x is None else x
        y = self.y if y is None else y
        z = self.z if z is None else z
        c = self.c if c is None else c
        return {"expert": x * 2 + c, "fsdp": z * 2 + y}

    def block(self, x, y, z, c):
        return (x * 2 + c) * 8 + z * 2 + y

    def greet(self):
        barrier = pltpu.get_barrier_semaphore()
        for target in (self.place(x=self.ox), self.place(y=self.oy), self.place(c=self.oc)):
            pl.semaphore_signal(barrier, inc=1, device_id=target, device_id_type=MESH_ID)
        for step in (-1, 1):

            @pl.when(self.inside(self.z + step))
            def _(step=step):
                pl.semaphore_signal(
                    barrier, inc=1, device_id=self.along(step), device_id_type=MESH_ID
                )

        pl.semaphore_wait(barrier, 4 + self.z * (DEEP - 1 - self.z) // 2)

    def wrap(self, step):
        return lax.rem(self.z + step + DEEP, DEEP)

    def along(self, step):
        return self.place(z=self.wrap(step))

    def inside(self, z):
        return (z >= 0) & (z < DEEP)


def dense_gather_kernel(cut, x_ref, out_ref, send_sems, recv_sems, own_sem):
    me = Spot()
    rows = x_ref.shape[0]
    spans = [(0, cut), (cut, rows - cut)]
    pending = []

    def view(ref, h):
        return ref.at[pl.ds(*spans[h])]

    def send(src, blk, h, target, cond):
        copy = pltpu.make_async_remote_copy(
            src_ref=src,
            dst_ref=view(out_ref.at[blk], h),
            send_sem=send_sems.at[len(pending)],
            recv_sem=recv_sems.at[blk, h],
            device_id=target,
            device_id_type=MESH_ID,
        )
        pending.append((copy, cond))
        if cond is None:
            copy.start()
        else:
            pl.when(cond)(copy.start)

    def arrive(blk, h, cond):
        copy = pltpu.make_async_remote_copy(
            src_ref=view(out_ref.at[blk], h),
            dst_ref=view(out_ref.at[blk], h),
            send_sem=send_sems.at[0],
            recv_sem=recv_sems.at[blk, h],
            device_id=me.place(c=me.oc),
            device_id_type=MESH_ID,
        )
        if cond is None:
            copy.wait_recv()
        else:
            pl.when(cond)(copy.wait_recv)

    def both(a, b):
        return b if a is None else (a if b is None else a & b)

    by_y, by_x = me.place(y=me.oy), me.place(x=me.ox)
    core = me.place(c=me.oc)
    me.greet()
    mine = me.block(me.x, me.y, me.z, me.c)
    own = pltpu.make_async_copy(x_ref, out_ref.at[mine], own_sem)
    own.start()
    for h in range(2):
        for step in (-1, 1):
            send(view(x_ref, h), mine, h, me.along(step), me.inside(me.z + step))
    for h in range(2):
        for target in (by_y, by_x, core):
            send(view(x_ref, h), mine, h, target, None)

    def line(dist):
        if dist == 0:
            return [(me.z, None, 0)]
        return [(me.wrap(s * dist), me.inside(me.z + s * dist), s) for s in (-1, 1)]

    def from_line(dist):
        for zb, cond, sign in line(dist):
            blk = me.block(me.x, me.y, zb, me.c)
            for h in range(2):
                arrive(blk, h, cond)
                src = view(out_ref.at[blk], h)
                send(src, blk, h, me.along(-sign), both(cond, me.inside(me.z - sign)))
                for target in (by_y, by_x, core):
                    send(src, blk, h, target, cond)

    def from_side(dist):
        for zb, cond, _ in line(dist):
            for h in range(2):
                one = me.block(me.x, me.oy, zb, me.c)
                two = me.block(me.ox, me.y, zb, me.c)
                onward, last = ((one, by_x), two) if h == 0 else ((two, by_y), one)
                arrive(onward[0], h, cond)
                src = view(out_ref.at[onward[0]], h)
                send(src, onward[0], h, onward[1], cond)
                send(src, onward[0], h, core, cond)
                arrive(last, h, cond)
                send(view(out_ref.at[last], h), last, h, core, cond)

    def from_corner(dist):
        for zb, cond, _ in line(dist):
            blk = me.block(me.ox, me.oy, zb, me.c)
            for h in range(2):
                arrive(blk, h, cond)
                send(view(out_ref.at[blk], h), blk, h, core, cond)

    for dist in range(DEEP):
        if dist > 0:
            from_line(dist)
        from_side(dist)
        if dist > 0:
            from_corner(dist - 1)
    from_corner(DEEP - 1)
    for x in range(2):
        for y in range(2):
            for z in range(DEEP):
                for h in range(2):
                    arrive(me.block(x, y, z, me.oc), h, None)
    own.wait()
    for copy, cond in pending:
        if cond is None:
            copy.wait_send()
        else:
            pl.when(cond)(copy.wait_send)


def dense_gather(x, count):
    rows = x.shape[0]
    if count != 32 or lax.axis_size("fsdp") != 2 * DEEP:
        return lax.all_gather(x, ("expert", "fsdp"), axis=0, tiled=False)
    cut = rows // 32 * 16 + 16 * (rows // 16 % 2)
    return pl.pallas_call(
        functools.partial(dense_gather_kernel, cut),
        out_shape=jax.ShapeDtypeStruct((count,) + x.shape, x.dtype),
        in_specs=[pl.BlockSpec(memory_space=pltpu.VMEM)],
        out_specs=pl.BlockSpec(memory_space=pl.ANY),
        scratch_shapes=[
            pltpu.SemaphoreType.DMA((128,)),
            pltpu.SemaphoreType.DMA((count, 2)),
            pltpu.SemaphoreType.DMA,
        ],
        compiler_params=pltpu.CompilerParams(collective_id=0, has_side_effects=True),
        cost_estimate=pl.CostEstimate(
            flops=0, bytes_accessed=100 * 10**6, transcendentals=0
        ),
        name="dense_gather",
    )(x)


def add_into(dst, src):
    def body(i, _):
        at = pl.ds(pl.multiple_of(i * 16, 16), 16)
        dst[at, :] = (dst[at, :].astype(F32) + src[at, :].astype(F32)).astype(BF)
        return 0

    lax.fori_loop(0, dst.shape[0] // 16, body, 0)


def dense_sum_kernel(
    cut, g_ref, out_ref, acc, cbuf, xbuf, ybuf, zbuf, send_sems, recv_sems, load_sems
):
    me = Spot()
    rows = out_ref.shape[0]
    top, low = pl.ds(0, cut), pl.ds(cut, rows - cut)
    pending = []

    def send(src, dst, at, target, cond=None):
        copy = pltpu.make_async_remote_copy(
            src_ref=src,
            dst_ref=dst,
            send_sem=send_sems.at[len(pending)],
            recv_sem=recv_sems.at[at],
            device_id=target,
            device_id_type=MESH_ID,
        )
        pending.append((copy, cond))
        if cond is None:
            copy.start()
        else:
            pl.when(cond)(copy.start)

    def arrive(dst, at):
        pltpu.make_async_remote_copy(
            src_ref=dst,
            dst_ref=dst,
            send_sem=send_sems.at[0],
            recv_sem=recv_sems.at[at],
            device_id=me.place(c=me.oc),
            device_id_type=MESH_ID,
        ).wait_recv()

    by_y, by_x, core = me.place(y=me.oy), me.place(x=me.ox), me.place(c=me.oc)
    me.greet()
    zs = (0, 3, 2, 1)
    loads = []
    for k in range(DEEP):
        for x in range(2):
            at = x * DEEP + k
            theirs = (x * 2 + me.oc) * 8 + zs[k] * 2
            send(g_ref.at[pl.ds(theirs, 2)], cbuf.at[at], at, core)
            ours = (x * 2 + me.c) * 8 + zs[k] * 2
            load = pltpu.make_async_copy(g_ref.at[pl.ds(ours, 2)], acc.at[at], load_sems.at[at])
            load.start()
            loads.append(load)

    def first(k):
        for x in range(2):
            at = x * DEEP + k
            loads[k * 2 + x].wait()
            arrive(cbuf.at[at], at)
            for y in range(2):
                add_into(acc.at[at, y], cbuf.at[at, y])
        base = 8 + k * 6
        for y in range(2):
            send(acc.at[me.ox * DEEP + k, y, top], xbuf.at[k, y, top], base + y, by_x)
        for x in range(2):
            send(acc.at[x * DEEP + k, me.oy, low], ybuf.at[k, x, low], base + 2 + x, by_y)

    def second(k):
        base = 8 + k * 6
        for y in range(2):
            arrive(xbuf.at[k, y, top], base + y)
            add_into(acc.at[me.x * DEEP + k, y, top], xbuf.at[k, y, top])
        for x in range(2):
            arrive(ybuf.at[k, x, low], base + 2 + x)
            add_into(acc.at[x * DEEP + k, me.y, low], ybuf.at[k, x, low])
        send(acc.at[me.x * DEEP + k, me.oy, top], ybuf.at[k, 0, top], base + 4, by_y)
        send(acc.at[me.ox * DEEP + k, me.y, low], xbuf.at[k, 0, low], base + 5, by_x)

    def third(k):
        base = 8 + k * 6
        block = acc.at[me.x * DEEP + k, me.y]
        arrive(ybuf.at[k, 0, top], base + 4)
        add_into(block.at[top], ybuf.at[k, 0, top])
        arrive(xbuf.at[k, 0, low], base + 5)
        add_into(block.at[low], xbuf.at[k, 0, low])

    def along(k, sign, behind):
        zo = zs[k]
        here = behind if sign > 0 else DEEP - 1 - behind
        term = acc.at[me.x * DEEP + k, me.y]
        base = 32 + k * 4 + (sign + 1)
        side = k * 4 + (sign + 1)
        is_here = me.z == here
        for h, at in ((0, top), (1, low)):
            if behind > 0:

                @pl.when(is_here)
                def _(h=h, at=at):
                    arrive(zbuf.at[side + h, at], base + h)
                    add_into(term.at[at], zbuf.at[side + h, at])

            if here != zo:
                send(
                    term.at[at], zbuf.at[side + h, at], base + h, me.along(sign), is_here
                )

    for step in range(DEEP + 6):
        if step < DEEP:
            first(step)
        if 0 <= step - 1 < DEEP:
            second(step - 1)
        if 0 <= step - 2 < DEEP:
            third(step - 2)
        for k in range(DEEP):
            behind = step - 2 - k
            if behind >= 0:
                if behind <= zs[k]:
                    along(k, 1, behind)
                if behind <= DEEP - 1 - zs[k]:
                    along(k, -1, behind)
    block = acc.at[me.x * DEEP + lax.rem(DEEP - me.z, DEEP), me.y]

    def put(i, _):
        at = pl.ds(pl.multiple_of(i * 16, 16), 16)
        out_ref[at, :] = block[at, :].astype(F32)
        return 0

    lax.fori_loop(0, rows // 16, put, 0)
    for copy, cond in pending:
        if cond is None:
            copy.wait_send()
        else:
            pl.when(cond)(copy.wait_send)


def dense_sum(x):
    count, rows, width = x.shape
    if count != 32 or lax.axis_size("fsdp") != 2 * DEEP:
        flat = x.reshape(count * rows, width)
        return lax.psum_scatter(
            flat, ("expert", "fsdp"), scatter_dimension=0, tiled=True
        ).astype(F32)
    cut = rows // 32 * 16 + 16 * (rows // 16 % 2)
    pair = (2 * DEEP, 2, rows, width)
    return pl.pallas_call(
        functools.partial(dense_sum_kernel, cut),
        out_shape=jax.ShapeDtypeStruct((rows, width), F32),
        in_specs=[pl.BlockSpec(memory_space=pl.ANY)],
        out_specs=pl.BlockSpec(memory_space=pltpu.VMEM),
        scratch_shapes=[
            pltpu.VMEM(pair, BF),
            pltpu.VMEM(pair, BF),
            pltpu.VMEM((DEEP, 2, rows, width), BF),
            pltpu.VMEM((DEEP, 2, rows, width), BF),
            pltpu.VMEM((4 * DEEP, rows, width), BF),
            pltpu.SemaphoreType.DMA((72,)),
            pltpu.SemaphoreType.DMA((48,)),
            pltpu.SemaphoreType.DMA((8,)),
        ],
        compiler_params=pltpu.CompilerParams(
            collective_id=1, has_side_effects=True, vmem_limit_bytes=40 * 1024 * 1024
        ),
        cost_estimate=pl.CostEstimate(
            flops=0, bytes_accessed=100 * 10**6, transcendentals=0
        ),
        name="dense_sum",
    )(x)


SLICE = 256


def gelu_terms(x):
    root = 0.7978845608028654
    square = x * x
    t = jnp.tanh(root * (x + 0.044715 * square * x))
    half = 0.5 * (1.0 + t)
    slope = half + 0.5 * x * (1.0 - t * t) * (root * (1.0 + 3 * 0.044715 * square))
    return x * half, slope


def chunk_pieces(index, split, ff_shard):
    if not split:
        return [(0, m * ff_shard, m, index * ff_shard, ff_shard) for m in range(3)]
    half = ff_shard // 2
    base = index * ff_shard
    return [
        (0, 0, 0, base, ff_shard),
        (0, ff_shard, 1, base, half),
        (1, 0, 1, base + half, half),
        (1, half, 2, base, ff_shard),
    ]


def chunk_copies(refs, whole, sems, ff_shard, outward):
    count = len(refs) - 1
    far = count // 2
    out = []
    for k in range(count):
        own = refs[k : k + 1] if k < far else (refs[k : k + 2] if k == far else refs[k + 1 : k + 2])
        pieces = []
        for n, (src, at, m, row, rows) in enumerate(chunk_pieces(k, k == far, ff_shard)):
            block = own[src].at[pl.ds(at, rows)]
            spot = whole.at[m, pl.ds(row, rows)]
            a, b = (spot, block) if outward else (block, spot)
            pieces.append(pltpu.make_async_copy(a, b, sems.at[k, n]))
        out.append(pieces)
    return out


def fetch_weights(refs, whole, sems, ff_shard, t):
    copies = chunk_copies(refs, whole, sems, ff_shard, False)

    @pl.when(t == 0)
    def _():
        for pieces in copies:
            for c in pieces:
                c.start()

    for k, pieces in enumerate(copies):

        @pl.when(t == k * ff_shard // SLICE)
        def _(pieces=pieces):
            for c in pieces:
                c.wait()


def ffn_forward_kernel(count, ff_shard, rows_ref, *refs):
    chunks, rest = refs[: count + 1], refs[count + 1 :]
    out_ref, act_ref, turn_ref, hid_ref, whole, acc, sems = rest
    t = pl.program_id(0)
    fetch_weights(chunks, whole, sems, ff_shard, t)
    at = pl.ds(pl.multiple_of(t * SLICE, SLICE), SLICE)
    rows = rows_ref[...]
    gate = lax.dot_general(rows, whole[0, at], NT, preferred_element_type=F32)
    up = lax.dot_general(rows, whole[1, at], NT, preferred_element_type=F32)
    act, slope = gelu_terms(gate)
    hidden = (act * up).astype(BF)
    act_ref[0] = act
    turn_ref[0] = up * slope
    hid_ref[0] = hidden
    more = jnp.dot(hidden, whole[2, at], preferred_element_type=F32)

    @pl.when(t == 0)
    def _():
        acc[...] = more

    @pl.when(t > 0)
    def _():
        acc[...] += more

    @pl.when(t == pl.num_programs(0) - 1)
    def _():
        out_ref[...] = acc[...].astype(BF)


def ffn_backward_kernel(count, ff_shard, grad_ref, act_ref, turn_ref, *refs):
    chunks, rest = refs[: count + 1], refs[count + 1 :]
    out_ref, dgate_ref, dup_ref, whole, acc, sems = rest
    t = pl.program_id(0)
    fetch_weights(chunks, whole, sems, ff_shard, t)
    at = pl.ds(pl.multiple_of(t * SLICE, SLICE), SLICE)
    dhid = lax.dot_general(grad_ref[...], whole[2, at], NT, preferred_element_type=F32)
    dgate = (dhid * turn_ref[0]).astype(BF)
    dup = (dhid * act_ref[0]).astype(BF)
    dgate_ref[0] = dgate
    dup_ref[0] = dup
    more = jnp.dot(
        jnp.concatenate([dgate, dup], axis=1),
        jnp.concatenate([whole[0, at], whole[1, at]], axis=0),
        preferred_element_type=F32,
    )

    @pl.when(t == 0)
    def _():
        acc[...] = more

    @pl.when(t > 0)
    def _():
        acc[...] += more

    @pl.when(t == pl.num_programs(0) - 1)
    def _():
        out_ref[...] = acc[...].astype(BF)


def ffn_weights_kernel(count, ff_shard, rows_ref, grad_ref, hid_ref, dgate_ref, dup_ref, *refs):
    chunks, (whole, sems) = refs[: count + 1], refs[count + 1 :]
    t = pl.program_id(0)
    at = pl.ds(pl.multiple_of(t * SLICE, SLICE), SLICE)
    for m, (left, right) in enumerate(
        ((dgate_ref, rows_ref), (dup_ref, rows_ref), (hid_ref, grad_ref))
    ):
        whole[m, at] = lax.dot_general(
            left[0], right[...], TN, preferred_element_type=F32
        ).astype(BF)
    copies = chunk_copies(chunks, whole, sems, ff_shard, True)
    for k, pieces in enumerate(copies):

        @pl.when(t == ((k + 1) * ff_shard - 1) // SLICE)
        def _(pieces=pieces):
            for c in pieces:
                c.start()

    @pl.when(t == pl.num_programs(0) - 1)
    def _():
        for pieces in copies:
            for c in pieces:
                c.wait()


def fixed(shape):
    return pl.BlockSpec(shape, lambda t: (0,) * len(shape))


def stepped(shape):
    return pl.BlockSpec(shape, lambda t: (t, 0, 0))


ANY_SPEC = pl.BlockSpec(memory_space=pl.ANY)


def ffn_cost(slots, hidden):
    work = 6 * slots * D * hidden
    return pl.CostEstimate(flops=work, bytes_accessed=40 * 10**6, transcendentals=slots * hidden)


def ffn_params():
    return pltpu.CompilerParams(
        dimension_semantics=("arbitrary",), vmem_limit_bytes=60 * 1024 * 1024
    )


def ffn_forward(rows, chunks, ff_shard):
    slots, count = rows.shape[0], len(chunks) - 1
    hidden = count * ff_shard
    steps = hidden // SLICE
    return pl.pallas_call(
        functools.partial(ffn_forward_kernel, count, ff_shard),
        grid=(steps,),
        out_shape=(
            jax.ShapeDtypeStruct((slots, D), BF),
            jax.ShapeDtypeStruct((steps, slots, SLICE), F32),
            jax.ShapeDtypeStruct((steps, slots, SLICE), F32),
            jax.ShapeDtypeStruct((steps, slots, SLICE), BF),
        ),
        in_specs=[fixed((slots, D))] + [ANY_SPEC] * (count + 1),
        out_specs=(
            fixed((slots, D)),
            stepped((1, slots, SLICE)),
            stepped((1, slots, SLICE)),
            stepped((1, slots, SLICE)),
        ),
        scratch_shapes=[
            pltpu.VMEM((3, hidden, D), BF),
            pltpu.VMEM((slots, D), F32),
            pltpu.SemaphoreType.DMA((count, 4)),
        ],
        compiler_params=ffn_params(),
        cost_estimate=ffn_cost(slots, hidden),
        name="ffn_forward",
    )(rows, *chunks)


def ffn_backward(grad, act, turn, chunks, ff_shard):
    slots, count = grad.shape[0], len(chunks) - 1
    hidden = count * ff_shard
    steps = hidden // SLICE
    tile = jax.ShapeDtypeStruct((steps, slots, SLICE), BF)
    return pl.pallas_call(
        functools.partial(ffn_backward_kernel, count, ff_shard),
        grid=(steps,),
        out_shape=(jax.ShapeDtypeStruct((slots, D), BF), tile, tile),
        in_specs=[fixed((slots, D))]
        + [stepped((1, slots, SLICE))] * 2
        + [ANY_SPEC] * (count + 1),
        out_specs=(fixed((slots, D)),) + (stepped((1, slots, SLICE)),) * 2,
        scratch_shapes=[
            pltpu.VMEM((3, hidden, D), BF),
            pltpu.VMEM((slots, D), F32),
            pltpu.SemaphoreType.DMA((count, 4)),
        ],
        compiler_params=ffn_params(),
        cost_estimate=ffn_cost(slots, hidden),
        name="ffn_backward",
    )(grad, act, turn, *chunks)


def ffn_weights(rows, grad, hid, dgate, dup, count, ff_shard):
    slots = rows.shape[0]
    hidden = count * ff_shard
    steps = hidden // SLICE
    full = jax.ShapeDtypeStruct((3 * ff_shard, D), BF)
    half = jax.ShapeDtypeStruct((3 * ff_shard // 2, D), BF)
    far = count // 2
    shapes = [full] * far + [half] * 2 + [full] * (count - far - 1)
    return pl.pallas_call(
        functools.partial(ffn_weights_kernel, count, ff_shard),
        grid=(steps,),
        out_shape=tuple(shapes),
        in_specs=[fixed((slots, D))] * 2 + [stepped((1, slots, SLICE))] * 3,
        out_specs=(ANY_SPEC,) * (count + 1),
        scratch_shapes=[
            pltpu.VMEM((3, hidden, D), BF),
            pltpu.SemaphoreType.DMA((count, 4)),
        ],
        compiler_params=ffn_params(),
        cost_estimate=ffn_cost(slots, hidden),
        name="ffn_weights",
    )(rows, grad, hid, dgate, dup)


def local(
    inputs,
    w_qkv,
    w_out,
    attn_gain,
    moe_gain,
    w_router,
    bias_table,
    w_gate,
    w_up,
    w_down,
    routes,
    slot_order,
    group_map,
    buckets,
    grad_output,
):
    tok_count = inputs.shape[0]
    expert_count = w_router.shape[1]
    capacity = (5 * TOPK * tok_count + 4 * expert_count - 1) // (4 * expert_count)
    fsdp_count = lax.axis_size("fsdp")
    fsdp_place = lax.axis_index("fsdp")
    expert_place = lax.axis_index("expert")
    group_count = lax.axis_size("expert") * fsdp_count
    sh = Shape(fsdp_count)
    prompt_rows = sh.part * G_LINE
    slot_total = expert_count * capacity
    shard = w_qkv.shape[0]
    ff_shard = w_down.shape[1]

    def by_prompt(x):
        head = x[:prompt_rows].reshape(sh.part, G_LINE, -1).transpose(1, 0, 2)
        return jnp.concatenate([head.reshape(prompt_rows, -1), x[prompt_rows:]], 0)

    def by_token(x):
        head = x[:prompt_rows].reshape(G_LINE, sh.part, -1).transpose(1, 0, 2)
        return jnp.concatenate([head.reshape(prompt_rows, -1), x[prompt_rows:]], 0)

    own_weights = jnp.concatenate([w_gate[0].T, w_up[0].T, w_down[0]], 0)
    spread = [fsdp_count // 8] * 4
    spread[0] += fsdp_count // 2 - sum(spread)

    def run(ring, count):
        for _ in range(count):
            ring.step()

    small = jnp.concatenate(
        [attn_gain, moe_gain, w_router.reshape(-1), bias_table, group_map.astype(BF)]
    )
    small_rows = -(-small.shape[0] // D)
    small_rows = -(-small_rows // 16) * 16
    small = jnp.pad(small, (0, small_rows * D - small.shape[0])).reshape(small_rows, D)
    pack = jnp.concatenate([w_qkv[:, i * D : (i + 1) * D] for i in range(3)] + [w_out, small], 0)
    gathered = dense_gather(pack, group_count)
    own_weights, tail = tied(own_weights, gathered[:, 4 * shard])
    weights = RingGather(own_weights, fsdp_count)
    run(weights, spread[0])
    qkv_full = jnp.concatenate(
        [gathered[:, i * shard : (i + 1) * shard].reshape(D, D) for i in range(3)], 1
    )
    out_full = gathered[:, 3 * shard : 4 * shard].reshape(D, D)
    marks = [0, shard, 2 * shard, 2 * shard + shard * expert_count]
    marks += [marks[-1] + bias_table.shape[0]]
    attn_scale = tail[:, marks[0] : marks[1]].reshape(D).astype(F32)
    moe_scale = tail[:, marks[1] : marks[2]].reshape(D).astype(F32)
    router = tail[:, marks[2] : marks[3]].reshape(D, expert_count).astype(F32)
    table = tail[:, marks[3] : marks[4]].reshape(fsdp_count, sh.hp, BUCKETS)
    my_table = lax.dynamic_index_in_dim(table, fsdp_place, 0, keepdims=False).astype(F32)
    groups = tail[:, marks[4]].reshape(-1, fsdp_count)
    my_groups = lax.dynamic_index_in_dim(groups, expert_place, 0, keepdims=False)
    my_groups = my_groups.astype(jnp.int32)
    bucket = buckets.reshape(SPAN_BLOCKS, HALF)

    token_input = by_prompt(inputs)
    grad_rows_low = by_prompt(grad_output)
    routes = by_prompt(routes)
    slot_order = by_prompt(slot_order)

    input_float = token_input.astype(F32)
    normed, first_pull = jax.vjp(rms_scale, input_float, attn_scale)
    normed_low = normed.astype(BF)
    qkv_rows = jnp.dot(normed_low, qkv_full, preferred_element_type=F32).astype(BF)
    by_heads = (
        qkv_rows.reshape(tok_count, 3, fsdp_count, sh.width)
        .transpose(2, 0, 1, 3)
        .reshape(fsdp_count, tok_count, 3 * sh.width)
    )
    head_qkv = lax.all_to_all(by_heads, "fsdp", split_axis=0, concat_axis=0, tiled=True)
    head_qkv = weights.tie(head_qkv)
    run(weights, spread[1])
    head_att, att_turned, att_lse = attend_forward(sh, my_groups, my_table, bucket, head_qkv)
    att_back = lax.all_to_all(head_att, "fsdp", split_axis=0, concat_axis=0, tiled=True)
    att_back = weights.tie(att_back)
    run(weights, spread[2])
    run(weights, spread[3])
    attn_low = att_back.transpose(1, 0, 2).reshape(tok_count, D)

    middle = input_float + jnp.dot(attn_low, out_full, preferred_element_type=F32)
    second_normed, second_pull = jax.vjp(rms_scale, middle, moe_scale)
    (gate_pair, losses), router_pull = jax.vjp(
        lambda normed_rows, router_rows: route_local(normed_rows, router_rows, routes),
        second_normed,
        router,
    )
    kept_mask = (slot_order < capacity).astype(F32)
    gate_kept = gate_pair * kept_mask
    slot_ids = jnp.arange(slot_total, dtype=jnp.int32)
    slot_place = jnp.where(slot_order < capacity, routes * capacity + slot_order, -1)
    hot = [slot_place[:, k : k + 1] == slot_ids[None, :] for k in range(TOPK)]
    any_low = (hot[0] | hot[1]).astype(BF)
    outgoing = lax.dot_general(
        any_low, second_normed.astype(BF), TN, preferred_element_type=F32
    ).astype(BF)

    def swap_experts(rows):
        rows = rows.reshape(expert_count, capacity, D)
        rows = lax.all_to_all(rows, "expert", split_axis=0, concat_axis=0, tiled=True)
        return rows.reshape(slot_total, D)

    expert_rows = swap_experts(outgoing)
    slot_gate = jnp.sum(
        jnp.where(hot[0], gate_kept[:, 0:1], 0.0) + jnp.where(hot[1], gate_kept[:, 1:2], 0.0),
        axis=0,
    )
    slot_grad = lax.dot_general(any_low, grad_rows_low, TN, preferred_element_type=F32)
    grad_result = swap_experts((slot_gate[:, None] * slot_grad).astype(BF))

    far = fsdp_count // 2
    blocks = weights.chunks[:far] + list(weights.chunks[far]) + weights.chunks[far + 1 :]
    result_rows, act, turn, hidden = ffn_forward(expert_rows, blocks, ff_shard)
    returned = swap_experts(result_rows)
    grad_rows, grad_gate_pre, grad_up_pre = ffn_backward(
        grad_result, act, turn, blocks, ff_shard
    )
    grad_sent = swap_experts(grad_rows)
    totals = ffn_weights(
        expert_rows, grad_result, hidden, grad_gate_pre, grad_up_pre, fsdp_count, ff_shard
    )

    def part(k):
        if k == far:
            return totals[far : far + 2]
        return totals[k if k < far else k + 1]

    sums = RingScatter(part, fsdp_count)
    run(sums, spread[0])

    picked = [
        jnp.dot(h.astype(BF), returned, preferred_element_type=F32) for h in hot
    ]
    block_out = middle + gate_kept[:, 0:1] * picked[0] + gate_kept[:, 1:2] * picked[1]
    output = by_token(block_out.astype(BF))
    grad_final = grad_rows_low.astype(F32)
    grad_pair = (
        jnp.stack([jnp.sum(grad_final * p, axis=-1) for p in picked], -1) * kept_mask
    )
    grad_second = jnp.dot(any_low, grad_sent, preferred_element_type=F32)
    loss_weights = jnp.array([ZLOSS_FACTOR, BALANCE_FACTOR], F32) / group_count
    router_normed, grad_router = router_pull((grad_pair, loss_weights))
    grad_middle_part, grad_moe_gain = second_pull(grad_second + router_normed)
    grad_middle = grad_final + grad_middle_part
    grad_branch = grad_middle.astype(BF)
    grad_attn = lax.dot_general(grad_branch, out_full, NT, preferred_element_type=F32).astype(BF)
    head_grad = (
        grad_attn.reshape(tok_count, fsdp_count, sh.width).transpose(1, 0, 2)
    )
    head_grad = sums.tie(head_grad)
    head_grad = lax.all_to_all(head_grad, "fsdp", split_axis=0, concat_axis=0, tiled=True)
    run(sums, spread[1])
    head_grad = sums.tie(head_grad)
    head_dqkv, head_table = attend_backward(
        sh, my_groups, my_table, bucket, head_qkv, head_grad, att_turned, att_lse
    )
    run(sums, spread[2])
    head_dqkv = sums.tie(head_dqkv)
    back_dqkv = lax.all_to_all(head_dqkv, "fsdp", split_axis=0, concat_axis=0, tiled=True)
    back_dqkv = sums.step(back_dqkv)
    run(sums, spread[3] - 1)
    expert_sums = sums.finish()
    grad_gate = expert_sums[:ff_shard].T
    grad_up = expert_sums[ff_shard : 2 * ff_shard].T
    grad_down = expert_sums[2 * ff_shard :]
    grad_qkv = (
        back_dqkv.reshape(fsdp_count, tok_count, 3, sh.width)
        .transpose(1, 2, 0, 3)
        .reshape(tok_count, 3 * D)
    )
    grad_out_w = lax.dot_general(attn_low, grad_branch, TN, preferred_element_type=F32)
    grad_qkv_w = lax.dot_general(normed_low, grad_qkv, TN, preferred_element_type=F32)
    grad_normed = lax.dot_general(grad_qkv, qkv_full, NT, preferred_element_type=F32)
    grad_input_part, grad_attn_gain = first_pull(grad_normed)
    grad_inputs = by_token(grad_middle + grad_input_part)

    def rows_of(x):
        return x.astype(BF).reshape(group_count, shard, -1)

    def small_block(parts):
        flat = jnp.concatenate([p.astype(BF).reshape(group_count, -1) for p in parts], 1)
        flat = jnp.pad(flat, ((0, 0), (0, 16 * D - flat.shape[1])))
        return flat.reshape(group_count, 16, D)

    place_table = (jnp.arange(fsdp_count) == fsdp_place).astype(F32)
    whole_table = place_table[:, None] * head_table[:, 0][None, :]
    parts = [rows_of(grad_qkv_w[:, i * D : (i + 1) * D]) for i in range(3)]
    parts.append(rows_of(grad_out_w))
    parts.append(
        small_block([grad_attn_gain, grad_moe_gain, grad_router, whole_table.reshape(-1)])
    )
    sums_dense = dense_sum(jnp.concatenate(parts, 1))
    sum_qkv = jnp.concatenate([sums_dense[i * shard : (i + 1) * shard] for i in range(3)], 1)
    sum_out = sums_dense[3 * shard : 4 * shard]
    sum_small = sums_dense[4 * shard]
    sum_attn = sum_small[marks[0] : marks[1]]
    sum_moe = sum_small[marks[1] : marks[2]]
    sum_router = sum_small[marks[2] : marks[3]].reshape(shard, expert_count)
    sum_table = sum_small[marks[3] : marks[4]]
    return (
        output,
        losses[None, :],
        grad_inputs,
        sum_qkv,
        sum_out,
        sum_attn,
        sum_moe,
        sum_router,
        sum_table,
        grad_gate[None],
        grad_up[None],
        grad_down[None],
    )


def solution(mesh):
    rows = P(("expert", "fsdp"), None)
    flat = P(("expert", "fsdp"))
    cols = P("expert", None, "fsdp")
    deep = P("expert", "fsdp", None)
    in_specs = (
        rows, rows, rows, flat, flat, rows, flat, cols, cols, deep, rows, rows, flat, P(), rows,
    )
    out_specs = (rows, rows, rows, rows, rows, flat, flat, rows, flat, cols, cols, deep)

    return jax.shard_map(local, mesh=mesh, in_specs=in_specs, out_specs=out_specs, check_vma=False)
```

```python
import functools

import jax
import jax.numpy as jnp
from jax import lax
from jax.experimental import pallas as pl
from jax.experimental.pallas import tpu as pltpu
from jax.sharding import PartitionSpec as P


D = 1024
HEADS = 16
HDIM = 64
BUCKETS = 32
TOPK = 2
PLEN = 1024
CLEN = 128
G_LINE = 2

EPSILON = 1e-06
ZLOSS_FACTOR = 0.001
BALANCE_FACTOR = 0.01
MASK_VALUE = -1e30
LOG2E = 1.4426950408889634
HIGHEST = lax.Precision.HIGHEST
TILE = 256
HALF = 128
SPAN_BLOCKS = (PLEN + CLEN) // HALF
BF = jnp.bfloat16
F32 = jnp.float32
NT = (((1,), (1,)), ((), ()))
TN = (((0,), (0,)), ((), ()))


def rms_scale(values, scale_row):
    inverse = lax.rsqrt(jnp.mean(values * values, axis=-1, keepdims=True) + EPSILON)
    return values * inverse * scale_row


def route_local(normed, router, routes):
    logits = jnp.dot(normed, router, precision=HIGHEST)
    log_total = jax.nn.logsumexp(logits, axis=-1)
    chances = jnp.exp(logits - log_total[:, None])
    expert_ids = jnp.arange(router.shape[1], dtype=jnp.int32)
    first_hot = (routes[:, 0:1] == expert_ids[None, :]).astype(F32)
    second_hot = (routes[:, 1:2] == expert_ids[None, :]).astype(F32)
    first_chance = jnp.sum(chances * first_hot, axis=-1)
    second_chance = jnp.sum(chances * second_hot, axis=-1)
    both_chances = first_chance + second_chance
    gate_pair = jnp.stack([first_chance / both_chances, second_chance / both_chances], -1)
    z_loss = jnp.mean(log_total * log_total)
    expert_share = jnp.sum(first_hot + second_hot, axis=0) / (TOPK * routes.shape[0])
    balance = router.shape[1] * jnp.sum(expert_share * jnp.mean(chances, axis=0))
    return (gate_pair, jnp.stack([z_loss, balance]))


class Shape:
    def __init__(self, fsdp_count):
        self.srcs = fsdp_count
        self.hp = HEADS // fsdp_count
        self.width = self.hp * HDIM
        self.part = PLEN // fsdp_count
        self.rows = G_LINE * self.part + CLEN
        self.spt = TILE // self.part
        self.tiles = PLEN // TILE
        self.pairs = fsdp_count // 2
        self.prompt_pairs = self.pairs // G_LINE
        self.units = G_LINE * self.tiles + self.pairs


def order_conts(sh, group_ref, perm_ref):
    counts = [jnp.int32(0), jnp.int32(sh.srcs // G_LINE)]
    for c in range(sh.srcs):
        first = group_ref[c] == 0
        perm_ref[jnp.where(first, counts[0], counts[1])] = jnp.int32(c)
        step = first.astype(jnp.int32)
        counts = [counts[0] + step, counts[1] + 1 - step]


def build_bias(sh, table_ref, bucket_ref, bias_ref):
    bucket = bucket_ref[...]
    for h in range(sh.hp):
        dist = jnp.zeros(bucket.shape, F32)
        for b in range(BUCKETS):
            dist = jnp.where(bucket == b, table_ref[h, b] * LOG2E, dist)
        bias_ref[h, 0] = jnp.full((HALF, HALF), MASK_VALUE, F32)
        before = jnp.full((1, HALF), MASK_VALUE, F32)
        for n in range(SPAN_BLOCKS):
            now = dist[n : n + 1, :]
            both = jnp.broadcast_to(jnp.concatenate([before, now], axis=1), (HALF, 2 * HALF))
            turned = pltpu.roll(both, HALF, 1, stride=1, stride_axis=0)
            bias_ref[h, 1 + n] = turned[:, :HALF]
            before = now


def head_mask(sh, h):
    if sh.hp == 1:
        return None
    lane = lax.broadcasted_iota(jnp.int32, (1, sh.width), 1)
    return (lane >= h * HDIM) & (lane < (h + 1) * HDIM)


def only_head(sh, h, x):
    mask = head_mask(sh, h)
    return x if mask is None else jnp.where(mask, x, jnp.zeros_like(x))


def prompt_rows_of(sh, ref, g, t, part):
    lanes = slice(part * sh.width, (part + 1) * sh.width)
    start = pl.multiple_of(g * sh.part, sh.part)
    return jnp.concatenate(
        [ref[t * sh.spt + s, pl.ds(start, sh.part), lanes] for s in range(sh.spt)], axis=0
    )


def cont_rows_of(sh, ref, c, part):
    lanes = slice(part * sh.width, (part + 1) * sh.width)
    return ref[c, G_LINE * sh.part :, lanes]


def put_prompt_rows(sh, ref, g, t, part, value):
    lanes = slice(part * sh.width, (part + 1) * sh.width)
    start = pl.multiple_of(g * sh.part, sh.part)
    for s in range(sh.spt):
        ref[t * sh.spt + s, pl.ds(start, sh.part), lanes] = value[
            s * sh.part : (s + 1) * sh.part
        ].astype(ref.dtype)


def transpose_low(x):
    return x.astype(F32).T.astype(BF)


def add_bias(scores, bias_ref, h, base, step_q):
    rows = []
    for a in range(2):
        cols = []
        for b in range(2):
            part = scores[a * HALF : (a + 1) * HALF, b * HALF : (b + 1) * HALF]
            cols.append(part * LOG2E + bias_ref[h, base + b * step_q - a])
        rows.append(jnp.concatenate(cols, axis=1))
    return jnp.concatenate(rows, axis=0)


def fold_max(x):
    return jnp.max(x.reshape(-1, 8, x.shape[-1]), axis=0)


def fold_sum(x):
    return jnp.sum(x.reshape(-1, 8, x.shape[-1]), axis=0)


def attn_forward_kernel(
    sh, group_ref, table_ref, bucket_ref, x_ref, o_ref, ot_ref, lse_ref, bias, vt, vtc, sc, perm
):
    order_conts(sh, group_ref, perm)
    build_bias(sh, table_ref, bucket_ref, bias)

    def make_vt(i, _):
        g, t = i // sh.tiles, lax.rem(i, sh.tiles)
        vt[i] = transpose_low(prompt_rows_of(sh, x_ref, g, t, 2))
        return 0

    lax.fori_loop(0, G_LINE * sh.tiles, make_vt, 0)

    def make_vtc(c, _):
        vtc[c] = transpose_low(cont_rows_of(sh, x_ref, c, 2))
        return 0

    lax.fori_loop(0, sh.srcs, make_vtc, 0)

    def scores_tile(keys, qh, base, step_q, kt, peaks):
        out = []
        for h in range(sh.hp):
            s = lax.dot_general(keys, qh[h], NT, preferred_element_type=F32)
            s = add_bias(s, bias, h, base, step_q)
            sc[h, pl.ds(pl.multiple_of(kt * TILE, TILE), TILE), :] = s
            out.append(jnp.maximum(peaks[h], fold_max(s)))
        return tuple(out)

    def value_tile(g, kt, peaks, carry):
        out = []
        for h in range(sh.hp):
            total, acc = carry[h]
            p = jnp.exp2(sc[h, pl.ds(pl.multiple_of(kt * TILE, TILE), TILE), :] - peaks[h])
            total = total + fold_sum(p)
            values = vt[g * sh.tiles + kt, h * HDIM : (h + 1) * HDIM, :]
            acc = acc + jnp.dot(values, p.astype(BF), preferred_element_type=F32)
            out.append((total, acc))
        return tuple(out)

    first_peaks = tuple(jnp.full((8, TILE), MASK_VALUE, F32) for _ in range(sh.hp))
    first_carry = tuple(
        (jnp.zeros((8, TILE), F32), jnp.zeros((HDIM, TILE), F32)) for _ in range(sh.hp)
    )

    def finish(unit, peaks, carry):
        outs = []
        for h in range(sh.hp):
            total = jnp.sum(carry[h][0], axis=0, keepdims=True)
            outs.append(carry[h][1] / total)
            lse_ref[unit, h : h + 1, :] = peaks[h] + jnp.log2(total)
        whole = jnp.concatenate(outs, axis=0) if sh.hp > 1 else outs[0]
        ot_ref[unit] = whole
        return whole.T

    def prompt_unit(i, _):
        g, qt = i // sh.tiles, lax.rem(i, sh.tiles)
        q = prompt_rows_of(sh, x_ref, g, qt, 0) * BF(HDIM**-0.5)
        qh = [only_head(sh, h, q) for h in range(sh.hp)]

        def first(kt, peaks):
            keys = prompt_rows_of(sh, x_ref, g, kt, 1)
            return scores_tile(keys, qh, 2 * (qt - kt) + 1, 1, kt, peaks)

        peaks = lax.fori_loop(0, qt + 1, first, first_peaks)
        peaks = [jnp.max(p, axis=0, keepdims=True) for p in peaks]
        carry = lax.fori_loop(0, qt + 1, lambda kt, c: value_tile(g, kt, peaks, c), first_carry)
        put_prompt_rows(sh, o_ref, g, qt, 0, finish(i, peaks, carry))
        return 0

    lax.fori_loop(0, G_LINE * sh.tiles, prompt_unit, 0)

    def cont_unit(i, _):
        conts = [perm[2 * i], perm[2 * i + 1]]
        g = i // sh.prompt_pairs
        q = jnp.concatenate([cont_rows_of(sh, x_ref, c, 0) for c in conts], axis=0)
        q = q * BF(HDIM**-0.5)
        qh = [only_head(sh, h, q) for h in range(sh.hp)]

        def first(kt, peaks):
            keys = prompt_rows_of(sh, x_ref, g, kt, 1)
            return scores_tile(keys, qh, SPAN_BLOCKS - 2 * kt, 0, kt, peaks)

        peaks = lax.fori_loop(0, sh.tiles, first, first_peaks)
        own = []
        next_peaks = []
        for h in range(sh.hp):
            parts = []
            for b in range(2):
                keys = cont_rows_of(sh, x_ref, conts[b], 1)
                s = lax.dot_general(
                    keys, qh[h][b * HALF : (b + 1) * HALF], NT, preferred_element_type=F32
                )
                parts.append(s * LOG2E + bias[h, 1])
            own.append(jnp.concatenate(parts, axis=1))
            next_peaks.append(jnp.maximum(peaks[h], fold_max(own[h])))
        peaks = [jnp.max(p, axis=0, keepdims=True) for p in next_peaks]
        start = []
        for h in range(sh.hp):
            p = jnp.exp2(own[h] - peaks[h])
            low = p.astype(BF)
            acc = jnp.concatenate(
                [
                    jnp.dot(
                        vtc[conts[b], h * HDIM : (h + 1) * HDIM, :],
                        low[:, b * HALF : (b + 1) * HALF],
                        preferred_element_type=F32,
                    )
                    for b in range(2)
                ],
                axis=1,
            )
            start.append((fold_sum(p), acc))
        carry = lax.fori_loop(
            0, sh.tiles, lambda kt, c: value_tile(g, kt, peaks, c), tuple(start)
        )
        done = finish(G_LINE * sh.tiles + i, peaks, carry)
        for b in range(2):
            o_ref[conts[b], G_LINE * sh.part :, :] = done[b * HALF : (b + 1) * HALF].astype(BF)
        return 0

    lax.fori_loop(0, sh.pairs, cont_unit, 0)


def attn_backward_kernel(
    sh,
    group_ref,
    table_ref,
    bucket_ref,
    x_ref,
    do_ref,
    ot_ref,
    lse_ref,
    dx_ref,
    dtable_ref,
    bias,
    dbias,
    ktr,
    ktc,
    dk,
    dv,
    perm,
):
    order_conts(sh, group_ref, perm)
    build_bias(sh, table_ref, bucket_ref, bias)
    dbias[...] = jnp.zeros_like(dbias)
    dk[...] = jnp.zeros_like(dk)
    dv[...] = jnp.zeros_like(dv)

    def make_kt(i, _):
        g, t = i // sh.tiles, lax.rem(i, sh.tiles)
        ktr[i] = transpose_low(prompt_rows_of(sh, x_ref, g, t, 1))
        return 0

    lax.fori_loop(0, G_LINE * sh.tiles, make_kt, 0)

    def make_ktc(c, _):
        ktc[c] = transpose_low(cont_rows_of(sh, x_ref, c, 1))
        return 0

    lax.fori_loop(0, sh.srcs, make_ktc, 0)

    def inner_terms(unit, do):
        outs = []
        turned = do.astype(F32).T
        for h in range(sh.hp):
            rows = slice(h * HDIM, (h + 1) * HDIM)
            prod = ot_ref[unit, rows, :] * turned[rows, :]
            outs.append(jnp.sum(prod, axis=0, keepdims=True))
        return outs

    def grads_tile(g, kt, qh, doh, lse, inner, base, step_q, dqs):
        keys = prompt_rows_of(sh, x_ref, g, kt, 1)
        values = prompt_rows_of(sh, x_ref, g, kt, 2)
        slot = g * sh.tiles + kt
        out = []
        dkey = dvalue = None
        for h in range(sh.hp):
            s = lax.dot_general(keys, qh[h], NT, preferred_element_type=F32)
            dp = lax.dot_general(values, doh[h], NT, preferred_element_type=F32)
            p = jnp.exp2(add_bias(s, bias, h, base, step_q) - lse[h])
            ds = p * (dp - inner[h])
            for a in range(2):
                for b in range(2):
                    dbias[h, base + b * step_q - a] += ds[
                        a * HALF : (a + 1) * HALF, b * HALF : (b + 1) * HALF
                    ]
            low = ds.astype(BF)
            more_k = jnp.dot(low, qh[h], preferred_element_type=F32)
            more_v = jnp.dot(p.astype(BF), doh[h], preferred_element_type=F32)
            dkey = more_k if dkey is None else dkey + more_k
            dvalue = more_v if dvalue is None else dvalue + more_v
            turned = ktr[slot, h * HDIM : (h + 1) * HDIM, :]
            out.append(dqs[h] + jnp.dot(turned, low, preferred_element_type=F32))
        dk[slot] += dkey
        dv[slot] += dvalue
        return tuple(out)

    def finish(dqs):
        whole = jnp.concatenate(dqs, axis=0) if sh.hp > 1 else dqs[0]
        return whole.T * (HDIM**-0.5)

    first_dq = tuple(jnp.zeros((HDIM, TILE), F32) for _ in range(sh.hp))

    def prompt_unit(i, _):
        g, qt = i // sh.tiles, lax.rem(i, sh.tiles)
        q = prompt_rows_of(sh, x_ref, g, qt, 0) * BF(HDIM**-0.5)
        do = prompt_rows_of(sh, do_ref, g, qt, 0)
        qh = [only_head(sh, h, q) for h in range(sh.hp)]
        doh = [only_head(sh, h, do) for h in range(sh.hp)]
        inner = inner_terms(i, do)
        lse = [lse_ref[i, h : h + 1, :] for h in range(sh.hp)]

        def body(kt, dqs):
            return grads_tile(g, kt, qh, doh, lse, inner, 2 * (qt - kt) + 1, 1, dqs)

        dqs = lax.fori_loop(0, qt + 1, body, first_dq)
        put_prompt_rows(sh, dx_ref, g, qt, 0, finish(dqs))
        return 0

    lax.fori_loop(0, G_LINE * sh.tiles, prompt_unit, 0)

    def cont_unit(i, _):
        conts = [perm[2 * i], perm[2 * i + 1]]
        unit = G_LINE * sh.tiles + i
        g = i // sh.prompt_pairs
        q = jnp.concatenate([cont_rows_of(sh, x_ref, c, 0) for c in conts], axis=0)
        q = q * BF(HDIM**-0.5)
        do = jnp.concatenate([cont_rows_of(sh, do_ref, c, 0) for c in conts], axis=0)
        qh = [only_head(sh, h, q) for h in range(sh.hp)]
        doh = [only_head(sh, h, do) for h in range(sh.hp)]
        inner = inner_terms(unit, do)
        lse = [lse_ref[unit, h : h + 1, :] for h in range(sh.hp)]

        def body(kt, dqs):
            return grads_tile(g, kt, qh, doh, lse, inner, SPAN_BLOCKS - 2 * kt, 0, dqs)

        dqs = lax.fori_loop(0, sh.tiles, body, first_dq)
        more = [[None] * 2 for _ in range(sh.hp)]
        for b in range(2):
            cols = slice(b * HALF, (b + 1) * HALF)
            keys = cont_rows_of(sh, x_ref, conts[b], 1)
            values = cont_rows_of(sh, x_ref, conts[b], 2)
            dkey = dvalue = None
            for h in range(sh.hp):
                s = lax.dot_general(keys, qh[h][cols], NT, preferred_element_type=F32)
                dp = lax.dot_general(values, doh[h][cols], NT, preferred_element_type=F32)
                p = jnp.exp2(s * LOG2E + bias[h, 1] - lse[h][:, cols])
                ds = p * (dp - inner[h][:, cols])
                dbias[h, 1] += ds
                low = ds.astype(BF)
                more_k = jnp.dot(low, qh[h][cols], preferred_element_type=F32)
                more_v = jnp.dot(p.astype(BF), doh[h][cols], preferred_element_type=F32)
                dkey = more_k if dkey is None else dkey + more_k
                dvalue = more_v if dvalue is None else dvalue + more_v
                turned = ktc[conts[b], h * HDIM : (h + 1) * HDIM, :]
                more[h][b] = jnp.dot(turned, low, preferred_element_type=F32)
            w = sh.width
            dx_ref[conts[b], G_LINE * sh.part :, w : 2 * w] = dkey.astype(BF)
            dx_ref[conts[b], G_LINE * sh.part :, 2 * w :] = dvalue.astype(BF)
        dqs = [dqs[h] + jnp.concatenate(more[h], axis=1) for h in range(sh.hp)]
        done = finish(dqs)
        for b in range(2):
            dx_ref[conts[b], G_LINE * sh.part :, : sh.width] = done[
                b * HALF : (b + 1) * HALF
            ].astype(BF)
        return 0

    lax.fori_loop(0, sh.pairs, cont_unit, 0)

    def put_keys(i, _):
        g, t = i // sh.tiles, lax.rem(i, sh.tiles)
        put_prompt_rows(sh, dx_ref, g, t, 1, dk[i])
        put_prompt_rows(sh, dx_ref, g, t, 2, dv[i])
        return 0

    lax.fori_loop(0, G_LINE * sh.tiles, put_keys, 0)

    bucket = bucket_ref[...]
    key_row = lax.broadcasted_iota(jnp.int32, (HALF, 2 * HALF), 0)
    for h in range(sh.hp):
        spread = []
        for n in range(SPAN_BLOCKS):
            wide = jnp.concatenate(
                [jnp.zeros((HALF, HALF), F32), dbias[h, 1 + n]], axis=1
            )
            for bit in range(7):
                moved = pltpu.roll(wide, 2 * HALF - (1 << bit), 1)
                wide = jnp.where((key_row & (1 << bit)) != 0, moved, wide)
            spread.append(jnp.sum(wide, axis=0, keepdims=True))
        rows = []
        for n in range(SPAN_BLOCKS):
            row = spread[n][:, HALF:]
            if n + 1 < SPAN_BLOCKS:
                row = row + spread[n + 1][:, :HALF]
            rows.append(row)
        by_dist = jnp.concatenate(rows, axis=0)
        sums = [
            jnp.sum(jnp.where(bucket == b, by_dist, 0.0), axis=0, keepdims=True)
            for b in range(BUCKETS)
        ]
        lanes = jnp.concatenate(sums, axis=0)
        dtable_ref[h * BUCKETS : (h + 1) * BUCKETS, :] = jnp.broadcast_to(
            jnp.sum(lanes, axis=1, keepdims=True), (BUCKETS, HALF)
        )


SMEM_SPEC = pl.BlockSpec(memory_space=pltpu.SMEM)
VMEM_SPEC = pl.BlockSpec(memory_space=pltpu.VMEM)
GRANT = 48 * 1024 * 1024


def attend_forward(sh, group, table, bucket, x):
    return pl.pallas_call(
        functools.partial(attn_forward_kernel, sh),
        out_shape=(
            jax.ShapeDtypeStruct((sh.srcs, sh.rows, sh.width), BF),
            jax.ShapeDtypeStruct((sh.units, sh.width, TILE), F32),
            jax.ShapeDtypeStruct((sh.units, 8, TILE), F32),
        ),
        in_specs=[SMEM_SPEC, SMEM_SPEC, VMEM_SPEC, VMEM_SPEC],
        out_specs=(VMEM_SPEC, VMEM_SPEC, VMEM_SPEC),
        scratch_shapes=[
            pltpu.VMEM((sh.hp, SPAN_BLOCKS + 1, HALF, HALF), F32),
            pltpu.VMEM((G_LINE * sh.tiles, sh.width, TILE), BF),
            pltpu.VMEM((sh.srcs, sh.width, HALF), BF),
            pltpu.VMEM((sh.hp, PLEN, TILE), F32),
            pltpu.SMEM((sh.srcs,), jnp.int32),
        ],
        compiler_params=pltpu.CompilerParams(vmem_limit_bytes=GRANT),
        cost_estimate=pl.CostEstimate(
            flops=10**10, bytes_accessed=8 * 10**6, transcendentals=5 * 10**6
        ),
        name="attend_forward",
    )(group, table, bucket, x)


def attend_backward(sh, group, table, bucket, x, do, ot, lse):
    return pl.pallas_call(
        functools.partial(attn_backward_kernel, sh),
        out_shape=(
            jax.ShapeDtypeStruct((sh.srcs, sh.rows, 3 * sh.width), BF),
            jax.ShapeDtypeStruct((sh.hp * BUCKETS, HALF), F32),
        ),
        in_specs=[SMEM_SPEC, SMEM_SPEC, VMEM_SPEC, VMEM_SPEC, VMEM_SPEC, VMEM_SPEC, VMEM_SPEC],
        out_specs=(VMEM_SPEC, VMEM_SPEC),
        scratch_shapes=[
            pltpu.VMEM((sh.hp, SPAN_BLOCKS + 1, HALF, HALF), F32),
            pltpu.VMEM((sh.hp, SPAN_BLOCKS + 1, HALF, HALF), F32),
            pltpu.VMEM((G_LINE * sh.tiles, sh.width, TILE), BF),
            pltpu.VMEM((sh.srcs, sh.width, HALF), BF),
            pltpu.VMEM((G_LINE * sh.tiles, TILE, sh.width), F32),
            pltpu.VMEM((G_LINE * sh.tiles, TILE, sh.width), F32),
            pltpu.SMEM((sh.srcs,), jnp.int32),
        ],
        compiler_params=pltpu.CompilerParams(vmem_limit_bytes=GRANT),
        cost_estimate=pl.CostEstimate(
            flops=2 * 10**10, bytes_accessed=12 * 10**6, transcendentals=5 * 10**6
        ),
        name="attend_backward",
    )(group, table, bucket, x, do, ot, lse)


def ring_order(count):
    deep, wide = 4, count // 4
    order = [a * wide for a in range(deep)]
    for turn, a in enumerate(reversed(range(deep))):
        row = [a * wide + b for b in range(1, wide)]
        order += row if turn % 2 == 0 else row[::-1]
    return order


def ring_hop(x, count, step):
    ring = ring_order(count)
    return lax.ppermute(x, "fsdp", [(ring[i], ring[(i + step) % count]) for i in range(count)])


def tied(*values):
    return lax.optimization_barrier(values)


class RingGather:
    def __init__(self, own, count):
        self.count = count
        self.chunks = [None] * count
        self.chunks[0] = own
        self.right = self.left = own
        self.done = 0
        self.steps = count // 2

    def step(self):
        self.done += 1
        s = self.done
        if s < self.steps:
            self.right = ring_hop(self.right, self.count, 1)
            self.left = ring_hop(self.left, self.count, -1)
        else:
            half = self.right.shape[0] // 2
            self.right = ring_hop(self.right[:half], self.count, 1)
            self.left = ring_hop(self.left[half:], self.count, -1)
        self.keep()

    def keep(self):
        s = self.done
        if s < self.steps:
            self.chunks[self.count - s] = self.right
            self.chunks[s] = self.left
        else:
            self.chunks[s] = (self.right, self.left)

    def tie(self, value):
        value, self.right, self.left = tied(value, self.right, self.left)
        self.keep()
        return value


class RingScatter:
    def __init__(self, part, count):
        self.part, self.count = part, count
        self.right = self.left = None
        self.done = 0
        self.steps = count // 2

    def step(self, after=None):
        count, s = self.count, self.done
        away = self.steps - s
        if s == 0:
            send_left, send_right = self.part(away)
        else:
            near_left = self.part(count - away).astype(F32)
            near_right = self.part(away).astype(F32)
            if s == 1:
                half = near_left.shape[0] // 2
                send_left = jnp.concatenate(
                    [near_left[:half] + self.left.astype(F32), near_left[half:]], 0
                )
                send_right = jnp.concatenate(
                    [near_right[:half], near_right[half:] + self.right.astype(F32)], 0
                )
            else:
                send_left = near_left + self.left.astype(F32)
                send_right = near_right + self.right.astype(F32)
        send_left, send_right = send_left.astype(BF), send_right.astype(BF)
        if after is not None:
            after, send_left, send_right = tied(after, send_left, send_right)
        self.left = ring_hop(send_left, count, -1)
        self.right = ring_hop(send_right, count, 1)
        self.done += 1
        return after

    def tie(self, value):
        value, self.right, self.left = tied(value, self.right, self.left)
        return value

    def finish(self):
        return self.part(0).astype(F32) + self.right.astype(F32) + self.left.astype(F32)


MESH_ID = pl.DeviceIdType.MESH
DEEP = 4


class Spot:
    def __init__(self):
        e, f = lax.axis_index("expert"), lax.axis_index("fsdp")
        self.x, self.c = e // 2, lax.rem(e, 2)
        self.z, self.y = f // 2, lax.rem(f, 2)
        self.ox, self.oy, self.oc = 1 - self.x, 1 - self.y, 1 - self.c

    def place(self, x=None, y=None, z=None, c=None):
        x = self.x if x is None else x
        y = self.y if y is None else y
        z = self.z if z is None else z
        c = self.c if c is None else c
        return {"expert": x * 2 + c, "fsdp": z * 2 + y}

    def block(self, x, y, z, c):
        return (x * 2 + c) * 8 + z * 2 + y

    def greet(self):
        barrier = pltpu.get_barrier_semaphore()
        for target in (self.place(x=self.ox), self.place(y=self.oy), self.place(c=self.oc)):
            pl.semaphore_signal(barrier, inc=1, device_id=target, device_id_type=MESH_ID)
        for step in (-1, 1):

            @pl.when(self.inside(self.z + step))
            def _(step=step):
                pl.semaphore_signal(
                    barrier, inc=1, device_id=self.along(step), device_id_type=MESH_ID
                )

        pl.semaphore_wait(barrier, 4 + self.z * (DEEP - 1 - self.z) // 2)

    def wrap(self, step):
        return lax.rem(self.z + step + DEEP, DEEP)

    def along(self, step):
        return self.place(z=self.wrap(step))

    def inside(self, z):
        return (z >= 0) & (z < DEEP)


def dense_gather_kernel(cut, x_ref, out_ref, send_sems, recv_sems, own_sem):
    me = Spot()
    rows = x_ref.shape[0]
    spans = [(0, cut), (cut, rows - cut)]
    pending = []

    def view(ref, h):
        return ref.at[pl.ds(*spans[h])]

    def send(src, blk, h, target, cond):
        copy = pltpu.make_async_remote_copy(
            src_ref=src,
            dst_ref=view(out_ref.at[blk], h),
            send_sem=send_sems.at[len(pending)],
            recv_sem=recv_sems.at[blk, h],
            device_id=target,
            device_id_type=MESH_ID,
        )
        pending.append((copy, cond))
        if cond is None:
            copy.start()
        else:
            pl.when(cond)(copy.start)

    def arrive(blk, h, cond):
        copy = pltpu.make_async_remote_copy(
            src_ref=view(out_ref.at[blk], h),
            dst_ref=view(out_ref.at[blk], h),
            send_sem=send_sems.at[0],
            recv_sem=recv_sems.at[blk, h],
            device_id=me.place(c=me.oc),
            device_id_type=MESH_ID,
        )
        if cond is None:
            copy.wait_recv()
        else:
            pl.when(cond)(copy.wait_recv)

    def both(a, b):
        return b if a is None else (a if b is None else a & b)

    by_y, by_x = me.place(y=me.oy), me.place(x=me.ox)
    core = me.place(c=me.oc)
    me.greet()
    mine = me.block(me.x, me.y, me.z, me.c)
    own = pltpu.make_async_copy(x_ref, out_ref.at[mine], own_sem)
    own.start()
    for h in range(2):
        for step in (-1, 1):
            send(view(x_ref, h), mine, h, me.along(step), me.inside(me.z + step))
    for h in range(2):
        for target in (by_y, by_x, core):
            send(view(x_ref, h), mine, h, target, None)

    def line(dist):
        if dist == 0:
            return [(me.z, None, 0)]
        return [(me.wrap(s * dist), me.inside(me.z + s * dist), s) for s in (-1, 1)]

    def from_line(dist):
        for zb, cond, sign in line(dist):
            blk = me.block(me.x, me.y, zb, me.c)
            for h in range(2):
                arrive(blk, h, cond)
                src = view(out_ref.at[blk], h)
                send(src, blk, h, me.along(-sign), both(cond, me.inside(me.z - sign)))
                for target in (by_y, by_x, core):
                    send(src, blk, h, target, cond)

    def from_side(dist):
        for zb, cond, _ in line(dist):
            for h in range(2):
                one = me.block(me.x, me.oy, zb, me.c)
                two = me.block(me.ox, me.y, zb, me.c)
                onward, last = ((one, by_x), two) if h == 0 else ((two, by_y), one)
                arrive(onward[0], h, cond)
                src = view(out_ref.at[onward[0]], h)
                send(src, onward[0], h, onward[1], cond)
                send(src, onward[0], h, core, cond)
                arrive(last, h, cond)
                send(view(out_ref.at[last], h), last, h, core, cond)

    def from_corner(dist):
        for zb, cond, _ in line(dist):
            blk = me.block(me.ox, me.oy, zb, me.c)
            for h in range(2):
                arrive(blk, h, cond)
                send(view(out_ref.at[blk], h), blk, h, core, cond)

    for dist in range(DEEP):
        if dist > 0:
            from_line(dist)
        from_side(dist)
        if dist > 0:
            from_corner(dist - 1)
    from_corner(DEEP - 1)
    for x in range(2):
        for y in range(2):
            for z in range(DEEP):
                for h in range(2):
                    arrive(me.block(x, y, z, me.oc), h, None)
    own.wait()
    for copy, cond in pending:
        if cond is None:
            copy.wait_send()
        else:
            pl.when(cond)(copy.wait_send)


def dense_gather(x, count):
    rows = x.shape[0]
    if count != 32 or lax.axis_size("fsdp") != 2 * DEEP:
        return lax.all_gather(x, ("expert", "fsdp"), axis=0, tiled=False)
    cut = rows // 32 * 16 + 16 * (rows // 16 % 2)
    return pl.pallas_call(
        functools.partial(dense_gather_kernel, cut),
        out_shape=jax.ShapeDtypeStruct((count,) + x.shape, x.dtype),
        in_specs=[pl.BlockSpec(memory_space=pltpu.VMEM)],
        out_specs=pl.BlockSpec(memory_space=pl.ANY),
        scratch_shapes=[
            pltpu.SemaphoreType.DMA((128,)),
            pltpu.SemaphoreType.DMA((count, 2)),
            pltpu.SemaphoreType.DMA,
        ],
        compiler_params=pltpu.CompilerParams(collective_id=0, has_side_effects=True),
        cost_estimate=pl.CostEstimate(
            flops=0, bytes_accessed=100 * 10**6, transcendentals=0
        ),
        name="dense_gather",
    )(x)


def add_into(dst, src):
    def body(i, _):
        at = pl.ds(pl.multiple_of(i * 16, 16), 16)
        dst[at, :] = (dst[at, :].astype(F32) + src[at, :].astype(F32)).astype(BF)
        return 0

    lax.fori_loop(0, dst.shape[0] // 16, body, 0)


def dense_sum_kernel(
    cut, g_ref, out_ref, acc, cbuf, xbuf, ybuf, zbuf, send_sems, recv_sems, load_sems
):
    me = Spot()
    rows = out_ref.shape[0]
    top, low = pl.ds(0, cut), pl.ds(cut, rows - cut)
    pending = []

    def send(src, dst, at, target, cond=None):
        copy = pltpu.make_async_remote_copy(
            src_ref=src,
            dst_ref=dst,
            send_sem=send_sems.at[len(pending)],
            recv_sem=recv_sems.at[at],
            device_id=target,
            device_id_type=MESH_ID,
        )
        pending.append((copy, cond))
        if cond is None:
            copy.start()
        else:
            pl.when(cond)(copy.start)

    def arrive(dst, at):
        pltpu.make_async_remote_copy(
            src_ref=dst,
            dst_ref=dst,
            send_sem=send_sems.at[0],
            recv_sem=recv_sems.at[at],
            device_id=me.place(c=me.oc),
            device_id_type=MESH_ID,
        ).wait_recv()

    by_y, by_x, core = me.place(y=me.oy), me.place(x=me.ox), me.place(c=me.oc)
    me.greet()
    zs = (0, 3, 2, 1)
    loads = []
    for k in range(DEEP):
        for x in range(2):
            at = x * DEEP + k
            theirs = (x * 2 + me.oc) * 8 + zs[k] * 2
            send(g_ref.at[pl.ds(theirs, 2)], cbuf.at[at], at, core)
            ours = (x * 2 + me.c) * 8 + zs[k] * 2
            load = pltpu.make_async_copy(g_ref.at[pl.ds(ours, 2)], acc.at[at], load_sems.at[at])
            load.start()
            loads.append(load)

    def first(k):
        for x in range(2):
            at = x * DEEP + k
            loads[k * 2 + x].wait()
            arrive(cbuf.at[at], at)
            for y in range(2):
                add_into(acc.at[at, y], cbuf.at[at, y])
        base = 8 + k * 6
        for y in range(2):
            send(acc.at[me.ox * DEEP + k, y, top], xbuf.at[k, y, top], base + y, by_x)
        for x in range(2):
            send(acc.at[x * DEEP + k, me.oy, low], ybuf.at[k, x, low], base + 2 + x, by_y)

    def second(k):
        base = 8 + k * 6
        for y in range(2):
            arrive(xbuf.at[k, y, top], base + y)
            add_into(acc.at[me.x * DEEP + k, y, top], xbuf.at[k, y, top])
        for x in range(2):
            arrive(ybuf.at[k, x, low], base + 2 + x)
            add_into(acc.at[x * DEEP + k, me.y, low], ybuf.at[k, x, low])
        send(acc.at[me.x * DEEP + k, me.oy, top], ybuf.at[k, 0, top], base + 4, by_y)
        send(acc.at[me.ox * DEEP + k, me.y, low], xbuf.at[k, 0, low], base + 5, by_x)

    def third(k):
        base = 8 + k * 6
        block = acc.at[me.x * DEEP + k, me.y]
        arrive(ybuf.at[k, 0, top], base + 4)
        add_into(block.at[top], ybuf.at[k, 0, top])
        arrive(xbuf.at[k, 0, low], base + 5)
        add_into(block.at[low], xbuf.at[k, 0, low])

    def along(k, sign, behind):
        zo = zs[k]
        here = behind if sign > 0 else DEEP - 1 - behind
        term = acc.at[me.x * DEEP + k, me.y]
        base = 32 + k * 4 + (sign + 1)
        side = k * 4 + (sign + 1)
        is_here = me.z == here
        for h, at in ((0, top), (1, low)):
            if behind > 0:

                @pl.when(is_here)
                def _(h=h, at=at):
                    arrive(zbuf.at[side + h, at], base + h)
                    add_into(term.at[at], zbuf.at[side + h, at])

            if here != zo:
                send(
                    term.at[at], zbuf.at[side + h, at], base + h, me.along(sign), is_here
                )

    for step in range(DEEP + 6):
        if step < DEEP:
            first(step)
        if 0 <= step - 1 < DEEP:
            second(step - 1)
        if 0 <= step - 2 < DEEP:
            third(step - 2)
        for k in range(DEEP):
            behind = step - 2 - k
            if behind >= 0:
                if behind <= zs[k]:
                    along(k, 1, behind)
                if behind <= DEEP - 1 - zs[k]:
                    along(k, -1, behind)
    block = acc.at[me.x * DEEP + lax.rem(DEEP - me.z, DEEP), me.y]

    def put(i, _):
        at = pl.ds(pl.multiple_of(i * 16, 16), 16)
        out_ref[at, :] = block[at, :].astype(F32)
        return 0

    lax.fori_loop(0, rows // 16, put, 0)
    for copy, cond in pending:
        if cond is None:
            copy.wait_send()
        else:
            pl.when(cond)(copy.wait_send)


def dense_sum(x):
    count, rows, width = x.shape
    if count != 32 or lax.axis_size("fsdp") != 2 * DEEP:
        flat = x.reshape(count * rows, width)
        return lax.psum_scatter(
            flat, ("expert", "fsdp"), scatter_dimension=0, tiled=True
        ).astype(F32)
    cut = rows // 32 * 16 + 16 * (rows // 16 % 2)
    pair = (2 * DEEP, 2, rows, width)
    return pl.pallas_call(
        functools.partial(dense_sum_kernel, cut),
        out_shape=jax.ShapeDtypeStruct((rows, width), F32),
        in_specs=[pl.BlockSpec(memory_space=pl.ANY)],
        out_specs=pl.BlockSpec(memory_space=pltpu.VMEM),
        scratch_shapes=[
            pltpu.VMEM(pair, BF),
            pltpu.VMEM(pair, BF),
            pltpu.VMEM((DEEP, 2, rows, width), BF),
            pltpu.VMEM((DEEP, 2, rows, width), BF),
            pltpu.VMEM((4 * DEEP, rows, width), BF),
            pltpu.SemaphoreType.DMA((72,)),
            pltpu.SemaphoreType.DMA((48,)),
            pltpu.SemaphoreType.DMA((8,)),
        ],
        compiler_params=pltpu.CompilerParams(
            collective_id=1, has_side_effects=True, vmem_limit_bytes=40 * 1024 * 1024
        ),
        cost_estimate=pl.CostEstimate(
            flops=0, bytes_accessed=100 * 10**6, transcendentals=0
        ),
        name="dense_sum",
    )(x)


SLICE = 256


def gelu_terms(x):
    root = 0.7978845608028654
    square = x * x
    t = jnp.tanh(root * (x + 0.044715 * square * x))
    half = 0.5 * (1.0 + t)
    slope = half + 0.5 * x * (1.0 - t * t) * (root * (1.0 + 3 * 0.044715 * square))
    return x * half, slope


def block_order(count):
    far = count // 2
    order = [far]
    for away in range(1, far + 1):
        order += [k for k in (far - away, far + away) if k < count]
    return order


def chunk_pieces(base, split, ff_shard):
    if not split:
        return [(0, m * ff_shard, m, base, ff_shard) for m in range(3)]
    half = ff_shard // 2
    return [
        (0, 0, 0, base, ff_shard),
        (0, ff_shard, 1, base, half),
        (1, 0, 1, base + half, half),
        (1, half, 2, base, ff_shard),
    ]


def chunk_copies(refs, whole, sems, ff_shard, outward, start=0):
    out = []
    for p, own in enumerate(refs):
        pieces = []
        places = chunk_pieces(p * ff_shard + start, len(own) == 2, ff_shard)
        for n, (src, at, m, row, rows) in enumerate(places):
            block = own[src].at[pl.ds(at, rows)]
            spot = whole.at[m, pl.ds(row, rows)]
            a, b = (spot, block) if outward else (block, spot)
            pieces.append(pltpu.make_async_copy(a, b, sems.at[p, n]))
        out.append(pieces)
    return out


def pair_first(refs):
    return [refs[:2]] + [refs[k : k + 1] for k in range(2, len(refs))]


def fetch_weights(refs, whole, sems, ff_shard, t):
    copies = chunk_copies(pair_first(refs), whole, sems, ff_shard, False)
    ahead = 3

    @pl.when(t == 0)
    def _():
        for pieces in copies[:ahead]:
            for c in pieces:
                c.start()

    for p, pieces in enumerate(copies):
        more = copies[p + ahead] if p + ahead < len(copies) else []

        @pl.when(t == p * ff_shard // SLICE)
        def _(pieces=pieces, more=more):
            for c in more:
                c.start()
            for c in pieces:
                c.wait()


def ffn_forward_kernel(count, ff_shard, rows_ref, *refs):
    chunks, rest = refs[: count + 1], refs[count + 1 :]
    out_ref, act_ref, turn_ref, hid_ref, whole, acc, sems = rest
    t = pl.program_id(0)
    fetch_weights(chunks, whole, sems, ff_shard, t)
    at = pl.ds(pl.multiple_of(t * SLICE, SLICE), SLICE)
    rows = rows_ref[...]
    gate = lax.dot_general(rows, whole[0, at], NT, preferred_element_type=F32)
    up = lax.dot_general(rows, whole[1, at], NT, preferred_element_type=F32)
    act, slope = gelu_terms(gate)
    hidden = (act * up).astype(BF)
    act_ref[0] = act
    turn_ref[0] = up * slope
    hid_ref[0] = hidden
    more = jnp.dot(hidden, whole[2, at], preferred_element_type=F32)

    @pl.when(t == 0)
    def _():
        acc[...] = more

    @pl.when(t > 0)
    def _():
        acc[...] += more

    @pl.when(t == pl.num_programs(0) - 1)
    def _():
        out_ref[...] = acc[...].astype(BF)


def ffn_backward_kernel(count, ff_shard, grad_ref, act_ref, turn_ref, *refs):
    chunks, rest = refs[: count + 1], refs[count + 1 :]
    out_ref, dgate_ref, dup_ref, whole, acc, sems = rest
    t = pl.program_id(0)
    fetch_weights(chunks, whole, sems, ff_shard, t)
    at = pl.ds(pl.multiple_of(t * SLICE, SLICE), SLICE)
    dhid = lax.dot_general(grad_ref[...], whole[2, at], NT, preferred_element_type=F32)
    dgate = (dhid * turn_ref[0]).astype(BF)
    dup = (dhid * act_ref[0]).astype(BF)
    dgate_ref[0] = dgate
    dup_ref[0] = dup
    more = jnp.dot(
        jnp.concatenate([dgate, dup], axis=1),
        jnp.concatenate([whole[0, at], whole[1, at]], axis=0),
        preferred_element_type=F32,
    )

    @pl.when(t == 0)
    def _():
        acc[...] = more

    @pl.when(t > 0)
    def _():
        acc[...] += more

    @pl.when(t == pl.num_programs(0) - 1)
    def _():
        out_ref[...] = acc[...].astype(BF)


def ffn_weights_kernel(
    lead, first, ff_shard, rows_ref, grad_ref, hid_ref, dgate_ref, dup_ref, *refs
):
    chunks, (whole, sems) = refs[:-2], refs[-2:]
    chunks = pair_first(chunks) if lead else [chunks[k : k + 1] for k in range(len(chunks))]
    base = first * ff_shard // SLICE
    t = pl.program_id(0)
    at = pl.ds(pl.multiple_of(t * SLICE, SLICE), SLICE)
    for m, (left, right) in enumerate(
        ((dgate_ref, rows_ref), (dup_ref, rows_ref), (hid_ref, grad_ref))
    ):
        whole[m, at] = lax.dot_general(
            left[0], right[...], TN, preferred_element_type=F32
        ).astype(BF)
    copies = chunk_copies(
        chunks, whole, sems, ff_shard, True, first * ff_shard - base * SLICE
    )
    for p, pieces in enumerate(copies):

        @pl.when(t == ((first + p + 1) * ff_shard - 1) // SLICE - base)
        def _(pieces=pieces):
            for c in pieces:
                c.start()

    @pl.when(t == pl.num_programs(0) - 1)
    def _():
        for pieces in copies:
            for c in pieces:
                c.wait()


def fixed(shape):
    return pl.BlockSpec(shape, lambda t: (0,) * len(shape))


def stepped(shape):
    return pl.BlockSpec(shape, lambda t: (t, 0, 0))


ANY_SPEC = pl.BlockSpec(memory_space=pl.ANY)


def ffn_cost(slots, hidden):
    work = 6 * slots * D * hidden
    return pl.CostEstimate(flops=work, bytes_accessed=40 * 10**6, transcendentals=slots * hidden)


def ffn_params():
    return pltpu.CompilerParams(
        dimension_semantics=("arbitrary",), vmem_limit_bytes=60 * 1024 * 1024
    )


def ffn_forward(rows, chunks, ff_shard):
    slots, count = rows.shape[0], len(chunks) - 1
    hidden = count * ff_shard
    steps = hidden // SLICE
    return pl.pallas_call(
        functools.partial(ffn_forward_kernel, count, ff_shard),
        grid=(steps,),
        out_shape=(
            jax.ShapeDtypeStruct((slots, D), BF),
            jax.ShapeDtypeStruct((steps, slots, SLICE), F32),
            jax.ShapeDtypeStruct((steps, slots, SLICE), F32),
            jax.ShapeDtypeStruct((steps, slots, SLICE), BF),
        ),
        in_specs=[fixed((slots, D))] + [ANY_SPEC] * (count + 1),
        out_specs=(
            fixed((slots, D)),
            stepped((1, slots, SLICE)),
            stepped((1, slots, SLICE)),
            stepped((1, slots, SLICE)),
        ),
        scratch_shapes=[
            pltpu.VMEM((3, hidden, D), BF),
            pltpu.VMEM((slots, D), F32),
            pltpu.SemaphoreType.DMA((count, 4)),
        ],
        compiler_params=ffn_params(),
        cost_estimate=ffn_cost(slots, hidden),
        name="ffn_forward",
    )(rows, *chunks)


def ffn_backward(grad, act, turn, chunks, ff_shard):
    slots, count = grad.shape[0], len(chunks) - 1
    hidden = count * ff_shard
    steps = hidden // SLICE
    tile = jax.ShapeDtypeStruct((steps, slots, SLICE), BF)
    return pl.pallas_call(
        functools.partial(ffn_backward_kernel, count, ff_shard),
        grid=(steps,),
        out_shape=(jax.ShapeDtypeStruct((slots, D), BF), tile, tile),
        in_specs=[fixed((slots, D))]
        + [stepped((1, slots, SLICE))] * 2
        + [ANY_SPEC] * (count + 1),
        out_specs=(fixed((slots, D)),) + (stepped((1, slots, SLICE)),) * 2,
        scratch_shapes=[
            pltpu.VMEM((3, hidden, D), BF),
            pltpu.VMEM((slots, D), F32),
            pltpu.SemaphoreType.DMA((count, 4)),
        ],
        compiler_params=ffn_params(),
        cost_estimate=ffn_cost(slots, hidden),
        name="ffn_backward",
    )(grad, act, turn, *chunks)


def ffn_weights(rows, grad, hid, dgate, dup, first, last, ff_shard):
    slots = rows.shape[0]
    lead = first == 0
    base, end = first * ff_shard // SLICE, -(-last * ff_shard // SLICE)
    full = jax.ShapeDtypeStruct((3 * ff_shard, D), BF)
    half = jax.ShapeDtypeStruct((3 * ff_shard // 2, D), BF)
    shapes = ([half] * 2 if lead else [full]) + [full] * (last - first - 1)
    tile = pl.BlockSpec((1, slots, SLICE), lambda t: (t + base, 0, 0))
    return pl.pallas_call(
        functools.partial(ffn_weights_kernel, lead, first, ff_shard),
        grid=(end - base,),
        out_shape=tuple(shapes),
        in_specs=[fixed((slots, D))] * 2 + [tile] * 3,
        out_specs=(ANY_SPEC,) * len(shapes),
        scratch_shapes=[
            pltpu.VMEM((3, (end - base) * SLICE, D), BF),
            pltpu.SemaphoreType.DMA((last - first, 4)),
        ],
        compiler_params=ffn_params(),
        cost_estimate=ffn_cost(slots, (end - base) * SLICE),
    )(rows, grad, hid, dgate, dup)


def norm_inverse(x):
    return lax.rsqrt(jnp.mean(x * x, axis=-1, keepdims=True) + EPSILON)


def qkv_forward_kernel(x_ref, scale_ref, wq_ref, wk_ref, wv_ref, out_ref, normed_ref):
    @pl.when(pl.program_id(0) == 0)
    def _():
        x = x_ref[...].astype(F32)
        normed_ref[...] = (x * norm_inverse(x) * scale_ref[...]).astype(BF)

    normed = normed_ref[...]
    for c, w in enumerate((wq_ref, wk_ref, wv_ref)):
        y = jnp.dot(normed, w[...].reshape(D, TILE), preferred_element_type=F32).astype(BF)
        for s in range(2):
            out_ref[s, :, c * HALF : (c + 1) * HALF] = y[:, s * HALF : (s + 1) * HALF]


def qkv_forward(x, scale, gathered, shard):
    tokens = x.shape[0]
    count = D // HALF
    weight = [
        pl.BlockSpec((D // shard, shard, TILE), lambda j, c=c: (0, c, j)) for c in range(3)
    ]
    whole = pl.BlockSpec((tokens, D), lambda j: (0, 0))
    return pl.pallas_call(
        qkv_forward_kernel,
        grid=(count // 2,),
        out_shape=(
            jax.ShapeDtypeStruct((count, tokens, 3 * HALF), BF),
            jax.ShapeDtypeStruct((tokens, D), BF),
        ),
        in_specs=[whole, pl.BlockSpec((1, D), lambda j: (0, 0))] + weight,
        out_specs=(pl.BlockSpec((2, tokens, 3 * HALF), lambda j: (j, 0, 0)), whole),
        compiler_params=ffn_params(),
        cost_estimate=pl.CostEstimate(
            flops=6 * tokens * D * D, bytes_accessed=10 * 10**6, transcendentals=0
        ),
        name="qkv_forward",
    )(x, scale, gathered, gathered, gathered)


def qkv_backward_kernel(
    dq_ref, normed_ref, w_ref, x_ref, scale_ref, mid_ref, kept_ref, pack_ref, gin_ref, gain_ref,
    turned, acc,
):
    step = pl.program_id(0) * pl.num_programs(1) + pl.program_id(1)
    dq = jnp.concatenate([dq_ref[0], dq_ref[1]], axis=1)

    @pl.when(step == 0)
    def _():
        turned[...] = transpose_low(normed_ref[...])

    weights = jnp.dot(turned[...], dq, preferred_element_type=F32).astype(BF)
    pack_ref[...] = weights.reshape(pack_ref.shape)
    more = lax.dot_general(dq, w_ref[...].reshape(D, TILE), NT, preferred_element_type=F32)

    @pl.when(step == 0)
    def _():
        acc[...] = more

    @pl.when(step > 0)
    def _():
        acc[...] += more

    @pl.when(step == pl.num_programs(0) * pl.num_programs(1) - 1)
    def _():
        x = x_ref[...].astype(F32)
        inverse = norm_inverse(x)
        grad = acc[...]
        scaled = grad * scale_ref[...]
        inner = jnp.mean(x * scaled, axis=-1, keepdims=True)
        gin_ref[...] = mid_ref[...] + inverse * scaled - x * (inverse * inverse * inverse * inner)
        gain_ref[...] = jnp.broadcast_to(
            jnp.sum(grad * (x * inverse), axis=0, keepdims=True), gain_ref.shape
        )


def qkv_backward(dq, normed, gathered, x, scale, middle, kept, shard):
    tokens = x.shape[0]
    count = D // HALF
    whole = pl.BlockSpec((tokens, D), lambda j, c: (0, 0))
    weight = pl.BlockSpec((D // shard, shard, TILE), lambda j, c: (0, c, j))
    return pl.pallas_call(
        qkv_backward_kernel,
        grid=(count // 2, 3),
        out_shape=(
            jax.ShapeDtypeStruct(kept.shape, BF),
            jax.ShapeDtypeStruct((tokens, D), F32),
            jax.ShapeDtypeStruct((8, D), F32),
        ),
        in_specs=[
            pl.BlockSpec((2, tokens, HALF), lambda j, c: (j, 0, c)),
            whole,
            weight,
            whole,
            pl.BlockSpec((1, D), lambda j, c: (0, 0)),
            whole,
            ANY_SPEC,
        ],
        out_specs=(weight, whole, pl.BlockSpec((8, D), lambda j, c: (0, 0))),
        scratch_shapes=[pltpu.VMEM((D, tokens), BF), pltpu.VMEM((tokens, D), F32)],
        input_output_aliases={6: 0},
        compiler_params=pltpu.CompilerParams(
            dimension_semantics=("arbitrary", "arbitrary"), vmem_limit_bytes=40 * 1024 * 1024
        ),
        cost_estimate=pl.CostEstimate(
            flops=12 * tokens * D * D, bytes_accessed=25 * 10**6, transcendentals=0
        ),
        name="qkv_backward",
    )(dq, normed, gathered, x, scale, middle, kept)


def local(
    inputs,
    w_qkv,
    w_out,
    attn_gain,
    moe_gain,
    w_router,
    bias_table,
    w_gate,
    w_up,
    w_down,
    routes,
    slot_order,
    group_map,
    buckets,
    grad_output,
):
    tok_count = inputs.shape[0]
    expert_count = w_router.shape[1]
    capacity = (5 * TOPK * tok_count + 4 * expert_count - 1) // (4 * expert_count)
    fsdp_count = lax.axis_size("fsdp")
    fsdp_place = lax.axis_index("fsdp")
    expert_place = lax.axis_index("expert")
    group_count = lax.axis_size("expert") * fsdp_count
    sh = Shape(fsdp_count)
    prompt_rows = sh.part * G_LINE
    slot_total = expert_count * capacity
    shard = w_qkv.shape[0]
    ff_shard = w_down.shape[1]

    def by_prompt(x):
        head = x[:prompt_rows].reshape(sh.part, G_LINE, -1).transpose(1, 0, 2)
        return jnp.concatenate([head.reshape(prompt_rows, -1), x[prompt_rows:]], 0)

    def by_token(x):
        head = x[:prompt_rows].reshape(G_LINE, sh.part, -1).transpose(1, 0, 2)
        return jnp.concatenate([head.reshape(prompt_rows, -1), x[prompt_rows:]], 0)

    own_weights = jnp.concatenate([w_gate[0].T, w_up[0].T, w_down[0]], 0)
    spread = [fsdp_count // 8] * 4
    spread[0] += fsdp_count // 2 - sum(spread)

    def run(ring, count):
        for _ in range(count):
            ring.step()

    small = jnp.concatenate(
        [attn_gain, moe_gain, w_router.reshape(-1), bias_table, group_map.astype(BF)]
    )
    small_rows = -(-small.shape[0] // D)
    small_rows = -(-small_rows // 16) * 16
    small = jnp.pad(small, (0, small_rows * D - small.shape[0])).reshape(small_rows, D)
    pack = jnp.concatenate([w_qkv[:, i * D : (i + 1) * D] for i in range(3)] + [w_out, small], 0)
    gathered = dense_gather(pack, group_count)
    own_weights, tail = tied(own_weights, gathered[:, 4 * shard])
    weights = RingGather(own_weights, fsdp_count)
    run(weights, spread[0])
    fused = sh.width == HALF
    out_full = gathered[:, 3 * shard : 4 * shard].reshape(D, D)
    marks = [0, shard, 2 * shard, 2 * shard + shard * expert_count]
    marks += [marks[-1] + bias_table.shape[0]]
    attn_scale = tail[:, marks[0] : marks[1]].reshape(D).astype(F32)
    moe_scale = tail[:, marks[1] : marks[2]].reshape(D).astype(F32)
    router = tail[:, marks[2] : marks[3]].reshape(D, expert_count).astype(F32)
    table = tail[:, marks[3] : marks[4]].reshape(fsdp_count, sh.hp, BUCKETS)
    my_table = lax.dynamic_index_in_dim(table, fsdp_place, 0, keepdims=False).astype(F32)
    groups = tail[:, marks[4]].reshape(-1, fsdp_count)
    my_groups = lax.dynamic_index_in_dim(groups, expert_place, 0, keepdims=False)
    my_groups = my_groups.astype(jnp.int32)
    bucket = buckets.reshape(SPAN_BLOCKS, HALF)

    token_input = by_prompt(inputs)
    grad_rows_low = by_prompt(grad_output)
    routes = by_prompt(routes)
    slot_order = by_prompt(slot_order)

    input_float = token_input.astype(F32)
    if fused:
        by_heads, normed_low = qkv_forward(token_input, attn_scale[None, :], gathered, shard)
    else:
        qkv_full = jnp.concatenate(
            [gathered[:, i * shard : (i + 1) * shard].reshape(D, D) for i in range(3)], 1
        )
        normed, first_pull = jax.vjp(rms_scale, input_float, attn_scale)
        normed_low = normed.astype(BF)
        qkv_rows = jnp.dot(normed_low, qkv_full, preferred_element_type=F32).astype(BF)
        by_heads = (
            qkv_rows.reshape(tok_count, 3, fsdp_count, sh.width)
            .transpose(2, 0, 1, 3)
            .reshape(fsdp_count, tok_count, 3 * sh.width)
        )
    head_qkv = lax.all_to_all(by_heads, "fsdp", split_axis=0, concat_axis=0, tiled=True)
    run(weights, spread[1])
    head_qkv = weights.tie(head_qkv)
    head_att, att_turned, att_lse = attend_forward(sh, my_groups, my_table, bucket, head_qkv)
    att_back = lax.all_to_all(head_att, "fsdp", split_axis=0, concat_axis=0, tiled=True)
    run(weights, spread[2])
    att_back = weights.tie(att_back)
    run(weights, spread[3])
    attn_low = att_back.transpose(1, 0, 2).reshape(tok_count, D)

    middle = input_float + jnp.dot(attn_low, out_full, preferred_element_type=F32)
    second_normed, second_pull = jax.vjp(rms_scale, middle, moe_scale)
    (gate_pair, losses), router_pull = jax.vjp(
        lambda normed_rows, router_rows: route_local(normed_rows, router_rows, routes),
        second_normed,
        router,
    )
    kept_mask = (slot_order < capacity).astype(F32)
    gate_kept = gate_pair * kept_mask
    slot_ids = jnp.arange(slot_total, dtype=jnp.int32)
    slot_place = jnp.where(slot_order < capacity, routes * capacity + slot_order, -1)
    hot = [slot_place[:, k : k + 1] == slot_ids[None, :] for k in range(TOPK)]
    any_low = (hot[0] | hot[1]).astype(BF)
    outgoing = lax.dot_general(
        any_low, second_normed.astype(BF), TN, preferred_element_type=F32
    ).astype(BF)

    def swap_experts(rows):
        rows = rows.reshape(expert_count, capacity, D)
        rows = lax.all_to_all(rows, "expert", split_axis=0, concat_axis=0, tiled=True)
        return rows.reshape(slot_total, D)

    expert_rows = swap_experts(outgoing)
    slot_gate = jnp.sum(
        jnp.where(hot[0], gate_kept[:, 0:1], 0.0) + jnp.where(hot[1], gate_kept[:, 1:2], 0.0),
        axis=0,
    )
    slot_grad = lax.dot_general(any_low, grad_rows_low, TN, preferred_element_type=F32)
    grad_result = swap_experts((slot_gate[:, None] * slot_grad).astype(BF))

    order = block_order(fsdp_count)
    far = order[0]
    blocks = list(weights.chunks[far]) + [weights.chunks[k] for k in order[1:]]
    result_rows, act, turn, hidden = ffn_forward(expert_rows, blocks, ff_shard)
    returned = swap_experts(result_rows)
    grad_rows, grad_gate_pre, grad_up_pre = ffn_backward(
        grad_result, act, turn, blocks, ff_shard
    )
    grad_sent = swap_experts(grad_rows)
    halves = (expert_rows, grad_result, hidden, grad_gate_pre, grad_up_pre)
    early = ffn_weights(*halves, 0, 3, ff_shard)
    late = ffn_weights(*halves, 3, fsdp_count, ff_shard)
    totals = dict(zip(order[1:], early[2:] + late))
    totals[far] = early[:2]

    def part(k):
        return totals[k]

    sums = RingScatter(part, fsdp_count)
    run(sums, spread[0])

    picked = [
        jnp.dot(h.astype(BF), returned, preferred_element_type=F32) for h in hot
    ]
    block_out = middle + gate_kept[:, 0:1] * picked[0] + gate_kept[:, 1:2] * picked[1]
    output = by_token(block_out.astype(BF))
    grad_final = grad_rows_low.astype(F32)
    grad_pair = (
        jnp.stack([jnp.sum(grad_final * p, axis=-1) for p in picked], -1) * kept_mask
    )
    grad_second = jnp.dot(any_low, grad_sent, preferred_element_type=F32)
    loss_weights = jnp.array([ZLOSS_FACTOR, BALANCE_FACTOR], F32) / group_count
    router_normed, grad_router = router_pull((grad_pair, loss_weights))
    grad_middle_part, grad_moe_gain = second_pull(grad_second + router_normed)
    grad_middle = grad_final + grad_middle_part
    grad_branch = grad_middle.astype(BF)
    grad_attn = lax.dot_general(grad_branch, out_full, NT, preferred_element_type=F32)
    grad_attn = grad_attn.astype(BF)
    head_grad = (
        grad_attn.reshape(tok_count, fsdp_count, sh.width).transpose(1, 0, 2)
    )
    head_grad = lax.all_to_all(head_grad, "fsdp", split_axis=0, concat_axis=0, tiled=True)
    run(sums, spread[1])
    head_grad = sums.tie(head_grad)
    head_dqkv, head_table = attend_backward(
        sh, my_groups, my_table, bucket, head_qkv, head_grad, att_turned, att_lse
    )
    run(sums, spread[2])
    head_dqkv = sums.tie(head_dqkv)
    back_dqkv = lax.all_to_all(head_dqkv, "fsdp", split_axis=0, concat_axis=0, tiled=True)
    sums.step()
    run(sums, spread[3] - 1)
    expert_sums = sums.finish()
    grad_gate = expert_sums[:ff_shard].T
    grad_up = expert_sums[ff_shard : 2 * ff_shard].T
    grad_down = expert_sums[2 * ff_shard :]
    grad_out_w = lax.dot_general(attn_low, grad_branch, TN, preferred_element_type=F32)

    def rows_of(x):
        return x.astype(BF).reshape(group_count, shard, -1)

    place_table = (jnp.arange(fsdp_count) == fsdp_place).astype(F32)
    whole_table = place_table[:, None] * head_table[:, 0][None, :]
    if fused:
        kept = jnp.pad(rows_of(grad_out_w), ((0, 0), (3 * shard, small_rows), (0, 0)))
        kept, grad_inputs, gains = qkv_backward(
            back_dqkv, normed_low, gathered, token_input, attn_scale[None, :], grad_middle, kept,
            shard,
        )
        grad_attn_gain = gains[0]
    else:
        grad_qkv = (
            back_dqkv.reshape(fsdp_count, tok_count, 3, sh.width)
            .transpose(1, 2, 0, 3)
            .reshape(tok_count, 3 * D)
        )
        grad_qkv_w = lax.dot_general(normed_low, grad_qkv, TN, preferred_element_type=F32)
        grad_normed = lax.dot_general(grad_qkv, qkv_full, NT, preferred_element_type=F32)
        grad_input_part, grad_attn_gain = first_pull(grad_normed)
        grad_inputs = grad_middle + grad_input_part
        parts = [rows_of(grad_qkv_w[:, i * D : (i + 1) * D]) for i in range(3)]
        kept = jnp.concatenate(parts + [rows_of(grad_out_w)], 1)
        kept = jnp.pad(kept, ((0, 0), (0, small_rows), (0, 0)))
    smalls = [grad_attn_gain, grad_moe_gain, grad_router, whole_table.reshape(-1)]
    smalls = jnp.concatenate([p.astype(BF).reshape(group_count, -1) for p in smalls], 1)
    smalls = jnp.pad(smalls, ((0, 0), (0, small_rows * D - smalls.shape[1])))
    smalls = smalls.reshape(group_count, small_rows, D)
    sums_dense = dense_sum(lax.dynamic_update_slice(kept, smalls, (0, 4 * shard, 0)))
    grad_inputs = by_token(grad_inputs)
    sum_qkv = jnp.concatenate([sums_dense[i * shard : (i + 1) * shard] for i in range(3)], 1)
    sum_out = sums_dense[3 * shard : 4 * shard]
    sum_small = sums_dense[4 * shard]
    sum_attn = sum_small[marks[0] : marks[1]]
    sum_moe = sum_small[marks[1] : marks[2]]
    sum_router = sum_small[marks[2] : marks[3]].reshape(shard, expert_count)
    sum_table = sum_small[marks[3] : marks[4]]
    return (
        output,
        losses[None, :],
        grad_inputs,
        sum_qkv,
        sum_out,
        sum_attn,
        sum_moe,
        sum_router,
        sum_table,
        grad_gate[None],
        grad_up[None],
        grad_down[None],
    )


def solution(mesh):
    rows = P(("expert", "fsdp"), None)
    flat = P(("expert", "fsdp"))
    cols = P("expert", None, "fsdp")
    deep = P("expert", "fsdp", None)
    in_specs = (
        rows, rows, rows, flat, flat, rows, flat, cols, cols, deep, rows, rows, flat, P(), rows,
    )
    out_specs = (rows, rows, rows, rows, rows, flat, flat, rows, flat, cols, cols, deep)

    return jax.shard_map(local, mesh=mesh, in_specs=in_specs, out_specs=out_specs, check_vma=False)
```

```python
import functools

import jax
import jax.numpy as jnp
from jax import lax
from jax.experimental import pallas as pl
from jax.experimental.pallas import tpu as pltpu
from jax.sharding import PartitionSpec as P


D = 1024
HEADS = 16
HDIM = 64
BUCKETS = 32
TOPK = 2
PLEN = 1024
CLEN = 128
G_LINE = 2

EPSILON = 1e-06
ZLOSS_FACTOR = 0.001
BALANCE_FACTOR = 0.01
MASK_VALUE = -1e30
LOG2E = 1.4426950408889634
HIGHEST = lax.Precision.HIGHEST
TILE = 256
HALF = 128
SPAN_BLOCKS = (PLEN + CLEN) // HALF
BF = jnp.bfloat16
F32 = jnp.float32
NT = (((1,), (1,)), ((), ()))
TN = (((0,), (0,)), ((), ()))


def rms_scale(values, scale_row):
    inverse = lax.rsqrt(jnp.mean(values * values, axis=-1, keepdims=True) + EPSILON)
    return values * inverse * scale_row


def route_local(normed, router, routes):
    logits = jnp.dot(normed, router, precision=HIGHEST)
    log_total = jax.nn.logsumexp(logits, axis=-1)
    chances = jnp.exp(logits - log_total[:, None])
    expert_ids = jnp.arange(router.shape[1], dtype=jnp.int32)
    first_hot = (routes[:, 0:1] == expert_ids[None, :]).astype(F32)
    second_hot = (routes[:, 1:2] == expert_ids[None, :]).astype(F32)
    first_chance = jnp.sum(chances * first_hot, axis=-1)
    second_chance = jnp.sum(chances * second_hot, axis=-1)
    both_chances = first_chance + second_chance
    gate_pair = jnp.stack([first_chance / both_chances, second_chance / both_chances], -1)
    z_loss = jnp.mean(log_total * log_total)
    expert_share = jnp.sum(first_hot + second_hot, axis=0) / (TOPK * routes.shape[0])
    balance = router.shape[1] * jnp.sum(expert_share * jnp.mean(chances, axis=0))
    return (gate_pair, jnp.stack([z_loss, balance]))


class Shape:
    def __init__(self, fsdp_count):
        self.srcs = fsdp_count
        self.hp = HEADS // fsdp_count
        self.width = self.hp * HDIM
        self.part = PLEN // fsdp_count
        self.rows = G_LINE * self.part + CLEN
        self.spt = TILE // self.part
        self.tiles = PLEN // TILE
        self.pairs = fsdp_count // 2
        self.prompt_pairs = self.pairs // G_LINE
        self.units = G_LINE * self.tiles + self.pairs


def order_conts(sh, group_ref, perm_ref):
    counts = [jnp.int32(0), jnp.int32(sh.srcs // G_LINE)]
    for c in range(sh.srcs):
        first = group_ref[c] == 0
        perm_ref[jnp.where(first, counts[0], counts[1])] = jnp.int32(c)
        step = first.astype(jnp.int32)
        counts = [counts[0] + step, counts[1] + 1 - step]


def build_bias(sh, table_ref, bucket_ref, bias_ref):
    bucket = bucket_ref[...]
    for h in range(sh.hp):
        dist = jnp.zeros(bucket.shape, F32)
        for b in range(BUCKETS):
            dist = jnp.where(bucket == b, table_ref[h, b] * LOG2E, dist)
        bias_ref[h, 0] = jnp.full((HALF, HALF), MASK_VALUE, F32)
        before = jnp.full((1, HALF), MASK_VALUE, F32)
        for n in range(SPAN_BLOCKS):
            now = dist[n : n + 1, :]
            both = jnp.broadcast_to(jnp.concatenate([before, now], axis=1), (HALF, 2 * HALF))
            turned = pltpu.roll(both, HALF, 1, stride=1, stride_axis=0)
            bias_ref[h, 1 + n] = turned[:, :HALF]
            before = now


def head_mask(sh, h):
    if sh.hp == 1:
        return None
    lane = lax.broadcasted_iota(jnp.int32, (1, sh.width), 1)
    return (lane >= h * HDIM) & (lane < (h + 1) * HDIM)


def only_head(sh, h, x):
    mask = head_mask(sh, h)
    return x if mask is None else jnp.where(mask, x, jnp.zeros_like(x))


def prompt_rows_of(sh, ref, g, t, part):
    lanes = slice(part * sh.width, (part + 1) * sh.width)
    start = pl.multiple_of(g * sh.part, sh.part)
    return jnp.concatenate(
        [ref[t * sh.spt + s, pl.ds(start, sh.part), lanes] for s in range(sh.spt)], axis=0
    )


def cont_rows_of(sh, ref, c, part):
    lanes = slice(part * sh.width, (part + 1) * sh.width)
    return ref[c, G_LINE * sh.part :, lanes]


def put_prompt_rows(sh, ref, g, t, part, value):
    lanes = slice(part * sh.width, (part + 1) * sh.width)
    start = pl.multiple_of(g * sh.part, sh.part)
    for s in range(sh.spt):
        ref[t * sh.spt + s, pl.ds(start, sh.part), lanes] = value[
            s * sh.part : (s + 1) * sh.part
        ].astype(ref.dtype)


def transpose_low(x):
    return x.astype(F32).T.astype(BF)


def add_bias(scores, bias_ref, h, base, step_q):
    rows = []
    for a in range(2):
        cols = []
        for b in range(2):
            part = scores[a * HALF : (a + 1) * HALF, b * HALF : (b + 1) * HALF]
            cols.append(part * LOG2E + bias_ref[h, base + b * step_q - a])
        rows.append(jnp.concatenate(cols, axis=1))
    return jnp.concatenate(rows, axis=0)


def fold_max(x):
    return jnp.max(x.reshape(-1, 8, x.shape[-1]), axis=0)


def fold_sum(x):
    return jnp.sum(x.reshape(-1, 8, x.shape[-1]), axis=0)


def attn_forward_kernel(
    sh, group_ref, table_ref, bucket_ref, x_ref, o_ref, ot_ref, lse_ref, bias, vt, vtc, sc, perm
):
    order_conts(sh, group_ref, perm)
    build_bias(sh, table_ref, bucket_ref, bias)

    def make_vt(i, _):
        g, t = i // sh.tiles, lax.rem(i, sh.tiles)
        vt[i] = transpose_low(prompt_rows_of(sh, x_ref, g, t, 2))
        return 0

    lax.fori_loop(0, G_LINE * sh.tiles, make_vt, 0)

    def make_vtc(c, _):
        vtc[c] = transpose_low(cont_rows_of(sh, x_ref, c, 2))
        return 0

    lax.fori_loop(0, sh.srcs, make_vtc, 0)

    def scores_tile(keys, qh, base, step_q, kt, peaks):
        out = []
        for h in range(sh.hp):
            s = lax.dot_general(keys, qh[h], NT, preferred_element_type=F32)
            s = add_bias(s, bias, h, base, step_q)
            sc[h, pl.ds(pl.multiple_of(kt * TILE, TILE), TILE), :] = s
            out.append(jnp.maximum(peaks[h], fold_max(s)))
        return tuple(out)

    def value_tile(g, kt, peaks, carry):
        out = []
        for h in range(sh.hp):
            total, acc = carry[h]
            p = jnp.exp2(sc[h, pl.ds(pl.multiple_of(kt * TILE, TILE), TILE), :] - peaks[h])
            total = total + fold_sum(p)
            values = vt[g * sh.tiles + kt, h * HDIM : (h + 1) * HDIM, :]
            acc = acc + jnp.dot(values, p.astype(BF), preferred_element_type=F32)
            out.append((total, acc))
        return tuple(out)

    first_peaks = tuple(jnp.full((8, TILE), MASK_VALUE, F32) for _ in range(sh.hp))
    first_carry = tuple(
        (jnp.zeros((8, TILE), F32), jnp.zeros((HDIM, TILE), F32)) for _ in range(sh.hp)
    )

    def finish(unit, peaks, carry):
        outs = []
        for h in range(sh.hp):
            total = jnp.sum(carry[h][0], axis=0, keepdims=True)
            outs.append(carry[h][1] / total)
            lse_ref[unit, h : h + 1, :] = peaks[h] + jnp.log2(total)
        whole = jnp.concatenate(outs, axis=0) if sh.hp > 1 else outs[0]
        ot_ref[unit] = whole
        return whole.T

    def prompt_unit(i, _):
        g, qt = i // sh.tiles, lax.rem(i, sh.tiles)
        q = prompt_rows_of(sh, x_ref, g, qt, 0) * BF(HDIM**-0.5)
        qh = [only_head(sh, h, q) for h in range(sh.hp)]

        def first(kt, peaks):
            keys = prompt_rows_of(sh, x_ref, g, kt, 1)
            return scores_tile(keys, qh, 2 * (qt - kt) + 1, 1, kt, peaks)

        peaks = lax.fori_loop(0, qt + 1, first, first_peaks)
        peaks = [jnp.max(p, axis=0, keepdims=True) for p in peaks]
        carry = lax.fori_loop(0, qt + 1, lambda kt, c: value_tile(g, kt, peaks, c), first_carry)
        put_prompt_rows(sh, o_ref, g, qt, 0, finish(i, peaks, carry))
        return 0

    lax.fori_loop(0, G_LINE * sh.tiles, prompt_unit, 0)

    def cont_unit(i, _):
        conts = [perm[2 * i], perm[2 * i + 1]]
        g = i // sh.prompt_pairs
        q = jnp.concatenate([cont_rows_of(sh, x_ref, c, 0) for c in conts], axis=0)
        q = q * BF(HDIM**-0.5)
        qh = [only_head(sh, h, q) for h in range(sh.hp)]

        def first(kt, peaks):
            keys = prompt_rows_of(sh, x_ref, g, kt, 1)
            return scores_tile(keys, qh, SPAN_BLOCKS - 2 * kt, 0, kt, peaks)

        peaks = lax.fori_loop(0, sh.tiles, first, first_peaks)
        own = []
        next_peaks = []
        for h in range(sh.hp):
            parts = []
            for b in range(2):
                keys = cont_rows_of(sh, x_ref, conts[b], 1)
                s = lax.dot_general(
                    keys, qh[h][b * HALF : (b + 1) * HALF], NT, preferred_element_type=F32
                )
                parts.append(s * LOG2E + bias[h, 1])
            own.append(jnp.concatenate(parts, axis=1))
            next_peaks.append(jnp.maximum(peaks[h], fold_max(own[h])))
        peaks = [jnp.max(p, axis=0, keepdims=True) for p in next_peaks]
        start = []
        for h in range(sh.hp):
            p = jnp.exp2(own[h] - peaks[h])
            low = p.astype(BF)
            acc = jnp.concatenate(
                [
                    jnp.dot(
                        vtc[conts[b], h * HDIM : (h + 1) * HDIM, :],
                        low[:, b * HALF : (b + 1) * HALF],
                        preferred_element_type=F32,
                    )
                    for b in range(2)
                ],
                axis=1,
            )
            start.append((fold_sum(p), acc))
        carry = lax.fori_loop(
            0, sh.tiles, lambda kt, c: value_tile(g, kt, peaks, c), tuple(start)
        )
        done = finish(G_LINE * sh.tiles + i, peaks, carry)
        for b in range(2):
            o_ref[conts[b], G_LINE * sh.part :, :] = done[b * HALF : (b + 1) * HALF].astype(BF)
        return 0

    lax.fori_loop(0, sh.pairs, cont_unit, 0)


def attn_backward_kernel(
    sh,
    group_ref,
    table_ref,
    bucket_ref,
    x_ref,
    do_ref,
    ot_ref,
    lse_ref,
    dx_ref,
    dtable_ref,
    bias,
    dbias,
    ktr,
    ktc,
    dk,
    dv,
    perm,
):
    order_conts(sh, group_ref, perm)
    build_bias(sh, table_ref, bucket_ref, bias)
    dbias[...] = jnp.zeros_like(dbias)
    dk[...] = jnp.zeros_like(dk)
    dv[...] = jnp.zeros_like(dv)

    def make_kt(i, _):
        g, t = i // sh.tiles, lax.rem(i, sh.tiles)
        ktr[i] = transpose_low(prompt_rows_of(sh, x_ref, g, t, 1))
        return 0

    lax.fori_loop(0, G_LINE * sh.tiles, make_kt, 0)

    def make_ktc(c, _):
        ktc[c] = transpose_low(cont_rows_of(sh, x_ref, c, 1))
        return 0

    lax.fori_loop(0, sh.srcs, make_ktc, 0)

    def inner_terms(unit, do):
        outs = []
        turned = do.astype(F32).T
        for h in range(sh.hp):
            rows = slice(h * HDIM, (h + 1) * HDIM)
            prod = ot_ref[unit, rows, :] * turned[rows, :]
            outs.append(jnp.sum(prod, axis=0, keepdims=True))
        return outs

    def grads_tile(g, kt, qh, doh, lse, inner, base, step_q, dqs):
        keys = prompt_rows_of(sh, x_ref, g, kt, 1)
        values = prompt_rows_of(sh, x_ref, g, kt, 2)
        slot = g * sh.tiles + kt
        out = []
        dkey = dvalue = None
        for h in range(sh.hp):
            s = lax.dot_general(keys, qh[h], NT, preferred_element_type=F32)
            dp = lax.dot_general(values, doh[h], NT, preferred_element_type=F32)
            p = jnp.exp2(add_bias(s, bias, h, base, step_q) - lse[h])
            ds = p * (dp - inner[h])
            for a in range(2):
                for b in range(2):
                    dbias[h, base + b * step_q - a] += ds[
                        a * HALF : (a + 1) * HALF, b * HALF : (b + 1) * HALF
                    ]
            low = ds.astype(BF)
            more_k = jnp.dot(low, qh[h], preferred_element_type=F32)
            more_v = jnp.dot(p.astype(BF), doh[h], preferred_element_type=F32)
            dkey = more_k if dkey is None else dkey + more_k
            dvalue = more_v if dvalue is None else dvalue + more_v
            turned = ktr[slot, h * HDIM : (h + 1) * HDIM, :]
            out.append(dqs[h] + jnp.dot(turned, low, preferred_element_type=F32))
        dk[slot] += dkey
        dv[slot] += dvalue
        return tuple(out)

    def finish(dqs):
        whole = jnp.concatenate(dqs, axis=0) if sh.hp > 1 else dqs[0]
        return whole.T * (HDIM**-0.5)

    first_dq = tuple(jnp.zeros((HDIM, TILE), F32) for _ in range(sh.hp))

    def prompt_unit(i, _):
        g, qt = i // sh.tiles, lax.rem(i, sh.tiles)
        q = prompt_rows_of(sh, x_ref, g, qt, 0) * BF(HDIM**-0.5)
        do = prompt_rows_of(sh, do_ref, g, qt, 0)
        qh = [only_head(sh, h, q) for h in range(sh.hp)]
        doh = [only_head(sh, h, do) for h in range(sh.hp)]
        inner = inner_terms(i, do)
        lse = [lse_ref[i, h : h + 1, :] for h in range(sh.hp)]

        def body(kt, dqs):
            return grads_tile(g, kt, qh, doh, lse, inner, 2 * (qt - kt) + 1, 1, dqs)

        dqs = lax.fori_loop(0, qt + 1, body, first_dq)
        put_prompt_rows(sh, dx_ref, g, qt, 0, finish(dqs))
        return 0

    lax.fori_loop(0, G_LINE * sh.tiles, prompt_unit, 0)

    def cont_unit(i, _):
        conts = [perm[2 * i], perm[2 * i + 1]]
        unit = G_LINE * sh.tiles + i
        g = i // sh.prompt_pairs
        q = jnp.concatenate([cont_rows_of(sh, x_ref, c, 0) for c in conts], axis=0)
        q = q * BF(HDIM**-0.5)
        do = jnp.concatenate([cont_rows_of(sh, do_ref, c, 0) for c in conts], axis=0)
        qh = [only_head(sh, h, q) for h in range(sh.hp)]
        doh = [only_head(sh, h, do) for h in range(sh.hp)]
        inner = inner_terms(unit, do)
        lse = [lse_ref[unit, h : h + 1, :] for h in range(sh.hp)]

        def body(kt, dqs):
            return grads_tile(g, kt, qh, doh, lse, inner, SPAN_BLOCKS - 2 * kt, 0, dqs)

        dqs = lax.fori_loop(0, sh.tiles, body, first_dq)
        more = [[None] * 2 for _ in range(sh.hp)]
        for b in range(2):
            cols = slice(b * HALF, (b + 1) * HALF)
            keys = cont_rows_of(sh, x_ref, conts[b], 1)
            values = cont_rows_of(sh, x_ref, conts[b], 2)
            dkey = dvalue = None
            for h in range(sh.hp):
                s = lax.dot_general(keys, qh[h][cols], NT, preferred_element_type=F32)
                dp = lax.dot_general(values, doh[h][cols], NT, preferred_element_type=F32)
                p = jnp.exp2(s * LOG2E + bias[h, 1] - lse[h][:, cols])
                ds = p * (dp - inner[h][:, cols])
                dbias[h, 1] += ds
                low = ds.astype(BF)
                more_k = jnp.dot(low, qh[h][cols], preferred_element_type=F32)
                more_v = jnp.dot(p.astype(BF), doh[h][cols], preferred_element_type=F32)
                dkey = more_k if dkey is None else dkey + more_k
                dvalue = more_v if dvalue is None else dvalue + more_v
                turned = ktc[conts[b], h * HDIM : (h + 1) * HDIM, :]
                more[h][b] = jnp.dot(turned, low, preferred_element_type=F32)
            w = sh.width
            dx_ref[conts[b], G_LINE * sh.part :, w : 2 * w] = dkey.astype(BF)
            dx_ref[conts[b], G_LINE * sh.part :, 2 * w :] = dvalue.astype(BF)
        dqs = [dqs[h] + jnp.concatenate(more[h], axis=1) for h in range(sh.hp)]
        done = finish(dqs)
        for b in range(2):
            dx_ref[conts[b], G_LINE * sh.part :, : sh.width] = done[
                b * HALF : (b + 1) * HALF
            ].astype(BF)
        return 0

    lax.fori_loop(0, sh.pairs, cont_unit, 0)

    def put_keys(i, _):
        g, t = i // sh.tiles, lax.rem(i, sh.tiles)
        put_prompt_rows(sh, dx_ref, g, t, 1, dk[i])
        put_prompt_rows(sh, dx_ref, g, t, 2, dv[i])
        return 0

    lax.fori_loop(0, G_LINE * sh.tiles, put_keys, 0)

    bucket = bucket_ref[...]
    key_row = lax.broadcasted_iota(jnp.int32, (HALF, 2 * HALF), 0)
    for h in range(sh.hp):
        spread = []
        for n in range(SPAN_BLOCKS):
            wide = jnp.concatenate(
                [jnp.zeros((HALF, HALF), F32), dbias[h, 1 + n]], axis=1
            )
            for bit in range(7):
                moved = pltpu.roll(wide, 2 * HALF - (1 << bit), 1)
                wide = jnp.where((key_row & (1 << bit)) != 0, moved, wide)
            spread.append(jnp.sum(wide, axis=0, keepdims=True))
        rows = []
        for n in range(SPAN_BLOCKS):
            row = spread[n][:, HALF:]
            if n + 1 < SPAN_BLOCKS:
                row = row + spread[n + 1][:, :HALF]
            rows.append(row)
        by_dist = jnp.concatenate(rows, axis=0)
        sums = [
            jnp.sum(jnp.where(bucket == b, by_dist, 0.0), axis=0, keepdims=True)
            for b in range(BUCKETS)
        ]
        lanes = jnp.concatenate(sums, axis=0)
        dtable_ref[h * BUCKETS : (h + 1) * BUCKETS, :] = jnp.broadcast_to(
            jnp.sum(lanes, axis=1, keepdims=True), (BUCKETS, HALF)
        )


SMEM_SPEC = pl.BlockSpec(memory_space=pltpu.SMEM)
VMEM_SPEC = pl.BlockSpec(memory_space=pltpu.VMEM)
GRANT = 48 * 1024 * 1024


def attend_forward(sh, group, table, bucket, x):
    return pl.pallas_call(
        functools.partial(attn_forward_kernel, sh),
        out_shape=(
            jax.ShapeDtypeStruct((sh.srcs, sh.rows, sh.width), BF),
            jax.ShapeDtypeStruct((sh.units, sh.width, TILE), F32),
            jax.ShapeDtypeStruct((sh.units, 8, TILE), F32),
        ),
        in_specs=[SMEM_SPEC, SMEM_SPEC, VMEM_SPEC, VMEM_SPEC],
        out_specs=(VMEM_SPEC, VMEM_SPEC, VMEM_SPEC),
        scratch_shapes=[
            pltpu.VMEM((sh.hp, SPAN_BLOCKS + 1, HALF, HALF), F32),
            pltpu.VMEM((G_LINE * sh.tiles, sh.width, TILE), BF),
            pltpu.VMEM((sh.srcs, sh.width, HALF), BF),
            pltpu.VMEM((sh.hp, PLEN, TILE), F32),
            pltpu.SMEM((sh.srcs,), jnp.int32),
        ],
        compiler_params=pltpu.CompilerParams(vmem_limit_bytes=GRANT),
        cost_estimate=pl.CostEstimate(
            flops=10**10, bytes_accessed=8 * 10**6, transcendentals=5 * 10**6
        ),
        name="attend_forward",
    )(group, table, bucket, x)


def attend_backward(sh, group, table, bucket, x, do, ot, lse):
    return pl.pallas_call(
        functools.partial(attn_backward_kernel, sh),
        out_shape=(
            jax.ShapeDtypeStruct((sh.srcs, sh.rows, 3 * sh.width), BF),
            jax.ShapeDtypeStruct((sh.hp * BUCKETS, HALF), F32),
        ),
        in_specs=[SMEM_SPEC, SMEM_SPEC, VMEM_SPEC, VMEM_SPEC, VMEM_SPEC, VMEM_SPEC, VMEM_SPEC],
        out_specs=(VMEM_SPEC, VMEM_SPEC),
        scratch_shapes=[
            pltpu.VMEM((sh.hp, SPAN_BLOCKS + 1, HALF, HALF), F32),
            pltpu.VMEM((sh.hp, SPAN_BLOCKS + 1, HALF, HALF), F32),
            pltpu.VMEM((G_LINE * sh.tiles, sh.width, TILE), BF),
            pltpu.VMEM((sh.srcs, sh.width, HALF), BF),
            pltpu.VMEM((G_LINE * sh.tiles, TILE, sh.width), F32),
            pltpu.VMEM((G_LINE * sh.tiles, TILE, sh.width), F32),
            pltpu.SMEM((sh.srcs,), jnp.int32),
        ],
        compiler_params=pltpu.CompilerParams(vmem_limit_bytes=GRANT),
        cost_estimate=pl.CostEstimate(
            flops=2 * 10**10, bytes_accessed=12 * 10**6, transcendentals=5 * 10**6
        ),
        name="attend_backward",
    )(group, table, bucket, x, do, ot, lse)


def ring_order(count):
    deep, wide = 4, count // 4
    order = [a * wide for a in range(deep)]
    for turn, a in enumerate(reversed(range(deep))):
        row = [a * wide + b for b in range(1, wide)]
        order += row if turn % 2 == 0 else row[::-1]
    return order


def ring_hop(x, count, step):
    ring = ring_order(count)
    return lax.ppermute(x, "fsdp", [(ring[i], ring[(i + step) % count]) for i in range(count)])


def tied(*values):
    return lax.optimization_barrier(values)


class RingGather:
    def __init__(self, own, count):
        self.count = count
        self.chunks = [None] * count
        self.chunks[0] = own
        self.right = self.left = own
        self.done = 0
        self.steps = count // 2

    def step(self):
        self.done += 1
        s = self.done
        if s < self.steps:
            self.right = ring_hop(self.right, self.count, 1)
            self.left = ring_hop(self.left, self.count, -1)
        else:
            half = self.right.shape[0] // 2
            self.right = ring_hop(self.right[:half], self.count, 1)
            self.left = ring_hop(self.left[half:], self.count, -1)
        self.keep()

    def keep(self):
        s = self.done
        if s < self.steps:
            self.chunks[self.count - s] = self.right
            self.chunks[s] = self.left
        else:
            self.chunks[s] = (self.right, self.left)


class RingScatter:
    def __init__(self, part, count):
        self.part, self.count = part, count
        self.right = self.left = None
        self.done = 0
        self.steps = count // 2

    def step(self, after=None):
        count, s = self.count, self.done
        away = self.steps - s
        if s == 0:
            send_left, send_right = self.part(away)
        else:
            near_left = self.part(count - away).astype(F32)
            near_right = self.part(away).astype(F32)
            if s == 1:
                half = near_left.shape[0] // 2
                send_left = jnp.concatenate(
                    [near_left[:half] + self.left.astype(F32), near_left[half:]], 0
                )
                send_right = jnp.concatenate(
                    [near_right[:half], near_right[half:] + self.right.astype(F32)], 0
                )
            else:
                send_left = near_left + self.left.astype(F32)
                send_right = near_right + self.right.astype(F32)
        send_left, send_right = send_left.astype(BF), send_right.astype(BF)
        if after is not None:
            after, send_left, send_right = tied(after, send_left, send_right)
        self.left = ring_hop(send_left, count, -1)
        self.right = ring_hop(send_right, count, 1)
        self.done += 1
        return after

    def tie(self, value):
        value, self.right, self.left = tied(value, self.right, self.left)
        return value

    def finish(self):
        return self.part(0).astype(F32) + self.right.astype(F32) + self.left.astype(F32)


MESH_ID = pl.DeviceIdType.MESH
DEEP = 4


class Spot:
    def __init__(self):
        e, f = lax.axis_index("expert"), lax.axis_index("fsdp")
        self.x, self.c = e // 2, lax.rem(e, 2)
        self.z, self.y = f // 2, lax.rem(f, 2)
        self.ox, self.oy, self.oc = 1 - self.x, 1 - self.y, 1 - self.c

    def place(self, x=None, y=None, z=None, c=None):
        x = self.x if x is None else x
        y = self.y if y is None else y
        z = self.z if z is None else z
        c = self.c if c is None else c
        return {"expert": x * 2 + c, "fsdp": z * 2 + y}

    def block(self, x, y, z, c):
        return (x * 2 + c) * 8 + z * 2 + y

    def greet(self):
        barrier = pltpu.get_barrier_semaphore()
        for target in (self.place(x=self.ox), self.place(y=self.oy), self.place(c=self.oc)):
            pl.semaphore_signal(barrier, inc=1, device_id=target, device_id_type=MESH_ID)
        for step in (-1, 1):

            @pl.when(self.inside(self.z + step))
            def _(step=step):
                pl.semaphore_signal(
                    barrier, inc=1, device_id=self.along(step), device_id_type=MESH_ID
                )

        pl.semaphore_wait(barrier, 4 + self.z * (DEEP - 1 - self.z) // 2)

    def wrap(self, step):
        return lax.rem(self.z + step + DEEP, DEEP)

    def along(self, step):
        return self.place(z=self.wrap(step))

    def inside(self, z):
        return (z >= 0) & (z < DEEP)


def dense_gather_kernel(cut, x_ref, out_ref, send_sems, recv_sems, own_sem):
    me = Spot()
    rows = x_ref.shape[0]
    spans = [(0, cut), (cut, rows - cut)]
    pending = []

    def view(ref, h):
        return ref.at[pl.ds(*spans[h])]

    def send(src, blk, h, target, cond):
        copy = pltpu.make_async_remote_copy(
            src_ref=src,
            dst_ref=view(out_ref.at[blk], h),
            send_sem=send_sems.at[len(pending)],
            recv_sem=recv_sems.at[blk, h],
            device_id=target,
            device_id_type=MESH_ID,
        )
        pending.append((copy, cond))
        if cond is None:
            copy.start()
        else:
            pl.when(cond)(copy.start)

    def arrive(blk, h, cond):
        copy = pltpu.make_async_remote_copy(
            src_ref=view(out_ref.at[blk], h),
            dst_ref=view(out_ref.at[blk], h),
            send_sem=send_sems.at[0],
            recv_sem=recv_sems.at[blk, h],
            device_id=me.place(c=me.oc),
            device_id_type=MESH_ID,
        )
        if cond is None:
            copy.wait_recv()
        else:
            pl.when(cond)(copy.wait_recv)

    def both(a, b):
        return b if a is None else (a if b is None else a & b)

    by_y, by_x = me.place(y=me.oy), me.place(x=me.ox)
    core = me.place(c=me.oc)
    me.greet()
    mine = me.block(me.x, me.y, me.z, me.c)
    own = pltpu.make_async_copy(x_ref, out_ref.at[mine], own_sem)
    own.start()
    for h in range(2):
        for step in (-1, 1):
            send(view(x_ref, h), mine, h, me.along(step), me.inside(me.z + step))
    for h in range(2):
        for target in (by_y, by_x, core):
            send(view(x_ref, h), mine, h, target, None)

    def line(dist):
        if dist == 0:
            return [(me.z, None, 0)]
        return [(me.wrap(s * dist), me.inside(me.z + s * dist), s) for s in (-1, 1)]

    def from_line(dist):
        for zb, cond, sign in line(dist):
            blk = me.block(me.x, me.y, zb, me.c)
            for h in range(2):
                arrive(blk, h, cond)
                src = view(out_ref.at[blk], h)
                send(src, blk, h, me.along(-sign), both(cond, me.inside(me.z - sign)))
                for target in (by_y, by_x, core):
                    send(src, blk, h, target, cond)

    def from_side(dist):
        for zb, cond, _ in line(dist):
            for h in range(2):
                one = me.block(me.x, me.oy, zb, me.c)
                two = me.block(me.ox, me.y, zb, me.c)
                onward, last = ((one, by_x), two) if h == 0 else ((two, by_y), one)
                arrive(onward[0], h, cond)
                src = view(out_ref.at[onward[0]], h)
                send(src, onward[0], h, onward[1], cond)
                send(src, onward[0], h, core, cond)
                arrive(last, h, cond)
                send(view(out_ref.at[last], h), last, h, core, cond)

    def from_corner(dist):
        for zb, cond, _ in line(dist):
            blk = me.block(me.ox, me.oy, zb, me.c)
            for h in range(2):
                arrive(blk, h, cond)
                send(view(out_ref.at[blk], h), blk, h, core, cond)

    for dist in range(DEEP):
        if dist > 0:
            from_line(dist)
        from_side(dist)
        if dist > 0:
            from_corner(dist - 1)
    from_corner(DEEP - 1)
    for x in range(2):
        for y in range(2):
            for z in range(DEEP):
                for h in range(2):
                    arrive(me.block(x, y, z, me.oc), h, None)
    own.wait()
    for copy, cond in pending:
        if cond is None:
            copy.wait_send()
        else:
            pl.when(cond)(copy.wait_send)


def dense_gather(x, count):
    rows = x.shape[0]
    if count != 32 or lax.axis_size("fsdp") != 2 * DEEP:
        return lax.all_gather(x, ("expert", "fsdp"), axis=0, tiled=False)
    cut = rows // 32 * 16 + 16 * (rows // 16 % 2)
    return pl.pallas_call(
        functools.partial(dense_gather_kernel, cut),
        out_shape=jax.ShapeDtypeStruct((count,) + x.shape, x.dtype),
        in_specs=[pl.BlockSpec(memory_space=pltpu.VMEM)],
        out_specs=pl.BlockSpec(memory_space=pl.ANY),
        scratch_shapes=[
            pltpu.SemaphoreType.DMA((128,)),
            pltpu.SemaphoreType.DMA((count, 2)),
            pltpu.SemaphoreType.DMA,
        ],
        compiler_params=pltpu.CompilerParams(collective_id=0, has_side_effects=True),
        cost_estimate=pl.CostEstimate(
            flops=0, bytes_accessed=100 * 10**6, transcendentals=0
        ),
        name="dense_gather",
    )(x)


def add_into(dst, src):
    def body(i, _):
        at = pl.ds(pl.multiple_of(i * 16, 16), 16)
        dst[at, :] = (dst[at, :].astype(F32) + src[at, :].astype(F32)).astype(BF)
        return 0

    lax.fori_loop(0, dst.shape[0] // 16, body, 0)


def dense_sum_kernel(
    cut, g_ref, out_ref, acc, cbuf, xbuf, ybuf, zbuf, send_sems, recv_sems, load_sems
):
    me = Spot()
    rows = out_ref.shape[0]
    top, low = pl.ds(0, cut), pl.ds(cut, rows - cut)
    pending = []

    def send(src, dst, at, target, cond=None):
        copy = pltpu.make_async_remote_copy(
            src_ref=src,
            dst_ref=dst,
            send_sem=send_sems.at[len(pending)],
            recv_sem=recv_sems.at[at],
            device_id=target,
            device_id_type=MESH_ID,
        )
        pending.append((copy, cond))
        if cond is None:
            copy.start()
        else:
            pl.when(cond)(copy.start)

    def arrive(dst, at):
        pltpu.make_async_remote_copy(
            src_ref=dst,
            dst_ref=dst,
            send_sem=send_sems.at[0],
            recv_sem=recv_sems.at[at],
            device_id=me.place(c=me.oc),
            device_id_type=MESH_ID,
        ).wait_recv()

    by_y, by_x, core = me.place(y=me.oy), me.place(x=me.ox), me.place(c=me.oc)
    me.greet()
    zs = (0, 3, 2, 1)
    loads = []
    for k in range(DEEP):
        for x in range(2):
            at = x * DEEP + k
            theirs = (x * 2 + me.oc) * 8 + zs[k] * 2
            send(g_ref.at[pl.ds(theirs, 2)], cbuf.at[at], at, core)
            ours = (x * 2 + me.c) * 8 + zs[k] * 2
            load = pltpu.make_async_copy(g_ref.at[pl.ds(ours, 2)], acc.at[at], load_sems.at[at])
            load.start()
            loads.append(load)

    def first(k):
        for x in range(2):
            at = x * DEEP + k
            loads[k * 2 + x].wait()
            arrive(cbuf.at[at], at)
            for y in range(2):
                add_into(acc.at[at, y], cbuf.at[at, y])
        base = 8 + k * 6
        for y in range(2):
            send(acc.at[me.ox * DEEP + k, y, top], xbuf.at[k, y, top], base + y, by_x)
        for x in range(2):
            send(acc.at[x * DEEP + k, me.oy, low], ybuf.at[k, x, low], base + 2 + x, by_y)

    def second(k):
        base = 8 + k * 6
        for y in range(2):
            arrive(xbuf.at[k, y, top], base + y)
            add_into(acc.at[me.x * DEEP + k, y, top], xbuf.at[k, y, top])
        for x in range(2):
            arrive(ybuf.at[k, x, low], base + 2 + x)
            add_into(acc.at[x * DEEP + k, me.y, low], ybuf.at[k, x, low])
        send(acc.at[me.x * DEEP + k, me.oy, top], ybuf.at[k, 0, top], base + 4, by_y)
        send(acc.at[me.ox * DEEP + k, me.y, low], xbuf.at[k, 0, low], base + 5, by_x)

    def third(k):
        base = 8 + k * 6
        block = acc.at[me.x * DEEP + k, me.y]
        arrive(ybuf.at[k, 0, top], base + 4)
        add_into(block.at[top], ybuf.at[k, 0, top])
        arrive(xbuf.at[k, 0, low], base + 5)
        add_into(block.at[low], xbuf.at[k, 0, low])

    def along(k, sign, behind):
        zo = zs[k]
        here = behind if sign > 0 else DEEP - 1 - behind
        term = acc.at[me.x * DEEP + k, me.y]
        base = 32 + k * 4 + (sign + 1)
        side = k * 4 + (sign + 1)
        is_here = me.z == here
        for h, at in ((0, top), (1, low)):
            if behind > 0:

                @pl.when(is_here)
                def _(h=h, at=at):
                    arrive(zbuf.at[side + h, at], base + h)
                    add_into(term.at[at], zbuf.at[side + h, at])

            if here != zo:
                send(
                    term.at[at], zbuf.at[side + h, at], base + h, me.along(sign), is_here
                )

    for step in range(DEEP + 6):
        if step < DEEP:
            first(step)
        if 0 <= step - 1 < DEEP:
            second(step - 1)
        if 0 <= step - 2 < DEEP:
            third(step - 2)
        for k in range(DEEP):
            behind = step - 2 - k
            if behind >= 0:
                if behind <= zs[k]:
                    along(k, 1, behind)
                if behind <= DEEP - 1 - zs[k]:
                    along(k, -1, behind)
    block = acc.at[me.x * DEEP + lax.rem(DEEP - me.z, DEEP), me.y]

    def put(i, _):
        at = pl.ds(pl.multiple_of(i * 16, 16), 16)
        out_ref[at, :] = block[at, :].astype(F32)
        return 0

    lax.fori_loop(0, rows // 16, put, 0)
    for copy, cond in pending:
        if cond is None:
            copy.wait_send()
        else:
            pl.when(cond)(copy.wait_send)


def dense_sum(x):
    count, rows, width = x.shape
    if count != 32 or lax.axis_size("fsdp") != 2 * DEEP:
        flat = x.reshape(count * rows, width)
        return lax.psum_scatter(
            flat, ("expert", "fsdp"), scatter_dimension=0, tiled=True
        ).astype(F32)
    cut = rows // 32 * 16 + 16 * (rows // 16 % 2)
    pair = (2 * DEEP, 2, rows, width)
    return pl.pallas_call(
        functools.partial(dense_sum_kernel, cut),
        out_shape=jax.ShapeDtypeStruct((rows, width), F32),
        in_specs=[pl.BlockSpec(memory_space=pl.ANY)],
        out_specs=pl.BlockSpec(memory_space=pltpu.VMEM),
        scratch_shapes=[
            pltpu.VMEM(pair, BF),
            pltpu.VMEM(pair, BF),
            pltpu.VMEM((DEEP, 2, rows, width), BF),
            pltpu.VMEM((DEEP, 2, rows, width), BF),
            pltpu.VMEM((4 * DEEP, rows, width), BF),
            pltpu.SemaphoreType.DMA((72,)),
            pltpu.SemaphoreType.DMA((48,)),
            pltpu.SemaphoreType.DMA((8,)),
        ],
        compiler_params=pltpu.CompilerParams(
            collective_id=1, has_side_effects=True, vmem_limit_bytes=40 * 1024 * 1024
        ),
        cost_estimate=pl.CostEstimate(
            flops=0, bytes_accessed=100 * 10**6, transcendentals=0
        ),
        name="dense_sum",
    )(x)


SLICE = 256


def gelu_terms(x):
    root = 0.7978845608028654
    square = x * x
    t = jnp.tanh(root * (x + 0.044715 * square * x))
    half = 0.5 * (1.0 + t)
    slope = half + 0.5 * x * (1.0 - t * t) * (root * (1.0 + 3 * 0.044715 * square))
    return x * half, slope


def block_order(count):
    far = count // 2
    order = [far]
    for away in range(1, far + 1):
        order += [k for k in (far - away, far + away) if k < count]
    return order


def chunk_pieces(base, split, ff_shard):
    if not split:
        return [(0, m * ff_shard, m, base, ff_shard) for m in range(3)]
    half = ff_shard // 2
    return [
        (0, 0, 0, base, ff_shard),
        (0, ff_shard, 1, base, half),
        (1, 0, 1, base + half, half),
        (1, half, 2, base, ff_shard),
    ]


def chunk_copies(refs, whole, sems, ff_shard, outward, start=0):
    out = []
    for p, own in enumerate(refs):
        pieces = []
        places = chunk_pieces(p * ff_shard + start, len(own) == 2, ff_shard)
        for n, (src, at, m, row, rows) in enumerate(places):
            block = own[src].at[pl.ds(at, rows)]
            spot = whole.at[m, pl.ds(row, rows)]
            a, b = (spot, block) if outward else (block, spot)
            pieces.append(pltpu.make_async_copy(a, b, sems.at[p, n]))
        out.append(pieces)
    return out


def pair_first(refs):
    return [refs[:2]] + [refs[k : k + 1] for k in range(2, len(refs))]


def fetch_weights(refs, whole, sems, ff_shard, t):
    copies = chunk_copies(pair_first(refs), whole, sems, ff_shard, False)
    ahead = 3

    @pl.when(t == 0)
    def _():
        for pieces in copies[:ahead]:
            for c in pieces:
                c.start()

    for p, pieces in enumerate(copies):
        more = copies[p + ahead] if p + ahead < len(copies) else []

        @pl.when(t == p * ff_shard // SLICE)
        def _(pieces=pieces, more=more):
            for c in more:
                c.start()
            for c in pieces:
                c.wait()


def ffn_forward_kernel(count, ff_shard, rows_ref, *refs):
    chunks, rest = refs[: count + 1], refs[count + 1 :]
    out_ref, act_ref, turn_ref, hid_ref, whole, acc, sems = rest
    t = pl.program_id(0)
    fetch_weights(chunks, whole, sems, ff_shard, t)
    at = pl.ds(pl.multiple_of(t * SLICE, SLICE), SLICE)
    rows = rows_ref[...]
    gate = lax.dot_general(rows, whole[0, at], NT, preferred_element_type=F32)
    up = lax.dot_general(rows, whole[1, at], NT, preferred_element_type=F32)
    act, slope = gelu_terms(gate)
    hidden = (act * up).astype(BF)
    act_ref[0] = act
    turn_ref[0] = up * slope
    hid_ref[0] = hidden
    more = jnp.dot(hidden, whole[2, at], preferred_element_type=F32)

    @pl.when(t == 0)
    def _():
        acc[...] = more

    @pl.when(t > 0)
    def _():
        acc[...] += more

    @pl.when(t == pl.num_programs(0) - 1)
    def _():
        out_ref[...] = acc[...].astype(BF)


def ffn_backward_kernel(count, ff_shard, grad_ref, act_ref, turn_ref, *refs):
    chunks, rest = refs[: count + 1], refs[count + 1 :]
    out_ref, dgate_ref, dup_ref, whole, acc, sems = rest
    t = pl.program_id(0)
    fetch_weights(chunks, whole, sems, ff_shard, t)
    at = pl.ds(pl.multiple_of(t * SLICE, SLICE), SLICE)
    dhid = lax.dot_general(grad_ref[...], whole[2, at], NT, preferred_element_type=F32)
    dgate = (dhid * turn_ref[0]).astype(BF)
    dup = (dhid * act_ref[0]).astype(BF)
    dgate_ref[0] = dgate
    dup_ref[0] = dup
    more = jnp.dot(
        jnp.concatenate([dgate, dup], axis=1),
        jnp.concatenate([whole[0, at], whole[1, at]], axis=0),
        preferred_element_type=F32,
    )

    @pl.when(t == 0)
    def _():
        acc[...] = more

    @pl.when(t > 0)
    def _():
        acc[...] += more

    @pl.when(t == pl.num_programs(0) - 1)
    def _():
        out_ref[...] = acc[...].astype(BF)


def ffn_weights_kernel(
    lead, first, ff_shard, rows_ref, grad_ref, hid_ref, dgate_ref, dup_ref, *refs
):
    chunks, (whole, sems) = refs[:-2], refs[-2:]
    chunks = pair_first(chunks) if lead else [chunks[k : k + 1] for k in range(len(chunks))]
    base = first * ff_shard // SLICE
    t = pl.program_id(0)
    at = pl.ds(pl.multiple_of(t * SLICE, SLICE), SLICE)
    for m, (left, right) in enumerate(
        ((dgate_ref, rows_ref), (dup_ref, rows_ref), (hid_ref, grad_ref))
    ):
        whole[m, at] = lax.dot_general(
            left[0], right[...], TN, preferred_element_type=F32
        ).astype(BF)
    copies = chunk_copies(
        chunks, whole, sems, ff_shard, True, first * ff_shard - base * SLICE
    )
    for p, pieces in enumerate(copies):

        @pl.when(t == ((first + p + 1) * ff_shard - 1) // SLICE - base)
        def _(pieces=pieces):
            for c in pieces:
                c.start()

    @pl.when(t == pl.num_programs(0) - 1)
    def _():
        for pieces in copies:
            for c in pieces:
                c.wait()


def fixed(shape):
    return pl.BlockSpec(shape, lambda t: (0,) * len(shape))


def stepped(shape):
    return pl.BlockSpec(shape, lambda t: (t, 0, 0))


ANY_SPEC = pl.BlockSpec(memory_space=pl.ANY)


def ffn_cost(slots, hidden):
    work = 6 * slots * D * hidden
    return pl.CostEstimate(flops=work, bytes_accessed=40 * 10**6, transcendentals=slots * hidden)


def ffn_params():
    return pltpu.CompilerParams(
        dimension_semantics=("arbitrary",), vmem_limit_bytes=60 * 1024 * 1024
    )


def ffn_forward(rows, chunks, ff_shard):
    slots, count = rows.shape[0], len(chunks) - 1
    hidden = count * ff_shard
    steps = hidden // SLICE
    return pl.pallas_call(
        functools.partial(ffn_forward_kernel, count, ff_shard),
        grid=(steps,),
        out_shape=(
            jax.ShapeDtypeStruct((slots, D), BF),
            jax.ShapeDtypeStruct((steps, slots, SLICE), F32),
            jax.ShapeDtypeStruct((steps, slots, SLICE), F32),
            jax.ShapeDtypeStruct((steps, slots, SLICE), BF),
        ),
        in_specs=[fixed((slots, D))] + [ANY_SPEC] * (count + 1),
        out_specs=(
            fixed((slots, D)),
            stepped((1, slots, SLICE)),
            stepped((1, slots, SLICE)),
            stepped((1, slots, SLICE)),
        ),
        scratch_shapes=[
            pltpu.VMEM((3, hidden, D), BF),
            pltpu.VMEM((slots, D), F32),
            pltpu.SemaphoreType.DMA((count, 4)),
        ],
        compiler_params=ffn_params(),
        cost_estimate=ffn_cost(slots, hidden),
        name="ffn_forward",
    )(rows, *chunks)


def ffn_backward(grad, act, turn, chunks, ff_shard):
    slots, count = grad.shape[0], len(chunks) - 1
    hidden = count * ff_shard
    steps = hidden // SLICE
    tile = jax.ShapeDtypeStruct((steps, slots, SLICE), BF)
    return pl.pallas_call(
        functools.partial(ffn_backward_kernel, count, ff_shard),
        grid=(steps,),
        out_shape=(jax.ShapeDtypeStruct((slots, D), BF), tile, tile),
        in_specs=[fixed((slots, D))]
        + [stepped((1, slots, SLICE))] * 2
        + [ANY_SPEC] * (count + 1),
        out_specs=(fixed((slots, D)),) + (stepped((1, slots, SLICE)),) * 2,
        scratch_shapes=[
            pltpu.VMEM((3, hidden, D), BF),
            pltpu.VMEM((slots, D), F32),
            pltpu.SemaphoreType.DMA((count, 4)),
        ],
        compiler_params=ffn_params(),
        cost_estimate=ffn_cost(slots, hidden),
        name="ffn_backward",
    )(grad, act, turn, *chunks)


def ffn_weights(rows, grad, hid, dgate, dup, first, last, ff_shard):
    slots = rows.shape[0]
    lead = first == 0
    base, end = first * ff_shard // SLICE, -(-last * ff_shard // SLICE)
    full = jax.ShapeDtypeStruct((3 * ff_shard, D), BF)
    half = jax.ShapeDtypeStruct((3 * ff_shard // 2, D), BF)
    shapes = ([half] * 2 if lead else [full]) + [full] * (last - first - 1)
    tile = pl.BlockSpec((1, slots, SLICE), lambda t: (t + base, 0, 0))
    return pl.pallas_call(
        functools.partial(ffn_weights_kernel, lead, first, ff_shard),
        grid=(end - base,),
        out_shape=tuple(shapes),
        in_specs=[fixed((slots, D))] * 2 + [tile] * 3,
        out_specs=(ANY_SPEC,) * len(shapes),
        scratch_shapes=[
            pltpu.VMEM((3, (end - base) * SLICE, D), BF),
            pltpu.SemaphoreType.DMA((last - first, 4)),
        ],
        compiler_params=ffn_params(),
        cost_estimate=ffn_cost(slots, (end - base) * SLICE),
    )(rows, grad, hid, dgate, dup)


def norm_inverse(x):
    return lax.rsqrt(jnp.mean(x * x, axis=-1, keepdims=True) + EPSILON)


def qkv_forward_kernel(x_ref, scale_ref, wq_ref, wk_ref, wv_ref, out_ref, normed_ref):
    @pl.when(pl.program_id(0) == 0)
    def _():
        x = x_ref[...].astype(F32)
        normed_ref[...] = (x * norm_inverse(x) * scale_ref[...]).astype(BF)

    normed = normed_ref[...]
    for c, w in enumerate((wq_ref, wk_ref, wv_ref)):
        y = jnp.dot(normed, w[...].reshape(D, TILE), preferred_element_type=F32).astype(BF)
        for s in range(2):
            out_ref[s, :, c * HALF : (c + 1) * HALF] = y[:, s * HALF : (s + 1) * HALF]


def qkv_forward(x, scale, gathered, shard):
    tokens = x.shape[0]
    count = D // HALF
    weight = [
        pl.BlockSpec((D // shard, shard, TILE), lambda j, c=c: (0, c, j)) for c in range(3)
    ]
    whole = pl.BlockSpec((tokens, D), lambda j: (0, 0))
    return pl.pallas_call(
        qkv_forward_kernel,
        grid=(count // 2,),
        out_shape=(
            jax.ShapeDtypeStruct((count, tokens, 3 * HALF), BF),
            jax.ShapeDtypeStruct((tokens, D), BF),
        ),
        in_specs=[whole, pl.BlockSpec((1, D), lambda j: (0, 0))] + weight,
        out_specs=(pl.BlockSpec((2, tokens, 3 * HALF), lambda j: (j, 0, 0)), whole),
        compiler_params=ffn_params(),
        cost_estimate=pl.CostEstimate(
            flops=6 * tokens * D * D, bytes_accessed=10 * 10**6, transcendentals=0
        ),
        name="qkv_forward",
    )(x, scale, gathered, gathered, gathered)


def qkv_backward_kernel(
    dq_ref, normed_ref, w_ref, x_ref, scale_ref, mid_ref, kept_ref, pack_ref, gin_ref, gain_ref,
    turned, acc,
):
    step = pl.program_id(0) * pl.num_programs(1) + pl.program_id(1)
    dq = jnp.concatenate([dq_ref[0], dq_ref[1]], axis=1)

    @pl.when(step == 0)
    def _():
        turned[...] = transpose_low(normed_ref[...])

    weights = jnp.dot(turned[...], dq, preferred_element_type=F32).astype(BF)
    pack_ref[...] = weights.reshape(pack_ref.shape)
    more = lax.dot_general(dq, w_ref[...].reshape(D, TILE), NT, preferred_element_type=F32)

    @pl.when(step == 0)
    def _():
        acc[...] = more

    @pl.when(step > 0)
    def _():
        acc[...] += more

    @pl.when(step == pl.num_programs(0) * pl.num_programs(1) - 1)
    def _():
        x = x_ref[...].astype(F32)
        inverse = norm_inverse(x)
        grad = acc[...]
        scaled = grad * scale_ref[...]
        inner = jnp.mean(x * scaled, axis=-1, keepdims=True)
        gin_ref[...] = mid_ref[...] + inverse * scaled - x * (inverse * inverse * inverse * inner)
        gain_ref[...] = jnp.broadcast_to(
            jnp.sum(grad * (x * inverse), axis=0, keepdims=True), gain_ref.shape
        )


def qkv_backward(dq, normed, gathered, x, scale, middle, kept, shard):
    tokens = x.shape[0]
    count = D // HALF
    whole = pl.BlockSpec((tokens, D), lambda j, c: (0, 0))
    weight = pl.BlockSpec((D // shard, shard, TILE), lambda j, c: (0, c, j))
    return pl.pallas_call(
        qkv_backward_kernel,
        grid=(count // 2, 3),
        out_shape=(
            jax.ShapeDtypeStruct(kept.shape, BF),
            jax.ShapeDtypeStruct((tokens, D), F32),
            jax.ShapeDtypeStruct((8, D), F32),
        ),
        in_specs=[
            pl.BlockSpec((2, tokens, HALF), lambda j, c: (j, 0, c)),
            whole,
            weight,
            whole,
            pl.BlockSpec((1, D), lambda j, c: (0, 0)),
            whole,
            ANY_SPEC,
        ],
        out_specs=(weight, whole, pl.BlockSpec((8, D), lambda j, c: (0, 0))),
        scratch_shapes=[pltpu.VMEM((D, tokens), BF), pltpu.VMEM((tokens, D), F32)],
        input_output_aliases={6: 0},
        compiler_params=pltpu.CompilerParams(
            dimension_semantics=("arbitrary", "arbitrary"), vmem_limit_bytes=40 * 1024 * 1024
        ),
        cost_estimate=pl.CostEstimate(
            flops=12 * tokens * D * D, bytes_accessed=25 * 10**6, transcendentals=0
        ),
        name="qkv_backward",
    )(dq, normed, gathered, x, scale, middle, kept)


def local(
    inputs,
    w_qkv,
    w_out,
    attn_gain,
    moe_gain,
    w_router,
    bias_table,
    w_gate,
    w_up,
    w_down,
    routes,
    slot_order,
    group_map,
    buckets,
    grad_output,
):
    tok_count = inputs.shape[0]
    expert_count = w_router.shape[1]
    capacity = (5 * TOPK * tok_count + 4 * expert_count - 1) // (4 * expert_count)
    fsdp_count = lax.axis_size("fsdp")
    fsdp_place = lax.axis_index("fsdp")
    expert_place = lax.axis_index("expert")
    group_count = lax.axis_size("expert") * fsdp_count
    sh = Shape(fsdp_count)
    prompt_rows = sh.part * G_LINE
    slot_total = expert_count * capacity
    shard = w_qkv.shape[0]
    ff_shard = w_down.shape[1]

    def by_prompt(x):
        head = x[:prompt_rows].reshape(sh.part, G_LINE, -1).transpose(1, 0, 2)
        return jnp.concatenate([head.reshape(prompt_rows, -1), x[prompt_rows:]], 0)

    def by_token(x):
        head = x[:prompt_rows].reshape(G_LINE, sh.part, -1).transpose(1, 0, 2)
        return jnp.concatenate([head.reshape(prompt_rows, -1), x[prompt_rows:]], 0)

    own_weights = jnp.concatenate([w_gate[0].T, w_up[0].T, w_down[0]], 0)
    spread = [fsdp_count // 8] * 4
    spread[0] += fsdp_count // 2 - sum(spread)

    def run(ring, count):
        for _ in range(count):
            ring.step()

    small = jnp.concatenate(
        [attn_gain, moe_gain, w_router.reshape(-1), bias_table, group_map.astype(BF)]
    )
    small_rows = -(-small.shape[0] // D)
    small_rows = -(-small_rows // 16) * 16
    small = jnp.pad(small, (0, small_rows * D - small.shape[0])).reshape(small_rows, D)
    pack = jnp.concatenate([w_qkv[:, i * D : (i + 1) * D] for i in range(3)] + [w_out, small], 0)
    gathered = dense_gather(pack, group_count)
    own_weights, tail = tied(own_weights, gathered[:, 4 * shard])
    weights = RingGather(own_weights, fsdp_count)
    run(weights, spread[0])
    fused = sh.width == HALF
    out_full = gathered[:, 3 * shard : 4 * shard].reshape(D, D)
    marks = [0, shard, 2 * shard, 2 * shard + shard * expert_count]
    marks += [marks[-1] + bias_table.shape[0]]
    attn_scale = tail[:, marks[0] : marks[1]].reshape(D).astype(F32)
    moe_scale = tail[:, marks[1] : marks[2]].reshape(D).astype(F32)
    router = tail[:, marks[2] : marks[3]].reshape(D, expert_count).astype(F32)
    table = tail[:, marks[3] : marks[4]].reshape(fsdp_count, sh.hp, BUCKETS)
    my_table = lax.dynamic_index_in_dim(table, fsdp_place, 0, keepdims=False).astype(F32)
    groups = tail[:, marks[4]].reshape(-1, fsdp_count)
    my_groups = lax.dynamic_index_in_dim(groups, expert_place, 0, keepdims=False)
    my_groups = my_groups.astype(jnp.int32)
    bucket = buckets.reshape(SPAN_BLOCKS, HALF)

    token_input = by_prompt(inputs)
    grad_rows_low = by_prompt(grad_output)
    routes = by_prompt(routes)
    slot_order = by_prompt(slot_order)

    input_float = token_input.astype(F32)
    if fused:
        by_heads, normed_low = qkv_forward(token_input, attn_scale[None, :], gathered, shard)
    else:
        qkv_full = jnp.concatenate(
            [gathered[:, i * shard : (i + 1) * shard].reshape(D, D) for i in range(3)], 1
        )
        normed, first_pull = jax.vjp(rms_scale, input_float, attn_scale)
        normed_low = normed.astype(BF)
        qkv_rows = jnp.dot(normed_low, qkv_full, preferred_element_type=F32).astype(BF)
        by_heads = (
            qkv_rows.reshape(tok_count, 3, fsdp_count, sh.width)
            .transpose(2, 0, 1, 3)
            .reshape(fsdp_count, tok_count, 3 * sh.width)
        )
    head_qkv = lax.all_to_all(by_heads, "fsdp", split_axis=0, concat_axis=0, tiled=True)
    run(weights, spread[1])
    head_att, att_turned, att_lse = attend_forward(sh, my_groups, my_table, bucket, head_qkv)
    att_back = lax.all_to_all(head_att, "fsdp", split_axis=0, concat_axis=0, tiled=True)
    run(weights, spread[2])
    run(weights, spread[3])
    attn_low = att_back.transpose(1, 0, 2).reshape(tok_count, D)

    middle = input_float + jnp.dot(attn_low, out_full, preferred_element_type=F32)
    second_normed, second_pull = jax.vjp(rms_scale, middle, moe_scale)
    (gate_pair, losses), router_pull = jax.vjp(
        lambda normed_rows, router_rows: route_local(normed_rows, router_rows, routes),
        second_normed,
        router,
    )
    kept_mask = (slot_order < capacity).astype(F32)
    gate_kept = gate_pair * kept_mask
    slot_ids = jnp.arange(slot_total, dtype=jnp.int32)
    slot_place = jnp.where(slot_order < capacity, routes * capacity + slot_order, -1)
    hot = [slot_place[:, k : k + 1] == slot_ids[None, :] for k in range(TOPK)]
    any_low = (hot[0] | hot[1]).astype(BF)
    outgoing = lax.dot_general(
        any_low, second_normed.astype(BF), TN, preferred_element_type=F32
    ).astype(BF)

    def swap_experts(rows):
        rows = rows.reshape(expert_count, capacity, D)
        rows = lax.all_to_all(rows, "expert", split_axis=0, concat_axis=0, tiled=True)
        return rows.reshape(slot_total, D)

    expert_rows = swap_experts(outgoing)
    slot_gate = jnp.sum(
        jnp.where(hot[0], gate_kept[:, 0:1], 0.0) + jnp.where(hot[1], gate_kept[:, 1:2], 0.0),
        axis=0,
    )
    slot_grad = lax.dot_general(any_low, grad_rows_low, TN, preferred_element_type=F32)
    grad_result = swap_experts((slot_gate[:, None] * slot_grad).astype(BF))

    order = block_order(fsdp_count)
    far = order[0]
    blocks = list(weights.chunks[far]) + [weights.chunks[k] for k in order[1:]]
    result_rows, act, turn, hidden = ffn_forward(expert_rows, blocks, ff_shard)
    returned = swap_experts(result_rows)
    grad_rows, grad_gate_pre, grad_up_pre = ffn_backward(
        grad_result, act, turn, blocks, ff_shard
    )
    grad_sent = swap_experts(grad_rows)
    halves = (expert_rows, grad_result, hidden, grad_gate_pre, grad_up_pre)
    early = ffn_weights(*halves, 0, 3, ff_shard)
    late = ffn_weights(*halves, 3, fsdp_count, ff_shard)
    totals = dict(zip(order[1:], early[2:] + late))
    totals[far] = early[:2]

    def part(k):
        return totals[k]

    sums = RingScatter(part, fsdp_count)
    run(sums, spread[0])

    picked = [
        jnp.dot(h.astype(BF), returned, preferred_element_type=F32) for h in hot
    ]
    block_out = middle + gate_kept[:, 0:1] * picked[0] + gate_kept[:, 1:2] * picked[1]
    output = by_token(block_out.astype(BF))
    grad_final = grad_rows_low.astype(F32)
    grad_pair = (
        jnp.stack([jnp.sum(grad_final * p, axis=-1) for p in picked], -1) * kept_mask
    )
    grad_second = jnp.dot(any_low, grad_sent, preferred_element_type=F32)
    loss_weights = jnp.array([ZLOSS_FACTOR, BALANCE_FACTOR], F32) / group_count
    router_normed, grad_router = router_pull((grad_pair, loss_weights))
    grad_middle_part, grad_moe_gain = second_pull(grad_second + router_normed)
    grad_middle = grad_final + grad_middle_part
    grad_branch = grad_middle.astype(BF)
    grad_attn = lax.dot_general(grad_branch, out_full, NT, preferred_element_type=F32)
    grad_attn = grad_attn.astype(BF)
    head_grad = (
        grad_attn.reshape(tok_count, fsdp_count, sh.width).transpose(1, 0, 2)
    )
    head_grad = lax.all_to_all(head_grad, "fsdp", split_axis=0, concat_axis=0, tiled=True)
    run(sums, spread[1])
    head_grad = sums.tie(head_grad)
    head_dqkv, head_table = attend_backward(
        sh, my_groups, my_table, bucket, head_qkv, head_grad, att_turned, att_lse
    )
    run(sums, spread[2])
    head_dqkv = sums.tie(head_dqkv)
    back_dqkv = lax.all_to_all(head_dqkv, "fsdp", split_axis=0, concat_axis=0, tiled=True)
    sums.step()
    run(sums, spread[3] - 1)
    expert_sums = sums.finish()
    grad_gate = expert_sums[:ff_shard].T
    grad_up = expert_sums[ff_shard : 2 * ff_shard].T
    grad_down = expert_sums[2 * ff_shard :]
    grad_out_w = lax.dot_general(attn_low, grad_branch, TN, preferred_element_type=F32)

    def rows_of(x):
        return x.astype(BF).reshape(group_count, shard, -1)

    place_table = (jnp.arange(fsdp_count) == fsdp_place).astype(F32)
    whole_table = place_table[:, None] * head_table[:, 0][None, :]
    if fused:
        kept = jnp.pad(rows_of(grad_out_w), ((0, 0), (3 * shard, small_rows), (0, 0)))
        kept, grad_inputs, gains = qkv_backward(
            back_dqkv, normed_low, gathered, token_input, attn_scale[None, :], grad_middle, kept,
            shard,
        )
        grad_attn_gain = gains[0]
    else:
        grad_qkv = (
            back_dqkv.reshape(fsdp_count, tok_count, 3, sh.width)
            .transpose(1, 2, 0, 3)
            .reshape(tok_count, 3 * D)
        )
        grad_qkv_w = lax.dot_general(normed_low, grad_qkv, TN, preferred_element_type=F32)
        grad_normed = lax.dot_general(grad_qkv, qkv_full, NT, preferred_element_type=F32)
        grad_input_part, grad_attn_gain = first_pull(grad_normed)
        grad_inputs = grad_middle + grad_input_part
        parts = [rows_of(grad_qkv_w[:, i * D : (i + 1) * D]) for i in range(3)]
        kept = jnp.concatenate(parts + [rows_of(grad_out_w)], 1)
        kept = jnp.pad(kept, ((0, 0), (0, small_rows), (0, 0)))
    smalls = [grad_attn_gain, grad_moe_gain, grad_router, whole_table.reshape(-1)]
    smalls = jnp.concatenate([p.astype(BF).reshape(group_count, -1) for p in smalls], 1)
    smalls = jnp.pad(smalls, ((0, 0), (0, small_rows * D - smalls.shape[1])))
    smalls = smalls.reshape(group_count, small_rows, D)
    sums_dense = dense_sum(lax.dynamic_update_slice(kept, smalls, (0, 4 * shard, 0)))
    grad_inputs = by_token(grad_inputs)
    sum_qkv = jnp.concatenate([sums_dense[i * shard : (i + 1) * shard] for i in range(3)], 1)
    sum_out = sums_dense[3 * shard : 4 * shard]
    sum_small = sums_dense[4 * shard]
    sum_attn = sum_small[marks[0] : marks[1]]
    sum_moe = sum_small[marks[1] : marks[2]]
    sum_router = sum_small[marks[2] : marks[3]].reshape(shard, expert_count)
    sum_table = sum_small[marks[3] : marks[4]]
    return (
        output,
        losses[None, :],
        grad_inputs,
        sum_qkv,
        sum_out,
        sum_attn,
        sum_moe,
        sum_router,
        sum_table,
        grad_gate[None],
        grad_up[None],
        grad_down[None],
    )


def solution(mesh):
    rows = P(("expert", "fsdp"), None)
    flat = P(("expert", "fsdp"))
    cols = P("expert", None, "fsdp")
    deep = P("expert", "fsdp", None)
    in_specs = (
        rows, rows, rows, flat, flat, rows, flat, cols, cols, deep, rows, rows, flat, P(), rows,
    )
    out_specs = (rows, rows, rows, rows, rows, flat, flat, rows, flat, cols, cols, deep)

    return jax.shard_map(local, mesh=mesh, in_specs=in_specs, out_specs=out_specs, check_vma=False)
```

```python
import functools

import jax
import jax.numpy as jnp
from jax import lax
from jax.experimental import pallas as pl
from jax.experimental.pallas import tpu as pltpu
from jax.sharding import PartitionSpec as P


D = 1024
HEADS = 16
HDIM = 64
BUCKETS = 32
TOPK = 2
PLEN = 1024
CLEN = 128
G_LINE = 2

EPSILON = 1e-06
ZLOSS_FACTOR = 0.001
BALANCE_FACTOR = 0.01
MASK_VALUE = -1e30
LOG2E = 1.4426950408889634
HIGHEST = lax.Precision.HIGHEST
TILE = 256
HALF = 128
SPAN_BLOCKS = (PLEN + CLEN) // HALF
BF = jnp.bfloat16
F32 = jnp.float32
NT = (((1,), (1,)), ((), ()))
TN = (((0,), (0,)), ((), ()))


def rms_scale(values, scale_row):
    inverse = lax.rsqrt(jnp.mean(values * values, axis=-1, keepdims=True) + EPSILON)
    return values * inverse * scale_row


def route_local(normed, router, routes):
    logits = jnp.dot(normed, router, precision=HIGHEST)
    log_total = jax.nn.logsumexp(logits, axis=-1)
    chances = jnp.exp(logits - log_total[:, None])
    expert_ids = jnp.arange(router.shape[1], dtype=jnp.int32)
    first_hot = (routes[:, 0:1] == expert_ids[None, :]).astype(F32)
    second_hot = (routes[:, 1:2] == expert_ids[None, :]).astype(F32)
    first_chance = jnp.sum(chances * first_hot, axis=-1)
    second_chance = jnp.sum(chances * second_hot, axis=-1)
    both_chances = first_chance + second_chance
    gate_pair = jnp.stack([first_chance / both_chances, second_chance / both_chances], -1)
    z_loss = jnp.mean(log_total * log_total)
    expert_share = jnp.sum(first_hot + second_hot, axis=0) / (TOPK * routes.shape[0])
    balance = router.shape[1] * jnp.sum(expert_share * jnp.mean(chances, axis=0))
    return (gate_pair, jnp.stack([z_loss, balance]))


class Shape:
    def __init__(self, fsdp_count):
        self.srcs = fsdp_count
        self.hp = HEADS // fsdp_count
        self.width = self.hp * HDIM
        self.part = PLEN // fsdp_count
        self.rows = G_LINE * self.part + CLEN
        self.spt = TILE // self.part
        self.tiles = PLEN // TILE
        self.pairs = fsdp_count // 2
        self.prompt_pairs = self.pairs // G_LINE
        self.units = G_LINE * self.tiles + self.pairs


def order_conts(sh, group_ref, perm_ref):
    counts = [jnp.int32(0), jnp.int32(sh.srcs // G_LINE)]
    for c in range(sh.srcs):
        first = group_ref[c] == 0
        perm_ref[jnp.where(first, counts[0], counts[1])] = jnp.int32(c)
        step = first.astype(jnp.int32)
        counts = [counts[0] + step, counts[1] + 1 - step]


def build_bias(sh, table_ref, bucket_ref, bias_ref):
    bucket = bucket_ref[...]
    for h in range(sh.hp):
        dist = jnp.zeros(bucket.shape, F32)
        for b in range(BUCKETS):
            dist = jnp.where(bucket == b, table_ref[h, b] * LOG2E, dist)
        bias_ref[h, 0] = jnp.full((HALF, HALF), MASK_VALUE, F32)
        before = jnp.full((1, HALF), MASK_VALUE, F32)
        for n in range(SPAN_BLOCKS):
            now = dist[n : n + 1, :]
            both = jnp.broadcast_to(jnp.concatenate([before, now], axis=1), (HALF, 2 * HALF))
            turned = pltpu.roll(both, HALF, 1, stride=1, stride_axis=0)
            bias_ref[h, 1 + n] = turned[:, :HALF]
            before = now


def head_mask(sh, h):
    if sh.hp == 1:
        return None
    lane = lax.broadcasted_iota(jnp.int32, (1, sh.width), 1)
    return (lane >= h * HDIM) & (lane < (h + 1) * HDIM)


def only_head(sh, h, x):
    mask = head_mask(sh, h)
    return x if mask is None else jnp.where(mask, x, jnp.zeros_like(x))


def prompt_rows_of(sh, ref, g, t, part):
    lanes = slice(part * sh.width, (part + 1) * sh.width)
    start = pl.multiple_of(g * sh.part, sh.part)
    return jnp.concatenate(
        [ref[t * sh.spt + s, pl.ds(start, sh.part), lanes] for s in range(sh.spt)], axis=0
    )


def cont_rows_of(sh, ref, c, part):
    lanes = slice(part * sh.width, (part + 1) * sh.width)
    return ref[c, G_LINE * sh.part :, lanes]


def put_prompt_rows(sh, ref, g, t, part, value):
    lanes = slice(part * sh.width, (part + 1) * sh.width)
    start = pl.multiple_of(g * sh.part, sh.part)
    for s in range(sh.spt):
        ref[t * sh.spt + s, pl.ds(start, sh.part), lanes] = value[
            s * sh.part : (s + 1) * sh.part
        ].astype(ref.dtype)


def transpose_low(x):
    return x.astype(F32).T.astype(BF)


def add_bias(scores, bias_ref, h, base, step_q):
    rows = []
    for a in range(2):
        cols = []
        for b in range(2):
            part = scores[a * HALF : (a + 1) * HALF, b * HALF : (b + 1) * HALF]
            cols.append(part * LOG2E + bias_ref[h, base + b * step_q - a])
        rows.append(jnp.concatenate(cols, axis=1))
    return jnp.concatenate(rows, axis=0)


def fold_max(x):
    return jnp.max(x.reshape(-1, 8, x.shape[-1]), axis=0)


def fold_sum(x):
    return jnp.sum(x.reshape(-1, 8, x.shape[-1]), axis=0)


def attn_forward_kernel(
    sh, group_ref, table_ref, bucket_ref, x_ref, o_ref, ot_ref, lse_ref, bias, vt, vtc, sc, perm
):
    order_conts(sh, group_ref, perm)
    build_bias(sh, table_ref, bucket_ref, bias)

    def make_vt(i, _):
        g, t = i // sh.tiles, lax.rem(i, sh.tiles)
        vt[i] = transpose_low(prompt_rows_of(sh, x_ref, g, t, 2))
        return 0

    lax.fori_loop(0, G_LINE * sh.tiles, make_vt, 0)

    def make_vtc(c, _):
        vtc[c] = transpose_low(cont_rows_of(sh, x_ref, c, 2))
        return 0

    lax.fori_loop(0, sh.srcs, make_vtc, 0)

    def scores_tile(keys, qh, base, step_q, kt, peaks):
        out = []
        for h in range(sh.hp):
            s = lax.dot_general(keys, qh[h], NT, preferred_element_type=F32)
            s = add_bias(s, bias, h, base, step_q)
            sc[h, pl.ds(pl.multiple_of(kt * TILE, TILE), TILE), :] = s
            out.append(jnp.maximum(peaks[h], fold_max(s)))
        return tuple(out)

    def value_tile(g, kt, peaks, carry):
        out = []
        for h in range(sh.hp):
            total, acc = carry[h]
            p = jnp.exp2(sc[h, pl.ds(pl.multiple_of(kt * TILE, TILE), TILE), :] - peaks[h])
            total = total + fold_sum(p)
            values = vt[g * sh.tiles + kt, h * HDIM : (h + 1) * HDIM, :]
            acc = acc + jnp.dot(values, p.astype(BF), preferred_element_type=F32)
            out.append((total, acc))
        return tuple(out)

    first_peaks = tuple(jnp.full((8, TILE), MASK_VALUE, F32) for _ in range(sh.hp))
    first_carry = tuple(
        (jnp.zeros((8, TILE), F32), jnp.zeros((HDIM, TILE), F32)) for _ in range(sh.hp)
    )

    def finish(unit, peaks, carry):
        outs = []
        for h in range(sh.hp):
            total = jnp.sum(carry[h][0], axis=0, keepdims=True)
            outs.append(carry[h][1] / total)
            lse_ref[unit, h : h + 1, :] = peaks[h] + jnp.log2(total)
        whole = jnp.concatenate(outs, axis=0) if sh.hp > 1 else outs[0]
        ot_ref[unit] = whole
        return whole.T

    def prompt_unit(i, _):
        g, qt = i // sh.tiles, lax.rem(i, sh.tiles)
        q = prompt_rows_of(sh, x_ref, g, qt, 0) * BF(HDIM**-0.5)
        qh = [only_head(sh, h, q) for h in range(sh.hp)]

        def first(kt, peaks):
            keys = prompt_rows_of(sh, x_ref, g, kt, 1)
            return scores_tile(keys, qh, 2 * (qt - kt) + 1, 1, kt, peaks)

        peaks = lax.fori_loop(0, qt + 1, first, first_peaks)
        peaks = [jnp.max(p, axis=0, keepdims=True) for p in peaks]
        carry = lax.fori_loop(0, qt + 1, lambda kt, c: value_tile(g, kt, peaks, c), first_carry)
        put_prompt_rows(sh, o_ref, g, qt, 0, finish(i, peaks, carry))
        return 0

    lax.fori_loop(0, G_LINE * sh.tiles, prompt_unit, 0)

    def cont_unit(i, _):
        conts = [perm[2 * i], perm[2 * i + 1]]
        g = i // sh.prompt_pairs
        q = jnp.concatenate([cont_rows_of(sh, x_ref, c, 0) for c in conts], axis=0)
        q = q * BF(HDIM**-0.5)
        qh = [only_head(sh, h, q) for h in range(sh.hp)]

        def first(kt, peaks):
            keys = prompt_rows_of(sh, x_ref, g, kt, 1)
            return scores_tile(keys, qh, SPAN_BLOCKS - 2 * kt, 0, kt, peaks)

        peaks = lax.fori_loop(0, sh.tiles, first, first_peaks)
        own = []
        next_peaks = []
        for h in range(sh.hp):
            parts = []
            for b in range(2):
                keys = cont_rows_of(sh, x_ref, conts[b], 1)
                s = lax.dot_general(
                    keys, qh[h][b * HALF : (b + 1) * HALF], NT, preferred_element_type=F32
                )
                parts.append(s * LOG2E + bias[h, 1])
            own.append(jnp.concatenate(parts, axis=1))
            next_peaks.append(jnp.maximum(peaks[h], fold_max(own[h])))
        peaks = [jnp.max(p, axis=0, keepdims=True) for p in next_peaks]
        start = []
        for h in range(sh.hp):
            p = jnp.exp2(own[h] - peaks[h])
            low = p.astype(BF)
            acc = jnp.concatenate(
                [
                    jnp.dot(
                        vtc[conts[b], h * HDIM : (h + 1) * HDIM, :],
                        low[:, b * HALF : (b + 1) * HALF],
                        preferred_element_type=F32,
                    )
                    for b in range(2)
                ],
                axis=1,
            )
            start.append((fold_sum(p), acc))
        carry = lax.fori_loop(
            0, sh.tiles, lambda kt, c: value_tile(g, kt, peaks, c), tuple(start)
        )
        done = finish(G_LINE * sh.tiles + i, peaks, carry)
        for b in range(2):
            o_ref[conts[b], G_LINE * sh.part :, :] = done[b * HALF : (b + 1) * HALF].astype(BF)
        return 0

    lax.fori_loop(0, sh.pairs, cont_unit, 0)


def attn_backward_kernel(
    sh,
    group_ref,
    table_ref,
    bucket_ref,
    x_ref,
    do_ref,
    ot_ref,
    lse_ref,
    dx_ref,
    dtable_ref,
    bias,
    dbias,
    ktr,
    ktc,
    dk,
    dv,
    perm,
):
    order_conts(sh, group_ref, perm)
    build_bias(sh, table_ref, bucket_ref, bias)
    dbias[...] = jnp.zeros_like(dbias)
    dk[...] = jnp.zeros_like(dk)
    dv[...] = jnp.zeros_like(dv)

    def make_kt(i, _):
        g, t = i // sh.tiles, lax.rem(i, sh.tiles)
        ktr[i] = transpose_low(prompt_rows_of(sh, x_ref, g, t, 1))
        return 0

    lax.fori_loop(0, G_LINE * sh.tiles, make_kt, 0)

    def make_ktc(c, _):
        ktc[c] = transpose_low(cont_rows_of(sh, x_ref, c, 1))
        return 0

    lax.fori_loop(0, sh.srcs, make_ktc, 0)

    def inner_terms(unit, do):
        outs = []
        turned = do.astype(F32).T
        for h in range(sh.hp):
            rows = slice(h * HDIM, (h + 1) * HDIM)
            prod = ot_ref[unit, rows, :] * turned[rows, :]
            outs.append(jnp.sum(prod, axis=0, keepdims=True))
        return outs

    def grads_tile(g, kt, qh, doh, lse, inner, base, step_q, dqs):
        keys = prompt_rows_of(sh, x_ref, g, kt, 1)
        values = prompt_rows_of(sh, x_ref, g, kt, 2)
        slot = g * sh.tiles + kt
        out = []
        dkey = dvalue = None
        for h in range(sh.hp):
            s = lax.dot_general(keys, qh[h], NT, preferred_element_type=F32)
            dp = lax.dot_general(values, doh[h], NT, preferred_element_type=F32)
            p = jnp.exp2(add_bias(s, bias, h, base, step_q) - lse[h])
            ds = p * (dp - inner[h])
            for a in range(2):
                for b in range(2):
                    dbias[h, base + b * step_q - a] += ds[
                        a * HALF : (a + 1) * HALF, b * HALF : (b + 1) * HALF
                    ]
            low = ds.astype(BF)
            more_k = jnp.dot(low, qh[h], preferred_element_type=F32)
            more_v = jnp.dot(p.astype(BF), doh[h], preferred_element_type=F32)
            dkey = more_k if dkey is None else dkey + more_k
            dvalue = more_v if dvalue is None else dvalue + more_v
            turned = ktr[slot, h * HDIM : (h + 1) * HDIM, :]
            out.append(dqs[h] + jnp.dot(turned, low, preferred_element_type=F32))
        dk[slot] += dkey
        dv[slot] += dvalue
        return tuple(out)

    def finish(dqs):
        whole = jnp.concatenate(dqs, axis=0) if sh.hp > 1 else dqs[0]
        return whole.T * (HDIM**-0.5)

    first_dq = tuple(jnp.zeros((HDIM, TILE), F32) for _ in range(sh.hp))

    def prompt_unit(i, _):
        g, qt = i // sh.tiles, lax.rem(i, sh.tiles)
        q = prompt_rows_of(sh, x_ref, g, qt, 0) * BF(HDIM**-0.5)
        do = prompt_rows_of(sh, do_ref, g, qt, 0)
        qh = [only_head(sh, h, q) for h in range(sh.hp)]
        doh = [only_head(sh, h, do) for h in range(sh.hp)]
        inner = inner_terms(i, do)
        lse = [lse_ref[i, h : h + 1, :] for h in range(sh.hp)]

        def body(kt, dqs):
            return grads_tile(g, kt, qh, doh, lse, inner, 2 * (qt - kt) + 1, 1, dqs)

        dqs = lax.fori_loop(0, qt + 1, body, first_dq)
        put_prompt_rows(sh, dx_ref, g, qt, 0, finish(dqs))
        return 0

    lax.fori_loop(0, G_LINE * sh.tiles, prompt_unit, 0)

    def cont_unit(i, _):
        conts = [perm[2 * i], perm[2 * i + 1]]
        unit = G_LINE * sh.tiles + i
        g = i // sh.prompt_pairs
        q = jnp.concatenate([cont_rows_of(sh, x_ref, c, 0) for c in conts], axis=0)
        q = q * BF(HDIM**-0.5)
        do = jnp.concatenate([cont_rows_of(sh, do_ref, c, 0) for c in conts], axis=0)
        qh = [only_head(sh, h, q) for h in range(sh.hp)]
        doh = [only_head(sh, h, do) for h in range(sh.hp)]
        inner = inner_terms(unit, do)
        lse = [lse_ref[unit, h : h + 1, :] for h in range(sh.hp)]

        def body(kt, dqs):
            return grads_tile(g, kt, qh, doh, lse, inner, SPAN_BLOCKS - 2 * kt, 0, dqs)

        dqs = lax.fori_loop(0, sh.tiles, body, first_dq)
        more = [[None] * 2 for _ in range(sh.hp)]
        for b in range(2):
            cols = slice(b * HALF, (b + 1) * HALF)
            keys = cont_rows_of(sh, x_ref, conts[b], 1)
            values = cont_rows_of(sh, x_ref, conts[b], 2)
            dkey = dvalue = None
            for h in range(sh.hp):
                s = lax.dot_general(keys, qh[h][cols], NT, preferred_element_type=F32)
                dp = lax.dot_general(values, doh[h][cols], NT, preferred_element_type=F32)
                p = jnp.exp2(s * LOG2E + bias[h, 1] - lse[h][:, cols])
                ds = p * (dp - inner[h][:, cols])
                dbias[h, 1] += ds
                low = ds.astype(BF)
                more_k = jnp.dot(low, qh[h][cols], preferred_element_type=F32)
                more_v = jnp.dot(p.astype(BF), doh[h][cols], preferred_element_type=F32)
                dkey = more_k if dkey is None else dkey + more_k
                dvalue = more_v if dvalue is None else dvalue + more_v
                turned = ktc[conts[b], h * HDIM : (h + 1) * HDIM, :]
                more[h][b] = jnp.dot(turned, low, preferred_element_type=F32)
            w = sh.width
            dx_ref[conts[b], G_LINE * sh.part :, w : 2 * w] = dkey.astype(BF)
            dx_ref[conts[b], G_LINE * sh.part :, 2 * w :] = dvalue.astype(BF)
        dqs = [dqs[h] + jnp.concatenate(more[h], axis=1) for h in range(sh.hp)]
        done = finish(dqs)
        for b in range(2):
            dx_ref[conts[b], G_LINE * sh.part :, : sh.width] = done[
                b * HALF : (b + 1) * HALF
            ].astype(BF)
        return 0

    lax.fori_loop(0, sh.pairs, cont_unit, 0)

    def put_keys(i, _):
        g, t = i // sh.tiles, lax.rem(i, sh.tiles)
        put_prompt_rows(sh, dx_ref, g, t, 1, dk[i])
        put_prompt_rows(sh, dx_ref, g, t, 2, dv[i])
        return 0

    lax.fori_loop(0, G_LINE * sh.tiles, put_keys, 0)

    bucket = bucket_ref[...]
    key_row = lax.broadcasted_iota(jnp.int32, (HALF, 2 * HALF), 0)
    for h in range(sh.hp):
        spread = []
        for n in range(SPAN_BLOCKS):
            wide = jnp.concatenate(
                [jnp.zeros((HALF, HALF), F32), dbias[h, 1 + n]], axis=1
            )
            for bit in range(7):
                moved = pltpu.roll(wide, 2 * HALF - (1 << bit), 1)
                wide = jnp.where((key_row & (1 << bit)) != 0, moved, wide)
            spread.append(jnp.sum(wide, axis=0, keepdims=True))
        rows = []
        for n in range(SPAN_BLOCKS):
            row = spread[n][:, HALF:]
            if n + 1 < SPAN_BLOCKS:
                row = row + spread[n + 1][:, :HALF]
            rows.append(row)
        by_dist = jnp.concatenate(rows, axis=0)
        sums = [
            jnp.sum(jnp.where(bucket == b, by_dist, 0.0), axis=0, keepdims=True)
            for b in range(BUCKETS)
        ]
        lanes = jnp.concatenate(sums, axis=0)
        dtable_ref[h * BUCKETS : (h + 1) * BUCKETS, :] = jnp.broadcast_to(
            jnp.sum(lanes, axis=1, keepdims=True), (BUCKETS, HALF)
        )


SMEM_SPEC = pl.BlockSpec(memory_space=pltpu.SMEM)
VMEM_SPEC = pl.BlockSpec(memory_space=pltpu.VMEM)
GRANT = 48 * 1024 * 1024


def attend_forward(sh, group, table, bucket, x):
    return pl.pallas_call(
        functools.partial(attn_forward_kernel, sh),
        out_shape=(
            jax.ShapeDtypeStruct((sh.srcs, sh.rows, sh.width), BF),
            jax.ShapeDtypeStruct((sh.units, sh.width, TILE), F32),
            jax.ShapeDtypeStruct((sh.units, 8, TILE), F32),
        ),
        in_specs=[SMEM_SPEC, SMEM_SPEC, VMEM_SPEC, VMEM_SPEC],
        out_specs=(VMEM_SPEC, VMEM_SPEC, VMEM_SPEC),
        scratch_shapes=[
            pltpu.VMEM((sh.hp, SPAN_BLOCKS + 1, HALF, HALF), F32),
            pltpu.VMEM((G_LINE * sh.tiles, sh.width, TILE), BF),
            pltpu.VMEM((sh.srcs, sh.width, HALF), BF),
            pltpu.VMEM((sh.hp, PLEN, TILE), F32),
            pltpu.SMEM((sh.srcs,), jnp.int32),
        ],
        compiler_params=pltpu.CompilerParams(vmem_limit_bytes=GRANT),
        cost_estimate=pl.CostEstimate(
            flops=10**10, bytes_accessed=8 * 10**6, transcendentals=5 * 10**6
        ),
        name="attend_forward",
    )(group, table, bucket, x)


def attend_backward(sh, group, table, bucket, x, do, ot, lse):
    return pl.pallas_call(
        functools.partial(attn_backward_kernel, sh),
        out_shape=(
            jax.ShapeDtypeStruct((sh.srcs, sh.rows, 3 * sh.width), BF),
            jax.ShapeDtypeStruct((sh.hp * BUCKETS, HALF), F32),
        ),
        in_specs=[SMEM_SPEC, SMEM_SPEC, VMEM_SPEC, VMEM_SPEC, VMEM_SPEC, VMEM_SPEC, VMEM_SPEC],
        out_specs=(VMEM_SPEC, VMEM_SPEC),
        scratch_shapes=[
            pltpu.VMEM((sh.hp, SPAN_BLOCKS + 1, HALF, HALF), F32),
            pltpu.VMEM((sh.hp, SPAN_BLOCKS + 1, HALF, HALF), F32),
            pltpu.VMEM((G_LINE * sh.tiles, sh.width, TILE), BF),
            pltpu.VMEM((sh.srcs, sh.width, HALF), BF),
            pltpu.VMEM((G_LINE * sh.tiles, TILE, sh.width), F32),
            pltpu.VMEM((G_LINE * sh.tiles, TILE, sh.width), F32),
            pltpu.SMEM((sh.srcs,), jnp.int32),
        ],
        compiler_params=pltpu.CompilerParams(vmem_limit_bytes=GRANT),
        cost_estimate=pl.CostEstimate(
            flops=2 * 10**10, bytes_accessed=12 * 10**6, transcendentals=5 * 10**6
        ),
        name="attend_backward",
    )(group, table, bucket, x, do, ot, lse)


def ring_order(count):
    deep, wide = 4, count // 4
    order = [a * wide for a in range(deep)]
    for turn, a in enumerate(reversed(range(deep))):
        row = [a * wide + b for b in range(1, wide)]
        order += row if turn % 2 == 0 else row[::-1]
    return order


def ring_hop(x, count, step):
    ring = ring_order(count)
    return lax.ppermute(x, "fsdp", [(ring[i], ring[(i + step) % count]) for i in range(count)])


def tied(*values):
    return lax.optimization_barrier(values)


class RingGather:
    def __init__(self, own, count):
        self.count = count
        self.chunks = [None] * count
        self.chunks[0] = own
        self.right = self.left = own
        self.done = 0
        self.steps = count // 2

    def step(self):
        self.done += 1
        s = self.done
        if s < self.steps:
            self.right = ring_hop(self.right, self.count, 1)
            self.left = ring_hop(self.left, self.count, -1)
        else:
            half = self.right.shape[0] // 2
            self.right = ring_hop(self.right[:half], self.count, 1)
            self.left = ring_hop(self.left[half:], self.count, -1)
        self.keep()

    def keep(self):
        s = self.done
        if s < self.steps:
            self.chunks[self.count - s] = self.right
            self.chunks[s] = self.left
        else:
            self.chunks[s] = (self.right, self.left)


class RingScatter:
    def __init__(self, part, count):
        self.part, self.count = part, count
        self.right = self.left = None
        self.done = 0
        self.steps = count // 2

    def step(self, after=None):
        count, s = self.count, self.done
        away = self.steps - s
        if s == 0:
            send_left, send_right = self.part(away)
        else:
            near_left = self.part(count - away).astype(F32)
            near_right = self.part(away).astype(F32)
            if s == 1:
                half = near_left.shape[0] // 2
                send_left = jnp.concatenate(
                    [near_left[:half] + self.left.astype(F32), near_left[half:]], 0
                )
                send_right = jnp.concatenate(
                    [near_right[:half], near_right[half:] + self.right.astype(F32)], 0
                )
            else:
                send_left = near_left + self.left.astype(F32)
                send_right = near_right + self.right.astype(F32)
        send_left, send_right = send_left.astype(BF), send_right.astype(BF)
        if after is not None:
            after, send_left, send_right = tied(after, send_left, send_right)
        self.left = ring_hop(send_left, count, -1)
        self.right = ring_hop(send_right, count, 1)
        self.done += 1
        return after

    def tie(self, value):
        value, self.right, self.left = tied(value, self.right, self.left)
        return value

    def finish(self):
        return self.part(0).astype(F32) + self.right.astype(F32) + self.left.astype(F32)


MESH_ID = pl.DeviceIdType.MESH
DEEP = 4


class Spot:
    def __init__(self):
        e, f = lax.axis_index("expert"), lax.axis_index("fsdp")
        self.x, self.c = e // 2, lax.rem(e, 2)
        self.z, self.y = f // 2, lax.rem(f, 2)
        self.ox, self.oy, self.oc = 1 - self.x, 1 - self.y, 1 - self.c

    def place(self, x=None, y=None, z=None, c=None):
        x = self.x if x is None else x
        y = self.y if y is None else y
        z = self.z if z is None else z
        c = self.c if c is None else c
        return {"expert": x * 2 + c, "fsdp": z * 2 + y}

    def block(self, x, y, z, c):
        return (x * 2 + c) * 8 + z * 2 + y

    def greet(self):
        barrier = pltpu.get_barrier_semaphore()
        for target in (self.place(x=self.ox), self.place(y=self.oy), self.place(c=self.oc)):
            pl.semaphore_signal(barrier, inc=1, device_id=target, device_id_type=MESH_ID)
        for step in (-1, 1):

            @pl.when(self.inside(self.z + step))
            def _(step=step):
                pl.semaphore_signal(
                    barrier, inc=1, device_id=self.along(step), device_id_type=MESH_ID
                )

        pl.semaphore_wait(barrier, 4 + self.z * (DEEP - 1 - self.z) // 2)

    def wrap(self, step):
        return lax.rem(self.z + step + DEEP, DEEP)

    def along(self, step):
        return self.place(z=self.wrap(step))

    def inside(self, z):
        return (z >= 0) & (z < DEEP)


def dense_gather_kernel(cut, x_ref, out_ref, send_sems, recv_sems, own_sem):
    me = Spot()
    rows = x_ref.shape[0]
    spans = [(0, cut), (cut, rows - cut)]
    pending = []

    def view(ref, h):
        return ref.at[pl.ds(*spans[h])]

    def send(src, blk, h, target, cond):
        copy = pltpu.make_async_remote_copy(
            src_ref=src,
            dst_ref=view(out_ref.at[blk], h),
            send_sem=send_sems.at[len(pending)],
            recv_sem=recv_sems.at[blk, h],
            device_id=target,
            device_id_type=MESH_ID,
        )
        pending.append((copy, cond))
        if cond is None:
            copy.start()
        else:
            pl.when(cond)(copy.start)

    def arrive(blk, h, cond):
        copy = pltpu.make_async_remote_copy(
            src_ref=view(out_ref.at[blk], h),
            dst_ref=view(out_ref.at[blk], h),
            send_sem=send_sems.at[0],
            recv_sem=recv_sems.at[blk, h],
            device_id=me.place(c=me.oc),
            device_id_type=MESH_ID,
        )
        if cond is None:
            copy.wait_recv()
        else:
            pl.when(cond)(copy.wait_recv)

    def both(a, b):
        return b if a is None else (a if b is None else a & b)

    by_y, by_x = me.place(y=me.oy), me.place(x=me.ox)
    core = me.place(c=me.oc)
    me.greet()
    mine = me.block(me.x, me.y, me.z, me.c)
    own = pltpu.make_async_copy(x_ref, out_ref.at[mine], own_sem)
    own.start()
    for h in range(2):
        for step in (-1, 1):
            send(view(x_ref, h), mine, h, me.along(step), me.inside(me.z + step))
    for h in range(2):
        for target in (by_y, by_x, core):
            send(view(x_ref, h), mine, h, target, None)

    def line(dist):
        if dist == 0:
            return [(me.z, None, 0)]
        return [(me.wrap(s * dist), me.inside(me.z + s * dist), s) for s in (-1, 1)]

    def from_line(dist):
        for zb, cond, sign in line(dist):
            blk = me.block(me.x, me.y, zb, me.c)
            for h in range(2):
                arrive(blk, h, cond)
                src = view(out_ref.at[blk], h)
                send(src, blk, h, me.along(-sign), both(cond, me.inside(me.z - sign)))
                for target in (by_y, by_x, core):
                    send(src, blk, h, target, cond)

    def from_side(dist):
        for zb, cond, _ in line(dist):
            for h in range(2):
                one = me.block(me.x, me.oy, zb, me.c)
                two = me.block(me.ox, me.y, zb, me.c)
                onward, last = ((one, by_x), two) if h == 0 else ((two, by_y), one)
                arrive(onward[0], h, cond)
                src = view(out_ref.at[onward[0]], h)
                send(src, onward[0], h, onward[1], cond)
                send(src, onward[0], h, core, cond)
                arrive(last, h, cond)
                send(view(out_ref.at[last], h), last, h, core, cond)

    def from_corner(dist):
        for zb, cond, _ in line(dist):
            blk = me.block(me.ox, me.oy, zb, me.c)
            for h in range(2):
                arrive(blk, h, cond)
                send(view(out_ref.at[blk], h), blk, h, core, cond)

    for dist in range(DEEP):
        if dist > 0:
            from_line(dist)
        from_side(dist)
        if dist > 0:
            from_corner(dist - 1)
    from_corner(DEEP - 1)
    for x in range(2):
        for y in range(2):
            for z in range(DEEP):
                for h in range(2):
                    arrive(me.block(x, y, z, me.oc), h, None)
    own.wait()
    for copy, cond in pending:
        if cond is None:
            copy.wait_send()
        else:
            pl.when(cond)(copy.wait_send)


def dense_gather(x, count):
    rows = x.shape[0]
    if count != 32 or lax.axis_size("fsdp") != 2 * DEEP:
        return lax.all_gather(x, ("expert", "fsdp"), axis=0, tiled=False)
    cut = rows // 32 * 16 + 16 * (rows // 16 % 2)
    return pl.pallas_call(
        functools.partial(dense_gather_kernel, cut),
        out_shape=jax.ShapeDtypeStruct((count,) + x.shape, x.dtype),
        in_specs=[pl.BlockSpec(memory_space=pltpu.VMEM)],
        out_specs=pl.BlockSpec(memory_space=pl.ANY),
        scratch_shapes=[
            pltpu.SemaphoreType.DMA((128,)),
            pltpu.SemaphoreType.DMA((count, 2)),
            pltpu.SemaphoreType.DMA,
        ],
        compiler_params=pltpu.CompilerParams(collective_id=0, has_side_effects=True),
        cost_estimate=pl.CostEstimate(
            flops=0, bytes_accessed=100 * 10**6, transcendentals=0
        ),
        name="dense_gather",
    )(x)


def add_into(dst, src):
    def body(i, _):
        at = pl.ds(pl.multiple_of(i * 16, 16), 16)
        dst[at, :] = (dst[at, :].astype(F32) + src[at, :].astype(F32)).astype(BF)
        return 0

    lax.fori_loop(0, dst.shape[0] // 16, body, 0)


def dense_sum_kernel(
    cut, g_ref, out_ref, acc, cbuf, xbuf, ybuf, zbuf, send_sems, recv_sems, load_sems
):
    me = Spot()
    rows = out_ref.shape[0]
    top, low = pl.ds(0, cut), pl.ds(cut, rows - cut)
    pending = []

    def send(src, dst, at, target, cond=None):
        copy = pltpu.make_async_remote_copy(
            src_ref=src,
            dst_ref=dst,
            send_sem=send_sems.at[len(pending)],
            recv_sem=recv_sems.at[at],
            device_id=target,
            device_id_type=MESH_ID,
        )
        pending.append((copy, cond))
        if cond is None:
            copy.start()
        else:
            pl.when(cond)(copy.start)

    def arrive(dst, at):
        pltpu.make_async_remote_copy(
            src_ref=dst,
            dst_ref=dst,
            send_sem=send_sems.at[0],
            recv_sem=recv_sems.at[at],
            device_id=me.place(c=me.oc),
            device_id_type=MESH_ID,
        ).wait_recv()

    by_y, by_x, core = me.place(y=me.oy), me.place(x=me.ox), me.place(c=me.oc)
    me.greet()
    zs = (0, 3, 2, 1)
    loads = []
    for k in range(DEEP):
        for x in range(2):
            at = x * DEEP + k
            theirs = (x * 2 + me.oc) * 8 + zs[k] * 2
            send(g_ref.at[pl.ds(theirs, 2)], cbuf.at[at], at, core)
            ours = (x * 2 + me.c) * 8 + zs[k] * 2
            load = pltpu.make_async_copy(g_ref.at[pl.ds(ours, 2)], acc.at[at], load_sems.at[at])
            load.start()
            loads.append(load)

    def first(k):
        for x in range(2):
            at = x * DEEP + k
            loads[k * 2 + x].wait()
            arrive(cbuf.at[at], at)
            for y in range(2):
                add_into(acc.at[at, y], cbuf.at[at, y])
        base = 8 + k * 6
        for y in range(2):
            send(acc.at[me.ox * DEEP + k, y, top], xbuf.at[k, y, top], base + y, by_x)
        for x in range(2):
            send(acc.at[x * DEEP + k, me.oy, low], ybuf.at[k, x, low], base + 2 + x, by_y)

    def second(k):
        base = 8 + k * 6
        for y in range(2):
            arrive(xbuf.at[k, y, top], base + y)
            add_into(acc.at[me.x * DEEP + k, y, top], xbuf.at[k, y, top])
        for x in range(2):
            arrive(ybuf.at[k, x, low], base + 2 + x)
            add_into(acc.at[x * DEEP + k, me.y, low], ybuf.at[k, x, low])
        send(acc.at[me.x * DEEP + k, me.oy, top], ybuf.at[k, 0, top], base + 4, by_y)
        send(acc.at[me.ox * DEEP + k, me.y, low], xbuf.at[k, 0, low], base + 5, by_x)

    def third(k):
        base = 8 + k * 6
        block = acc.at[me.x * DEEP + k, me.y]
        arrive(ybuf.at[k, 0, top], base + 4)
        add_into(block.at[top], ybuf.at[k, 0, top])
        arrive(xbuf.at[k, 0, low], base + 5)
        add_into(block.at[low], xbuf.at[k, 0, low])

    def along(k, sign, behind):
        zo = zs[k]
        here = behind if sign > 0 else DEEP - 1 - behind
        term = acc.at[me.x * DEEP + k, me.y]
        base = 32 + k * 4 + (sign + 1)
        side = k * 4 + (sign + 1)
        is_here = me.z == here
        for h, at in ((0, top), (1, low)):
            if behind > 0:

                @pl.when(is_here)
                def _(h=h, at=at):
                    arrive(zbuf.at[side + h, at], base + h)
                    add_into(term.at[at], zbuf.at[side + h, at])

            if here != zo:
                send(
                    term.at[at], zbuf.at[side + h, at], base + h, me.along(sign), is_here
                )

    for step in range(DEEP + 6):
        if step < DEEP:
            first(step)
        if 0 <= step - 1 < DEEP:
            second(step - 1)
        if 0 <= step - 2 < DEEP:
            third(step - 2)
        for k in range(DEEP):
            behind = step - 2 - k
            if behind >= 0:
                if behind <= zs[k]:
                    along(k, 1, behind)
                if behind <= DEEP - 1 - zs[k]:
                    along(k, -1, behind)
    block = acc.at[me.x * DEEP + lax.rem(DEEP - me.z, DEEP), me.y]

    def put(i, _):
        at = pl.ds(pl.multiple_of(i * 16, 16), 16)
        out_ref[at, :] = block[at, :].astype(F32)
        return 0

    lax.fori_loop(0, rows // 16, put, 0)
    for copy, cond in pending:
        if cond is None:
            copy.wait_send()
        else:
            pl.when(cond)(copy.wait_send)


def dense_sum(x):
    count, rows, width = x.shape
    if count != 32 or lax.axis_size("fsdp") != 2 * DEEP:
        flat = x.reshape(count * rows, width)
        return lax.psum_scatter(
            flat, ("expert", "fsdp"), scatter_dimension=0, tiled=True
        ).astype(F32)
    cut = rows // 32 * 16 + 16 * (rows // 16 % 2)
    pair = (2 * DEEP, 2, rows, width)
    return pl.pallas_call(
        functools.partial(dense_sum_kernel, cut),
        out_shape=jax.ShapeDtypeStruct((rows, width), F32),
        in_specs=[pl.BlockSpec(memory_space=pl.ANY)],
        out_specs=pl.BlockSpec(memory_space=pltpu.VMEM),
        scratch_shapes=[
            pltpu.VMEM(pair, BF),
            pltpu.VMEM(pair, BF),
            pltpu.VMEM((DEEP, 2, rows, width), BF),
            pltpu.VMEM((DEEP, 2, rows, width), BF),
            pltpu.VMEM((4 * DEEP, rows, width), BF),
            pltpu.SemaphoreType.DMA((72,)),
            pltpu.SemaphoreType.DMA((48,)),
            pltpu.SemaphoreType.DMA((8,)),
        ],
        compiler_params=pltpu.CompilerParams(
            collective_id=1, has_side_effects=True, vmem_limit_bytes=40 * 1024 * 1024
        ),
        cost_estimate=pl.CostEstimate(
            flops=0, bytes_accessed=100 * 10**6, transcendentals=0
        ),
        name="dense_sum",
    )(x)


SLICE = 256
MARGIN = 2


def gelu_terms(x):
    root = 0.7978845608028654
    square = x * x
    t = jnp.tanh(root * (x + 0.044715 * square * x))
    half = 0.5 * (1.0 + t)
    slope = half + 0.5 * x * (1.0 - t * t) * (root * (1.0 + 3 * 0.044715 * square))
    return x * half, slope


def block_order(count):
    far = count // 2
    order = [0]
    for away in range(1, far):
        order += [count - away, away]
    return order + [far]


def chunk_pieces(base, split, ff_shard):
    if not split:
        return [(0, m * ff_shard, m, base, ff_shard) for m in range(3)]
    half = ff_shard // 2
    return [
        (0, 0, 0, base, ff_shard),
        (0, ff_shard, 1, base, half),
        (1, 0, 1, base + half, half),
        (1, half, 2, base, ff_shard),
    ]


def chunk_copies(refs, whole, sems, ff_shard, outward, start=0):
    out = []
    for p, own in enumerate(refs):
        pieces = []
        places = chunk_pieces(p * ff_shard + start, len(own) == 2, ff_shard)
        for n, (src, at, m, row, rows) in enumerate(places):
            block = own[src].at[pl.ds(at, rows)]
            spot = whole.at[m, pl.ds(row, rows)]
            a, b = (spot, block) if outward else (block, spot)
            pieces.append(pltpu.make_async_copy(a, b, sems.at[p, n]))
        out.append(pieces)
    return out


def pair_last(refs):
    return [refs[k : k + 1] for k in range(len(refs) - 2)] + [refs[-2:]]


def single(refs):
    return [refs[k : k + 1] for k in range(len(refs))]


def fetch_weights(blocks, whole, sems, ff_shard, t, first=0, base=0, margin=0):
    start = first * ff_shard - (base - margin) * SLICE
    copies = chunk_copies(blocks, whole, sems, ff_shard, False, start)
    ahead = 3

    @pl.when(t == 0)
    def _():
        for pieces in copies[:ahead]:
            for c in pieces:
                c.start()

    for p, pieces in enumerate(copies):
        more = copies[p + ahead] if p + ahead < len(copies) else []

        @pl.when(t == max((first + p) * ff_shard // SLICE - base, 0))
        def _(pieces=pieces, more=more):
            for c in more:
                c.start()
            for c in pieces:
                c.wait()


def ffn_forward_kernel(count, near, ff_shard, last, rows_ref, *refs):
    if last:
        chunks, rest = refs[:3], refs[3:]
        before_ref, rest = rest[0], rest[4:]
    else:
        chunks, rest = refs[: count - 1], refs[count - 1 :]
    out_ref, act_ref, turn_ref, hid_ref, whole, acc, sems = rest
    t = pl.program_id(0)
    if last:
        fetch_weights(pair_last(chunks), whole, sems, ff_shard, t, count - 2, near, MARGIN)
        at = pl.ds(pl.multiple_of((t + MARGIN) * SLICE, SLICE), SLICE)
    else:
        fetch_weights(single(chunks), whole, sems, ff_shard, t)
        at = pl.ds(pl.multiple_of(t * SLICE, SLICE), SLICE)
    rows = rows_ref[...]
    gate = lax.dot_general(rows, whole[0, at], NT, preferred_element_type=F32)
    up = lax.dot_general(rows, whole[1, at], NT, preferred_element_type=F32)
    act, slope = gelu_terms(gate)
    hidden = (act * up).astype(BF)
    act_ref[0] = act
    turn_ref[0] = up * slope
    hid_ref[0] = hidden
    more = jnp.dot(hidden, whole[2, at], preferred_element_type=F32)

    @pl.when(t == 0)
    def _():
        acc[...] = before_ref[...] + more if last else more

    @pl.when(t > 0)
    def _():
        acc[...] += more

    @pl.when(t == pl.num_programs(0) - 1)
    def _():
        out_ref[...] = acc[...].astype(out_ref.dtype)


def ffn_backward_kernel(count, ff_shard, grad_ref, act_ref, turn_ref, *refs):
    chunks, rest = refs[: count + 1], refs[count + 1 :]
    out_ref, dgate_ref, dup_ref, whole, acc, sems = rest
    t = pl.program_id(0)
    fetch_weights(pair_last(chunks), whole, sems, ff_shard, t)
    at = pl.ds(pl.multiple_of(t * SLICE, SLICE), SLICE)
    dhid = lax.dot_general(grad_ref[...], whole[2, at], NT, preferred_element_type=F32)
    dgate = (dhid * turn_ref[0]).astype(BF)
    dup = (dhid * act_ref[0]).astype(BF)
    dgate_ref[0] = dgate
    dup_ref[0] = dup
    more = jnp.dot(
        jnp.concatenate([dgate, dup], axis=1),
        jnp.concatenate([whole[0, at], whole[1, at]], axis=0),
        preferred_element_type=F32,
    )

    @pl.when(t == 0)
    def _():
        acc[...] = more

    @pl.when(t > 0)
    def _():
        acc[...] += more

    @pl.when(t == pl.num_programs(0) - 1)
    def _():
        out_ref[...] = acc[...].astype(BF)


def ffn_weights_kernel(
    lead, first, ff_shard, rows_ref, grad_ref, hid_ref, dgate_ref, dup_ref, *refs
):
    chunks, (whole, sems) = refs[:-2], refs[-2:]
    chunks = pair_last(chunks) if lead else single(chunks)
    base = first * ff_shard // SLICE
    t = pl.program_id(0)
    at = pl.ds(pl.multiple_of(t * SLICE, SLICE), SLICE)
    for m, (left, right) in enumerate(
        ((dgate_ref, rows_ref), (dup_ref, rows_ref), (hid_ref, grad_ref))
    ):
        whole[m, at] = lax.dot_general(
            left[0], right[...], TN, preferred_element_type=F32
        ).astype(BF)
    copies = chunk_copies(
        chunks, whole, sems, ff_shard, True, first * ff_shard - base * SLICE
    )
    for p, pieces in enumerate(copies):

        @pl.when(t == ((first + p + 1) * ff_shard - 1) // SLICE - base)
        def _(pieces=pieces):
            for c in pieces:
                c.start()

    @pl.when(t == pl.num_programs(0) - 1)
    def _():
        for pieces in copies:
            for c in pieces:
                c.wait()


def fixed(shape):
    return pl.BlockSpec(shape, lambda t: (0,) * len(shape))


def stepped(shape):
    return pl.BlockSpec(shape, lambda t: (t, 0, 0))


ANY_SPEC = pl.BlockSpec(memory_space=pl.ANY)


def ffn_cost(slots, hidden):
    work = 6 * slots * D * hidden
    return pl.CostEstimate(flops=work, bytes_accessed=40 * 10**6, transcendentals=slots * hidden)


def ffn_params():
    return pltpu.CompilerParams(
        dimension_semantics=("arbitrary",), vmem_limit_bytes=60 * 1024 * 1024
    )


def ffn_forward(rows, chunks, ff_shard):
    slots, count = rows.shape[0], len(chunks) - 1
    hidden = count * ff_shard
    steps = hidden // SLICE
    near = (count - 1) * ff_shard // SLICE
    tiles = [jax.ShapeDtypeStruct((steps, slots, SLICE), kind) for kind in (F32, F32, BF)]
    part, *kept = pl.pallas_call(
        functools.partial(ffn_forward_kernel, count, near, ff_shard, False),
        grid=(near,),
        out_shape=(jax.ShapeDtypeStruct((slots, D), F32), *tiles),
        in_specs=[fixed((slots, D))] + [ANY_SPEC] * (count - 1),
        out_specs=(fixed((slots, D)),) + (stepped((1, slots, SLICE)),) * 3,
        scratch_shapes=[
            pltpu.VMEM((3, hidden, D), BF),
            pltpu.VMEM((slots, D), F32),
            pltpu.SemaphoreType.DMA((count, 4)),
        ],
        compiler_params=ffn_params(),
        cost_estimate=ffn_cost(slots, hidden),
        name="ffn_forward",
    )(rows, *chunks[: count - 1])
    later = pl.BlockSpec((1, slots, SLICE), lambda t: (t + near, 0, 0))
    return pl.pallas_call(
        functools.partial(ffn_forward_kernel, count, near, ff_shard, True),
        grid=(steps - near,),
        out_shape=(jax.ShapeDtypeStruct((slots, D), BF), *tiles),
        in_specs=[fixed((slots, D))] + [ANY_SPEC] * 3 + [fixed((slots, D))] + [ANY_SPEC] * 3,
        out_specs=(fixed((slots, D)),) + (later,) * 3,
        scratch_shapes=[
            pltpu.VMEM((3, (steps - near + MARGIN) * SLICE, D), BF),
            pltpu.VMEM((slots, D), F32),
            pltpu.SemaphoreType.DMA((count, 4)),
        ],
        input_output_aliases={5: 1, 6: 2, 7: 3},
        compiler_params=ffn_params(),
        cost_estimate=ffn_cost(slots, ff_shard),
        name="ffn_forward_last",
    )(rows, *chunks[count - 2 :], part, *kept)


def ffn_backward(grad, act, turn, chunks, ff_shard):
    slots, count = grad.shape[0], len(chunks) - 1
    hidden = count * ff_shard
    steps = hidden // SLICE
    tile = jax.ShapeDtypeStruct((steps, slots, SLICE), BF)
    return pl.pallas_call(
        functools.partial(ffn_backward_kernel, count, ff_shard),
        grid=(steps,),
        out_shape=(jax.ShapeDtypeStruct((slots, D), BF), tile, tile),
        in_specs=[fixed((slots, D))]
        + [stepped((1, slots, SLICE))] * 2
        + [ANY_SPEC] * (count + 1),
        out_specs=(fixed((slots, D)),) + (stepped((1, slots, SLICE)),) * 2,
        scratch_shapes=[
            pltpu.VMEM((3, hidden, D), BF),
            pltpu.VMEM((slots, D), F32),
            pltpu.SemaphoreType.DMA((count, 4)),
        ],
        compiler_params=ffn_params(),
        cost_estimate=ffn_cost(slots, hidden),
        name="ffn_backward",
    )(grad, act, turn, *chunks)


def count_hidden(tiles):
    return tiles.shape[0] * SLICE


def ffn_weights(rows, grad, hid, dgate, dup, first, last, ff_shard):
    slots = rows.shape[0]
    lead = last * ff_shard == count_hidden(dgate)
    base, end = first * ff_shard // SLICE, -(-last * ff_shard // SLICE)
    full = jax.ShapeDtypeStruct((3 * ff_shard, D), BF)
    half = jax.ShapeDtypeStruct((3 * ff_shard // 2, D), BF)
    shapes = [full] * (last - first - 1) + ([half] * 2 if lead else [full])
    tile = pl.BlockSpec((1, slots, SLICE), lambda t: (t + base, 0, 0))
    return pl.pallas_call(
        functools.partial(ffn_weights_kernel, lead, first, ff_shard),
        grid=(end - base,),
        out_shape=tuple(shapes),
        in_specs=[fixed((slots, D))] * 2 + [tile] * 3,
        out_specs=(ANY_SPEC,) * len(shapes),
        scratch_shapes=[
            pltpu.VMEM((3, (end - base) * SLICE, D), BF),
            pltpu.SemaphoreType.DMA((last - first, 4)),
        ],
        compiler_params=ffn_params(),
        cost_estimate=ffn_cost(slots, (end - base) * SLICE),
    )(rows, grad, hid, dgate, dup)


def norm_inverse(x):
    return lax.rsqrt(jnp.mean(x * x, axis=-1, keepdims=True) + EPSILON)


def qkv_forward_kernel(x_ref, scale_ref, wq_ref, wk_ref, wv_ref, out_ref, normed_ref):
    @pl.when(pl.program_id(0) == 0)
    def _():
        x = x_ref[...].astype(F32)
        normed_ref[...] = (x * norm_inverse(x) * scale_ref[...]).astype(BF)

    normed = normed_ref[...]
    for c, w in enumerate((wq_ref, wk_ref, wv_ref)):
        y = jnp.dot(normed, w[...].reshape(D, TILE), preferred_element_type=F32).astype(BF)
        for s in range(2):
            out_ref[s, :, c * HALF : (c + 1) * HALF] = y[:, s * HALF : (s + 1) * HALF]


def qkv_forward(x, scale, gathered, shard):
    tokens = x.shape[0]
    count = D // HALF
    weight = [
        pl.BlockSpec((D // shard, shard, TILE), lambda j, c=c: (0, c, j)) for c in range(3)
    ]
    whole = pl.BlockSpec((tokens, D), lambda j: (0, 0))
    return pl.pallas_call(
        qkv_forward_kernel,
        grid=(count // 2,),
        out_shape=(
            jax.ShapeDtypeStruct((count, tokens, 3 * HALF), BF),
            jax.ShapeDtypeStruct((tokens, D), BF),
        ),
        in_specs=[whole, pl.BlockSpec((1, D), lambda j: (0, 0))] + weight,
        out_specs=(pl.BlockSpec((2, tokens, 3 * HALF), lambda j: (j, 0, 0)), whole),
        compiler_params=ffn_params(),
        cost_estimate=pl.CostEstimate(
            flops=6 * tokens * D * D, bytes_accessed=10 * 10**6, transcendentals=0
        ),
        name="qkv_forward",
    )(x, scale, gathered, gathered, gathered)


def qkv_backward_kernel(
    dq_ref, normed_ref, w_ref, x_ref, scale_ref, mid_ref, kept_ref, pack_ref, gin_ref, gain_ref,
    turned, acc,
):
    step = pl.program_id(0) * pl.num_programs(1) + pl.program_id(1)
    dq = jnp.concatenate([dq_ref[0], dq_ref[1]], axis=1)

    @pl.when(step == 0)
    def _():
        turned[...] = transpose_low(normed_ref[...])

    weights = jnp.dot(turned[...], dq, preferred_element_type=F32).astype(BF)
    pack_ref[...] = weights.reshape(pack_ref.shape)
    more = lax.dot_general(dq, w_ref[...].reshape(D, TILE), NT, preferred_element_type=F32)

    @pl.when(step == 0)
    def _():
        acc[...] = more

    @pl.when(step > 0)
    def _():
        acc[...] += more

    @pl.when(step == pl.num_programs(0) * pl.num_programs(1) - 1)
    def _():
        x = x_ref[...].astype(F32)
        inverse = norm_inverse(x)
        grad = acc[...]
        scaled = grad * scale_ref[...]
        inner = jnp.mean(x * scaled, axis=-1, keepdims=True)
        gin_ref[...] = mid_ref[...] + inverse * scaled - x * (inverse * inverse * inverse * inner)
        gain_ref[...] = jnp.broadcast_to(
            jnp.sum(grad * (x * inverse), axis=0, keepdims=True), gain_ref.shape
        )


def qkv_backward(dq, normed, gathered, x, scale, middle, kept, shard):
    tokens = x.shape[0]
    count = D // HALF
    whole = pl.BlockSpec((tokens, D), lambda j, c: (0, 0))
    weight = pl.BlockSpec((D // shard, shard, TILE), lambda j, c: (0, c, j))
    return pl.pallas_call(
        qkv_backward_kernel,
        grid=(count // 2, 3),
        out_shape=(
            jax.ShapeDtypeStruct(kept.shape, BF),
            jax.ShapeDtypeStruct((tokens, D), F32),
            jax.ShapeDtypeStruct((8, D), F32),
        ),
        in_specs=[
            pl.BlockSpec((2, tokens, HALF), lambda j, c: (j, 0, c)),
            whole,
            weight,
            whole,
            pl.BlockSpec((1, D), lambda j, c: (0, 0)),
            whole,
            ANY_SPEC,
        ],
        out_specs=(weight, whole, pl.BlockSpec((8, D), lambda j, c: (0, 0))),
        scratch_shapes=[pltpu.VMEM((D, tokens), BF), pltpu.VMEM((tokens, D), F32)],
        input_output_aliases={6: 0},
        compiler_params=pltpu.CompilerParams(
            dimension_semantics=("arbitrary", "arbitrary"), vmem_limit_bytes=40 * 1024 * 1024
        ),
        cost_estimate=pl.CostEstimate(
            flops=12 * tokens * D * D, bytes_accessed=25 * 10**6, transcendentals=0
        ),
        name="qkv_backward",
    )(dq, normed, gathered, x, scale, middle, kept)


def local(
    inputs,
    w_qkv,
    w_out,
    attn_gain,
    moe_gain,
    w_router,
    bias_table,
    w_gate,
    w_up,
    w_down,
    routes,
    slot_order,
    group_map,
    buckets,
    grad_output,
):
    tok_count = inputs.shape[0]
    expert_count = w_router.shape[1]
    capacity = (5 * TOPK * tok_count + 4 * expert_count - 1) // (4 * expert_count)
    fsdp_count = lax.axis_size("fsdp")
    fsdp_place = lax.axis_index("fsdp")
    expert_place = lax.axis_index("expert")
    group_count = lax.axis_size("expert") * fsdp_count
    sh = Shape(fsdp_count)
    prompt_rows = sh.part * G_LINE
    slot_total = expert_count * capacity
    shard = w_qkv.shape[0]
    ff_shard = w_down.shape[1]

    def by_prompt(x):
        head = x[:prompt_rows].reshape(sh.part, G_LINE, -1).transpose(1, 0, 2)
        return jnp.concatenate([head.reshape(prompt_rows, -1), x[prompt_rows:]], 0)

    def by_token(x):
        head = x[:prompt_rows].reshape(G_LINE, sh.part, -1).transpose(1, 0, 2)
        return jnp.concatenate([head.reshape(prompt_rows, -1), x[prompt_rows:]], 0)

    own_weights = jnp.concatenate([w_gate[0].T, w_up[0].T, w_down[0]], 0)
    spread = [fsdp_count // 8] * 4
    spread[0] += fsdp_count // 2 - sum(spread)

    def run(ring, count):
        for _ in range(count):
            ring.step()

    small = jnp.concatenate(
        [attn_gain, moe_gain, w_router.reshape(-1), bias_table, group_map.astype(BF)]
    )
    small_rows = -(-small.shape[0] // D)
    small_rows = -(-small_rows // 16) * 16
    small = jnp.pad(small, (0, small_rows * D - small.shape[0])).reshape(small_rows, D)
    pack = jnp.concatenate([w_qkv[:, i * D : (i + 1) * D] for i in range(3)] + [w_out, small], 0)
    gathered = dense_gather(pack, group_count)
    own_weights, tail = tied(own_weights, gathered[:, 4 * shard])
    weights = RingGather(own_weights, fsdp_count)
    run(weights, spread[0])
    fused = sh.width == HALF
    out_full = gathered[:, 3 * shard : 4 * shard].reshape(D, D)
    marks = [0, shard, 2 * shard, 2 * shard + shard * expert_count]
    marks += [marks[-1] + bias_table.shape[0]]
    attn_scale = tail[:, marks[0] : marks[1]].reshape(D).astype(F32)
    moe_scale = tail[:, marks[1] : marks[2]].reshape(D).astype(F32)
    router = tail[:, marks[2] : marks[3]].reshape(D, expert_count).astype(F32)
    table = tail[:, marks[3] : marks[4]].reshape(fsdp_count, sh.hp, BUCKETS)
    my_table = lax.dynamic_index_in_dim(table, fsdp_place, 0, keepdims=False).astype(F32)
    groups = tail[:, marks[4]].reshape(-1, fsdp_count)
    my_groups = lax.dynamic_index_in_dim(groups, expert_place, 0, keepdims=False)
    my_groups = my_groups.astype(jnp.int32)
    bucket = buckets.reshape(SPAN_BLOCKS, HALF)

    token_input = by_prompt(inputs)
    grad_rows_low = by_prompt(grad_output)
    routes = by_prompt(routes)
    slot_order = by_prompt(slot_order)

    input_float = token_input.astype(F32)
    if fused:
        by_heads, normed_low = qkv_forward(token_input, attn_scale[None, :], gathered, shard)
    else:
        qkv_full = jnp.concatenate(
            [gathered[:, i * shard : (i + 1) * shard].reshape(D, D) for i in range(3)], 1
        )
        normed, first_pull = jax.vjp(rms_scale, input_float, attn_scale)
        normed_low = normed.astype(BF)
        qkv_rows = jnp.dot(normed_low, qkv_full, preferred_element_type=F32).astype(BF)
        by_heads = (
            qkv_rows.reshape(tok_count, 3, fsdp_count, sh.width)
            .transpose(2, 0, 1, 3)
            .reshape(fsdp_count, tok_count, 3 * sh.width)
        )
    head_qkv = lax.all_to_all(by_heads, "fsdp", split_axis=0, concat_axis=0, tiled=True)
    run(weights, spread[1])
    head_att, att_turned, att_lse = attend_forward(sh, my_groups, my_table, bucket, head_qkv)
    att_back = lax.all_to_all(head_att, "fsdp", split_axis=0, concat_axis=0, tiled=True)
    run(weights, spread[2])
    run(weights, spread[3])
    attn_low = att_back.transpose(1, 0, 2).reshape(tok_count, D)

    middle = input_float + jnp.dot(attn_low, out_full, preferred_element_type=F32)
    second_normed, second_pull = jax.vjp(rms_scale, middle, moe_scale)
    (gate_pair, losses), router_pull = jax.vjp(
        lambda normed_rows, router_rows: route_local(normed_rows, router_rows, routes),
        second_normed,
        router,
    )
    kept_mask = (slot_order < capacity).astype(F32)
    gate_kept = gate_pair * kept_mask
    slot_ids = jnp.arange(slot_total, dtype=jnp.int32)
    slot_place = jnp.where(slot_order < capacity, routes * capacity + slot_order, -1)
    hot = [slot_place[:, k : k + 1] == slot_ids[None, :] for k in range(TOPK)]
    any_low = (hot[0] | hot[1]).astype(BF)
    outgoing = lax.dot_general(
        any_low, second_normed.astype(BF), TN, preferred_element_type=F32
    ).astype(BF)

    def swap_experts(rows):
        rows = rows.reshape(expert_count, capacity, D)
        rows = lax.all_to_all(rows, "expert", split_axis=0, concat_axis=0, tiled=True)
        return rows.reshape(slot_total, D)

    expert_rows = swap_experts(outgoing)
    slot_gate = jnp.sum(
        jnp.where(hot[0], gate_kept[:, 0:1], 0.0) + jnp.where(hot[1], gate_kept[:, 1:2], 0.0),
        axis=0,
    )
    slot_grad = lax.dot_general(any_low, grad_rows_low, TN, preferred_element_type=F32)
    grad_result = swap_experts((slot_gate[:, None] * slot_grad).astype(BF))

    order = block_order(fsdp_count)
    far = order[-1]
    blocks = [weights.chunks[k] for k in order[:-1]] + list(weights.chunks[far])
    result_rows, act, turn, hidden = ffn_forward(expert_rows, blocks, ff_shard)
    returned = swap_experts(result_rows)
    grad_rows, grad_gate_pre, grad_up_pre = ffn_backward(
        grad_result, act, turn, blocks, ff_shard
    )
    grad_sent = swap_experts(grad_rows)
    halves = (expert_rows, grad_result, hidden, grad_gate_pre, grad_up_pre)
    split = fsdp_count - 3
    early = ffn_weights(*halves, split, fsdp_count, ff_shard)
    late = ffn_weights(*halves, 0, split, ff_shard)
    totals = dict(zip(order[:-1], late + early[:-2]))
    totals[far] = early[-2:]

    def part(k):
        return totals[k]

    sums = RingScatter(part, fsdp_count)
    run(sums, spread[0])

    picked = [
        jnp.dot(h.astype(BF), returned, preferred_element_type=F32) for h in hot
    ]
    block_out = middle + gate_kept[:, 0:1] * picked[0] + gate_kept[:, 1:2] * picked[1]
    output = by_token(block_out.astype(BF))
    grad_final = grad_rows_low.astype(F32)
    grad_pair = (
        jnp.stack([jnp.sum(grad_final * p, axis=-1) for p in picked], -1) * kept_mask
    )
    grad_second = jnp.dot(any_low, grad_sent, preferred_element_type=F32)
    loss_weights = jnp.array([ZLOSS_FACTOR, BALANCE_FACTOR], F32) / group_count
    router_normed, grad_router = router_pull((grad_pair, loss_weights))
    grad_middle_part, grad_moe_gain = second_pull(grad_second + router_normed)
    grad_middle = grad_final + grad_middle_part
    grad_branch = grad_middle.astype(BF)
    grad_attn = lax.dot_general(grad_branch, out_full, NT, preferred_element_type=F32)
    grad_attn = grad_attn.astype(BF)
    head_grad = (
        grad_attn.reshape(tok_count, fsdp_count, sh.width).transpose(1, 0, 2)
    )
    head_grad = lax.all_to_all(head_grad, "fsdp", split_axis=0, concat_axis=0, tiled=True)
    run(sums, spread[1])
    head_grad = sums.tie(head_grad)
    head_dqkv, head_table = attend_backward(
        sh, my_groups, my_table, bucket, head_qkv, head_grad, att_turned, att_lse
    )
    run(sums, spread[2])
    head_dqkv = sums.tie(head_dqkv)
    back_dqkv = lax.all_to_all(head_dqkv, "fsdp", split_axis=0, concat_axis=0, tiled=True)
    sums.step()
    run(sums, spread[3] - 1)
    expert_sums = sums.finish()
    grad_gate = expert_sums[:ff_shard].T
    grad_up = expert_sums[ff_shard : 2 * ff_shard].T
    grad_down = expert_sums[2 * ff_shard :]
    grad_out_w = lax.dot_general(attn_low, grad_branch, TN, preferred_element_type=F32)

    def rows_of(x):
        return x.astype(BF).reshape(group_count, shard, -1)

    place_table = (jnp.arange(fsdp_count) == fsdp_place).astype(F32)
    whole_table = place_table[:, None] * head_table[:, 0][None, :]
    if fused:
        kept = jnp.pad(rows_of(grad_out_w), ((0, 0), (3 * shard, small_rows), (0, 0)))
        kept, grad_inputs, gains = qkv_backward(
            back_dqkv, normed_low, gathered, token_input, attn_scale[None, :], grad_middle, kept,
            shard,
        )
        grad_attn_gain = gains[0]
    else:
        grad_qkv = (
            back_dqkv.reshape(fsdp_count, tok_count, 3, sh.width)
            .transpose(1, 2, 0, 3)
            .reshape(tok_count, 3 * D)
        )
        grad_qkv_w = lax.dot_general(normed_low, grad_qkv, TN, preferred_element_type=F32)
        grad_normed = lax.dot_general(grad_qkv, qkv_full, NT, preferred_element_type=F32)
        grad_input_part, grad_attn_gain = first_pull(grad_normed)
        grad_inputs = grad_middle + grad_input_part
        parts = [rows_of(grad_qkv_w[:, i * D : (i + 1) * D]) for i in range(3)]
        kept = jnp.concatenate(parts + [rows_of(grad_out_w)], 1)
        kept = jnp.pad(kept, ((0, 0), (0, small_rows), (0, 0)))
    smalls = [grad_attn_gain, grad_moe_gain, grad_router, whole_table.reshape(-1)]
    smalls = jnp.concatenate([p.astype(BF).reshape(group_count, -1) for p in smalls], 1)
    smalls = jnp.pad(smalls, ((0, 0), (0, small_rows * D - smalls.shape[1])))
    smalls = smalls.reshape(group_count, small_rows, D)
    sums_dense = dense_sum(lax.dynamic_update_slice(kept, smalls, (0, 4 * shard, 0)))
    grad_inputs = by_token(grad_inputs)
    sum_qkv = jnp.concatenate([sums_dense[i * shard : (i + 1) * shard] for i in range(3)], 1)
    sum_out = sums_dense[3 * shard : 4 * shard]
    sum_small = sums_dense[4 * shard]
    sum_attn = sum_small[marks[0] : marks[1]]
    sum_moe = sum_small[marks[1] : marks[2]]
    sum_router = sum_small[marks[2] : marks[3]].reshape(shard, expert_count)
    sum_table = sum_small[marks[3] : marks[4]]
    return (
        output,
        losses[None, :],
        grad_inputs,
        sum_qkv,
        sum_out,
        sum_attn,
        sum_moe,
        sum_router,
        sum_table,
        grad_gate[None],
        grad_up[None],
        grad_down[None],
    )


def solution(mesh):
    rows = P(("expert", "fsdp"), None)
    flat = P(("expert", "fsdp"))
    cols = P("expert", None, "fsdp")
    deep = P("expert", "fsdp", None)
    in_specs = (
        rows, rows, rows, flat, flat, rows, flat, cols, cols, deep, rows, rows, flat, P(), rows,
    )
    out_specs = (rows, rows, rows, rows, rows, flat, flat, rows, flat, cols, cols, deep)

    return jax.shard_map(local, mesh=mesh, in_specs=in_specs, out_specs=out_specs, check_vma=False)
```
